32 devices in a mesh: seq: 8 (over z, x), row: 4 (over y, core).
Axes of the slice: x: 2, y: 2, z: 4, core: 2. Of those that a mesh axis runs over, the one named last changes fastest.
Arguments:
- tokens: bfloat16 [4, 2048, 1024], P('row', 'seq'), may hold values from -6 to 6
- cotangent: bfloat16 [4, 2048, 1024], P('row', 'seq'), may hold values from -6 to 6
- segment_ids: int32 [4, 2048], P('row'), may hold values from 0 to 15, never falling along the last dimension, each value on 1 to 1536 neighbouring positions
- routes: int32 [4, 2048, 8], P('row', 'seq'), may hold values from 0 to 15, all different within a row; in each aligned block of 256 rows (0 to 255, 256 to 511, ..., all dimensions but the last counted through in order) at most 192 rows name the same one
- norm_attn: float32 [1024], P(('seq', 'row')), may hold values from 0.1 to 1.9
- w_query: float32 [1024, 1024], P(('seq', 'row')), may hold values from -0.75 to 0.75
- key_weight_matrix: float32 [1024, 512], P(('seq', 'row')), may hold values from -0.75 to 0.75
- value_weight_matrix: float32 [1024, 512], P(('seq', 'row')), may hold values from -0.1875 to 0.1875
- w_output: float32 [1024, 1024], P(('seq', 'row')), may hold values from -1.5 to 1.5
- norm_moe: float32 [1024], P(('seq', 'row')), may hold values from 0.1 to 1.9
- w_router: float32 [1024, 16], P(('seq', 'row')), may hold values from -0.09375 to 0.09375
- expert_in: float32 [16384, 1024], P(('seq', 'row')), may hold values from -0.1875 to 0.1875
- expert_out: float32 [16384, 512], P(('seq', 'row')), may hold values from -4 to 4
Outputs:
- layer_out: bfloat16 [4, 2048, 1024], P('row', 'seq')
- grad_tokens: float32 [4, 2048, 1024], P('row', 'seq')
- grad_norm_attn: float32 [1024], P(('seq', 'row'))
- grad_w_query: float32 [1024, 1024], P(('seq', 'row'))
- grad_w_key: float32 [1024, 512], P(('seq', 'row'))
- grad_w_value: float32 [1024, 512], P(('seq', 'row'))
- grad_w_output: float32 [1024, 1024], P(('seq', 'row'))
- grad_norm_moe: float32 [1024], P(('seq', 'row'))
- grad_w_router: float32 [1024, 16], P(('seq', 'row'))
- grad_expert_in: float32 [16384, 1024], P(('seq', 'row'))
- grad_expert_out: float32 [16384, 512], P(('seq', 'row'))
The draws below stay inside these ranges and needn't reach their ends.
Inputs may be any that keep to these rules, and one draw needn't show every extreme that they name: `segment_ids`: along each row the ids never fall; each document (run of equal ids) holds 1 to 1536 tokens, and some document holds exactly 1536. `routes`: each token names 8 different experts; within the 256 tokens of one device (aligned blocks along a row) no expert is named more than 192 times, and in some blocks an expert is named exactly 192 times.
All inputs are finite; a program needn't handle non-finite values.
Results may differ from the reference program's by a relative error of at most 0.019.
The reference program's roundings to bfloat16 on the way count: a program that leaves them out, or rounds other values in their place, can miss the bound.
Values may be sent and summed in bfloat16 or wider, within the bound.
No kernel may reach another device: no remote copies, remote signals or barrier semaphores. Data moves between devices by JAX's collectives and lax.ppermute only.
A program may use at most 320 MiB of HBM per device.

```python
import math
import jax
import jax.numpy as jnp
import numpy as np
from jax import lax

MODEL_WIDTH = 1024
QUERY_HEADS = 16
KEY_VALUE_HEADS = 8
HEAD_SIZE = 64
F = 512
E = 16
TOPK = 8
TOK_DEV = 256
ROW_LEN = 2048
ROWS = 4
CAP = 192
DOCS = 16
DOC_MOST = 1536


def shard_levels(key, shape, cuts, least, high):
    factor_of, own = 1.0, jax.random.fold_in(key, 6)
    for axis_at, blocks in cuts:
        heights = jnp.exp(jax.random.uniform(jax.random.fold_in(own, axis_at), (blocks,), jnp.float32, least / len(cuts), high / len(cuts)))
        factor_of = factor_of * jnp.repeat(heights, shape[axis_at] // blocks).reshape([-1 if axis == axis_at else 1 for axis in range(len(shape))])
    return factor_of


def length_profile(number_of, total, limit, slope):
    portions = [(1 << 20) // math.isqrt(grade ** slope) + 1 for grade in range(2, number_of + 1)]
    surplus, given = total - limit - (number_of - 1), [1] * (number_of - 1)
    while surplus > 0:
        free = [i for i in range(number_of - 1) if given[i] < limit]
        whole, remaining = sum([portions[i] for i in free]), surplus
        for i in free:
            more = min(limit - given[i], max(1, remaining * portions[i] // whole), surplus)
            given[i] = given[i] + more
            surplus = surplus - more
    return np.array([limit] + given)


def uneven_parts(own_key, amount, total, reach, lean):
    if amount == 2:
        one = jax.random.randint(own_key, (), max(1, total - reach), min(reach, total - 1) + 1)
        return jnp.stack([one, total - one])
    tallies = jnp.asarray(length_profile(amount, total, reach, lean), jnp.int32)
    pairs = (amount - 1) // 2
    donor, receiver = tallies[1:1 + 2 * pairs:2], tallies[2:2 + 2 * pairs:2]
    slack = jnp.minimum(donor - 1, reach - receiver)
    shifted = jax.random.randint(jax.random.fold_in(own_key, 1), (pairs,), 0, 1 << 20) % (slack + 1)
    tallies = tallies.at[1:1 + 2 * pairs:2].set(donor - shifted).at[2:2 + 2 * pairs:2].set(receiver + shifted)
    return tallies[jax.random.permutation(jax.random.fold_in(own_key, 2), amount)]


def assign_block(own_key, own, number, rows, amount, top, bound, slope):
    ranking = jax.random.permutation(own_key, amount)
    packed, ordinary = load_shares(amount, rows * top, bound, slope, True), load_shares(amount, rows * top, bound, slope, False)
    places = jnp.arange(amount)

    def named(tallies, offset_by):
        used = int((tallies > 0).sum())
        fixed = max(1, used // 4)
        passed = fixed + (places - fixed + offset_by * (used - fixed)) % max(1, amount - fixed)
        return jnp.zeros((amount,), jnp.int32).at[ranking[jnp.where(places < fixed, places, passed)]].set(jnp.asarray(tallies, jnp.int32))

    tallies = jnp.where(number % 4 == 0, named(packed, number // 4), named(ordinary, number - number // 4 - 1))
    mixed = jax.random.permutation(jax.random.fold_in(own, 3), amount)
    donor, taker = mixed[0:amount // 2 * 2:2], mixed[1:amount // 2 * 2:2]
    slack = jnp.minimum(tallies[donor] - 1, bound - tallies[taker]) // 2
    slack = jnp.where((donor == ranking[0]) | (taker == ranking[0]) | (tallies[taker] == 0), 0, jnp.maximum(slack, 0))
    passed = jax.random.randint(jax.random.fold_in(own, 4), (amount // 2,), 0, 1 << 20) % (slack + 1)
    tallies = tallies.at[donor].add(-passed).at[taker].add(passed)
    members = jnp.searchsorted(jnp.cumsum(tallies), jnp.arange(rows * top), side="right").astype(jnp.int32)
    table = members.reshape(top, rows).T
    table = table[jax.random.permutation(jax.random.fold_in(own, 1), rows)]
    offset_by = jax.random.randint(jax.random.fold_in(own, 2), (rows, 1), 0, top)
    return jnp.take_along_axis(table, (jnp.arange(top)[None, :] + offset_by) % top, axis=1)


def load_shares(number_of, total, most, skew, full):
    loads = [(1 << 20) // math.isqrt(standing ** skew) + 1 for standing in range(1, number_of + 1)]
    largest = most if full else min(most, max(-(-total // number_of), total * loads[0] // sum(loads)))
    least = 1 if total - largest >= number_of - 1 else 0
    given, surplus = [largest] + [least] * (number_of - 1), total - largest - least * (number_of - 1)
    while surplus > 0:
        movable = [i for i in range(1, number_of) if given[i] < largest] or [i for i in range(1, number_of) if given[i] < most]
        mass, budget = sum([loads[i] for i in movable]), surplus
        for i in movable:
            addition = min(most - given[i], max(1, budget * loads[i] // mass), surplus)
            given[i] = given[i] + addition
            surplus = surplus - addition
    return np.array(given)


def noise(key, shape, spread, limit, cuts=(), kind=jnp.bfloat16):
    level = shard_levels(key, shape, cuts, -0.22, 0.18) if cuts else 1.0
    drawn = jax.random.normal(key, shape, jnp.float32) * spread * level
    return jnp.minimum(jnp.maximum(drawn, -limit), limit).astype(kind)


def setup_inputs(seed: int = 0) -> dict:
    keys = jax.random.split(jax.random.key(seed), 14)
    tokens = noise(keys[0], (ROWS, ROW_LEN, MODEL_WIDTH), 1.0, 6.0, ((0, 4), (1, 8)))
    cotangent = noise(keys[1], (ROWS, ROW_LEN, MODEL_WIDTH), 1.0, 6.0, ((0, 4), (1, 8)))
    segment_ids = jax.vmap(lambda own: jnp.searchsorted(jnp.cumsum(uneven_parts(own, DOCS, ROW_LEN, DOC_MOST, 2)), jnp.arange(ROW_LEN), side="right"))(jax.random.split(keys[2], ROWS)).reshape((ROWS, ROW_LEN)).astype(jnp.int32)
    routes_keys = jax.random.split(jax.random.fold_in(keys[3], 1), ROWS * ROW_LEN // TOK_DEV)
    routes_turns = jax.random.permutation(jax.random.fold_in(keys[3], 3), ROWS * ROW_LEN // TOK_DEV)
    routes = jax.vmap(lambda own, number: assign_block(jax.random.fold_in(keys[3], 2), own, number, TOK_DEV, E, TOPK, CAP, 1))(routes_keys, routes_turns).reshape((ROWS, ROW_LEN, TOPK))
    norm_attn = jnp.clip(1.0 + 0.18 * jax.random.normal(keys[4], (MODEL_WIDTH,), jnp.float32), 0.1, 1.9)
    w_query = noise(keys[5], (MODEL_WIDTH, QUERY_HEADS * HEAD_SIZE), (MODEL_WIDTH // 16) ** -0.5, 0.75, ((0, 32),), jnp.float32)
    key_weight_matrix = noise(keys[6], (MODEL_WIDTH, KEY_VALUE_HEADS * HEAD_SIZE), (MODEL_WIDTH // 16) ** -0.5, 0.75, ((0, 32),), jnp.float32)
    value_weight_matrix = noise(keys[7], (MODEL_WIDTH, KEY_VALUE_HEADS * HEAD_SIZE), MODEL_WIDTH ** -0.5, 0.1875, ((0, 32),), jnp.float32)
    w_output = noise(keys[8], (QUERY_HEADS * HEAD_SIZE, MODEL_WIDTH), (MODEL_WIDTH // 64) ** -0.5, 1.5, ((0, 32),), jnp.float32)
    norm_moe = jnp.clip(1.0 + 0.18 * jax.random.normal(keys[9], (MODEL_WIDTH,), jnp.float32), 0.1, 1.9)
    w_router = noise(keys[10], (MODEL_WIDTH, E), (4 * MODEL_WIDTH) ** -0.5, 0.09375, ((0, 32),), jnp.float32)
    expert_in = noise(keys[11], (E * MODEL_WIDTH, 2 * F), MODEL_WIDTH ** -0.5, 0.1875, ((0, 32),), jnp.float32)
    expert_out = noise(keys[12], (E * MODEL_WIDTH, F), (max(F // 256, 1)) ** -0.5, 4.0, ((0, 32),), jnp.float32)
    return dict(tokens=tokens, cotangent=cotangent, segment_ids=segment_ids, routes=routes, norm_attn=norm_attn, w_query=w_query, key_weight_matrix=key_weight_matrix, value_weight_matrix=value_weight_matrix, w_output=w_output, norm_moe=norm_moe, w_router=w_router, expert_in=expert_in, expert_out=expert_out)


NORM_EPS = 1e-06
RESIDUAL_SCALE = 0.22
SCALE_OF_SCORES = 0.015625
ROPE_BASE = 10000.0
NEGATIVE_HUGE = -1e+30
HIGHEST_DOT = lax.Precision.HIGHEST

@jax.custom_vjp
def reduced_precision(v):
    return lax.optimization_barrier(v.astype(jnp.bfloat16)).astype(jnp.float32)

@jax.custom_vjp
def low_back(v):
    return v

def low_keep(v):
    return (reduced_precision(v), None)

def low_pass(kept, grad):
    return (grad,)

def back_keep(v):
    return (v, None)

def back_low(kept, grad):
    return (reduced_precision(grad),)
reduced_precision.defvjp(low_keep, low_pass)
low_back.defvjp(back_keep, back_low)

def doc_positions(seg_row):
    count_all = seg_row.shape[0]
    index_all = jnp.arange(count_all, dtype=jnp.int32)
    changed = jnp.concatenate([jnp.ones((1,), jnp.bool_), seg_row[1:] != seg_row[:-1]])
    starts = jnp.where(changed, index_all, jnp.zeros_like(index_all))
    return (index_all - lax.cummax(starts, axis=0)).astype(jnp.int32)

def rope_tables(positions, head_size):
    half_size = head_size // 2
    freq_scale = jnp.power(ROPE_BASE, -2.0 * jnp.arange(half_size, dtype=jnp.float32) / head_size)
    angle_table = positions.astype(jnp.float32)[:, None] * freq_scale[None, :]
    return (jnp.cos(angle_table), jnp.sin(angle_table))

def apply_rotation_heads(values, cosine_table, sine_table, head_count):
    token_count = values.shape[0]
    shaped = values.reshape(token_count, head_count, -1)
    half_size = shaped.shape[-1] // 2
    first_half = shaped[..., :half_size]
    second_half = shaped[..., half_size:]
    cos_b = cosine_table[:, None, :]
    sin_b = sine_table[:, None, :]
    turned = jnp.concatenate([first_half * cos_b - second_half * sin_b, second_half * cos_b + first_half * sin_b], axis=-1)
    return turned.reshape(token_count, -1)

def rms_scale(values, gain):
    mean_square = lax.optimization_barrier(jnp.mean(values * values, axis=-1, keepdims=True))
    return values * lax.rsqrt(mean_square + NORM_EPS) * gain

def attend_row(rotated_query, rotated_key, value_reduced_precision, seg_row):
    row_length_local = rotated_query.shape[0]
    query_group_width = QUERY_HEADS // KEY_VALUE_HEADS
    heads_of_keys = rotated_key.reshape(row_length_local, KEY_VALUE_HEADS, HEAD_SIZE)
    heads_of_values = value_reduced_precision.reshape(row_length_local, KEY_VALUE_HEADS, HEAD_SIZE)
    positions = jnp.arange(row_length_local, dtype=jnp.int32)
    block_length = math.gcd(row_length_local, 512)

    def one_block(block_index):
        initial_state = (block_index * block_length).astype(jnp.int32)
        query_block_rows = lax.dynamic_slice_in_dim(rotated_query, initial_state, block_length, 0).reshape(block_length, KEY_VALUE_HEADS, query_group_width, HEAD_SIZE)
        seg_query = lax.dynamic_slice_in_dim(seg_row, initial_state, block_length, 0)
        pos_query = lax.dynamic_slice_in_dim(positions, initial_state, block_length, 0)
        scores = jnp.einsum('tkgd,skd->kgts', query_block_rows, heads_of_keys, precision=HIGHEST_DOT) * SCALE_OF_SCORES
        scores = low_back(scores)
        allowed = (seg_query[:, None] == seg_row[None, :]) & (pos_query[:, None] >= positions[None, :])
        masked = jnp.where(allowed, scores, NEGATIVE_HUGE)
        row_top = lax.optimization_barrier(jnp.max(masked, axis=-1, keepdims=True))
        row_total = lax.optimization_barrier(jnp.sum(jnp.where(allowed, jnp.exp(masked - row_top), 0.0), axis=-1, keepdims=True))
        log_total = row_top + jnp.log(row_total)
        probs_low = reduced_precision(jnp.where(allowed, jnp.exp(masked - log_total), 0.0))
        mixed_sum = jnp.einsum('kgts,skd->tkgd', probs_low, heads_of_values, precision=HIGHEST_DOT)
        return mixed_sum.reshape(block_length, QUERY_HEADS * HEAD_SIZE)
    outputs = lax.map(jax.checkpoint(one_block), jnp.arange(row_length_local // block_length, dtype=jnp.int32))
    return outputs.reshape(row_length_local, QUERY_HEADS * HEAD_SIZE)

def experts_row(normed_low, combine, in_stack, out_stack):
    row_length_local = normed_low.shape[0]

    def one_expert(carried, pieces):
        in_one, out_one, weight_col = pieces
        pre_act = low_back(jnp.dot(normed_low, in_one, precision=HIGHEST_DOT))
        hidden = reduced_precision(jax.nn.silu(pre_act[:, :F]) * pre_act[:, F:])
        result = low_back(jnp.dot(hidden, out_one.T, precision=HIGHEST_DOT))
        return (carried + weight_col[:, None] * result, None)
    start_sum = jnp.zeros((row_length_local, MODEL_WIDTH), jnp.float32)
    moe_sum, _ = lax.scan(jax.checkpoint(one_expert), start_sum, (in_stack, out_stack, combine.T))
    return moe_sum

def layer_row(x_row, seg_row, route_row, weights):
    gain_attn, query_w, key_w, value_w, output_w, gain_moe, router_w, in_stack, out_stack = weights
    normed_low = reduced_precision(rms_scale(x_row, gain_attn))
    query_pre = low_back(jnp.dot(normed_low, query_w, precision=HIGHEST_DOT))
    key_before_rotation = low_back(jnp.dot(normed_low, key_w, precision=HIGHEST_DOT))
    value_pre = low_back(jnp.dot(normed_low, value_w, precision=HIGHEST_DOT))
    cosine_table, sine_table = rope_tables(doc_positions(seg_row), HEAD_SIZE)
    rotated_query = reduced_precision(apply_rotation_heads(query_pre, cosine_table, sine_table, QUERY_HEADS))
    rotated_key = reduced_precision(apply_rotation_heads(key_before_rotation, cosine_table, sine_table, KEY_VALUE_HEADS))
    value_reduced_precision = reduced_precision(value_pre)
    attention_result = reduced_precision(low_back(attend_row(rotated_query, rotated_key, value_reduced_precision, seg_row)))
    attn_out = low_back(jnp.dot(attention_result, output_w, precision=HIGHEST_DOT))
    resid = x_row + RESIDUAL_SCALE * attn_out
    normed_two = reduced_precision(rms_scale(resid, gain_moe))
    logits = jnp.dot(normed_two, router_w, precision=HIGHEST_DOT)
    route_hot = (route_row[:, :, None] == jnp.arange(E, dtype=jnp.int32)[None, None, :]).astype(jnp.float32)
    chosen = lax.optimization_barrier(jnp.sum(route_hot * logits[:, None, :], axis=-1))
    gates = jax.nn.softmax(chosen, axis=-1)
    combine = lax.optimization_barrier(jnp.sum(route_hot * gates[:, :, None], axis=1))
    moe_sum = experts_row(normed_two, combine, in_stack, out_stack)
    return resid + RESIDUAL_SCALE * moe_sum

def reference(tokens, cotangent, segment_ids, routes, norm_attn, w_query, key_weight_matrix, value_weight_matrix, w_output, norm_moe, w_router, expert_in, expert_out):

    def forward(x_all, gain_attn, query_w, key_w, value_w, output_w, gain_moe, router_w, in_w, out_w):
        weights = (reduced_precision(gain_attn), reduced_precision(query_w), reduced_precision(key_w), reduced_precision(value_w), reduced_precision(output_w), reduced_precision(gain_moe), reduced_precision(router_w), reduced_precision(in_w).reshape(E, MODEL_WIDTH, 2 * F), reduced_precision(out_w).reshape(E, MODEL_WIDTH, F))

        def per_row(pieces):
            x_row, seg_row, route_row = pieces
            return layer_row(x_row, seg_row, route_row, weights)
        return lax.map(jax.checkpoint(per_row), (x_all, segment_ids, routes))
    primal = (tokens.astype(jnp.float32), norm_attn, w_query, key_weight_matrix, value_weight_matrix, w_output, norm_moe, w_router, expert_in, expert_out)
    layer_sum, pullback = jax.vjp(forward, *primal)
    gradients = pullback(cotangent.astype(jnp.float32))
    return (layer_sum.astype(jnp.bfloat16), gradients[0], gradients[1], gradients[2], gradients[3], gradients[4], gradients[5], gradients[6], gradients[7], gradients[8], gradients[9])
```

```python
import math

import jax
import jax.numpy as jnp
from jax import lax
from jax.sharding import Mesh, PartitionSpec as P

QUERY_HEADS = 16
KEY_VALUE_HEADS = 8
HEAD_SIZE = 64
F = 512
E = 16
GROUPS = 4
EXPERTS_HERE = E // GROUPS

NORM_EPS = 1e-06
RESIDUAL_SCALE = 0.22
SCALE_OF_SCORES = 0.015625
ROPE_BASE = 10000.0
NEGATIVE_HUGE = -1e30
HIGHEST_DOT = lax.Precision.HIGHEST

PLANE = ("b", "row")
SEQ = ("a", "b")
ALL = ("a", "b", "row")


def rope_tables(positions, head_size):
    half_size = head_size // 2
    freq_scale = jnp.power(ROPE_BASE, -2.0 * jnp.arange(half_size, dtype=jnp.float32) / head_size)
    angle_table = positions.astype(jnp.float32)[:, None] * freq_scale[None, :]
    return (jnp.cos(angle_table), jnp.sin(angle_table))


def apply_rotation_heads(values, cosine_table, sine_table, head_count):
    token_count = values.shape[0]
    shaped = values.reshape(token_count, head_count, -1)
    half_size = shaped.shape[-1] // 2
    first_half = shaped[..., :half_size]
    second_half = shaped[..., half_size:]
    cos_b = cosine_table[:, None, :]
    sin_b = sine_table[:, None, :]
    turned = jnp.concatenate(
        [first_half * cos_b - second_half * sin_b, second_half * cos_b + first_half * sin_b],
        axis=-1,
    )
    return turned.reshape(token_count, -1)


def reverse_rotation_heads(grads_in, cosine_table, sine_table, head_count):
    return apply_rotation_heads(grads_in, cosine_table, -sine_table, head_count)


def rms_scale(values, gain):
    mean_square = jnp.mean(values * values, axis=-1, keepdims=True)
    return values * lax.rsqrt(mean_square + NORM_EPS) * gain


def rms_back(values, gain, grad_norm):
    mean_square = jnp.mean(values * values, axis=-1, keepdims=True)
    inverse = lax.rsqrt(mean_square + NORM_EPS)
    scaled_grad = grad_norm * gain
    grad_values = inverse * scaled_grad - values * inverse**3 * jnp.mean(
        values * scaled_grad, axis=-1, keepdims=True
    )
    grad_gain = jnp.sum(grad_norm * values * inverse, axis=0)
    return (grad_values, grad_gain)


def contract_rows(left_side, right_side):
    return lax.dot_general(
        left_side, right_side, (((0,), (0,)), ((), ())), preferred_element_type=jnp.float32
    )


def contract_cols(left_side, right_side):
    return lax.dot_general(
        left_side, right_side, (((1,), (1,)), ((), ())), preferred_element_type=jnp.float32
    )


def gather(x, axes):
    return lax.all_gather(x, axes, axis=0, tiled=True)


def scatter_sum(x, axes):
    return lax.psum_scatter(x, axes, scatter_dimension=0, tiled=True)


def pad_lanes(x, lanes):
    return jnp.pad(x, ((0, 0), (0, lanes - x.shape[1])))


def dense_sum(x):
    rows, cols = x.shape
    groups, plane = lax.axis_size("a"), lax.axis_size(PLANE)
    own = rows // (groups * plane)
    x = x.reshape(groups, plane, own, cols).transpose(1, 0, 2, 3).reshape(rows, cols)
    return scatter_sum(scatter_sum(x, PLANE), "a").astype(jnp.float32)


def body(
    tokens,
    cotangent,
    segment_ids,
    routes,
    norm_attn,
    w_query,
    key_weight_matrix,
    value_weight_matrix,
    w_output,
    norm_moe,
    w_router,
    expert_in,
    expert_out,
):
    bf16 = jnp.bfloat16
    x_local = tokens[0].astype(jnp.float32)
    token_count, width = x_local.shape
    seg_row = segment_ids[0]
    row_length_local = seg_row.shape[0]
    query_group_width = QUERY_HEADS // KEY_VALUE_HEADS
    group = lax.axis_index("a")
    seq_index = lax.axis_index(SEQ)
    tok_start = seq_index * token_count
    positions = tok_start + jnp.arange(token_count, dtype=jnp.int32)
    seg_local = lax.dynamic_slice_in_dim(seg_row, tok_start, token_count)
    doc_start = jnp.sum((seg_row[None, :] < seg_local[:, None]).astype(jnp.int32), axis=1)
    rope_local = positions - doc_start

    qkv_width = 2 * QUERY_HEADS * HEAD_SIZE
    first_pack = jnp.concatenate(
        [
            w_query.astype(bf16),
            key_weight_matrix.astype(bf16),
            value_weight_matrix.astype(bf16),
            pad_lanes(norm_attn.astype(bf16)[:, None], 128),
        ],
        axis=1,
    )
    second_pack = jnp.concatenate(
        [
            w_output.astype(bf16),
            pad_lanes(
                jnp.concatenate([w_router.astype(bf16), norm_moe.astype(bf16)[:, None]], axis=1),
                128,
            ),
        ],
        axis=1,
    )
    first_all = gather(first_pack, ALL)
    second_all = gather(second_pack, ALL)
    qkv_w = first_all[:, :qkv_width]
    gain_one_f = first_all[:, qkv_width].astype(jnp.float32)
    output_w = second_all[:, :width]
    router_w = second_all[:, width : width + E]
    gain_two_f = second_all[:, width + E].astype(jnp.float32)

    normed_one = rms_scale(x_local, gain_one_f).astype(bf16)
    qkv_pre = jnp.dot(normed_one, qkv_w, preferred_element_type=jnp.float32)
    q_width = QUERY_HEADS * HEAD_SIZE
    kv_width = KEY_VALUE_HEADS * HEAD_SIZE
    cosine_table, sine_table = rope_tables(rope_local, HEAD_SIZE)
    rotated_query = apply_rotation_heads(
        qkv_pre[:, :q_width], cosine_table, sine_table, QUERY_HEADS
    ).astype(bf16)
    rotated_key = apply_rotation_heads(
        qkv_pre[:, q_width : q_width + kv_width], cosine_table, sine_table, KEY_VALUE_HEADS
    ).astype(bf16)
    value_reduced_precision = qkv_pre[:, q_width + kv_width :].astype(bf16)
    kv_all = gather(jnp.concatenate([rotated_key, value_reduced_precision], axis=1), SEQ)
    key_all, value_all = kv_all[:, :kv_width], kv_all[:, kv_width:]

    out_w = gather(expert_out.astype(bf16), PLANE).reshape(EXPERTS_HERE, width, F)
    in_w = gather(expert_in.astype(bf16), PLANE).reshape(EXPERTS_HERE, width, 2 * F)
    grad_all = gather(cotangent[0], "a")
    routes_all = gather(routes[0], "a")

    heads_of_queries = rotated_query.reshape(
        token_count, KEY_VALUE_HEADS, query_group_width, HEAD_SIZE
    )
    block_of_keys = math.gcd(row_length_local, 512)
    first_key = doc_start[0]
    lower_triangle_block = first_key // block_of_keys
    upper_triangle_block = (tok_start + token_count - 1) // block_of_keys + 1

    def block_scores(block_index):
        key_start = block_index * block_of_keys
        key_blk = lax.dynamic_slice_in_dim(key_all, key_start, block_of_keys).reshape(
            block_of_keys, KEY_VALUE_HEADS, HEAD_SIZE
        )
        value_blk = lax.dynamic_slice_in_dim(value_all, key_start, block_of_keys).reshape(
            block_of_keys, KEY_VALUE_HEADS, HEAD_SIZE
        )
        key_pos = key_start + jnp.arange(block_of_keys, dtype=jnp.int32)
        scores = (
            jnp.einsum(
                "tkgd,skd->kgts", heads_of_queries, key_blk, preferred_element_type=jnp.float32
            )
            * SCALE_OF_SCORES
        )
        allowed = (doc_start[:, None] <= key_pos[None, :]) & (
            positions[:, None] >= key_pos[None, :]
        )
        return (scores, allowed, key_blk, value_blk)

    def max_step(block_index, carried):
        running_max, running_sum = carried
        scores, allowed, _, _ = block_scores(block_index)
        masked = jnp.where(allowed, scores, NEGATIVE_HUGE)
        new_max = jnp.maximum(running_max, jnp.max(masked, axis=-1))
        fresh = jnp.sum(jnp.where(allowed, jnp.exp(masked - new_max[..., None]), 0.0), axis=-1)
        return (new_max, running_sum * jnp.exp(running_max - new_max) + fresh)

    initial_maximum = jnp.full(
        (KEY_VALUE_HEADS, query_group_width, token_count), NEGATIVE_HUGE, jnp.float32
    )
    initial_running_sum = jnp.zeros((KEY_VALUE_HEADS, query_group_width, token_count), jnp.float32)
    final_max, final_total = lax.fori_loop(
        lower_triangle_block, upper_triangle_block, max_step, (initial_maximum, initial_running_sum)
    )
    log_total = final_max + jnp.log(final_total)

    def mixing_update(block_index, mixed_sum):
        scores, allowed, _, value_blk = block_scores(block_index)
        probs_low = jnp.where(allowed, jnp.exp(scores - log_total[..., None]), 0.0).astype(
            bf16
        )
        return mixed_sum + jnp.einsum(
            "kgts,skd->tkgd", probs_low, value_blk, preferred_element_type=jnp.float32
        )

    attention_result = lax.fori_loop(
        lower_triangle_block,
        upper_triangle_block,
        mixing_update,
        jnp.zeros((token_count, KEY_VALUE_HEADS, query_group_width, HEAD_SIZE), jnp.float32),
    ).reshape(token_count, q_width)
    attended_low = attention_result.astype(bf16)
    attn_out = jnp.dot(attended_low, output_w, preferred_element_type=jnp.float32)
    resid = x_local + RESIDUAL_SCALE * attn_out
    normed_two = rms_scale(resid, gain_two_f).astype(bf16)

    normed_all = gather(normed_two, "a")
    expert_ids = jnp.arange(E, dtype=jnp.int32)
    routed = jnp.any(routes_all[:, :, None] == expert_ids[None, None, :], axis=1)
    logits = jnp.dot(normed_all, router_w, preferred_element_type=jnp.float32)
    top_logit = jnp.max(jnp.where(routed, logits, NEGATIVE_HUGE), axis=-1, keepdims=True)
    weights = jnp.where(routed, jnp.exp(jnp.minimum(logits - top_logit, 0.0)), 0.0)
    gates_all = weights / jnp.sum(weights, axis=-1, keepdims=True)
    gates_group = lax.dynamic_slice_in_dim(gates_all, group * EXPERTS_HERE, EXPERTS_HERE, 1)
    gate_cols = gates_group.T[:, :, None]

    grad_hidden = jnp.einsum(
        "td,edf->etf", grad_all, out_w, preferred_element_type=jnp.float32
    )
    pre_act = jnp.einsum("td,edf->etf", normed_all, in_w, preferred_element_type=jnp.float32)
    gate_pre = pre_act[..., :F]
    up_pre = pre_act[..., F:]
    gate_sig = jax.nn.sigmoid(gate_pre)
    gate_act = gate_pre * gate_sig
    hidden = gate_act * up_pre
    gated_hidden = (gate_cols * hidden).astype(bf16)
    grad_gates = RESIDUAL_SCALE * jnp.sum(
        hidden.astype(bf16).astype(jnp.float32) * grad_hidden, axis=-1
    )
    scaled_grad = (RESIDUAL_SCALE * gate_cols) * grad_hidden
    grad_gate = scaled_grad * up_pre * (gate_sig + gate_pre * gate_sig * (1.0 - gate_sig))
    grad_up = scaled_grad * gate_act
    grad_pre = jnp.concatenate([grad_gate, grad_up], axis=-1).astype(bf16)

    back_part = jnp.einsum("etf,edf->td", grad_pre, in_w, preferred_element_type=jnp.float32)
    gate_grads = jnp.zeros((gates_all.shape[0], E), jnp.float32)
    gate_grads = lax.dynamic_update_slice_in_dim(
        gate_grads, grad_gates.T, group * EXPERTS_HERE, 1
    )
    gate_high = gate_grads.astype(bf16)
    gate_low = (gate_grads - lax.reduce_precision(gate_grads, 8, 7)).astype(bf16)
    back_own = scatter_sum(
        jnp.concatenate(
            [back_part.astype(bf16), pad_lanes(jnp.concatenate([gate_high, gate_low], 1), 128)],
            axis=1,
        ),
        "a",
    ).astype(jnp.float32)
    moe_part = jnp.einsum("etf,edf->td", gated_hidden, out_w, preferred_element_type=jnp.float32)
    moe_sum = scatter_sum(moe_part.astype(bf16), "a").astype(jnp.float32)
    layer_sum = resid + RESIDUAL_SCALE * moe_sum

    grad_in_part = jnp.einsum("td,etf->edf", normed_all, grad_pre, preferred_element_type=jnp.float32)
    grad_out_part = RESIDUAL_SCALE * jnp.einsum(
        "td,etf->edf", grad_all, gated_hidden, preferred_element_type=jnp.float32
    )
    grad_expert_in = scatter_sum(
        grad_in_part.astype(bf16).reshape(EXPERTS_HERE * width, 2 * F), PLANE
    ).astype(jnp.float32)
    grad_expert_out = scatter_sum(
        grad_out_part.astype(bf16).reshape(EXPERTS_HERE * width, F), PLANE
    ).astype(jnp.float32)

    grad_out = cotangent[0].astype(jnp.float32)
    gates = lax.dynamic_slice_in_dim(gates_all, group * token_count, token_count)
    gate_grads_own = back_own[:, width : width + E] + back_own[:, width + E : width + 2 * E]
    grad_logits = gates * (
        gate_grads_own - jnp.sum(gates * gate_grads_own, axis=-1, keepdims=True)
    )
    grad_normed_two = back_own[:, :width] + jnp.dot(
        grad_logits, router_w.astype(jnp.float32).T, precision=HIGHEST_DOT
    )
    grad_router = jnp.dot(normed_two.astype(jnp.float32).T, grad_logits, precision=HIGHEST_DOT)
    grad_resid_norm, grad_gain_two = rms_back(resid, gain_two_f, grad_normed_two)
    grad_resid = grad_out + grad_resid_norm
    grad_attn_low = (RESIDUAL_SCALE * grad_resid).astype(bf16)
    grad_output_w = contract_rows(attended_low, grad_attn_low)
    second_sum = dense_sum(
        jnp.concatenate(
            [
                grad_output_w.astype(bf16),
                pad_lanes(
                    jnp.concatenate([grad_router, grad_gain_two[:, None]], axis=1), 128
                ).astype(bf16),
            ],
            axis=1,
        )
    )
    gradient_attention_lowered = contract_cols(grad_attn_low, output_w).astype(bf16)
    gradient_of_heads = gradient_attention_lowered.reshape(
        token_count, KEY_VALUE_HEADS, query_group_width, HEAD_SIZE
    )
    row_delta = jnp.sum(
        gradient_of_heads.astype(jnp.float32)
        * attention_result.reshape(token_count, KEY_VALUE_HEADS, query_group_width, HEAD_SIZE),
        axis=-1,
    )
    delta_heads = jnp.transpose(row_delta, (1, 2, 0))

    def back_step(block_index, carried):
        grad_query, grad_keys, grad_values = carried
        scores, allowed, key_blk, value_blk = block_scores(block_index)
        probs = jnp.where(allowed, jnp.exp(scores - log_total[..., None]), 0.0)
        probs_low = probs.astype(bf16)
        grad_probs = jnp.einsum(
            "tkgd,skd->kgts", gradient_of_heads, value_blk, preferred_element_type=jnp.float32
        )
        grad_scores = (probs * (grad_probs - delta_heads[..., None])).astype(bf16)
        grad_query = grad_query + jnp.einsum(
            "kgts,skd->tkgd", grad_scores, key_blk, preferred_element_type=jnp.float32
        )
        key_part = jnp.einsum(
            "kgts,tkgd->skd", grad_scores, heads_of_queries, preferred_element_type=jnp.float32
        ).reshape(block_of_keys, kv_width)
        value_part = jnp.einsum(
            "kgts,tkgd->skd", probs_low, gradient_of_heads, preferred_element_type=jnp.float32
        ).reshape(block_of_keys, kv_width)
        key_start = block_index * block_of_keys
        grad_keys = lax.dynamic_update_slice_in_dim(grad_keys, key_part, key_start, 0)
        grad_values = lax.dynamic_update_slice_in_dim(grad_values, value_part, key_start, 0)
        return (grad_query, grad_keys, grad_values)

    start_grads = (
        jnp.zeros((token_count, KEY_VALUE_HEADS, query_group_width, HEAD_SIZE), jnp.float32),
        jnp.zeros((row_length_local, kv_width), jnp.float32),
        jnp.zeros((row_length_local, kv_width), jnp.float32),
    )
    grad_query, grad_keys, grad_values = lax.fori_loop(
        lower_triangle_block, upper_triangle_block, back_step, start_grads
    )
    kv_own = scatter_sum(
        jnp.concatenate([grad_keys.astype(bf16), grad_values.astype(bf16)], axis=1), SEQ
    ).astype(jnp.float32)
    grad_query_pre = reverse_rotation_heads(
        grad_query.reshape(token_count, q_width) * SCALE_OF_SCORES,
        cosine_table,
        sine_table,
        QUERY_HEADS,
    ).astype(bf16)
    gradient_key_unrotated = reverse_rotation_heads(
        kv_own[:, :kv_width] * SCALE_OF_SCORES, cosine_table, sine_table, KEY_VALUE_HEADS
    ).astype(bf16)
    grad_value_pre = kv_own[:, kv_width:].astype(bf16)
    grad_qkv = jnp.concatenate([grad_query_pre, gradient_key_unrotated, grad_value_pre], axis=1)
    grad_qkv_w = contract_rows(normed_one, grad_qkv)
    grad_normed_one = contract_cols(grad_qkv, qkv_w)
    grad_x_norm, grad_gain_one = rms_back(x_local, gain_one_f, grad_normed_one)
    grad_input = grad_resid + grad_x_norm
    first_sum = dense_sum(
        jnp.concatenate(
            [grad_qkv_w.astype(bf16), pad_lanes(grad_gain_one[:, None], 128).astype(bf16)], axis=1
        )
    )
    return (
        layer_sum.astype(bf16)[None],
        grad_input[None],
        first_sum[:, qkv_width],
        first_sum[:, :q_width],
        first_sum[:, q_width : q_width + kv_width],
        first_sum[:, q_width + kv_width : qkv_width],
        second_sum[:, :width],
        second_sum[:, width + E],
        second_sum[:, width : width + E],
        grad_expert_in,
        grad_expert_out,
    )


def solution(mesh):
    seq, row = mesh.shape["seq"], mesh.shape["row"]
    cut = Mesh(mesh.devices.reshape(GROUPS, seq // GROUPS, row), ("a", "b", "row"))
    token_spec = P("row", SEQ, None)
    row_spec = P(ALL, None)
    flat_spec = P(ALL)
    in_specs = (
        token_spec,
        token_spec,
        P("row", None),
        token_spec,
        flat_spec,
        row_spec,
        row_spec,
        row_spec,
        row_spec,
        flat_spec,
        row_spec,
        row_spec,
        row_spec,
    )
    out_specs = (
        token_spec,
        token_spec,
        flat_spec,
        row_spec,
        row_spec,
        row_spec,
        row_spec,
        flat_spec,
        row_spec,
        row_spec,
        row_spec,
    )
    return jax.shard_map(body, mesh=cut, in_specs=in_specs, out_specs=out_specs, check_vma=False)
```

```python
import functools

import jax
import jax.numpy as jnp
from jax import lax
from jax.experimental import pallas as pl
from jax.experimental.pallas import tpu as pltpu
from jax.sharding import Mesh, PartitionSpec as P

QUERY_HEADS = 16
KEY_VALUE_HEADS = 8
HEAD_SIZE = 64
F = 512
E = 16
GROUPS = 4
EXPERTS_HERE = E // GROUPS
LANES = 128
PAIR = 2 * HEAD_SIZE
HEAD_PACK = 4 * HEAD_SIZE
BLOCK = 256

NORM_EPS = 1e-06
RESIDUAL_SCALE = 0.22
SCALE_OF_SCORES = 0.015625
ROPE_BASE = 10000.0
NEGATIVE_HUGE = -1e30
HIGHEST_DOT = lax.Precision.HIGHEST
VMEM_LIMIT = 60 * 1024 * 1024

PLANE = ("b", "y", "c")
SEQ = ("a", "b")
ALL = ("a", "b", "y", "c")

f32 = jnp.float32
bf16 = jnp.bfloat16


def rotation_tables(positions, with_values):
    half = HEAD_SIZE // 2
    freq = jnp.power(ROPE_BASE, -2.0 * jnp.arange(half, dtype=f32) / HEAD_SIZE)
    angle = positions.astype(f32)[:, None] * freq[None, :]
    cos, sin = jnp.cos(angle), jnp.sin(angle)
    cos, sin = jnp.concatenate([cos, cos], 1), jnp.concatenate([-sin, sin], 1)
    return (
        jnp.concatenate([cos, cos, cos, jnp.ones_like(cos)], 1),
        jnp.concatenate([sin, sin, sin, jnp.zeros_like(sin)], 1),
    )


def rms_back(values, gain, grad_norm):
    mean_square = jnp.mean(values * values, axis=-1, keepdims=True)
    inverse = lax.rsqrt(mean_square + NORM_EPS)
    scaled_grad = grad_norm * gain
    grad_values = inverse * scaled_grad - values * inverse**3 * jnp.mean(
        values * scaled_grad, axis=-1, keepdims=True
    )
    grad_gain = jnp.sum(grad_norm * values * inverse, axis=0)
    return (grad_values, grad_gain)


def rms_scale(values, gain):
    mean_square = jnp.mean(values * values, axis=-1, keepdims=True)
    return values * lax.rsqrt(mean_square + NORM_EPS) * gain


def contract_rows(left_side, right_side):
    return lax.dot_general(
        left_side, right_side, (((0,), (0,)), ((), ())), preferred_element_type=f32
    )


def contract_cols(left_side, right_side):
    return lax.dot_general(
        left_side, right_side, (((1,), (1,)), ((), ())), preferred_element_type=f32
    )


def gather(x, axes):
    return lax.all_gather(x, axes, axis=0, tiled=True)


def scatter_sum(x, axes):
    return lax.psum_scatter(x, axes, scatter_dimension=0, tiled=True)


def pad_lanes(x, lanes):
    return jnp.pad(x, ((0, 0), (0, lanes - x.shape[1])))


def chain_gather(x, axis):
    n, me = lax.axis_size(axis), lax.axis_index(axis)
    up = down = x
    ups, downs = [None], [None]
    for _ in range(n - 1):
        up = lax.ppermute(up, axis, [(i, i + 1) for i in range(n - 1)])
        down = lax.ppermute(down, axis, [(i + 1, i) for i in range(n - 1)])
        ups.append(up)
        downs.append(down)
    out = jnp.zeros((n,) + x.shape, x.dtype)
    out = lax.dynamic_update_index_in_dim(out, x, me, 0)
    for k in range(1, n):
        piece = jnp.where(me >= k, ups[k], downs[n - k])
        out = lax.dynamic_update_index_in_dim(out, piece, (me - k) % n, 0)
    return out.reshape((n * x.shape[0],) + x.shape[1:])


def halve(v, axis):
    if lax.axis_size(axis) != 2:
        return scatter_sum(v, axis)
    me = lax.axis_index(axis)
    v = v.reshape((2, v.shape[0] // 2) + v.shape[1:])
    other = lax.ppermute(lax.dynamic_index_in_dim(v, 1 - me, 0, False), axis, [(0, 1), (1, 0)])
    own = lax.dynamic_index_in_dim(v, me, 0, False)
    return (own.astype(f32) + other.astype(f32)).astype(v.dtype)


def line_sum(v, axis):
    n, me = lax.axis_size(axis), lax.axis_index(axis)
    v = v.reshape((n, v.shape[0] // n) + v.shape[1:])
    total = lax.dynamic_index_in_dim(v, me, 0, False).astype(f32)
    for k in range(n - 1, 0, -1):
        for step in (k, -k):
            pairs = [(i, i + step) for i in range(n) if 0 <= i + step < n]
            block = lax.dynamic_index_in_dim(v, jnp.clip(me + step, 0, n - 1), 0, False)
            total = total + lax.ppermute(block, axis, pairs).astype(f32)
    return total


def rows_for(x, order):
    sizes = tuple(lax.axis_size(axis) for axis in ALL)
    shape = sizes + (x.shape[0] // lax.axis_size(ALL),) + x.shape[1:]
    moved = [ALL.index(axis) for axis in order] + list(range(4, len(shape)))
    return x.reshape(shape).transpose(moved).reshape(x.shape)


def rotate_lanes(x, cos, sin):
    width = x.shape[-1]
    lane = lax.broadcasted_iota(jnp.int32, x.shape, x.ndim - 1)
    swapped = jnp.where(
        lane % HEAD_SIZE < HEAD_SIZE // 2,
        pltpu.roll(x, width - HEAD_SIZE // 2, x.ndim - 1),
        pltpu.roll(x, HEAD_SIZE // 2, x.ndim - 1),
    )
    return x * cos + swapped * sin


def project_kernel(x_ref, gain_ref, w_ref, cos_ref, sin_ref, qkv_ref, normed_ref):
    @pl.when(pl.program_id(0) == 0)
    def _():
        x = x_ref[...].astype(f32)
        gain = jnp.transpose(gain_ref[...].astype(f32))[0:1, :]
        normed_ref[...] = rms_scale(x, gain).astype(bf16)

    pre = jnp.dot(normed_ref[...], w_ref[...], preferred_element_type=f32)
    qkv_ref[0] = rotate_lanes(pre, cos_ref[...], sin_ref[...]).astype(bf16)


def project(x, packed, cos, sin):
    tokens, width = x.shape
    whole = pl.BlockSpec((tokens, width), lambda h: (0, 0))
    table = pl.BlockSpec((tokens, HEAD_PACK), lambda h: (0, 0))
    gain_at = KEY_VALUE_HEADS * HEAD_PACK // LANES
    return pl.pallas_call(
        project_kernel,
        grid=(KEY_VALUE_HEADS,),
        in_specs=[
            whole,
            pl.BlockSpec((width, LANES), lambda h: (0, gain_at)),
            pl.BlockSpec((width, HEAD_PACK), lambda h: (0, h)),
            table,
            table,
        ],
        out_specs=[pl.BlockSpec((1, tokens, HEAD_PACK), lambda h: (h, 0, 0)), whole],
        out_shape=[
            jax.ShapeDtypeStruct((KEY_VALUE_HEADS, tokens, HEAD_PACK), bf16),
            jax.ShapeDtypeStruct((tokens, width), bf16),
        ],
        compiler_params=pltpu.CompilerParams(vmem_limit_bytes=VMEM_LIMIT),
        cost_estimate=pl.CostEstimate(
            flops=2 * tokens * width * KEY_VALUE_HEADS * HEAD_PACK,
            bytes_accessed=6 * 2**20,
            transcendentals=0,
        ),
        name="project",
    )(x, packed, packed, cos, sin)


def lower_lanes(shape):
    return lax.broadcasted_iota(jnp.int32, shape, len(shape) - 1) < HEAD_SIZE


def both_heads_low(pair):
    low = lower_lanes(pair.shape)
    return jnp.concatenate(
        [jnp.where(low, pair, 0.0), jnp.where(low, pltpu.roll(pair, HEAD_SIZE, 1), 0.0)], axis=0
    )


def both_heads_high(pair):
    low = lower_lanes(pair.shape)
    return jnp.concatenate(
        [jnp.where(low, 0.0, pltpu.roll(pair, HEAD_SIZE, 1)), jnp.where(low, 0.0, pair)], axis=0
    )


def allowed_pairs(shape, query_start, key_start, doc):
    rows = lax.broadcasted_iota(jnp.int32, (shape[0] // 2, 1), 0) + query_start
    rows = jnp.concatenate([rows, rows], axis=0)
    keys = lax.broadcasted_iota(jnp.int32, shape, 1) + key_start
    return (keys >= jnp.concatenate([doc, doc], axis=0)) & (keys <= rows)


def attend_kernel(bounds_ref, q_ref, kv_ref, doc_ref, o_ref, low_ref, lse_ref, top, total, acc):
    i = pl.program_id(0)
    steps = pl.num_programs(0)
    offset = bounds_ref[steps]
    q = both_heads_low(q_ref[...].astype(f32) * SCALE_OF_SCORES).astype(bf16)
    doc = doc_ref[...]
    top[...] = jnp.full_like(top, NEGATIVE_HUGE)
    total[...] = jnp.zeros_like(total)
    acc[...] = jnp.zeros_like(acc)

    def step(j, carried):
        start = pl.multiple_of(j * BLOCK, BLOCK)
        kv = kv_ref[pl.ds(start, BLOCK), :]
        scores = contract_cols(q, kv)
        allowed = allowed_pairs(scores.shape, (i + offset) * BLOCK, j * BLOCK, doc)
        scores = jnp.where(allowed, scores, NEGATIVE_HUGE)
        old = top[...]
        new = jnp.maximum(old, jnp.max(scores, axis=1, keepdims=True))
        probs = jnp.exp(scores - new)
        keep = jnp.exp(old - new)
        top[...] = new
        total[...] = total[...] * keep + jnp.sum(probs, axis=1, keepdims=True)
        acc[...] = acc[...] * keep + jnp.dot(probs.astype(bf16), kv, preferred_element_type=f32)
        return carried

    lax.fori_loop(bounds_ref[i], i + offset + 1, step, 0)
    mixed = acc[...] / total[...]
    first, second = mixed[:BLOCK], mixed[BLOCK:]
    out = jnp.where(lower_lanes(first.shape), pltpu.roll(first, HEAD_SIZE, 1), second)
    o_ref[...] = out
    low_ref[...] = out.astype(bf16)
    lse_ref[0] = top[...] + jnp.log(total[...])


def attend(bounds, qkv, kv, kv_at, doc):
    queries, keys = qkv.shape[0], kv.shape[0]
    steps = queries // BLOCK
    pair = pl.BlockSpec((BLOCK, PAIR), lambda i, s: (i, 0))
    return pl.pallas_call(
        attend_kernel,
        grid_spec=pltpu.PrefetchScalarGridSpec(
            num_scalar_prefetch=1,
            grid=(steps,),
            in_specs=[
                pair,
                pl.BlockSpec((keys, PAIR), lambda i, s: (0, kv_at)),
                pl.BlockSpec((BLOCK, 1), lambda i, s: (i, 0)),
            ],
            out_specs=[pair, pair, pl.BlockSpec((1, 2 * BLOCK, 1), lambda i, s: (i, 0, 0))],
            scratch_shapes=[
                pltpu.VMEM((2 * BLOCK, 1), f32),
                pltpu.VMEM((2 * BLOCK, 1), f32),
                pltpu.VMEM((2 * BLOCK, PAIR), f32),
            ],
        ),
        out_shape=[
            jax.ShapeDtypeStruct((queries, PAIR), f32),
            jax.ShapeDtypeStruct((queries, PAIR), bf16),
            jax.ShapeDtypeStruct((steps, 2 * BLOCK, 1), f32),
        ],
        compiler_params=pltpu.CompilerParams(vmem_limit_bytes=VMEM_LIMIT),
        cost_estimate=pl.CostEstimate(
            flops=4 * queries * keys * PAIR, bytes_accessed=6 * 2**20, transcendentals=queries * keys
        ),
        name="attend",
    )(bounds, qkv, kv, doc)


def attend_back_kernel(
    bounds_ref, q_ref, kv_ref, doc_ref, do_ref, o_ref, lse_ref, dq_ref, dkv_ref, acc
):
    i = pl.program_id(0)
    steps = pl.num_programs(0)
    offset = bounds_ref[steps]

    @pl.when(i == 0)
    def _():
        dkv_ref[...] = jnp.zeros_like(dkv_ref)

    q = both_heads_low(q_ref[...].astype(f32) * SCALE_OF_SCORES).astype(bf16)
    grad = do_ref[...].astype(f32)
    product = grad * o_ref[...]
    low = lower_lanes(product.shape)
    delta = jnp.concatenate(
        [
            jnp.sum(jnp.where(low, product, 0.0), axis=1, keepdims=True),
            jnp.sum(jnp.where(low, 0.0, product), axis=1, keepdims=True),
        ],
        axis=0,
    )
    grad = both_heads_high(grad).astype(bf16)
    sources = jnp.concatenate([q, grad], axis=0)
    doc = doc_ref[...]
    lse = lse_ref[0]
    acc[...] = jnp.zeros_like(acc)

    def step(j, carried):
        start = pl.multiple_of(j * BLOCK, BLOCK)
        kv = kv_ref[pl.ds(start, BLOCK), :]
        scores = contract_cols(q, kv)
        allowed = allowed_pairs(scores.shape, (i + offset) * BLOCK, j * BLOCK, doc)
        probs = jnp.exp(jnp.where(allowed, scores - lse, NEGATIVE_HUGE))
        grad_probs = contract_cols(grad, kv)
        grad_scores = (probs * (grad_probs - delta)).astype(bf16)
        acc[...] += jnp.dot(grad_scores, kv, preferred_element_type=f32)
        both = jnp.concatenate([grad_scores, probs.astype(bf16)], axis=0)
        dkv_ref[pl.ds(start, BLOCK), :] += contract_rows(both, sources)
        return carried

    lax.fori_loop(bounds_ref[i], i + offset + 1, step, 0)
    first, second = acc[:BLOCK], acc[BLOCK:]
    dq_ref[...] = jnp.where(lower_lanes(first.shape), first, pltpu.roll(second, HEAD_SIZE, 1))


def attend_back(bounds, qkv, kv, kv_at, doc, grad, out, lse):
    queries, keys = qkv.shape[0], kv.shape[0]
    steps = queries // BLOCK
    pair = pl.BlockSpec((BLOCK, PAIR), lambda i, s: (i, 0))
    return pl.pallas_call(
        attend_back_kernel,
        grid_spec=pltpu.PrefetchScalarGridSpec(
            num_scalar_prefetch=1,
            grid=(steps,),
            in_specs=[
                pair,
                pl.BlockSpec((keys, PAIR), lambda i, s: (0, kv_at)),
                pl.BlockSpec((BLOCK, 1), lambda i, s: (i, 0)),
                pair,
                pair,
                pl.BlockSpec((1, 2 * BLOCK, 1), lambda i, s: (i, 0, 0)),
            ],
            out_specs=[pair, pl.BlockSpec((keys, PAIR), lambda i, s: (0, 0))],
            scratch_shapes=[pltpu.VMEM((2 * BLOCK, PAIR), f32)],
        ),
        out_shape=[
            jax.ShapeDtypeStruct((queries, PAIR), f32),
            jax.ShapeDtypeStruct((keys, PAIR), f32),
        ],
        compiler_params=pltpu.CompilerParams(vmem_limit_bytes=VMEM_LIMIT),
        cost_estimate=pl.CostEstimate(
            flops=10 * queries * keys * PAIR,
            bytes_accessed=8 * 2**20,
            transcendentals=queries * keys,
        ),
        name="attend_back",
    )(bounds, qkv, kv, doc, grad, out, lse)


def unrotate_kernel(dq_ref, dkv_ref, cos_ref, sin_ref, out_ref):
    cos, sin = cos_ref[...], sin_ref[...]
    dq = rotate_lanes(dq_ref[...] * SCALE_OF_SCORES, cos[:, :PAIR], -sin[:, :PAIR])
    dkv = rotate_lanes(dkv_ref[...], cos[:, PAIR:], -sin[:, PAIR:])
    out_ref[...] = jnp.concatenate([dq, dkv], axis=1).astype(bf16)


def unrotate(dq, dkv, cos, sin):
    rows = dq.shape[0]
    pair = pl.BlockSpec((2 * BLOCK, PAIR), lambda i: (i, 0))
    pack = pl.BlockSpec((2 * BLOCK, HEAD_PACK), lambda i: (i, 0))
    return pl.pallas_call(
        unrotate_kernel,
        grid=(rows // (2 * BLOCK),),
        in_specs=[pair, pair, pack, pack],
        out_specs=pack,
        out_shape=jax.ShapeDtypeStruct((rows, HEAD_PACK), bf16),
        cost_estimate=pl.CostEstimate(
            flops=rows * HEAD_PACK * 8, bytes_accessed=rows * HEAD_PACK * 14, transcendentals=0
        ),
        name="unrotate",
    )(dq, dkv, cos, sin)


def exchange(x, axes):
    return lax.all_to_all(x, axes, 0, 0, tiled=True)


def body(
    tokens,
    cotangent,
    segment_ids,
    routes,
    norm_attn,
    w_query,
    key_weight_matrix,
    value_weight_matrix,
    w_output,
    norm_moe,
    w_router,
    expert_in,
    expert_out,
):
    x_local = tokens[0].astype(f32)
    token_count, width = x_local.shape
    seg_row = segment_ids[0]
    group = lax.axis_index("a")
    head_axes = SEQ if lax.axis_size(SEQ) == KEY_VALUE_HEADS else ("b",)
    whole_rows = head_axes == SEQ
    span = token_count * KEY_VALUE_HEADS
    span_start = 0 if whole_rows else group * span
    tok_start = lax.axis_index(SEQ) * token_count

    def start_of_doc(ids):
        return jnp.sum((seg_row[None, :] < ids[:, None]).astype(jnp.int32), axis=1)

    seg_local = lax.dynamic_slice_in_dim(seg_row, tok_start, token_count)
    rope_local = tok_start + jnp.arange(token_count, dtype=jnp.int32) - start_of_doc(seg_local)
    cos_local, sin_local = rotation_tables(rope_local, True)
    seg_span = lax.dynamic_slice_in_dim(seg_row, span_start, span)
    doc_span = start_of_doc(seg_span)
    cos_span, sin_span = rotation_tables(
        span_start + jnp.arange(span, dtype=jnp.int32) - doc_span, True
    )
    bounds = jnp.concatenate(
        [
            doc_span.reshape(-1, BLOCK)[:, 0] // BLOCK,
            jnp.full((1,), span_start // BLOCK, jnp.int32),
        ]
    )
    doc_column = doc_span[:, None]

    own_rows = w_query.shape[0]
    by_head = jnp.concatenate(
        [
            w_query.astype(bf16).reshape(own_rows, KEY_VALUE_HEADS, PAIR),
            key_weight_matrix.astype(bf16).reshape(own_rows, KEY_VALUE_HEADS, HEAD_SIZE),
            value_weight_matrix.astype(bf16).reshape(own_rows, KEY_VALUE_HEADS, HEAD_SIZE),
        ],
        axis=2,
    ).reshape(own_rows, KEY_VALUE_HEADS * HEAD_PACK)
    qkv_width = KEY_VALUE_HEADS * HEAD_PACK
    first_all = gather(
        jnp.concatenate([by_head, pad_lanes(norm_attn.astype(bf16)[:, None], LANES)], axis=1), ALL
    )
    second_all = gather(
        jnp.concatenate(
            [
                w_output.astype(bf16),
                pad_lanes(
                    jnp.concatenate([w_router.astype(bf16), norm_moe.astype(bf16)[:, None]], axis=1),
                    LANES,
                ),
            ],
            axis=1,
        ),
        ALL,
    )
    experts_low = jnp.concatenate([expert_in.astype(bf16), expert_out.astype(bf16)], axis=1)
    experts_all = gather(experts_low, PLANE).reshape(EXPERTS_HERE, width, 3 * F)
    in_w, out_w = experts_all[:, :, : 2 * F], experts_all[:, :, 2 * F :]
    output_w = second_all[:, :width]
    router_w = second_all[:, width : width + E]
    gain_two_f = second_all[:, width + E].astype(f32)
    gain_one_f = first_all[:, qkv_width].astype(f32)

    expert_ids = jnp.arange(E, dtype=jnp.int32)
    routed_own = jnp.any(routes[0][:, :, None] == expert_ids[None, None, :], axis=1)
    early_all = chain_gather(
        jnp.concatenate([cotangent[0], pad_lanes(routed_own.astype(bf16), LANES)], axis=1), "a"
    )
    grad_all = early_all[:, :width]
    routed = early_all[:, width : width + E] > 0.5

    by_heads, normed_one = project(tokens[0], first_all, cos_local, sin_local)
    qkv = exchange(by_heads, head_axes).reshape(span, HEAD_PACK)
    if whole_rows:
        kv, kv_at = qkv, 1
    else:
        kv, kv_at = gather(qkv[:, PAIR:], "a"), 0
    attention_result, attended, log_total = attend(bounds, qkv, kv, kv_at, doc_column)
    attended_low = (
        exchange(attended.reshape(KEY_VALUE_HEADS, token_count, PAIR), head_axes)
        .transpose(1, 0, 2)
        .reshape(token_count, QUERY_HEADS * HEAD_SIZE)
    )
    attn_out = jnp.dot(attended_low, output_w, preferred_element_type=f32)
    resid = x_local + RESIDUAL_SCALE * attn_out
    normed_two = rms_scale(resid, gain_two_f).astype(bf16)

    normed_all = gather(normed_two, "a")
    logits = jnp.dot(normed_all, router_w, preferred_element_type=f32)
    top_logit = jnp.max(jnp.where(routed, logits, NEGATIVE_HUGE), axis=-1, keepdims=True)
    weights = jnp.where(routed, jnp.exp(jnp.minimum(logits - top_logit, 0.0)), 0.0)
    gates_all = weights / jnp.sum(weights, axis=-1, keepdims=True)
    gates_group = lax.dynamic_slice_in_dim(gates_all, group * EXPERTS_HERE, EXPERTS_HERE, 1)
    gate_cols = gates_group.T[:, :, None]

    grad_hidden = jnp.einsum("td,edf->etf", grad_all, out_w, preferred_element_type=f32)
    pre_act = jnp.einsum("td,edf->etf", normed_all, in_w, preferred_element_type=f32)
    gate_pre = pre_act[..., :F]
    up_pre = pre_act[..., F:]
    gate_sig = jax.nn.sigmoid(gate_pre)
    gate_act = gate_pre * gate_sig
    hidden = gate_act * up_pre
    gated_hidden = (gate_cols * hidden).astype(bf16)
    grad_gates = RESIDUAL_SCALE * jnp.sum(hidden.astype(bf16).astype(f32) * grad_hidden, axis=-1)
    scaled_grad = (RESIDUAL_SCALE * gate_cols) * grad_hidden
    grad_gate = scaled_grad * up_pre * (gate_sig + gate_pre * gate_sig * (1.0 - gate_sig))
    grad_up = scaled_grad * gate_act
    grad_pre = jnp.concatenate([grad_gate, grad_up], axis=-1).astype(bf16)

    back_part = jnp.einsum("etf,edf->td", grad_pre, in_w, preferred_element_type=f32)
    gate_grads = jnp.zeros((gates_all.shape[0], E), f32)
    gate_grads = lax.dynamic_update_slice_in_dim(gate_grads, grad_gates.T, group * EXPERTS_HERE, 1)
    gate_high = gate_grads.astype(bf16)
    gate_low = (gate_grads - lax.reduce_precision(gate_grads, 8, 7)).astype(bf16)
    back_own = scatter_sum(
        jnp.concatenate(
            [back_part.astype(bf16), pad_lanes(jnp.concatenate([gate_high, gate_low], 1), LANES)],
            axis=1,
        ),
        "a",
    ).astype(f32)

    grad_in_part = jnp.einsum("td,etf->edf", normed_all, grad_pre, preferred_element_type=f32)
    grad_out_part = RESIDUAL_SCALE * jnp.einsum(
        "td,etf->edf", grad_all, gated_hidden, preferred_element_type=f32
    )
    grad_experts = scatter_sum(
        jnp.concatenate([grad_in_part.astype(bf16), grad_out_part.astype(bf16)], axis=2).reshape(
            EXPERTS_HERE * width, 3 * F
        ),
        PLANE,
    ).astype(f32)
    moe_part = jnp.einsum("etf,edf->td", gated_hidden, out_w, preferred_element_type=f32)
    moe_sum = scatter_sum(moe_part.astype(bf16), "a").astype(f32)
    layer_sum = resid + RESIDUAL_SCALE * moe_sum

    grad_out = cotangent[0].astype(f32)
    gates = lax.dynamic_slice_in_dim(gates_all, group * token_count, token_count)
    gate_grads_own = back_own[:, width : width + E] + back_own[:, width + E : width + 2 * E]
    grad_logits = gates * (gate_grads_own - jnp.sum(gates * gate_grads_own, axis=-1, keepdims=True))
    grad_normed_two = back_own[:, :width] + jnp.dot(
        grad_logits, router_w.astype(f32).T, precision=HIGHEST_DOT
    )
    grad_router = jnp.dot(normed_two.astype(f32).T, grad_logits, precision=HIGHEST_DOT)
    grad_resid_norm, grad_gain_two = rms_back(resid, gain_two_f, grad_normed_two)
    grad_resid = grad_out + grad_resid_norm
    grad_attn_low = (RESIDUAL_SCALE * grad_resid).astype(bf16)
    grad_heads = contract_cols(grad_attn_low, output_w).astype(bf16)
    grad_mixed = exchange(
        grad_heads.reshape(token_count, KEY_VALUE_HEADS, PAIR).transpose(1, 0, 2), head_axes
    ).reshape(span, PAIR)
    grad_q, grad_kv = attend_back(
        bounds, qkv, kv, kv_at, doc_column, grad_mixed, attention_result, log_total
    )
    if not whole_rows:
        grad_kv = scatter_sum(grad_kv.astype(bf16), "a").astype(f32)
    grad_qkv = (
        exchange(
            unrotate(grad_q, grad_kv, cos_span, sin_span).reshape(
                KEY_VALUE_HEADS, token_count, HEAD_PACK
            ),
            head_axes,
        )
        .transpose(1, 0, 2)
        .reshape(token_count, qkv_width)
    )
    grad_normed_one = contract_cols(grad_qkv, first_all[:, :qkv_width])
    grad_x_norm, grad_gain_one = rms_back(x_local, gain_one_f, grad_normed_one)
    grad_input = grad_resid + grad_x_norm

    orders = (("c", "y", "b", "a"), ("c", "b", "y", "a"))
    cut = 3 * qkv_width // 4
    small = jnp.concatenate([grad_router, grad_gain_one[:, None], grad_gain_two[:, None]], axis=1)

    def weight_rows(acts, grads, order):
        return contract_rows(acts, grads).astype(bf16)

    left = jnp.concatenate(
        [
            rows_for(contract_rows(normed_one, grad_qkv[:, :cut]).astype(bf16), orders[0]),
            rows_for(pad_lanes(small, LANES).astype(bf16), orders[0]),
        ],
        axis=1,
    )
    right = jnp.concatenate(
        [
            rows_for(contract_rows(normed_one, grad_qkv[:, cut:]).astype(bf16), orders[1]),
            rows_for(contract_rows(attended_low, grad_attn_low).astype(bf16), orders[1]),
        ],
        axis=1,
    )
    left, right = halve(left, "c"), halve(right, "c")
    left, right = halve(left, "y"), halve(right, "b")
    left, right = halve(left, "b"), halve(right, "y")
    total = line_sum(jnp.concatenate([left, right], axis=1), "a")
    small_sum = total[:, cut : cut + LANES]
    qkv_sum = jnp.concatenate(
        [total[:, :cut], total[:, cut + LANES : qkv_width + LANES]], axis=1
    ).reshape(own_rows, KEY_VALUE_HEADS, HEAD_PACK)
    return (
        layer_sum.astype(bf16)[None],
        grad_input[None],
        small_sum[:, E],
        qkv_sum[:, :, :PAIR].reshape(own_rows, -1),
        qkv_sum[:, :, PAIR : PAIR + HEAD_SIZE].reshape(own_rows, -1),
        qkv_sum[:, :, PAIR + HEAD_SIZE :].reshape(own_rows, -1),
        total[:, qkv_width + LANES :],
        small_sum[:, E + 1],
        small_sum[:, :E],
        grad_experts[:, : 2 * F],
        grad_experts[:, 2 * F :],
    )


def solution(mesh):
    seq, row = mesh.shape["seq"], mesh.shape["row"]
    cut = Mesh(mesh.devices.reshape(GROUPS, seq // GROUPS, row // 2, 2), ALL)
    token_spec = P(("y", "c"), SEQ, None)
    row_spec = P(ALL, None)
    flat_spec = P(ALL)
    in_specs = (
        token_spec,
        token_spec,
        P(("y", "c"), None),
        token_spec,
        flat_spec,
        row_spec,
        row_spec,
        row_spec,
        row_spec,
        flat_spec,
        row_spec,
        row_spec,
        row_spec,
    )
    out_specs = (
        token_spec,
        token_spec,
        flat_spec,
        row_spec,
        row_spec,
        row_spec,
        row_spec,
        flat_spec,
        row_spec,
        row_spec,
        row_spec,
    )
    return jax.shard_map(body, mesh=cut, in_specs=in_specs, out_specs=out_specs, check_vma=False)
```

```python
import jax
import jax.numpy as jnp
from jax import lax
from jax.experimental import pallas as pl
from jax.experimental.pallas import tpu as pltpu
from jax.sharding import Mesh, PartitionSpec as P

QUERY_HEADS = 16
KEY_VALUE_HEADS = 8
HEAD_SIZE = 64
F = 512
E = 16
GROUPS = 4
EXPERTS_HERE = E // GROUPS
LANES = 128
PAIR = 2 * HEAD_SIZE
HEAD_PACK = 4 * HEAD_SIZE
BLOCK = 256

NORM_EPS = 1e-06
RESIDUAL_SCALE = 0.22
SCALE_OF_SCORES = 0.015625
ROPE_BASE = 10000.0
NEGATIVE_HUGE = -1e30
HIGHEST_DOT = lax.Precision.HIGHEST
VMEM_LIMIT = 60 * 1024 * 1024

PLANE = ("b", "y", "c")
SEQ = ("a", "b")
ALL = ("a", "b", "y", "c")

f32 = jnp.float32
bf16 = jnp.bfloat16


def rotation_tables(positions, with_values):
    half = HEAD_SIZE // 2
    freq = jnp.power(ROPE_BASE, -2.0 * jnp.arange(half, dtype=f32) / HEAD_SIZE)
    angle = positions.astype(f32)[:, None] * freq[None, :]
    cos, sin = jnp.cos(angle), jnp.sin(angle)
    cos, sin = jnp.concatenate([cos, cos], 1), jnp.concatenate([-sin, sin], 1)
    return (
        jnp.concatenate([cos, cos, cos, jnp.ones_like(cos)], 1),
        jnp.concatenate([sin, sin, sin, jnp.zeros_like(sin)], 1),
    )


def rms_back(values, gain, grad_norm):
    mean_square = jnp.mean(values * values, axis=-1, keepdims=True)
    inverse = lax.rsqrt(mean_square + NORM_EPS)
    scaled_grad = grad_norm * gain
    grad_values = inverse * scaled_grad - values * inverse**3 * jnp.mean(
        values * scaled_grad, axis=-1, keepdims=True
    )
    grad_gain = jnp.sum(grad_norm * values * inverse, axis=0)
    return (grad_values, grad_gain)


def rms_scale(values, gain):
    mean_square = jnp.mean(values * values, axis=-1, keepdims=True)
    return values * lax.rsqrt(mean_square + NORM_EPS) * gain


def contract_rows(left_side, right_side):
    return lax.dot_general(
        left_side, right_side, (((0,), (0,)), ((), ())), preferred_element_type=f32
    )


def contract_cols(left_side, right_side):
    return lax.dot_general(
        left_side, right_side, (((1,), (1,)), ((), ())), preferred_element_type=f32
    )


def gather(x, axes):
    return lax.all_gather(x, axes, axis=0, tiled=True)


def scatter_sum(x, axes):
    return lax.psum_scatter(x, axes, scatter_dimension=0, tiled=True)


def pad_lanes(x, lanes):
    return jnp.pad(x, ((0, 0), (0, lanes - x.shape[1])))


def chain_gather(x, axis):
    n, me = lax.axis_size(axis), lax.axis_index(axis)
    up = down = x
    ups, downs = [None], [None]
    for _ in range(n - 1):
        up = lax.ppermute(up, axis, [(i, i + 1) for i in range(n - 1)])
        down = lax.ppermute(down, axis, [(i + 1, i) for i in range(n - 1)])
        ups.append(up)
        downs.append(down)
    out = jnp.zeros((n,) + x.shape, x.dtype)
    out = lax.dynamic_update_index_in_dim(out, x, me, 0)
    for k in range(1, n):
        piece = jnp.where(me >= k, ups[k], downs[n - k])
        out = lax.dynamic_update_index_in_dim(out, piece, (me - k) % n, 0)
    return out.reshape((n * x.shape[0],) + x.shape[1:])


def halve(v, axis):
    if lax.axis_size(axis) != 2:
        return scatter_sum(v, axis)
    me = lax.axis_index(axis)
    v = v.reshape((2, v.shape[0] // 2) + v.shape[1:])
    other = lax.ppermute(lax.dynamic_index_in_dim(v, 1 - me, 0, False), axis, [(0, 1), (1, 0)])
    own = lax.dynamic_index_in_dim(v, me, 0, False)
    return (own.astype(f32) + other.astype(f32)).astype(v.dtype)


def rows_for(x, order):
    sizes = tuple(lax.axis_size(axis) for axis in ALL)
    shape = sizes + (x.shape[0] // lax.axis_size(ALL),) + x.shape[1:]
    moved = [ALL.index(axis) for axis in order] + list(range(4, len(shape)))
    return x.reshape(shape).transpose(moved).reshape(x.shape)


def rotate_lanes(x, cos, sin):
    width = x.shape[-1]
    lane = lax.broadcasted_iota(jnp.int32, x.shape, x.ndim - 1)
    swapped = jnp.where(
        lane % HEAD_SIZE < HEAD_SIZE // 2,
        pltpu.roll(x, width - HEAD_SIZE // 2, x.ndim - 1),
        pltpu.roll(x, HEAD_SIZE // 2, x.ndim - 1),
    )
    return x * cos + swapped * sin


def project_kernel(x_ref, gain_ref, w_ref, cos_ref, sin_ref, qkv_ref, normed_ref):
    @pl.when(pl.program_id(0) == 0)
    def _():
        x = x_ref[...].astype(f32)
        gain = jnp.transpose(gain_ref[...].astype(f32))[E : E + 1, :]
        normed_ref[...] = rms_scale(x, gain).astype(bf16)

    pre = jnp.dot(normed_ref[...], w_ref[...], preferred_element_type=f32)
    qkv_ref[0] = rotate_lanes(pre, cos_ref[...], sin_ref[...]).astype(bf16)


def project(x, packed, cos, sin):
    tokens, width = x.shape
    whole = pl.BlockSpec((tokens, width), lambda h: (0, 0))
    table = pl.BlockSpec((tokens, HEAD_PACK), lambda h: (0, 0))
    gain_at = packed.shape[1] // LANES - 1
    return pl.pallas_call(
        project_kernel,
        grid=(KEY_VALUE_HEADS,),
        in_specs=[
            whole,
            pl.BlockSpec((width, LANES), lambda h: (0, gain_at)),
            pl.BlockSpec((width, HEAD_PACK), lambda h: (0, h)),
            table,
            table,
        ],
        out_specs=[pl.BlockSpec((1, tokens, HEAD_PACK), lambda h: (h, 0, 0)), whole],
        out_shape=[
            jax.ShapeDtypeStruct((KEY_VALUE_HEADS, tokens, HEAD_PACK), bf16),
            jax.ShapeDtypeStruct((tokens, width), bf16),
        ],
        compiler_params=pltpu.CompilerParams(vmem_limit_bytes=VMEM_LIMIT),
        cost_estimate=pl.CostEstimate(
            flops=2 * tokens * width * KEY_VALUE_HEADS * HEAD_PACK,
            bytes_accessed=6 * 2**20,
            transcendentals=0,
        ),
        name="project",
    )(x, packed, packed, cos, sin)


def lower_lanes(shape):
    return lax.broadcasted_iota(jnp.int32, shape, len(shape) - 1) < HEAD_SIZE


def both_heads_low(pair):
    low = lower_lanes(pair.shape)
    return jnp.concatenate(
        [jnp.where(low, pair, 0.0), jnp.where(low, pltpu.roll(pair, HEAD_SIZE, 1), 0.0)], axis=0
    )


def both_heads_high(pair):
    low = lower_lanes(pair.shape)
    return jnp.concatenate(
        [jnp.where(low, 0.0, pltpu.roll(pair, HEAD_SIZE, 1)), jnp.where(low, 0.0, pair)], axis=0
    )


def allowed_pairs(shape, query_start, key_start, doc):
    rows = lax.broadcasted_iota(jnp.int32, (shape[0] // 2, 1), 0) + query_start
    rows = jnp.concatenate([rows, rows], axis=0)
    keys = lax.broadcasted_iota(jnp.int32, shape, 1) + key_start
    return (keys >= jnp.concatenate([doc, doc], axis=0)) & (keys <= rows)


def attend_kernel(bounds_ref, q_ref, kv_ref, doc_ref, o_ref, low_ref, lse_ref, kept, top, total, acc):
    i = pl.program_id(0)
    steps = pl.num_programs(0)
    offset = bounds_ref[steps]
    first, last = bounds_ref[i], i + offset + 1
    q = both_heads_low(q_ref[...].astype(f32) * SCALE_OF_SCORES).astype(bf16)
    doc = doc_ref[...]
    top[...] = jnp.full_like(top, NEGATIVE_HUGE)
    total[...] = jnp.zeros_like(total)
    acc[...] = jnp.zeros_like(acc)

    def score(j, carried):
        start = pl.multiple_of(j * BLOCK, BLOCK)
        scores = contract_cols(q, kv_ref[pl.ds(start, BLOCK), :])
        allowed = allowed_pairs(scores.shape, (i + offset) * BLOCK, j * BLOCK, doc)
        scores = jnp.where(allowed, scores, NEGATIVE_HUGE)
        kept[:, pl.ds(start, BLOCK)] = scores
        top[...] = jnp.maximum(top[...], jnp.maximum(scores[:, :LANES], scores[:, LANES:]))
        return carried

    lax.fori_loop(first, last, score, 0)
    highest = jnp.max(top[...], axis=1, keepdims=True)

    def mix(j, carried):
        start = pl.multiple_of(j * BLOCK, BLOCK)
        probs = jnp.exp(kept[:, pl.ds(start, BLOCK)] - highest)
        total[...] += probs[:, :LANES] + probs[:, LANES:]
        acc[...] += jnp.dot(
            probs.astype(bf16), kv_ref[pl.ds(start, BLOCK), :], preferred_element_type=f32
        )
        return carried

    lax.fori_loop(first, last, mix, 0)
    row_total = jnp.sum(total[...], axis=1, keepdims=True)
    mixed = acc[...] / row_total
    first_head, second_head = mixed[:BLOCK], mixed[BLOCK:]
    out = jnp.where(
        lower_lanes(first_head.shape), pltpu.roll(first_head, HEAD_SIZE, 1), second_head
    )
    o_ref[...] = out
    low_ref[...] = out.astype(bf16)
    lse_ref[0] = highest + jnp.log(row_total)


def attend(bounds, qkv, kv, kv_at, doc):
    queries, keys = qkv.shape[0], kv.shape[0]
    steps = queries // BLOCK
    pair = pl.BlockSpec((BLOCK, PAIR), lambda i, s: (i, 0))
    return pl.pallas_call(
        attend_kernel,
        grid_spec=pltpu.PrefetchScalarGridSpec(
            num_scalar_prefetch=1,
            grid=(steps,),
            in_specs=[
                pair,
                pl.BlockSpec((keys, PAIR), lambda i, s: (0, kv_at)),
                pl.BlockSpec((BLOCK, 1), lambda i, s: (i, 0)),
            ],
            out_specs=[pair, pair, pl.BlockSpec((1, 2 * BLOCK, 1), lambda i, s: (i, 0, 0))],
            scratch_shapes=[
                pltpu.VMEM((2 * BLOCK, keys), f32),
                pltpu.VMEM((2 * BLOCK, LANES), f32),
                pltpu.VMEM((2 * BLOCK, LANES), f32),
                pltpu.VMEM((2 * BLOCK, PAIR), f32),
            ],
        ),
        out_shape=[
            jax.ShapeDtypeStruct((queries, PAIR), f32),
            jax.ShapeDtypeStruct((queries, PAIR), bf16),
            jax.ShapeDtypeStruct((steps, 2 * BLOCK, 1), f32),
        ],
        compiler_params=pltpu.CompilerParams(vmem_limit_bytes=VMEM_LIMIT),
        cost_estimate=pl.CostEstimate(
            flops=4 * queries * keys * PAIR, bytes_accessed=6 * 2**20, transcendentals=queries * keys
        ),
        name="attend",
    )(bounds, qkv, kv, doc)


def attend_back_kernel(
    bounds_ref, q_ref, kv_ref, doc_ref, do_ref, o_ref, lse_ref, dq_ref, dkv_ref, acc
):
    i = pl.program_id(0)
    steps = pl.num_programs(0)
    offset = bounds_ref[steps]

    @pl.when(i == 0)
    def _():
        dkv_ref[...] = jnp.zeros_like(dkv_ref)

    q = both_heads_low(q_ref[...].astype(f32) * SCALE_OF_SCORES).astype(bf16)
    grad = do_ref[...].astype(f32)
    product = grad * o_ref[...]
    low = lower_lanes(product.shape)
    delta = jnp.concatenate(
        [
            jnp.sum(jnp.where(low, product, 0.0), axis=1, keepdims=True),
            jnp.sum(jnp.where(low, 0.0, product), axis=1, keepdims=True),
        ],
        axis=0,
    )
    grad = both_heads_high(grad).astype(bf16)
    sources = jnp.concatenate([q, grad], axis=0)
    doc = doc_ref[...]
    lse = lse_ref[0]
    acc[...] = jnp.zeros_like(acc)

    def step(j, carried):
        start = pl.multiple_of(j * BLOCK, BLOCK)
        kv = kv_ref[pl.ds(start, BLOCK), :]
        scores = contract_cols(q, kv)
        allowed = allowed_pairs(scores.shape, (i + offset) * BLOCK, j * BLOCK, doc)
        probs = jnp.exp(jnp.where(allowed, scores - lse, NEGATIVE_HUGE))
        grad_probs = contract_cols(grad, kv)
        grad_scores = (probs * (grad_probs - delta)).astype(bf16)
        acc[...] += jnp.dot(grad_scores, kv, preferred_element_type=f32)
        both = jnp.concatenate([grad_scores, probs.astype(bf16)], axis=0)
        dkv_ref[pl.ds(start, BLOCK), :] += contract_rows(both, sources)
        return carried

    lax.fori_loop(bounds_ref[i], i + offset + 1, step, 0)
    first, second = acc[:BLOCK], acc[BLOCK:]
    dq_ref[...] = jnp.where(lower_lanes(first.shape), first, pltpu.roll(second, HEAD_SIZE, 1))


def attend_back(bounds, qkv, kv, kv_at, doc, grad, out, lse):
    queries, keys = qkv.shape[0], kv.shape[0]
    steps = queries // BLOCK
    pair = pl.BlockSpec((BLOCK, PAIR), lambda i, s: (i, 0))
    return pl.pallas_call(
        attend_back_kernel,
        grid_spec=pltpu.PrefetchScalarGridSpec(
            num_scalar_prefetch=1,
            grid=(steps,),
            in_specs=[
                pair,
                pl.BlockSpec((keys, PAIR), lambda i, s: (0, kv_at)),
                pl.BlockSpec((BLOCK, 1), lambda i, s: (i, 0)),
                pair,
                pair,
                pl.BlockSpec((1, 2 * BLOCK, 1), lambda i, s: (i, 0, 0)),
            ],
            out_specs=[pair, pl.BlockSpec((keys, PAIR), lambda i, s: (0, 0))],
            scratch_shapes=[pltpu.VMEM((2 * BLOCK, PAIR), f32)],
        ),
        out_shape=[
            jax.ShapeDtypeStruct((queries, PAIR), f32),
            jax.ShapeDtypeStruct((keys, PAIR), f32),
        ],
        compiler_params=pltpu.CompilerParams(vmem_limit_bytes=VMEM_LIMIT),
        cost_estimate=pl.CostEstimate(
            flops=10 * queries * keys * PAIR,
            bytes_accessed=8 * 2**20,
            transcendentals=queries * keys,
        ),
        name="attend_back",
    )(bounds, qkv, kv, doc, grad, out, lse)


def unrotate_kernel(dq_ref, dkv_ref, cos_ref, sin_ref, out_ref):
    cos, sin = cos_ref[...], sin_ref[...]
    dq = rotate_lanes(dq_ref[...] * SCALE_OF_SCORES, cos[:, :PAIR], -sin[:, :PAIR])
    dkv = rotate_lanes(dkv_ref[...], cos[:, PAIR:], -sin[:, PAIR:])
    out_ref[...] = jnp.concatenate([dq, dkv], axis=1).astype(bf16)


def unrotate(dq, dkv, cos, sin):
    rows = dq.shape[0]
    pair = pl.BlockSpec((2 * BLOCK, PAIR), lambda i: (i, 0))
    pack = pl.BlockSpec((2 * BLOCK, HEAD_PACK), lambda i: (i, 0))
    return pl.pallas_call(
        unrotate_kernel,
        grid=(rows // (2 * BLOCK),),
        in_specs=[pair, pair, pack, pack],
        out_specs=pack,
        out_shape=jax.ShapeDtypeStruct((rows, HEAD_PACK), bf16),
        cost_estimate=pl.CostEstimate(
            flops=rows * HEAD_PACK * 8, bytes_accessed=rows * HEAD_PACK * 14, transcendentals=0
        ),
        name="unrotate",
    )(dq, dkv, cos, sin)


def lane_column(x, at):
    lane = lax.broadcasted_iota(jnp.int32, x.shape, 1)
    return jnp.sum(jnp.where(lane == at, x, 0.0), axis=1, keepdims=True)


def experts_kernel(
    group_ref, n_ref, routed_ref, router_ref, w_ref, z_ref,
    back_ref, gates_ref, hidden_ref, pre_ref, acc, dots,
):
    e = pl.program_id(0)
    own = group_ref[0] * EXPERTS_HERE + e
    rows = n_ref.shape[0]

    @pl.when(e == 0)
    def _():
        logits = jnp.dot(n_ref[...], router_ref[...], preferred_element_type=f32)
        routed = routed_ref[...].astype(f32) > 0.5
        highest = jnp.max(jnp.where(routed, logits, NEGATIVE_HUGE), axis=1, keepdims=True)
        weights = jnp.where(routed, jnp.exp(jnp.where(routed, logits - highest, 0.0)), 0.0)
        gates_ref[...] = weights / jnp.sum(weights, axis=1, keepdims=True)
        acc[...] = jnp.zeros_like(acc)
        dots[...] = jnp.zeros_like(dots)

    w_in = w_ref[0, :, : 2 * F]
    for t in range(rows // BLOCK):
        part = pl.ds(t * BLOCK, BLOCK)
        pre = jnp.dot(n_ref[part, :], w_in, preferred_element_type=f32)
        gate, up = pre[:, :F], pre[:, F:]
        z = z_ref[0, part, :]
        weight = lane_column(gates_ref[part, :], own)
        sig = 1.0 / (1.0 + jnp.exp(-gate))
        act = gate * sig
        hidden = act * up
        hidden_ref[0, part, :] = (weight * hidden).astype(bf16)
        dot = RESIDUAL_SCALE * jnp.sum(hidden.astype(bf16).astype(f32) * z, axis=1, keepdims=True)
        lane = lax.broadcasted_iota(jnp.int32, (BLOCK, LANES), 1)
        dots[part, :] += jnp.where(lane == own, dot, 0.0)
        scaled = (RESIDUAL_SCALE * weight) * z
        pre_ref[0, part, :F] = (scaled * up * (sig + act * (1.0 - sig))).astype(bf16)
        pre_ref[0, part, F:] = (scaled * act).astype(bf16)
        acc[part, :] += contract_cols(pre_ref[0, part, :], w_in)

    @pl.when(e == EXPERTS_HERE - 1)
    def _():
        width = n_ref.shape[1]
        back_ref[:, :width] = acc[...].astype(bf16)
        high = dots[...].astype(bf16)
        low = dots[...] - high.astype(f32)
        back_ref[:, width:] = (high.astype(f32) + pltpu.roll(low, E, 1)).astype(bf16)


def experts(group, normed, early, packed, w_all, z):
    rows, width = normed.shape
    count = w_all.shape[0]
    whole = pl.BlockSpec((rows, width), lambda e, g: (0, 0))
    column = width // LANES
    router_at = packed.shape[1] // LANES - 1
    return pl.pallas_call(
        experts_kernel,
        grid_spec=pltpu.PrefetchScalarGridSpec(
            num_scalar_prefetch=1,
            grid=(count,),
            in_specs=[
                whole,
                pl.BlockSpec((rows, LANES), lambda e, g: (0, column)),
                pl.BlockSpec((width, LANES), lambda e, g: (0, router_at)),
                pl.BlockSpec((1, width, 3 * F), lambda e, g: (e, 0, 0)),
                pl.BlockSpec((1, rows, F), lambda e, g: (e, 0, 0)),
            ],
            out_specs=[
                pl.BlockSpec((rows, width + LANES), lambda e, g: (0, 0)),
                pl.BlockSpec((rows, LANES), lambda e, g: (0, 0)),
                pl.BlockSpec((1, rows, F), lambda e, g: (e, 0, 0)),
                pl.BlockSpec((1, rows, 2 * F), lambda e, g: (e, 0, 0)),
            ],
            scratch_shapes=[pltpu.VMEM((rows, width), f32), pltpu.VMEM((rows, LANES), f32)],
        ),
        out_shape=[
            jax.ShapeDtypeStruct((rows, width + LANES), bf16),
            jax.ShapeDtypeStruct((rows, LANES), f32),
            jax.ShapeDtypeStruct((count, rows, F), bf16),
            jax.ShapeDtypeStruct((count, rows, 2 * F), bf16),
        ],
        compiler_params=pltpu.CompilerParams(vmem_limit_bytes=VMEM_LIMIT),
        cost_estimate=pl.CostEstimate(
            flops=2 * count * rows * width * 4 * F, bytes_accessed=40 * 2**20, transcendentals=0
        ),
        name="experts",
    )(group, normed, early, packed, w_all, z)


def expert_grads_kernel(n_ref, ct_ref, w_ref, hidden_ref, pre_ref, y_ref, grad_ref, n_t, ct_t, acc):
    e = pl.program_id(0)

    @pl.when(e == 0)
    def _():
        n_t[...] = jnp.transpose(n_ref[...])
        ct_t[...] = jnp.transpose(ct_ref[...])
        acc[...] = jnp.zeros_like(acc)

    grad_ref[0, :, : 2 * F] = jnp.dot(
        n_t[...], pre_ref[0], preferred_element_type=f32
    ).astype(bf16)
    grad_ref[0, :, 2 * F :] = (
        RESIDUAL_SCALE * jnp.dot(ct_t[...], hidden_ref[0], preferred_element_type=f32)
    ).astype(bf16)
    acc[...] += contract_cols(hidden_ref[0], w_ref[0, :, 2 * F :])

    @pl.when(e == EXPERTS_HERE - 1)
    def _():
        y_ref[...] = acc[...].astype(bf16)


def expert_grads(normed, early, w_all, hidden, pre):
    rows, width = normed.shape
    count = w_all.shape[0]
    whole = pl.BlockSpec((rows, width), lambda e: (0, 0))
    return pl.pallas_call(
        expert_grads_kernel,
        grid=(count,),
        in_specs=[
            whole,
            whole,
            pl.BlockSpec((1, width, 3 * F), lambda e: (e, 0, 0)),
            pl.BlockSpec((1, rows, F), lambda e: (e, 0, 0)),
            pl.BlockSpec((1, rows, 2 * F), lambda e: (e, 0, 0)),
        ],
        out_specs=[whole, pl.BlockSpec((1, width, 3 * F), lambda e: (e, 0, 0))],
        out_shape=[
            jax.ShapeDtypeStruct((rows, width), bf16),
            jax.ShapeDtypeStruct((count, width, 3 * F), bf16),
        ],
        scratch_shapes=[
            pltpu.VMEM((width, rows), bf16),
            pltpu.VMEM((width, rows), bf16),
            pltpu.VMEM((rows, width), f32),
        ],
        compiler_params=pltpu.CompilerParams(vmem_limit_bytes=VMEM_LIMIT),
        cost_estimate=pl.CostEstimate(
            flops=2 * count * rows * width * 4 * F, bytes_accessed=40 * 2**20, transcendentals=0
        ),
        name="expert_grads",
    )(normed, early, w_all, hidden, pre)


def exchange(x, axes):
    return lax.all_to_all(x, axes, 0, 0, tiled=True)


def body(
    tokens,
    cotangent,
    segment_ids,
    routes,
    norm_attn,
    w_query,
    key_weight_matrix,
    value_weight_matrix,
    w_output,
    norm_moe,
    w_router,
    expert_in,
    expert_out,
):
    x_local = tokens[0].astype(f32)
    token_count, width = x_local.shape
    seg_row = segment_ids[0]
    group = lax.axis_index("a")
    head_axes = SEQ if lax.axis_size(SEQ) == KEY_VALUE_HEADS else ("b",)
    whole_rows = head_axes == SEQ
    span = token_count * KEY_VALUE_HEADS
    span_start = 0 if whole_rows else group * span
    tok_start = lax.axis_index(SEQ) * token_count

    def start_of_doc(ids):
        return jnp.sum((seg_row[None, :] < ids[:, None]).astype(jnp.int32), axis=1)

    seg_local = lax.dynamic_slice_in_dim(seg_row, tok_start, token_count)
    rope_local = tok_start + jnp.arange(token_count, dtype=jnp.int32) - start_of_doc(seg_local)
    cos_local, sin_local = rotation_tables(rope_local, True)
    seg_span = lax.dynamic_slice_in_dim(seg_row, span_start, span)
    doc_span = start_of_doc(seg_span)
    cos_span, sin_span = rotation_tables(
        span_start + jnp.arange(span, dtype=jnp.int32) - doc_span, True
    )
    bounds = jnp.concatenate(
        [
            doc_span.reshape(-1, BLOCK)[:, 0] // BLOCK,
            jnp.full((1,), span_start // BLOCK, jnp.int32),
        ]
    )
    doc_column = doc_span[:, None]

    own_rows = w_query.shape[0]
    by_head = jnp.concatenate(
        [
            w_query.astype(bf16).reshape(own_rows, KEY_VALUE_HEADS, PAIR),
            key_weight_matrix.astype(bf16).reshape(own_rows, KEY_VALUE_HEADS, HEAD_SIZE),
            value_weight_matrix.astype(bf16).reshape(own_rows, KEY_VALUE_HEADS, HEAD_SIZE),
        ],
        axis=2,
    ).reshape(own_rows, KEY_VALUE_HEADS * HEAD_PACK)
    qkv_width = KEY_VALUE_HEADS * HEAD_PACK
    first_all = gather(
        jnp.concatenate(
            [
                by_head,
                w_output.astype(bf16),
                pad_lanes(
                    jnp.concatenate(
                        [
                            w_router.astype(bf16),
                            norm_attn.astype(bf16)[:, None],
                            norm_moe.astype(bf16)[:, None],
                        ],
                        axis=1,
                    ),
                    LANES,
                ),
            ],
            axis=1,
        ),
        ALL,
    )
    experts_low = jnp.concatenate([expert_in.astype(bf16), expert_out.astype(bf16)], axis=1)
    first_all, experts_low, cos_local, sin_local, cos_span, sin_span, bounds, doc_column = (
        lax.optimization_barrier(
            (first_all, experts_low, cos_local, sin_local, cos_span, sin_span, bounds, doc_column)
        )
    )
    experts_all = gather(experts_low, PLANE).reshape(EXPERTS_HERE, width, 3 * F)
    output_w = first_all[:, qkv_width : qkv_width + width]
    small_at = qkv_width + width
    router_w = first_all[:, small_at : small_at + E]
    gain_one_f = first_all[:, small_at + E].astype(f32)
    gain_two_f = first_all[:, small_at + E + 1].astype(f32)

    expert_ids = jnp.arange(E, dtype=jnp.int32)
    routed_own = jnp.any(routes[0][:, :, None] == expert_ids[None, None, :], axis=1)
    early_all = chain_gather(
        lax.optimization_barrier(
            (
                jnp.concatenate([cotangent[0], pad_lanes(routed_own.astype(bf16), LANES)], axis=1),
                first_all,
            )
        )[0],
        "a",
    )

    by_heads, normed_one = project(tokens[0], first_all, cos_local, sin_local)
    qkv = exchange(by_heads, head_axes).reshape(span, HEAD_PACK)
    if whole_rows:
        kv, kv_at = qkv, 1
    else:
        kv, kv_at = gather(qkv[:, PAIR:], "a"), 0
    attention_result, attended, log_total = attend(bounds, qkv, kv, kv_at, doc_column)
    attended_low = (
        exchange(attended.reshape(KEY_VALUE_HEADS, token_count, PAIR), head_axes)
        .transpose(1, 0, 2)
        .reshape(token_count, QUERY_HEADS * HEAD_SIZE)
    )
    attn_out = jnp.dot(attended_low, output_w, preferred_element_type=f32)
    resid = x_local + RESIDUAL_SCALE * attn_out
    normed_two = rms_scale(resid, gain_two_f).astype(bf16)

    normed_two, experts_all, early_all = lax.optimization_barrier(
        (normed_two, experts_all, early_all)
    )
    normed_all = gather(normed_two, "a")
    grad_hidden = jnp.einsum(
        "td,edf->etf",
        early_all[:, :width],
        experts_all[:, :, 2 * F :],
        preferred_element_type=f32,
    )
    back_part, gates_all, gated_hidden, grad_pre = experts(
        group.reshape(1), normed_all, early_all, first_all, experts_all, grad_hidden
    )
    back_own = scatter_sum(back_part, "a").astype(f32)
    moe_part, grad_experts = expert_grads(
        normed_all, early_all, experts_all, gated_hidden, grad_pre
    )
    back_own, moe_part, grad_experts = lax.optimization_barrier(
        (back_own, moe_part, grad_experts)
    )
    grad_experts = scatter_sum(grad_experts.reshape(EXPERTS_HERE * width, 3 * F), PLANE)
    moe_sum = scatter_sum(moe_part, "a")

    grad_out = cotangent[0].astype(f32)
    gates = lax.dynamic_slice_in_dim(gates_all, group * token_count, token_count)[:, :E]
    gate_grads_own = back_own[:, width : width + E] + back_own[:, width + E : width + 2 * E]
    grad_logits = gates * (gate_grads_own - jnp.sum(gates * gate_grads_own, axis=-1, keepdims=True))
    grad_normed_two = back_own[:, :width] + jnp.dot(
        grad_logits, router_w.astype(f32).T, precision=HIGHEST_DOT
    )
    grad_router = jnp.dot(normed_two.astype(f32).T, grad_logits, precision=HIGHEST_DOT)
    grad_resid_norm, grad_gain_two = rms_back(resid, gain_two_f, grad_normed_two)
    grad_resid = grad_out + grad_resid_norm
    grad_attn_low = (RESIDUAL_SCALE * grad_resid).astype(bf16)
    grad_heads = contract_cols(grad_attn_low, output_w).astype(bf16)
    grad_mixed = exchange(
        grad_heads.reshape(token_count, KEY_VALUE_HEADS, PAIR).transpose(1, 0, 2), head_axes
    ).reshape(span, PAIR)
    grad_q, grad_kv = attend_back(
        bounds, qkv, kv, kv_at, doc_column, grad_mixed, attention_result, log_total
    )
    if not whole_rows:
        grad_kv = scatter_sum(grad_kv.astype(bf16), "a").astype(f32)
    grad_qkv = (
        exchange(
            unrotate(grad_q, grad_kv, cos_span, sin_span).reshape(
                KEY_VALUE_HEADS, token_count, HEAD_PACK
            ),
            head_axes,
        )
        .transpose(1, 0, 2)
        .reshape(token_count, qkv_width)
    )
    grad_normed_one = contract_cols(grad_qkv, first_all[:, :qkv_width])
    grad_x_norm, grad_gain_one = rms_back(x_local, gain_one_f, grad_normed_one)
    grad_input = grad_resid + grad_x_norm

    orders = (("c", "y", "b", "a"), ("c", "b", "y", "a"))
    cut = 3 * qkv_width // 4
    small = jnp.concatenate([grad_router, grad_gain_one[:, None], grad_gain_two[:, None]], axis=1)

    left = jnp.concatenate(
        [
            rows_for(contract_rows(normed_one, grad_qkv[:, :cut]).astype(bf16), orders[0]),
            rows_for(pad_lanes(small, LANES).astype(bf16), orders[0]),
        ],
        axis=1,
    )
    right = jnp.concatenate(
        [
            rows_for(contract_rows(normed_one, grad_qkv[:, cut:]).astype(bf16), orders[1]),
            rows_for(contract_rows(attended_low, grad_attn_low).astype(bf16), orders[1]),
        ],
        axis=1,
    )
    left, right = halve(left, "c"), halve(right, "c")
    left, right = halve(left, "y"), halve(right, "b")
    left, right = halve(left, "b"), halve(right, "y")
    last, grad_experts, moe_sum, resid = lax.optimization_barrier(
        (jnp.concatenate([left, right], axis=1), grad_experts, moe_sum, resid)
    )
    total = scatter_sum(last, "a").astype(f32)
    grad_experts = grad_experts.astype(f32)
    layer_sum = resid + RESIDUAL_SCALE * moe_sum.astype(f32)
    small_sum = total[:, cut : cut + LANES]
    qkv_sum = jnp.concatenate(
        [total[:, :cut], total[:, cut + LANES : qkv_width + LANES]], axis=1
    ).reshape(own_rows, KEY_VALUE_HEADS, HEAD_PACK)
    return (
        layer_sum.astype(bf16)[None],
        grad_input[None],
        small_sum[:, E],
        qkv_sum[:, :, :PAIR].reshape(own_rows, -1),
        qkv_sum[:, :, PAIR : PAIR + HEAD_SIZE].reshape(own_rows, -1),
        qkv_sum[:, :, PAIR + HEAD_SIZE :].reshape(own_rows, -1),
        total[:, qkv_width + LANES :],
        small_sum[:, E + 1],
        small_sum[:, :E],
        grad_experts[:, : 2 * F],
        grad_experts[:, 2 * F :],
    )


def solution(mesh):
    seq, row = mesh.shape["seq"], mesh.shape["row"]
    cut = Mesh(mesh.devices.reshape(GROUPS, seq // GROUPS, row // 2, 2), ALL)
    token_spec = P(("y", "c"), SEQ, None)
    row_spec = P(ALL, None)
    flat_spec = P(ALL)
    in_specs = (
        token_spec,
        token_spec,
        P(("y", "c"), None),
        token_spec,
        flat_spec,
        row_spec,
        row_spec,
        row_spec,
        row_spec,
        flat_spec,
        row_spec,
        row_spec,
        row_spec,
    )
    out_specs = (
        token_spec,
        token_spec,
        flat_spec,
        row_spec,
        row_spec,
        row_spec,
        row_spec,
        flat_spec,
        row_spec,
        row_spec,
        row_spec,
    )
    return jax.shard_map(body, mesh=cut, in_specs=in_specs, out_specs=out_specs, check_vma=False)
```

```python
import jax
import jax.numpy as jnp
from jax import lax
from jax.experimental import pallas as pl
from jax.experimental.pallas import tpu as pltpu
from jax.sharding import Mesh, PartitionSpec as P

QUERY_HEADS = 16
KEY_VALUE_HEADS = 8
HEAD_SIZE = 64
F = 512
E = 16
GROUPS = 4
EXPERTS_HERE = E // GROUPS
LANES = 128
PAIR = 2 * HEAD_SIZE
HEAD_PACK = 4 * HEAD_SIZE
BLOCK = 256

NORM_EPS = 1e-06
RESIDUAL_SCALE = 0.22
SCALE_OF_SCORES = 0.015625
ROPE_BASE = 10000.0
NEGATIVE_HUGE = -1e30
HIGHEST_DOT = lax.Precision.HIGHEST
VMEM_LIMIT = 60 * 1024 * 1024

PLANE = ("b", "y", "c")
SEQ = ("a", "b")
ALL = ("a", "b", "y", "c")

f32 = jnp.float32
bf16 = jnp.bfloat16


def rotation_tables(positions, with_values):
    half = HEAD_SIZE // 2
    freq = jnp.power(ROPE_BASE, -2.0 * jnp.arange(half, dtype=f32) / HEAD_SIZE)
    angle = positions.astype(f32)[:, None] * freq[None, :]
    cos, sin = jnp.cos(angle), jnp.sin(angle)
    cos, sin = jnp.concatenate([cos, cos], 1), jnp.concatenate([-sin, sin], 1)
    return (
        jnp.concatenate([cos, cos, cos, jnp.ones_like(cos)], 1),
        jnp.concatenate([sin, sin, sin, jnp.zeros_like(sin)], 1),
    )


def rms_back(values, gain, grad_norm):
    mean_square = jnp.mean(values * values, axis=-1, keepdims=True)
    inverse = lax.rsqrt(mean_square + NORM_EPS)
    scaled_grad = grad_norm * gain
    grad_values = inverse * scaled_grad - values * inverse**3 * jnp.mean(
        values * scaled_grad, axis=-1, keepdims=True
    )
    grad_gain = jnp.sum(grad_norm * values * inverse, axis=0)
    return (grad_values, grad_gain)


def rms_scale(values, gain):
    mean_square = jnp.mean(values * values, axis=-1, keepdims=True)
    return values * lax.rsqrt(mean_square + NORM_EPS) * gain


def contract_rows(left_side, right_side):
    return lax.dot_general(
        left_side, right_side, (((0,), (0,)), ((), ())), preferred_element_type=f32
    )


def contract_cols(left_side, right_side):
    return lax.dot_general(
        left_side, right_side, (((1,), (1,)), ((), ())), preferred_element_type=f32
    )


def gather(x, axes):
    return lax.all_gather(x, axes, axis=0, tiled=True)


def scatter_sum(x, axes):
    return lax.psum_scatter(x, axes, scatter_dimension=0, tiled=True)


def pad_lanes(x, lanes):
    return jnp.pad(x, ((0, 0), (0, lanes - x.shape[1])))


def line_pairs(n, step):
    return [(i, i + step) for i in range(n) if 0 <= i + step < n]


def line_gather(x, axis):
    n, me = lax.axis_size(axis), lax.axis_index(axis)
    out = jnp.zeros((n,) + x.shape, x.dtype)
    out = lax.dynamic_update_index_in_dim(out, x, me, 0)
    arrived = {k: lax.ppermute(x, axis, line_pairs(n, k)) for j in range(n - 1, 0, -1) for k in (j, -j)}
    for k in range(1, n):
        piece = jnp.where(me >= k, arrived[k], arrived[k - n])
        out = lax.dynamic_update_index_in_dim(out, piece, (me - k) % n, 0)
    return out.reshape((n * x.shape[0],) + x.shape[1:])


def line_send(v, axis):
    n, me = lax.axis_size(axis), lax.axis_index(axis)
    v = v.reshape((n, v.shape[0] // n) + v.shape[1:])
    terms = [lax.dynamic_index_in_dim(v, me, 0, False)]
    for j in range(n - 1, 0, -1):
        for step in (j, -j):
            block = lax.dynamic_index_in_dim(v, jnp.clip(me + step, 0, n - 1), 0, False)
            terms.append(lax.ppermute(block, axis, line_pairs(n, step)))
    return tuple(terms)


def grid_gather(x):
    n, me = lax.axis_size("a"), lax.axis_index("a")
    mine = lax.axis_index("b")
    out = jnp.zeros((n + 1, 2) + x.shape, x.dtype)

    def cross(block, ends):
        return lax.ppermute(
            block, SEQ, [(2 * i + j, 2 * i + 1 - j) for i in range(n) if ends(i) for j in (0, 1)]
        )

    pieces = [(x, cross(x, lambda i: True), me)]
    up = down = x
    for k in range(1, n):
        up = lax.ppermute(up, "a", line_pairs(n, 1))
        down = lax.ppermute(down, "a", line_pairs(n, -1))
        pieces.append((up, cross(up, lambda i: i >= k), jnp.where(me >= k, me - k, n)))
        pieces.append((down, cross(down, lambda i: i + k < n), jnp.where(me + k < n, me + k, n)))
    for block, crossed, at in pieces:
        zero = jnp.zeros_like(at)
        out = lax.dynamic_update_slice(out, block[None, None], (at, mine, zero, zero))
        out = lax.dynamic_update_slice(out, crossed[None, None], (at, 1 - mine, zero, zero))
    return out


def halve(v, axis, at):
    if lax.axis_size(axis) != 2:
        return lax.psum_scatter(v, axis, scatter_dimension=at, tiled=False)
    me = lax.axis_index(axis)
    other = lax.ppermute(lax.dynamic_index_in_dim(v, 1 - me, at, False), axis, [(0, 1), (1, 0)])
    own = lax.dynamic_index_in_dim(v, me, at, False)
    return (own.astype(f32) + other.astype(f32)).astype(v.dtype)


def sum_over_row(v):
    sizes = tuple(lax.axis_size(axis) for axis in ALL)
    v = v.reshape(sizes + (v.shape[0] // lax.axis_size(ALL), v.shape[1]))
    return halve(halve(v, "c", 3), "y", 2)


def rotate_lanes(x, cos, sin):
    width = x.shape[-1]
    lane = lax.broadcasted_iota(jnp.int32, x.shape, x.ndim - 1)
    swapped = jnp.where(
        lane % HEAD_SIZE < HEAD_SIZE // 2,
        pltpu.roll(x, width - HEAD_SIZE // 2, x.ndim - 1),
        pltpu.roll(x, HEAD_SIZE // 2, x.ndim - 1),
    )
    return x * cos + swapped * sin


def project_kernel(head_ref, x_ref, small_ref, w_ref, cos_ref, sin_ref, qkv_ref, normed_ref, gain):
    @pl.when(pl.program_id(0) == 0)
    def _():
        gain[...] = jnp.transpose(small_ref[...].astype(f32))[E : E + 8, :]

    normed = rms_scale(x_ref[0, 0].astype(f32), gain[0:1, :]).astype(bf16)
    normed_ref[...] = normed
    pre = jnp.dot(normed, w_ref[...], preferred_element_type=f32)
    qkv_ref[...] = rotate_lanes(pre, cos_ref[...], sin_ref[...]).astype(bf16)


def project(head, x, packed, cos, sin):
    members, rows, width = x.shape[1:]
    small_at = packed.shape[1] // LANES - 1
    span = cos.shape[0]
    return pl.pallas_call(
        project_kernel,
        grid_spec=pltpu.PrefetchScalarGridSpec(
            num_scalar_prefetch=1,
            grid=(span // rows,),
            in_specs=[
                pl.BlockSpec((1, 1, rows, width), lambda i, h: (i // members, i % members, 0, 0)),
                pl.BlockSpec((width, LANES), lambda i, h: (0, small_at)),
                pl.BlockSpec((width, HEAD_PACK), lambda i, h: (0, h[0])),
                pl.BlockSpec((rows, HEAD_PACK), lambda i, h: (i, 0)),
                pl.BlockSpec((rows, HEAD_PACK), lambda i, h: (i, 0)),
            ],
            out_specs=[
                pl.BlockSpec((rows, HEAD_PACK), lambda i, h: (i, 0)),
                pl.BlockSpec((rows, width), lambda i, h: (i, 0)),
            ],
            scratch_shapes=[pltpu.VMEM((8, width), f32)],
        ),
        out_shape=[
            jax.ShapeDtypeStruct((span, HEAD_PACK), bf16),
            jax.ShapeDtypeStruct((span, width), bf16),
        ],
        compiler_params=pltpu.CompilerParams(vmem_limit_bytes=VMEM_LIMIT),
        cost_estimate=pl.CostEstimate(
            flops=2 * span * width * HEAD_PACK, bytes_accessed=14 * 2**20, transcendentals=0
        ),
        name="project",
    )(head, x, packed, packed, cos, sin)


def head_grads_kernel(head_ref, x_ref, normed_ref, w_ref, grad_ref, out_ref, acc, gain):
    i = pl.program_id(0)

    @pl.when(i == 0)
    def _():
        acc[...] = jnp.zeros_like(acc)
        gain[...] = jnp.zeros_like(gain)

    grad = grad_ref[...]
    acc[...] += contract_rows(grad, normed_ref[...])
    x = x_ref[0, 0].astype(f32)
    inverse = lax.rsqrt(jnp.mean(x * x, axis=-1, keepdims=True) + NORM_EPS)
    back = contract_cols(grad, w_ref[...]) * (x * inverse)
    gain[...] += jnp.sum(back.reshape(back.shape[0] // 8, 8, back.shape[1]), axis=0)

    @pl.when(i == pl.num_programs(0) - 1)
    def _():
        out_ref[:, :HEAD_PACK] = jnp.transpose(acc[...]).astype(bf16)
        total = jnp.sum(gain[...], axis=0, keepdims=True)
        rows = lax.broadcasted_iota(jnp.int32, (LANES, total.shape[1]), 0)
        out_ref[:, HEAD_PACK:] = jnp.transpose(
            jnp.where(rows == 0, jnp.broadcast_to(total, rows.shape), 0.0)
        ).astype(bf16)


def head_grads(head, x, normed, packed, grads):
    members, rows, width = x.shape[1:]
    span = grads.shape[0]
    return pl.pallas_call(
        head_grads_kernel,
        grid_spec=pltpu.PrefetchScalarGridSpec(
            num_scalar_prefetch=1,
            grid=(span // rows,),
            in_specs=[
                pl.BlockSpec((1, 1, rows, width), lambda i, h: (i // members, i % members, 0, 0)),
                pl.BlockSpec((rows, width), lambda i, h: (i, 0)),
                pl.BlockSpec((width, HEAD_PACK), lambda i, h: (0, h[0])),
                pl.BlockSpec((rows, HEAD_PACK), lambda i, h: (i, 0)),
            ],
            out_specs=pl.BlockSpec((width, HEAD_PACK + LANES), lambda i, h: (0, 0)),
            scratch_shapes=[pltpu.VMEM((HEAD_PACK, width), f32), pltpu.VMEM((8, width), f32)],
        ),
        out_shape=jax.ShapeDtypeStruct((width, HEAD_PACK + LANES), bf16),
        compiler_params=pltpu.CompilerParams(vmem_limit_bytes=VMEM_LIMIT),
        cost_estimate=pl.CostEstimate(
            flops=4 * span * width * HEAD_PACK, bytes_accessed=12 * 2**20, transcendentals=0
        ),
        name="head_grads",
    )(head, x, normed, packed, grads)


def lower_lanes(shape):
    return lax.broadcasted_iota(jnp.int32, shape, len(shape) - 1) < HEAD_SIZE


def both_heads_low(pair):
    low = lower_lanes(pair.shape)
    return jnp.concatenate(
        [jnp.where(low, pair, 0.0), jnp.where(low, pltpu.roll(pair, HEAD_SIZE, 1), 0.0)], axis=0
    )


def both_heads_high(pair):
    low = lower_lanes(pair.shape)
    return jnp.concatenate(
        [jnp.where(low, 0.0, pltpu.roll(pair, HEAD_SIZE, 1)), jnp.where(low, 0.0, pair)], axis=0
    )


def allowed_pairs(shape, query_start, key_start, doc):
    rows = lax.broadcasted_iota(jnp.int32, (shape[0] // 2, 1), 0) + query_start
    rows = jnp.concatenate([rows, rows], axis=0)
    keys = lax.broadcasted_iota(jnp.int32, shape, 1) + key_start
    return (keys >= jnp.concatenate([doc, doc], axis=0)) & (keys <= rows)


def attend_kernel(bounds_ref, q_ref, kv_ref, doc_ref, o_ref, low_ref, lse_ref, kept, top, total, acc):
    i = pl.program_id(0)
    steps = pl.num_programs(0)
    offset = bounds_ref[steps]
    first, last = bounds_ref[i], i + offset + 1
    q = both_heads_low(q_ref[...].astype(f32) * SCALE_OF_SCORES).astype(bf16)
    doc = doc_ref[...]
    top[...] = jnp.full_like(top, NEGATIVE_HUGE)
    total[...] = jnp.zeros_like(total)
    acc[...] = jnp.zeros_like(acc)

    def score(j, carried):
        start = pl.multiple_of(j * BLOCK, BLOCK)
        scores = contract_cols(q, kv_ref[pl.ds(start, BLOCK), :])
        allowed = allowed_pairs(scores.shape, (i + offset) * BLOCK, j * BLOCK, doc)
        scores = jnp.where(allowed, scores, NEGATIVE_HUGE)
        kept[:, pl.ds(start, BLOCK)] = scores
        top[...] = jnp.maximum(top[...], jnp.maximum(scores[:, :LANES], scores[:, LANES:]))
        return carried

    lax.fori_loop(first, last, score, 0)
    highest = jnp.max(top[...], axis=1, keepdims=True)

    def mix(j, carried):
        start = pl.multiple_of(j * BLOCK, BLOCK)
        probs = jnp.exp(kept[:, pl.ds(start, BLOCK)] - highest)
        total[...] += probs[:, :LANES] + probs[:, LANES:]
        acc[...] += jnp.dot(
            probs.astype(bf16), kv_ref[pl.ds(start, BLOCK), :], preferred_element_type=f32
        )
        return carried

    lax.fori_loop(first, last, mix, 0)
    row_total = jnp.sum(total[...], axis=1, keepdims=True)
    mixed = acc[...] / row_total
    first_head, second_head = mixed[:BLOCK], mixed[BLOCK:]
    out = jnp.where(
        lower_lanes(first_head.shape), pltpu.roll(first_head, HEAD_SIZE, 1), second_head
    )
    o_ref[...] = out
    low_ref[...] = out.astype(bf16)
    lse_ref[0] = highest + jnp.log(row_total)


def attend(bounds, qkv, kv, kv_at, doc):
    queries, keys = qkv.shape[0], kv.shape[0]
    steps = queries // BLOCK
    pair = pl.BlockSpec((BLOCK, PAIR), lambda i, s: (i, 0))
    return pl.pallas_call(
        attend_kernel,
        grid_spec=pltpu.PrefetchScalarGridSpec(
            num_scalar_prefetch=1,
            grid=(steps,),
            in_specs=[
                pair,
                pl.BlockSpec((keys, PAIR), lambda i, s: (0, kv_at)),
                pl.BlockSpec((BLOCK, 1), lambda i, s: (i, 0)),
            ],
            out_specs=[pair, pair, pl.BlockSpec((1, 2 * BLOCK, 1), lambda i, s: (i, 0, 0))],
            scratch_shapes=[
                pltpu.VMEM((2 * BLOCK, keys), f32),
                pltpu.VMEM((2 * BLOCK, LANES), f32),
                pltpu.VMEM((2 * BLOCK, LANES), f32),
                pltpu.VMEM((2 * BLOCK, PAIR), f32),
            ],
        ),
        out_shape=[
            jax.ShapeDtypeStruct((queries, PAIR), f32),
            jax.ShapeDtypeStruct((queries, PAIR), bf16),
            jax.ShapeDtypeStruct((steps, 2 * BLOCK, 1), f32),
        ],
        compiler_params=pltpu.CompilerParams(vmem_limit_bytes=VMEM_LIMIT),
        cost_estimate=pl.CostEstimate(
            flops=4 * queries * keys * PAIR, bytes_accessed=6 * 2**20, transcendentals=queries * keys
        ),
        name="attend",
    )(bounds, qkv, kv, doc)


def attend_back_kernel(
    bounds_ref, q_ref, kv_ref, doc_ref, do_ref, o_ref, lse_ref, dq_ref, dkv_ref, acc
):
    i = pl.program_id(0)
    steps = pl.num_programs(0)
    offset = bounds_ref[steps]

    @pl.when(i == 0)
    def _():
        dkv_ref[...] = jnp.zeros_like(dkv_ref)

    q = both_heads_low(q_ref[...].astype(f32) * SCALE_OF_SCORES).astype(bf16)
    grad = do_ref[...].astype(f32)
    product = grad * o_ref[...]
    low = lower_lanes(product.shape)
    delta = jnp.concatenate(
        [
            jnp.sum(jnp.where(low, product, 0.0), axis=1, keepdims=True),
            jnp.sum(jnp.where(low, 0.0, product), axis=1, keepdims=True),
        ],
        axis=0,
    )
    grad = both_heads_high(grad).astype(bf16)
    sources = jnp.concatenate([q, grad], axis=0)
    doc = doc_ref[...]
    lse = lse_ref[0]
    acc[...] = jnp.zeros_like(acc)

    def step(j, carried):
        start = pl.multiple_of(j * BLOCK, BLOCK)
        kv = kv_ref[pl.ds(start, BLOCK), :]
        scores = contract_cols(q, kv)
        allowed = allowed_pairs(scores.shape, (i + offset) * BLOCK, j * BLOCK, doc)
        probs = jnp.exp(jnp.where(allowed, scores - lse, NEGATIVE_HUGE))
        grad_probs = contract_cols(grad, kv)
        grad_scores = (probs * (grad_probs - delta)).astype(bf16)
        acc[...] += jnp.dot(grad_scores, kv, preferred_element_type=f32)
        both = jnp.concatenate([grad_scores, probs.astype(bf16)], axis=0)
        dkv_ref[pl.ds(start, BLOCK), :] += contract_rows(both, sources)
        return carried

    lax.fori_loop(bounds_ref[i], i + offset + 1, step, 0)
    first, second = acc[:BLOCK], acc[BLOCK:]
    dq_ref[...] = jnp.where(lower_lanes(first.shape), first, pltpu.roll(second, HEAD_SIZE, 1))


def attend_back(bounds, qkv, kv, kv_at, doc, grad, out, lse):
    queries, keys = qkv.shape[0], kv.shape[0]
    steps = queries // BLOCK
    pair = pl.BlockSpec((BLOCK, PAIR), lambda i, s: (i, 0))
    return pl.pallas_call(
        attend_back_kernel,
        grid_spec=pltpu.PrefetchScalarGridSpec(
            num_scalar_prefetch=1,
            grid=(steps,),
            in_specs=[
                pair,
                pl.BlockSpec((keys, PAIR), lambda i, s: (0, kv_at)),
                pl.BlockSpec((BLOCK, 1), lambda i, s: (i, 0)),
                pair,
                pair,
                pl.BlockSpec((1, 2 * BLOCK, 1), lambda i, s: (i, 0, 0)),
            ],
            out_specs=[pair, pl.BlockSpec((keys, PAIR), lambda i, s: (0, 0))],
            scratch_shapes=[pltpu.VMEM((2 * BLOCK, PAIR), f32)],
        ),
        out_shape=[
            jax.ShapeDtypeStruct((queries, PAIR), f32),
            jax.ShapeDtypeStruct((keys, PAIR), f32),
        ],
        compiler_params=pltpu.CompilerParams(vmem_limit_bytes=VMEM_LIMIT),
        cost_estimate=pl.CostEstimate(
            flops=10 * queries * keys * PAIR,
            bytes_accessed=8 * 2**20,
            transcendentals=queries * keys,
        ),
        name="attend_back",
    )(bounds, qkv, kv, doc, grad, out, lse)


def unrotate_kernel(dq_ref, dkv_ref, cos_ref, sin_ref, out_ref):
    cos, sin = cos_ref[...], sin_ref[...]
    dq = rotate_lanes(dq_ref[...] * SCALE_OF_SCORES, cos[:, :PAIR], -sin[:, :PAIR])
    dkv = rotate_lanes(dkv_ref[...], cos[:, PAIR:], -sin[:, PAIR:])
    out_ref[...] = jnp.concatenate([dq, dkv], axis=1).astype(bf16)


def unrotate(dq, dkv, cos, sin):
    rows = dq.shape[0]
    pair = pl.BlockSpec((2 * BLOCK, PAIR), lambda i: (i, 0))
    pack = pl.BlockSpec((2 * BLOCK, HEAD_PACK), lambda i: (i, 0))
    return pl.pallas_call(
        unrotate_kernel,
        grid=(rows // (2 * BLOCK),),
        in_specs=[pair, pair, pack, pack],
        out_specs=pack,
        out_shape=jax.ShapeDtypeStruct((rows, HEAD_PACK), bf16),
        cost_estimate=pl.CostEstimate(
            flops=rows * HEAD_PACK * 8, bytes_accessed=rows * HEAD_PACK * 14, transcendentals=0
        ),
        name="unrotate",
    )(dq, dkv, cos, sin)


def lane_column(x, at):
    lane = lax.broadcasted_iota(jnp.int32, x.shape, 1)
    return jnp.sum(jnp.where(lane == at, x, 0.0), axis=1, keepdims=True)


def experts_kernel(
    group_ref, n_ref, routed_ref, router_ref, w_ref, z_ref,
    back_ref, gates_ref, hidden_ref, pre_ref, acc, dots,
):
    e = pl.program_id(0)
    own = group_ref[0] * EXPERTS_HERE + e
    rows = n_ref.shape[0]

    @pl.when(e == 0)
    def _():
        logits = jnp.dot(n_ref[...], router_ref[...], preferred_element_type=f32)
        routed = routed_ref[...].astype(f32) > 0.5
        highest = jnp.max(jnp.where(routed, logits, NEGATIVE_HUGE), axis=1, keepdims=True)
        weights = jnp.where(routed, jnp.exp(jnp.where(routed, logits - highest, 0.0)), 0.0)
        gates_ref[...] = weights / jnp.sum(weights, axis=1, keepdims=True)
        acc[...] = jnp.zeros_like(acc)
        dots[...] = jnp.zeros_like(dots)

    w_in = w_ref[0, :, : 2 * F]
    for t in range(rows // BLOCK):
        part = pl.ds(t * BLOCK, BLOCK)
        pre = jnp.dot(n_ref[part, :], w_in, preferred_element_type=f32)
        gate, up = pre[:, :F], pre[:, F:]
        z = z_ref[0, part, :]
        weight = lane_column(gates_ref[part, :], own)
        sig = 1.0 / (1.0 + jnp.exp(-gate))
        act = gate * sig
        hidden = act * up
        hidden_ref[0, part, :] = (weight * hidden).astype(bf16)
        dot = RESIDUAL_SCALE * jnp.sum(hidden.astype(bf16).astype(f32) * z, axis=1, keepdims=True)
        lane = lax.broadcasted_iota(jnp.int32, (BLOCK, LANES), 1)
        dots[part, :] += jnp.where(lane == own, dot, 0.0)
        scaled = (RESIDUAL_SCALE * weight) * z
        pre_ref[0, part, :F] = (scaled * up * (sig + act * (1.0 - sig))).astype(bf16)
        pre_ref[0, part, F:] = (scaled * act).astype(bf16)
        acc[part, :] += contract_cols(pre_ref[0, part, :], w_in)

    @pl.when(e == EXPERTS_HERE - 1)
    def _():
        width = n_ref.shape[1]
        back_ref[:, :width] = acc[...].astype(bf16)
        high = dots[...].astype(bf16)
        low = dots[...] - high.astype(f32)
        back_ref[:, width:] = (high.astype(f32) + pltpu.roll(low, E, 1)).astype(bf16)


def experts(group, normed, early, packed, w_all, z):
    rows, width = normed.shape
    count = w_all.shape[0]
    whole = pl.BlockSpec((rows, width), lambda e, g: (0, 0))
    column = width // LANES
    router_at = packed.shape[1] // LANES - 1
    return pl.pallas_call(
        experts_kernel,
        grid_spec=pltpu.PrefetchScalarGridSpec(
            num_scalar_prefetch=1,
            grid=(count,),
            in_specs=[
                whole,
                pl.BlockSpec((rows, LANES), lambda e, g: (0, column)),
                pl.BlockSpec((width, LANES), lambda e, g: (0, router_at)),
                pl.BlockSpec((1, width, 3 * F), lambda e, g: (e, 0, 0)),
                pl.BlockSpec((1, rows, F), lambda e, g: (e, 0, 0)),
            ],
            out_specs=[
                pl.BlockSpec((rows, width + LANES), lambda e, g: (0, 0)),
                pl.BlockSpec((rows, LANES), lambda e, g: (0, 0)),
                pl.BlockSpec((1, rows, F), lambda e, g: (e, 0, 0)),
                pl.BlockSpec((1, rows, 2 * F), lambda e, g: (e, 0, 0)),
            ],
            scratch_shapes=[pltpu.VMEM((rows, width), f32), pltpu.VMEM((rows, LANES), f32)],
        ),
        out_shape=[
            jax.ShapeDtypeStruct((rows, width + LANES), bf16),
            jax.ShapeDtypeStruct((rows, LANES), f32),
            jax.ShapeDtypeStruct((count, rows, F), bf16),
            jax.ShapeDtypeStruct((count, rows, 2 * F), bf16),
        ],
        compiler_params=pltpu.CompilerParams(vmem_limit_bytes=VMEM_LIMIT),
        cost_estimate=pl.CostEstimate(
            flops=2 * count * rows * width * 4 * F, bytes_accessed=40 * 2**20, transcendentals=0
        ),
        name="experts",
    )(group, normed, early, packed, w_all, z)


def expert_grads_kernel(n_ref, ct_ref, w_ref, hidden_ref, pre_ref, y_ref, grad_ref, n_t, ct_t, acc):
    e = pl.program_id(0)

    @pl.when(e == 0)
    def _():
        n_t[...] = jnp.transpose(n_ref[...])
        ct_t[...] = jnp.transpose(ct_ref[...])
        acc[...] = jnp.zeros_like(acc)

    grad_ref[0, :, : 2 * F] = jnp.dot(
        n_t[...], pre_ref[0], preferred_element_type=f32
    ).astype(bf16)
    grad_ref[0, :, 2 * F :] = (
        RESIDUAL_SCALE * jnp.dot(ct_t[...], hidden_ref[0], preferred_element_type=f32)
    ).astype(bf16)
    acc[...] += contract_cols(hidden_ref[0], w_ref[0, :, 2 * F :])

    @pl.when(e == EXPERTS_HERE - 1)
    def _():
        y_ref[...] = acc[...].astype(bf16)


def expert_grads(normed, early, w_all, hidden, pre):
    rows, width = normed.shape
    count = w_all.shape[0]
    whole = pl.BlockSpec((rows, width), lambda e: (0, 0))
    return pl.pallas_call(
        expert_grads_kernel,
        grid=(count,),
        in_specs=[
            whole,
            whole,
            pl.BlockSpec((1, width, 3 * F), lambda e: (e, 0, 0)),
            pl.BlockSpec((1, rows, F), lambda e: (e, 0, 0)),
            pl.BlockSpec((1, rows, 2 * F), lambda e: (e, 0, 0)),
        ],
        out_specs=[whole, pl.BlockSpec((1, width, 3 * F), lambda e: (e, 0, 0))],
        out_shape=[
            jax.ShapeDtypeStruct((rows, width), bf16),
            jax.ShapeDtypeStruct((count, width, 3 * F), bf16),
        ],
        scratch_shapes=[
            pltpu.VMEM((width, rows), bf16),
            pltpu.VMEM((width, rows), bf16),
            pltpu.VMEM((rows, width), f32),
        ],
        compiler_params=pltpu.CompilerParams(vmem_limit_bytes=VMEM_LIMIT),
        cost_estimate=pl.CostEstimate(
            flops=2 * count * rows * width * 4 * F, bytes_accessed=40 * 2**20, transcendentals=0
        ),
        name="expert_grads",
    )(normed, early, w_all, hidden, pre)


def exchange(x, axes):
    return lax.all_to_all(x, axes, 0, 0, tiled=True)


def body(
    tokens,
    cotangent,
    segment_ids,
    routes,
    norm_attn,
    w_query,
    key_weight_matrix,
    value_weight_matrix,
    w_output,
    norm_moe,
    w_router,
    expert_in,
    expert_out,
):
    x_local = tokens[0].astype(f32)
    token_count, width = x_local.shape
    seg_row = segment_ids[0]
    group = lax.axis_index("a")
    head_axes = SEQ if lax.axis_size(SEQ) == KEY_VALUE_HEADS else ("b",)
    whole_rows = head_axes == SEQ
    span = token_count * KEY_VALUE_HEADS
    span_start = 0 if whole_rows else group * span
    head = lax.axis_index(head_axes).reshape(1)

    def start_of_doc(ids):
        return jnp.sum((seg_row[None, :] < ids[:, None]).astype(jnp.int32), axis=1)

    seg_span = lax.dynamic_slice_in_dim(seg_row, span_start, span)
    doc_span = start_of_doc(seg_span)
    cos_span, sin_span = rotation_tables(
        span_start + jnp.arange(span, dtype=jnp.int32) - doc_span, True
    )
    bounds = jnp.concatenate(
        [
            doc_span.reshape(-1, BLOCK)[:, 0] // BLOCK,
            jnp.full((1,), span_start // BLOCK, jnp.int32),
        ]
    )
    doc_column = doc_span[:, None]

    own_rows = w_query.shape[0]
    by_head = jnp.concatenate(
        [
            w_query.astype(bf16).reshape(own_rows, KEY_VALUE_HEADS, PAIR),
            key_weight_matrix.astype(bf16).reshape(own_rows, KEY_VALUE_HEADS, HEAD_SIZE),
            value_weight_matrix.astype(bf16).reshape(own_rows, KEY_VALUE_HEADS, HEAD_SIZE),
        ],
        axis=2,
    ).reshape(own_rows, KEY_VALUE_HEADS * HEAD_PACK)
    qkv_width = KEY_VALUE_HEADS * HEAD_PACK
    first_all = gather(
        jnp.concatenate(
            [
                by_head,
                w_output.astype(bf16),
                pad_lanes(
                    jnp.concatenate(
                        [
                            w_router.astype(bf16),
                            norm_attn.astype(bf16)[:, None],
                            norm_moe.astype(bf16)[:, None],
                        ],
                        axis=1,
                    ),
                    LANES,
                ),
            ],
            axis=1,
        ),
        ALL,
    )
    experts_low = jnp.concatenate([expert_in.astype(bf16), expert_out.astype(bf16)], axis=1)
    if whole_rows:
        x_span = grid_gather(tokens[0])
    else:
        x_span = gather(tokens[0], "b").reshape((1, KEY_VALUE_HEADS) + tokens.shape[1:])
    first_all, experts_low, x_span, cos_span, sin_span, bounds, doc_column = (
        lax.optimization_barrier(
            (first_all, experts_low, x_span, cos_span, sin_span, bounds, doc_column)
        )
    )
    experts_all = gather(experts_low, PLANE).reshape(EXPERTS_HERE, width, 3 * F)
    output_w = first_all[:, qkv_width : qkv_width + width]
    small_at = qkv_width + width
    router_w = first_all[:, small_at : small_at + E]
    gain_one_f = first_all[:, small_at + E].astype(f32)
    gain_two_f = first_all[:, small_at + E + 1].astype(f32)

    expert_ids = jnp.arange(E, dtype=jnp.int32)
    routed_own = jnp.any(routes[0][:, :, None] == expert_ids[None, None, :], axis=1)
    early = jnp.concatenate([cotangent[0], pad_lanes(routed_own.astype(bf16), LANES)], axis=1)
    early, x_span = lax.optimization_barrier((early, x_span))
    early_all = line_gather(early, "a")

    qkv, normed_span = project(head, x_span, first_all, cos_span, sin_span)
    if whole_rows:
        kv, kv_at = qkv, 1
    else:
        kv, kv_at = gather(qkv[:, PAIR:], "a"), 0
    attention_result, attended, log_total = attend(bounds, qkv, kv, kv_at, doc_column)
    attended_low = (
        exchange(attended.reshape(KEY_VALUE_HEADS, token_count, PAIR), head_axes)
        .transpose(1, 0, 2)
        .reshape(token_count, QUERY_HEADS * HEAD_SIZE)
    )
    attn_out = jnp.dot(attended_low, output_w, preferred_element_type=f32)
    resid = x_local + RESIDUAL_SCALE * attn_out
    normed_two = rms_scale(resid, gain_two_f).astype(bf16)

    normed_two, experts_all, early_all = lax.optimization_barrier(
        (normed_two, experts_all, early_all)
    )
    normed_all = gather(normed_two, "a")
    grad_hidden = jnp.einsum(
        "td,edf->etf",
        early_all[:, :width],
        experts_all[:, :, 2 * F :],
        preferred_element_type=f32,
    )
    back_part, gates_all, gated_hidden, grad_pre = experts(
        group.reshape(1), normed_all, early_all, first_all, experts_all, grad_hidden
    )
    back_own = scatter_sum(back_part, "a").astype(f32)
    moe_part, grad_experts = expert_grads(
        normed_all, early_all, experts_all, gated_hidden, grad_pre
    )
    grad_experts = scatter_sum(grad_experts.reshape(EXPERTS_HERE * width, 3 * F), PLANE)
    moe_terms = line_send(moe_part, "a")

    grad_out = cotangent[0].astype(f32)
    gates = lax.dynamic_slice_in_dim(gates_all, group * token_count, token_count)[:, :E]
    gate_grads_own = back_own[:, width : width + E] + back_own[:, width + E : width + 2 * E]
    grad_logits = gates * (gate_grads_own - jnp.sum(gates * gate_grads_own, axis=-1, keepdims=True))
    grad_normed_two = back_own[:, :width] + jnp.dot(
        grad_logits, router_w.astype(f32).T, precision=HIGHEST_DOT
    )
    grad_router = jnp.dot(normed_two.astype(f32).T, grad_logits, precision=HIGHEST_DOT)
    grad_resid_norm, grad_gain_two = rms_back(resid, gain_two_f, grad_normed_two)
    grad_resid = grad_out + grad_resid_norm
    grad_attn_low = (RESIDUAL_SCALE * grad_resid).astype(bf16)
    grad_heads = contract_cols(grad_attn_low, output_w).astype(bf16)
    grad_mixed = exchange(
        grad_heads.reshape(token_count, KEY_VALUE_HEADS, PAIR).transpose(1, 0, 2), head_axes
    ).reshape(span, PAIR)
    grad_q, grad_kv = attend_back(
        bounds, qkv, kv, kv_at, doc_column, grad_mixed, attention_result, log_total
    )
    if not whole_rows:
        grad_kv = scatter_sum(grad_kv.astype(bf16), "a").astype(f32)
    moe_terms, resid, grad_q = lax.optimization_barrier((moe_terms, resid, grad_q))
    small = jnp.concatenate([grad_router, grad_gain_two[:, None]], axis=1)
    second_part = sum_over_row(
        jnp.concatenate(
            [contract_rows(attended_low, grad_attn_low), pad_lanes(small, LANES)], axis=1
        ).astype(bf16)
    )
    grad_pack = unrotate(grad_q, grad_kv, cos_span, sin_span)
    first_part = sum_over_row(head_grads(head, x_span, normed_span, first_all, grad_pack))
    own = jnp.concatenate([first_part, second_part], axis=3)
    cols = own.shape[3]
    sums = lax.all_to_all(own.reshape(-1, own_rows, cols), SEQ, 0, 0, tiled=True).astype(f32)
    by_heads = sums[:, :, : HEAD_PACK].reshape(-1, KEY_VALUE_HEADS, own_rows, HEAD_PACK).sum(axis=0)
    rest = sums[:, :, HEAD_PACK:].sum(axis=0)
    grad_qkv = (
        exchange(grad_pack.reshape(KEY_VALUE_HEADS, token_count, HEAD_PACK), head_axes)
        .transpose(1, 0, 2)
        .reshape(token_count, qkv_width)
    )
    grad_normed_one = contract_cols(grad_qkv, first_all[:, :qkv_width])
    grad_x_norm, _ = rms_back(x_local, gain_one_f, grad_normed_one)
    grad_input = grad_resid + grad_x_norm
    layer_sum = resid + RESIDUAL_SCALE * sum(term.astype(f32) for term in moe_terms)
    grad_experts = grad_experts.astype(f32)
    by_rows = by_heads.transpose(1, 0, 2)
    small_at = LANES + width
    return (
        layer_sum.astype(bf16)[None],
        grad_input[None],
        rest[:, 0],
        by_rows[:, :, :PAIR].reshape(own_rows, -1),
        by_rows[:, :, PAIR : PAIR + HEAD_SIZE].reshape(own_rows, -1),
        by_rows[:, :, PAIR + HEAD_SIZE :].reshape(own_rows, -1),
        rest[:, LANES:small_at],
        rest[:, small_at + E],
        rest[:, small_at : small_at + E],
        grad_experts[:, : 2 * F],
        grad_experts[:, 2 * F :],
    )


def solution(mesh):
    seq, row = mesh.shape["seq"], mesh.shape["row"]
    cut = Mesh(mesh.devices.reshape(GROUPS, seq // GROUPS, row // 2, 2), ALL)
    token_spec = P(("y", "c"), SEQ, None)
    row_spec = P(ALL, None)
    flat_spec = P(ALL)
    in_specs = (
        token_spec,
        token_spec,
        P(("y", "c"), None),
        token_spec,
        flat_spec,
        row_spec,
        row_spec,
        row_spec,
        row_spec,
        flat_spec,
        row_spec,
        row_spec,
        row_spec,
    )
    out_specs = (
        token_spec,
        token_spec,
        flat_spec,
        row_spec,
        row_spec,
        row_spec,
        row_spec,
        flat_spec,
        row_spec,
        row_spec,
        row_spec,
    )
    return jax.shard_map(body, mesh=cut, in_specs=in_specs, out_specs=out_specs, check_vma=False)
```

```python
import functools

import jax
import jax.numpy as jnp
from jax import lax
from jax.experimental import pallas as pl
from jax.experimental.pallas import tpu as pltpu
from jax.sharding import Mesh, PartitionSpec as P

QUERY_HEADS = 16
KEY_VALUE_HEADS = 8
HEAD_SIZE = 64
F = 512
E = 16
GROUPS = 4
EXPERTS_HERE = E // GROUPS
LANES = 128
PAIR = 2 * HEAD_SIZE
HEAD_PACK = 4 * HEAD_SIZE
BLOCK = 256

NORM_EPS = 1e-06
RESIDUAL_SCALE = 0.22
SCALE_OF_SCORES = 0.015625
ROPE_BASE = 10000.0
NEGATIVE_HUGE = -1e30
HIGHEST_DOT = lax.Precision.HIGHEST
VMEM_LIMIT = 60 * 1024 * 1024

PLANE = ("b", "y", "c")
SEQ = ("a", "b")
ALL = ("a", "b", "y", "c")

f32 = jnp.float32
bf16 = jnp.bfloat16


def rotation_tables(positions):
    half = HEAD_SIZE // 2
    freq = jnp.power(ROPE_BASE, -2.0 * jnp.arange(half, dtype=f32) / HEAD_SIZE)
    angle = positions.astype(f32)[:, None] * freq[None, :]
    return jnp.cos(angle), jnp.sin(angle)


def rms_back(values, gain, grad_norm):
    mean_square = jnp.mean(values * values, axis=-1, keepdims=True)
    inverse = lax.rsqrt(mean_square + NORM_EPS)
    scaled_grad = grad_norm * gain
    grad_values = inverse * scaled_grad - values * inverse**3 * jnp.mean(
        values * scaled_grad, axis=-1, keepdims=True
    )
    grad_gain = jnp.sum(grad_norm * values * inverse, axis=0)
    return (grad_values, grad_gain)


def rms_scale(values, gain):
    mean_square = jnp.mean(values * values, axis=-1, keepdims=True)
    return values * lax.rsqrt(mean_square + NORM_EPS) * gain


def contract_rows(left_side, right_side):
    return lax.dot_general(
        left_side, right_side, (((0,), (0,)), ((), ())), preferred_element_type=f32
    )


def contract_cols(left_side, right_side):
    return lax.dot_general(
        left_side, right_side, (((1,), (1,)), ((), ())), preferred_element_type=f32
    )


def gather(x, axes):
    return lax.all_gather(x, axes, axis=0, tiled=True)


def scatter_sum(x, axes):
    return lax.psum_scatter(x, axes, scatter_dimension=0, tiled=True)


def pad_lanes(x, lanes):
    return jnp.pad(x, ((0, 0), (0, lanes - x.shape[1])))


def line_pairs(n, step):
    return [(i, i + step) for i in range(n) if 0 <= i + step < n]


def line_send(v, axis):
    n, me = lax.axis_size(axis), lax.axis_index(axis)
    v = v.reshape((n, v.shape[0] // n) + v.shape[1:])
    terms = [lax.dynamic_index_in_dim(v, me, 0, False)]
    for j in range(n - 1, 0, -1):
        for step in (j, -j):
            block = lax.dynamic_index_in_dim(v, jnp.clip(me + step, 0, n - 1), 0, False)
            terms.append(lax.ppermute(block, axis, line_pairs(n, step)))
    return tuple(terms)


def grid_gather(x):
    n = lax.axis_size("a")

    def cross(block, ends):
        return lax.ppermute(
            block, SEQ, [(2 * i + j, 2 * i + 1 - j) for i in range(n) if ends(i) for j in (0, 1)]
        )

    pieces = [(0, 0, x), (0, 1, cross(x, lambda i: True))]
    up = down = x
    for k in range(1, n):
        up = lax.ppermute(up, "a", line_pairs(n, 1))
        down = lax.ppermute(down, "a", line_pairs(n, -1))
        pieces += [(-k, 0, up), (-k, 1, cross(up, lambda i: i >= k))]
        pieces += [(k, 0, down), (k, 1, cross(down, lambda i: i + k < n))]
    return pieces


def plane_gather(x):
    swap = [(0, 1), (1, 0)]
    half = x.shape[0] // 2
    from_y = lax.ppermute(x, "y", swap)
    from_b = lax.ppermute(x, "b", swap)
    upper = lax.ppermute(from_b[:half], "y", swap)
    lower = lax.ppermute(from_y[half:], "b", swap)
    return [
        (block, lax.ppermute(block, "c", swap)) for block in (x, from_y, from_b, upper, lower)
    ]


def halve(v, axis, at):
    if lax.axis_size(axis) != 2:
        return lax.psum_scatter(v, axis, scatter_dimension=at, tiled=False)
    me = lax.axis_index(axis)
    other = lax.ppermute(lax.dynamic_index_in_dim(v, 1 - me, at, False), axis, [(0, 1), (1, 0)])
    own = lax.dynamic_index_in_dim(v, me, at, False)
    return (own.astype(f32) + other.astype(f32)).astype(v.dtype)


def sum_over_row(v):
    sizes = tuple(lax.axis_size(axis) for axis in ALL)
    v = v.reshape(sizes + (v.shape[0] // lax.axis_size(ALL), v.shape[1]))
    return halve(halve(v, "c", 3), "y", 2)


def rotate_lanes(x, cos, sin):
    width = x.shape[-1]
    lane = lax.broadcasted_iota(jnp.int32, x.shape, x.ndim - 1)
    swapped = jnp.where(
        lane % HEAD_SIZE < HEAD_SIZE // 2,
        pltpu.roll(x, width - HEAD_SIZE // 2, x.ndim - 1),
        pltpu.roll(x, HEAD_SIZE // 2, x.ndim - 1),
    )
    return x * cos + swapped * sin


def spread_tables(cos, sin):
    return jnp.concatenate([cos] * 4, axis=1), jnp.concatenate([-sin, sin, -sin, sin], axis=1)


def key_tables(cos, sin):
    low = lower_lanes(cos.shape)
    return jnp.where(low, cos, 1.0), jnp.where(low, sin, 0.0)


def project_kernel(places, place_ref, *refs):
    count = 1 if places is None else len(places)
    blocks, refs = refs[:count], refs[count:]
    small_ref, w_ref, cos_ref, sin_ref, qkv_ref, normed_ref, x_ref, gain, held, sems = refs
    i = pl.program_id(0)
    slots = held.shape[0]

    @pl.when(i == 0)
    def _():
        if places is None:
            for slot in range(slots):
                pltpu.make_async_copy(blocks[0].at[slot], held.at[slot], sems.at[slot]).start()
        else:
            for (distance, crossed), block in zip(places, blocks):
                at = place_ref[1] + distance
                member = 1 - place_ref[2] if crossed else place_ref[2]

                @pl.when((at >= 0) & (at < slots // 2))
                def _(block=block, slot=2 * at + member):
                    pltpu.make_async_copy(block, held.at[slot], sems.at[slot]).start()

        gain[...] = jnp.transpose(small_ref[...].astype(f32))[E : E + 8, :]

    arrived = blocks[0].at[0] if places is None else blocks[0]
    pltpu.make_async_copy(arrived, held.at[i], sems.at[i]).wait()
    x = held[i]
    x_ref[...] = x
    normed = rms_scale(x.astype(f32), gain[0:1, :]).astype(bf16)
    normed_ref[...] = normed
    pre = jnp.dot(normed, w_ref[...], preferred_element_type=f32)
    cos, sin = spread_tables(cos_ref[...], sin_ref[...])
    qkv_ref[:, :PAIR] = rotate_lanes(pre[:, :PAIR], cos, sin).astype(bf16)
    qkv_ref[:, PAIR:] = rotate_lanes(pre[:, PAIR:], *key_tables(cos, sin)).astype(bf16)


def project(place, places, blocks, rows, packed, cos, sin):
    width = packed.shape[0]
    small_at = packed.shape[1] // LANES - 1
    span = cos.shape[0]
    table = pl.BlockSpec((rows, HEAD_SIZE // 2), lambda i, h: (i, 0))
    token_rows = pl.BlockSpec((rows, width), lambda i, h: (i, 0))
    return pl.pallas_call(
        functools.partial(project_kernel, places),
        grid_spec=pltpu.PrefetchScalarGridSpec(
            num_scalar_prefetch=1,
            grid=(span // rows,),
            in_specs=[pl.BlockSpec(memory_space=pl.ANY)] * len(blocks)
            + [
                pl.BlockSpec((width, LANES), lambda i, h: (0, small_at)),
                pl.BlockSpec((width, HEAD_PACK), lambda i, h: (0, h[0])),
                table,
                table,
            ],
            out_specs=[
                pl.BlockSpec((rows, HEAD_PACK), lambda i, h: (i, 0)),
                token_rows,
                token_rows,
            ],
            scratch_shapes=[
                pltpu.VMEM((8, width), f32),
                pltpu.VMEM((span // rows, rows, width), bf16),
                pltpu.SemaphoreType.DMA((span // rows,)),
            ],
        ),
        out_shape=[
            jax.ShapeDtypeStruct((span, HEAD_PACK), bf16),
            jax.ShapeDtypeStruct((span, width), bf16),
            jax.ShapeDtypeStruct((span, width), bf16),
        ],
        compiler_params=pltpu.CompilerParams(vmem_limit_bytes=VMEM_LIMIT),
        cost_estimate=pl.CostEstimate(
            flops=2 * span * width * HEAD_PACK, bytes_accessed=18 * 2**20, transcendentals=0
        ),
        name="project",
    )(place, *blocks, packed, packed, cos, sin)


def head_grads_kernel(head_ref, x_ref, normed_ref, w_ref, grad_ref, out_ref, acc, gain):
    i = pl.program_id(0)

    @pl.when(i == 0)
    def _():
        acc[...] = jnp.zeros_like(acc)
        gain[...] = jnp.zeros_like(gain)

    grad = grad_ref[...]
    acc[...] += contract_rows(grad, normed_ref[...])
    x = x_ref[...].astype(f32)
    inverse = lax.rsqrt(jnp.mean(x * x, axis=-1, keepdims=True) + NORM_EPS)
    back = contract_cols(grad, w_ref[...]) * (x * inverse)
    gain[...] += jnp.sum(back.reshape(back.shape[0] // 8, 8, back.shape[1]), axis=0)

    @pl.when(i == pl.num_programs(0) - 1)
    def _():
        out_ref[:, :HEAD_PACK] = jnp.transpose(acc[...]).astype(bf16)
        total = jnp.sum(gain[...], axis=0, keepdims=True)
        rows = lax.broadcasted_iota(jnp.int32, (LANES, total.shape[1]), 0)
        out_ref[:, HEAD_PACK:] = jnp.transpose(
            jnp.where(rows == 0, jnp.broadcast_to(total, rows.shape), 0.0)
        ).astype(bf16)


def head_grads(head, x, normed, packed, grads):
    span, width = x.shape
    rows = BLOCK
    token_rows = pl.BlockSpec((rows, width), lambda i, h: (i, 0))
    return pl.pallas_call(
        head_grads_kernel,
        grid_spec=pltpu.PrefetchScalarGridSpec(
            num_scalar_prefetch=1,
            grid=(span // rows,),
            in_specs=[
                token_rows,
                token_rows,
                pl.BlockSpec((width, HEAD_PACK), lambda i, h: (0, h[0])),
                pl.BlockSpec((rows, HEAD_PACK), lambda i, h: (i, 0)),
            ],
            out_specs=pl.BlockSpec((width, HEAD_PACK + LANES), lambda i, h: (0, 0)),
            scratch_shapes=[pltpu.VMEM((HEAD_PACK, width), f32), pltpu.VMEM((8, width), f32)],
        ),
        out_shape=jax.ShapeDtypeStruct((width, HEAD_PACK + LANES), bf16),
        compiler_params=pltpu.CompilerParams(vmem_limit_bytes=VMEM_LIMIT),
        cost_estimate=pl.CostEstimate(
            flops=4 * span * width * HEAD_PACK, bytes_accessed=12 * 2**20, transcendentals=0
        ),
        name="head_grads",
    )(head, x, normed, packed, grads)


def lower_lanes(shape):
    return lax.broadcasted_iota(jnp.int32, shape, len(shape) - 1) < HEAD_SIZE


def both_heads_low(pair):
    low = lower_lanes(pair.shape)
    return jnp.concatenate(
        [jnp.where(low, pair, 0.0), jnp.where(low, pltpu.roll(pair, HEAD_SIZE, 1), 0.0)], axis=0
    )


def both_heads_high(pair):
    low = lower_lanes(pair.shape)
    return jnp.concatenate(
        [jnp.where(low, 0.0, pltpu.roll(pair, HEAD_SIZE, 1)), jnp.where(low, 0.0, pair)], axis=0
    )


def allowed_pairs(shape, query_start, key_start, doc):
    rows = lax.broadcasted_iota(jnp.int32, (shape[0] // 2, 1), 0) + query_start
    rows = jnp.concatenate([rows, rows], axis=0)
    keys = lax.broadcasted_iota(jnp.int32, shape, 1) + key_start
    return (keys >= jnp.concatenate([doc, doc], axis=0)) & (keys <= rows)


def attend_kernel(bounds_ref, q_ref, kv_ref, doc_ref, o_ref, low_ref, lse_ref, kept, top, total, acc):
    i = pl.program_id(0)
    steps = pl.num_programs(0)
    offset = bounds_ref[steps]
    first, last = bounds_ref[i], i + offset + 1
    q = both_heads_low(q_ref[...].astype(f32) * SCALE_OF_SCORES).astype(bf16)
    doc = doc_ref[...]
    top[...] = jnp.full_like(top, NEGATIVE_HUGE)
    total[...] = jnp.zeros_like(total)
    acc[...] = jnp.zeros_like(acc)

    def score(j, carried):
        start = pl.multiple_of(j * BLOCK, BLOCK)
        scores = contract_cols(q, kv_ref[pl.ds(start, BLOCK), :])
        allowed = allowed_pairs(scores.shape, (i + offset) * BLOCK, j * BLOCK, doc)
        scores = jnp.where(allowed, scores, NEGATIVE_HUGE)
        kept[:, pl.ds(start, BLOCK)] = scores
        top[...] = jnp.maximum(top[...], jnp.maximum(scores[:, :LANES], scores[:, LANES:]))
        return carried

    lax.fori_loop(first, last, score, 0)
    highest = jnp.max(top[...], axis=1, keepdims=True)

    def mix(j, carried):
        start = pl.multiple_of(j * BLOCK, BLOCK)
        probs = jnp.exp(kept[:, pl.ds(start, BLOCK)] - highest)
        total[...] += probs[:, :LANES] + probs[:, LANES:]
        acc[...] += jnp.dot(
            probs.astype(bf16), kv_ref[pl.ds(start, BLOCK), :], preferred_element_type=f32
        )
        return carried

    lax.fori_loop(first, last, mix, 0)
    row_total = jnp.sum(total[...], axis=1, keepdims=True)
    mixed = acc[...] / row_total
    first_head, second_head = mixed[:BLOCK], mixed[BLOCK:]
    out = jnp.where(
        lower_lanes(first_head.shape), pltpu.roll(first_head, HEAD_SIZE, 1), second_head
    )
    o_ref[...] = out
    low_ref[...] = out.astype(bf16)
    lse_ref[0] = highest + jnp.log(row_total)


def attend(bounds, qkv, kv, kv_at, doc):
    queries, keys = qkv.shape[0], kv.shape[0]
    steps = queries // BLOCK
    pair = pl.BlockSpec((BLOCK, PAIR), lambda i, s: (i, 0))
    return pl.pallas_call(
        attend_kernel,
        grid_spec=pltpu.PrefetchScalarGridSpec(
            num_scalar_prefetch=1,
            grid=(steps,),
            in_specs=[
                pair,
                pl.BlockSpec((keys, PAIR), lambda i, s: (0, kv_at)),
                pl.BlockSpec((BLOCK, 1), lambda i, s: (i, 0)),
            ],
            out_specs=[pair, pair, pl.BlockSpec((1, 2 * BLOCK, 1), lambda i, s: (i, 0, 0))],
            scratch_shapes=[
                pltpu.VMEM((2 * BLOCK, keys), f32),
                pltpu.VMEM((2 * BLOCK, LANES), f32),
                pltpu.VMEM((2 * BLOCK, LANES), f32),
                pltpu.VMEM((2 * BLOCK, PAIR), f32),
            ],
        ),
        out_shape=[
            jax.ShapeDtypeStruct((queries, PAIR), f32),
            jax.ShapeDtypeStruct((queries, PAIR), bf16),
            jax.ShapeDtypeStruct((steps, 2 * BLOCK, 1), f32),
        ],
        compiler_params=pltpu.CompilerParams(vmem_limit_bytes=VMEM_LIMIT),
        cost_estimate=pl.CostEstimate(
            flops=4 * queries * keys * PAIR, bytes_accessed=6 * 2**20, transcendentals=queries * keys
        ),
        name="attend",
    )(bounds, qkv, kv, doc)


def attend_back_kernel(
    fold, bounds_ref, q_ref, kv_ref, doc_ref, do_ref, o_ref, lse_ref, cos_ref, sin_ref, *refs
):
    if fold:
        out_ref, acc, dkv_ref = refs
    else:
        dq_ref, dkv_ref, acc = refs
    i = pl.program_id(0)
    steps = pl.num_programs(0)
    offset = bounds_ref[steps]

    @pl.when(i == 0)
    def _():
        dkv_ref[...] = jnp.zeros_like(dkv_ref)

    q = both_heads_low(q_ref[...].astype(f32) * SCALE_OF_SCORES).astype(bf16)
    grad = do_ref[...].astype(f32)
    product = grad * o_ref[...]
    low = lower_lanes(product.shape)
    delta = jnp.concatenate(
        [
            jnp.sum(jnp.where(low, product, 0.0), axis=1, keepdims=True),
            jnp.sum(jnp.where(low, 0.0, product), axis=1, keepdims=True),
        ],
        axis=0,
    )
    grad = both_heads_high(grad).astype(bf16)
    sources = jnp.concatenate([q, grad], axis=0)
    doc = doc_ref[...]
    lse = lse_ref[0]
    acc[...] = jnp.zeros_like(acc)

    def step(j, carried):
        start = pl.multiple_of(j * BLOCK, BLOCK)
        kv = kv_ref[pl.ds(start, BLOCK), :]
        scores = contract_cols(q, kv)
        allowed = allowed_pairs(scores.shape, (i + offset) * BLOCK, j * BLOCK, doc)
        probs = jnp.exp(jnp.where(allowed, scores - lse, NEGATIVE_HUGE))
        grad_probs = contract_cols(grad, kv)
        grad_scores = (probs * (grad_probs - delta)).astype(bf16)
        acc[...] += jnp.dot(grad_scores, kv, preferred_element_type=f32)
        both = jnp.concatenate([grad_scores, probs.astype(bf16)], axis=0)
        dkv_ref[pl.ds(start, BLOCK), :] += contract_rows(both, sources)
        return carried

    lax.fori_loop(bounds_ref[i], i + offset + 1, step, 0)
    first, second = acc[:BLOCK], acc[BLOCK:]
    dq = jnp.where(lower_lanes(first.shape), first, pltpu.roll(second, HEAD_SIZE, 1))
    if not fold:
        dq_ref[...] = dq
        return
    mine = pl.ds(pl.multiple_of(i * BLOCK, BLOCK), BLOCK)
    cos, sin = spread_tables(cos_ref[mine, :], sin_ref[mine, :])
    out_ref[mine, :PAIR] = rotate_lanes(dq * SCALE_OF_SCORES, cos, -sin).astype(bf16)

    @pl.when(i == steps - 1)
    def _():
        def finish(j, carried):
            part = pl.ds(pl.multiple_of(j * BLOCK, BLOCK), BLOCK)
            cos, sin = key_tables(*spread_tables(cos_ref[part, :], sin_ref[part, :]))
            out_ref[part, PAIR:] = rotate_lanes(dkv_ref[part, :], cos, -sin).astype(bf16)
            return carried

        lax.fori_loop(0, dkv_ref.shape[0] // BLOCK, finish, 0)


def attend_back(bounds, qkv, kv, kv_at, doc, grad, out, lse, cos, sin, fold):
    queries, keys = qkv.shape[0], kv.shape[0]
    steps = queries // BLOCK
    pair = pl.BlockSpec((BLOCK, PAIR), lambda i, s: (i, 0))
    table = pl.BlockSpec(cos.shape, lambda i, s: (0, 0))
    acc = pltpu.VMEM((2 * BLOCK, PAIR), f32)
    if fold:
        out_specs = pl.BlockSpec((queries, HEAD_PACK), lambda i, s: (0, 0))
        out_shape = jax.ShapeDtypeStruct((queries, HEAD_PACK), bf16)
        scratch = [acc, pltpu.VMEM((keys, PAIR), f32)]
    else:
        out_specs = [pair, pl.BlockSpec((keys, PAIR), lambda i, s: (0, 0))]
        out_shape = [
            jax.ShapeDtypeStruct((queries, PAIR), f32),
            jax.ShapeDtypeStruct((keys, PAIR), f32),
        ]
        scratch = [acc]
    return pl.pallas_call(
        functools.partial(attend_back_kernel, fold),
        grid_spec=pltpu.PrefetchScalarGridSpec(
            num_scalar_prefetch=1,
            grid=(steps,),
            in_specs=[
                pair,
                pl.BlockSpec((keys, PAIR), lambda i, s: (0, kv_at)),
                pl.BlockSpec((BLOCK, 1), lambda i, s: (i, 0)),
                pair,
                pair,
                pl.BlockSpec((1, 2 * BLOCK, 1), lambda i, s: (i, 0, 0)),
                table,
                table,
            ],
            out_specs=out_specs,
            scratch_shapes=scratch,
        ),
        out_shape=out_shape,
        compiler_params=pltpu.CompilerParams(vmem_limit_bytes=VMEM_LIMIT),
        cost_estimate=pl.CostEstimate(
            flops=10 * queries * keys * PAIR,
            bytes_accessed=8 * 2**20,
            transcendentals=queries * keys,
        ),
        name="attend_back",
    )(bounds, qkv, kv, doc, grad, out, lse, cos, sin)


def unrotate_kernel(dq_ref, dkv_ref, cos_ref, sin_ref, out_ref):
    cos, sin = spread_tables(cos_ref[...], sin_ref[...])
    dq = rotate_lanes(dq_ref[...] * SCALE_OF_SCORES, cos, -sin)
    cos, sin = key_tables(cos, sin)
    dkv = rotate_lanes(dkv_ref[...], cos, -sin)
    out_ref[...] = jnp.concatenate([dq, dkv], axis=1).astype(bf16)


def unrotate(dq, dkv, cos, sin):
    rows = dq.shape[0]
    pair = pl.BlockSpec((BLOCK, PAIR), lambda i: (i, 0))
    table = pl.BlockSpec((BLOCK, HEAD_SIZE // 2), lambda i: (i, 0))
    return pl.pallas_call(
        unrotate_kernel,
        grid=(rows // BLOCK,),
        in_specs=[pair, pair, table, table],
        out_specs=pl.BlockSpec((BLOCK, HEAD_PACK), lambda i: (i, 0)),
        out_shape=jax.ShapeDtypeStruct((rows, HEAD_PACK), bf16),
        cost_estimate=pl.CostEstimate(
            flops=rows * HEAD_PACK * 8, bytes_accessed=rows * HEAD_PACK * 14, transcendentals=0
        ),
        name="unrotate",
    )(dq, dkv, cos, sin)


def place_experts_kernel(place_ref, *refs):
    blocks, (ct_ref, w_ref, z_ref, sems) = refs[:10], refs[10:]
    core = place_ref[1]
    rows = w_ref.shape[1] // 2
    half = rows // 2
    sources = [[(0, 0, rows)], [(1, 0, rows)], [(2, 0, rows)], [(3, 0, half), (4, half, half)]]
    for step, parts in enumerate(sources):

        @pl.when(pl.program_id(0) == step)
        def _(parts=parts):
            copies = []
            for source, start, length in parts:
                for other in (0, 1):
                    first = jnp.where(core == other, 0, rows) + start
                    at = pl.ds(pl.multiple_of(first, half), length)
                    copies.append(
                        pltpu.make_async_copy(
                            blocks[2 * source + other], w_ref.at[0, at, :], sems.at[len(copies)]
                        )
                    )
            for copy in copies:
                copy.start()
            for copy in copies:
                copy.wait()

    z_ref[0] = jnp.dot(ct_ref[...], w_ref[0, :, 2 * F :], preferred_element_type=f32)


def place_experts(place, parts, early, width):
    rows = early.shape[0]
    blocks = [block for pair in parts for block in pair]
    return pl.pallas_call(
        place_experts_kernel,
        grid_spec=pltpu.PrefetchScalarGridSpec(
            num_scalar_prefetch=1,
            grid=(EXPERTS_HERE,),
            in_specs=[pl.BlockSpec(memory_space=pl.ANY)] * len(blocks)
            + [pl.BlockSpec((rows, width), lambda r, s: (0, 0))],
            out_specs=[
                pl.BlockSpec((1, width, 3 * F), lambda r, s: (s[0] ^ r, 0, 0)),
                pl.BlockSpec((1, rows, F), lambda r, s: (s[0] ^ r, 0, 0)),
            ],
            scratch_shapes=[pltpu.SemaphoreType.DMA((4,))],
        ),
        out_shape=[
            jax.ShapeDtypeStruct((EXPERTS_HERE, width, 3 * F), bf16),
            jax.ShapeDtypeStruct((EXPERTS_HERE, rows, F), f32),
        ],
        compiler_params=pltpu.CompilerParams(vmem_limit_bytes=VMEM_LIMIT),
        cost_estimate=pl.CostEstimate(
            flops=2 * EXPERTS_HERE * rows * width * F, bytes_accessed=36 * 2**20, transcendentals=0
        ),
        name="place_experts",
    )(place, *blocks, early)


def lane_column(x, at):
    lane = lax.broadcasted_iota(jnp.int32, x.shape, 1)
    return jnp.sum(jnp.where(lane == at, x, 0.0), axis=1, keepdims=True)


def experts_kernel(
    group_ref, n_ref, routed_ref, router_ref, w_ref, z_ref,
    back_ref, gates_ref, hidden_ref, pre_ref, acc, dots,
):
    e = pl.program_id(0)
    own = group_ref[0] * EXPERTS_HERE + e
    rows = n_ref.shape[0]

    @pl.when(e == 0)
    def _():
        logits = jnp.dot(n_ref[...], router_ref[...], preferred_element_type=f32)
        routed = routed_ref[...].astype(f32) > 0.5
        highest = jnp.max(jnp.where(routed, logits, NEGATIVE_HUGE), axis=1, keepdims=True)
        weights = jnp.where(routed, jnp.exp(jnp.where(routed, logits - highest, 0.0)), 0.0)
        gates_ref[...] = weights / jnp.sum(weights, axis=1, keepdims=True)
        acc[...] = jnp.zeros_like(acc)
        dots[...] = jnp.zeros_like(dots)

    w_in = w_ref[0, :, : 2 * F]
    for t in range(rows // BLOCK):
        part = pl.ds(t * BLOCK, BLOCK)
        pre = jnp.dot(n_ref[part, :], w_in, preferred_element_type=f32)
        gate, up = pre[:, :F], pre[:, F:]
        z = z_ref[0, part, :]
        weight = lane_column(gates_ref[part, :], own)
        sig = 1.0 / (1.0 + jnp.exp(-gate))
        act = gate * sig
        hidden = act * up
        hidden_ref[0, part, :] = (weight * hidden).astype(bf16)
        dot = RESIDUAL_SCALE * jnp.sum(hidden.astype(bf16).astype(f32) * z, axis=1, keepdims=True)
        lane = lax.broadcasted_iota(jnp.int32, (BLOCK, LANES), 1)
        dots[part, :] += jnp.where(lane == own, dot, 0.0)
        scaled = (RESIDUAL_SCALE * weight) * z
        pre_ref[0, part, :F] = (scaled * up * (sig + act * (1.0 - sig))).astype(bf16)
        pre_ref[0, part, F:] = (scaled * act).astype(bf16)
        acc[part, :] += contract_cols(pre_ref[0, part, :], w_in)

    @pl.when(e == EXPERTS_HERE - 1)
    def _():
        width = n_ref.shape[1]
        back_ref[:, :width] = acc[...].astype(bf16)
        high = dots[...].astype(bf16)
        low = dots[...] - high.astype(f32)
        back_ref[:, width:] = (high.astype(f32) + pltpu.roll(low, E, 1)).astype(bf16)


def experts(group, normed, early, packed, w_all, z):
    rows, width = normed.shape
    count = w_all.shape[0]
    whole = pl.BlockSpec((rows, width), lambda e, g: (0, 0))
    column = width // LANES
    router_at = packed.shape[1] // LANES - 1
    return pl.pallas_call(
        experts_kernel,
        grid_spec=pltpu.PrefetchScalarGridSpec(
            num_scalar_prefetch=1,
            grid=(count,),
            in_specs=[
                whole,
                pl.BlockSpec((rows, LANES), lambda e, g: (0, column)),
                pl.BlockSpec((width, LANES), lambda e, g: (0, router_at)),
                pl.BlockSpec((1, width, 3 * F), lambda e, g: (e, 0, 0)),
                pl.BlockSpec((1, rows, F), lambda e, g: (e, 0, 0)),
            ],
            out_specs=[
                pl.BlockSpec((rows, width + LANES), lambda e, g: (0, 0)),
                pl.BlockSpec((rows, LANES), lambda e, g: (0, 0)),
                pl.BlockSpec((1, rows, F), lambda e, g: (e, 0, 0)),
                pl.BlockSpec((1, rows, 2 * F), lambda e, g: (e, 0, 0)),
            ],
            scratch_shapes=[pltpu.VMEM((rows, width), f32), pltpu.VMEM((rows, LANES), f32)],
        ),
        out_shape=[
            jax.ShapeDtypeStruct((rows, width + LANES), bf16),
            jax.ShapeDtypeStruct((rows, LANES), f32),
            jax.ShapeDtypeStruct((count, rows, F), bf16),
            jax.ShapeDtypeStruct((count, rows, 2 * F), bf16),
        ],
        compiler_params=pltpu.CompilerParams(vmem_limit_bytes=VMEM_LIMIT),
        cost_estimate=pl.CostEstimate(
            flops=2 * count * rows * width * 4 * F, bytes_accessed=40 * 2**20, transcendentals=0
        ),
        name="experts",
    )(group, normed, early, packed, w_all, z)


def expert_grads_kernel(n_ref, ct_ref, w_ref, hidden_ref, pre_ref, y_ref, grad_ref, n_t, ct_t, acc):
    e = pl.program_id(0)

    @pl.when(e == 0)
    def _():
        n_t[...] = jnp.transpose(n_ref[...])
        ct_t[...] = jnp.transpose(ct_ref[...])
        acc[...] = jnp.zeros_like(acc)

    grad_ref[0, :, : 2 * F] = jnp.dot(
        n_t[...], pre_ref[0], preferred_element_type=f32
    ).astype(bf16)
    grad_ref[0, :, 2 * F :] = (
        RESIDUAL_SCALE * jnp.dot(ct_t[...], hidden_ref[0], preferred_element_type=f32)
    ).astype(bf16)
    acc[...] += contract_cols(hidden_ref[0], w_ref[0, :, 2 * F :])

    @pl.when(e == EXPERTS_HERE - 1)
    def _():
        y_ref[...] = acc[...].astype(bf16)


def expert_grads(normed, early, w_all, hidden, pre):
    rows, width = normed.shape
    count = w_all.shape[0]
    whole = pl.BlockSpec((rows, width), lambda e: (0, 0))
    return pl.pallas_call(
        expert_grads_kernel,
        grid=(count,),
        in_specs=[
            whole,
            whole,
            pl.BlockSpec((1, width, 3 * F), lambda e: (e, 0, 0)),
            pl.BlockSpec((1, rows, F), lambda e: (e, 0, 0)),
            pl.BlockSpec((1, rows, 2 * F), lambda e: (e, 0, 0)),
        ],
        out_specs=[whole, pl.BlockSpec((1, width, 3 * F), lambda e: (e, 0, 0))],
        out_shape=[
            jax.ShapeDtypeStruct((rows, width), bf16),
            jax.ShapeDtypeStruct((count, width, 3 * F), bf16),
        ],
        scratch_shapes=[
            pltpu.VMEM((width, rows), bf16),
            pltpu.VMEM((width, rows), bf16),
            pltpu.VMEM((rows, width), f32),
        ],
        compiler_params=pltpu.CompilerParams(vmem_limit_bytes=VMEM_LIMIT),
        cost_estimate=pl.CostEstimate(
            flops=2 * count * rows * width * 4 * F, bytes_accessed=40 * 2**20, transcendentals=0
        ),
        name="expert_grads",
    )(normed, early, w_all, hidden, pre)


def exchange(x, axes):
    return lax.all_to_all(x, axes, 0, 0, tiled=True)


def body(
    tokens,
    cotangent,
    segment_ids,
    routes,
    norm_attn,
    w_query,
    key_weight_matrix,
    value_weight_matrix,
    w_output,
    norm_moe,
    w_router,
    expert_in,
    expert_out,
):
    x_local = tokens[0].astype(f32)
    token_count, width = x_local.shape
    seg_row = segment_ids[0]
    group = lax.axis_index("a")
    head_axes = SEQ if lax.axis_size(SEQ) == KEY_VALUE_HEADS else ("b",)
    whole_rows = head_axes == SEQ
    span = token_count * KEY_VALUE_HEADS
    span_start = 0 if whole_rows else group * span

    def start_of_doc(ids):
        return jnp.sum((seg_row[None, :] < ids[:, None]).astype(jnp.int32), axis=1)

    seg_span = lax.dynamic_slice_in_dim(seg_row, span_start, span)
    doc_span = start_of_doc(seg_span)
    cos_span, sin_span = rotation_tables(
        span_start + jnp.arange(span, dtype=jnp.int32) - doc_span
    )
    bounds = jnp.concatenate(
        [
            doc_span.reshape(-1, BLOCK)[:, 0] // BLOCK,
            jnp.full((1,), span_start // BLOCK, jnp.int32),
        ]
    )
    doc_column = doc_span[:, None]

    own_rows = w_query.shape[0]
    by_head = jnp.concatenate(
        [
            w_query.astype(bf16).reshape(own_rows, KEY_VALUE_HEADS, PAIR),
            key_weight_matrix.astype(bf16).reshape(own_rows, KEY_VALUE_HEADS, HEAD_SIZE),
            value_weight_matrix.astype(bf16).reshape(own_rows, KEY_VALUE_HEADS, HEAD_SIZE),
        ],
        axis=2,
    ).reshape(own_rows, KEY_VALUE_HEADS * HEAD_PACK)
    qkv_width = KEY_VALUE_HEADS * HEAD_PACK
    first_all = gather(
        jnp.concatenate(
            [
                by_head,
                w_output.astype(bf16),
                pad_lanes(
                    jnp.concatenate(
                        [
                            w_router.astype(bf16),
                            norm_attn.astype(bf16)[:, None],
                            norm_moe.astype(bf16)[:, None],
                        ],
                        axis=1,
                    ),
                    LANES,
                ),
            ],
            axis=1,
        ),
        ALL,
    )
    experts_low = jnp.concatenate([expert_in.astype(bf16), expert_out.astype(bf16)], axis=1)
    if whole_rows:
        pieces = grid_gather(tokens[0])
        places = [piece[:2] for piece in pieces]
        blocks = tuple(piece[2] for piece in pieces)
    else:
        places = None
        blocks = (gather(tokens[0], "b").reshape((-1,) + tokens.shape[1:]),)
    first_all, experts_low, blocks, cos_span, sin_span, bounds, doc_column = (
        lax.optimization_barrier(
            (first_all, experts_low, blocks, cos_span, sin_span, bounds, doc_column)
        )
    )
    output_w = first_all[:, qkv_width : qkv_width + width]
    small_at = qkv_width + width
    router_w = first_all[:, small_at : small_at + E]
    gain_one_f = first_all[:, small_at + E].astype(f32)
    gain_two_f = first_all[:, small_at + E + 1].astype(f32)

    expert_ids = jnp.arange(E, dtype=jnp.int32)
    routed_own = jnp.any(routes[0][:, :, None] == expert_ids[None, None, :], axis=1)
    early = jnp.concatenate([cotangent[0], pad_lanes(routed_own.astype(bf16), LANES)], axis=1)
    early, first_all = lax.optimization_barrier((early, first_all))
    early_all = gather(early, "a")
    small_plane = lax.axis_size("b") == 2 and lax.axis_size("y") == 2
    if small_plane:
        parts = plane_gather(experts_low)
    else:
        parts = gather(experts_low, PLANE)

    place = jnp.stack([lax.axis_index(head_axes), group, lax.axis_index("b")])
    qkv, normed_span, x_span = project(
        place, places, blocks, token_count, first_all, cos_span, sin_span
    )
    if whole_rows:
        kv, kv_at = qkv, 1
    else:
        kv, kv_at = gather(qkv[:, PAIR:], "a"), 0
    attention_result, attended, log_total = attend(bounds, qkv, kv, kv_at, doc_column)
    attended_low = (
        exchange(attended.reshape(KEY_VALUE_HEADS, token_count, PAIR), head_axes)
        .transpose(1, 0, 2)
        .reshape(token_count, QUERY_HEADS * HEAD_SIZE)
    )
    attn_out = jnp.dot(attended_low, output_w, preferred_element_type=f32)
    resid = x_local + RESIDUAL_SCALE * attn_out
    normed_two = rms_scale(resid, gain_two_f).astype(bf16)

    normed_two, parts, early_all = lax.optimization_barrier((normed_two, parts, early_all))
    normed_all = gather(normed_two, "a")
    if small_plane:
        home = jnp.stack([lax.axis_index("b") * 2 + lax.axis_index("y"), lax.axis_index("c")])
        experts_all, grad_hidden = place_experts(home, parts, early_all, width)
    else:
        experts_all = parts.reshape(EXPERTS_HERE, width, 3 * F)
        grad_hidden = jnp.einsum(
            "td,edf->etf",
            early_all[:, :width],
            experts_all[:, :, 2 * F :],
            preferred_element_type=f32,
        )
    back_part, gates_all, gated_hidden, grad_pre = experts(
        group.reshape(1), normed_all, early_all, first_all, experts_all, grad_hidden
    )
    back_own = scatter_sum(back_part, "a").astype(f32)
    moe_part, grad_experts = expert_grads(
        normed_all, early_all, experts_all, gated_hidden, grad_pre
    )
    back_own, moe_part, grad_experts = lax.optimization_barrier(
        (back_own, moe_part, grad_experts)
    )
    grad_experts = scatter_sum(grad_experts.reshape(EXPERTS_HERE * width, 3 * F), PLANE)
    moe_terms = line_send(moe_part, "a")

    grad_out = cotangent[0].astype(f32)
    gates = lax.dynamic_slice_in_dim(gates_all, group * token_count, token_count)[:, :E]
    gate_grads_own = back_own[:, width : width + E] + back_own[:, width + E : width + 2 * E]
    grad_logits = gates * (gate_grads_own - jnp.sum(gates * gate_grads_own, axis=-1, keepdims=True))
    grad_normed_two = back_own[:, :width] + jnp.dot(
        grad_logits, router_w.astype(f32).T, precision=HIGHEST_DOT
    )
    grad_router = jnp.dot(normed_two.astype(f32).T, grad_logits, precision=HIGHEST_DOT)
    grad_resid_norm, grad_gain_two = rms_back(resid, gain_two_f, grad_normed_two)
    grad_resid = grad_out + grad_resid_norm
    grad_attn_low = (RESIDUAL_SCALE * grad_resid).astype(bf16)
    grad_heads = contract_cols(grad_attn_low, output_w).astype(bf16)
    grad_mixed = exchange(
        grad_heads.reshape(token_count, KEY_VALUE_HEADS, PAIR).transpose(1, 0, 2), head_axes
    ).reshape(span, PAIR)
    small = jnp.concatenate([grad_router, grad_gain_two[:, None]], axis=1)
    second_part = sum_over_row(
        jnp.concatenate(
            [contract_rows(attended_low, grad_attn_low), pad_lanes(small, LANES)], axis=1
        ).astype(bf16)
    )
    second_part = halve(second_part, "b", 1)
    rest = line_send(second_part.reshape(-1, second_part.shape[2]), "a")
    grads = attend_back(
        bounds, qkv, kv, kv_at, doc_column, grad_mixed, attention_result, log_total,
        cos_span, sin_span, whole_rows,
    )
    if whole_rows:
        grad_pack = grads
    else:
        grad_kv = scatter_sum(grads[1].astype(bf16), "a").astype(f32)
        grad_pack = unrotate(grads[0], grad_kv, cos_span, sin_span)
    moe_terms, resid, grad_pack = lax.optimization_barrier((moe_terms, resid, grad_pack))
    first_part = head_grads(place, x_span, normed_span, first_all, grad_pack)
    by_tokens = exchange(grad_pack.reshape(KEY_VALUE_HEADS, token_count, HEAD_PACK), head_axes)
    by_tokens, first_part = lax.optimization_barrier((by_tokens, first_part))
    sums = exchange(first_part.reshape(-1, own_rows, first_part.shape[1]), ALL).astype(f32)
    sums = sums.reshape(lax.axis_size(SEQ), -1, own_rows, first_part.shape[1]).sum(axis=1)
    by_heads = sums[:, :, :HEAD_PACK].reshape(-1, KEY_VALUE_HEADS, own_rows, HEAD_PACK).sum(axis=0)
    rest = sum(term.astype(f32) for term in rest)
    grad_qkv = by_tokens.transpose(1, 0, 2).reshape(token_count, qkv_width)
    grad_normed_one = contract_cols(grad_qkv, first_all[:, :qkv_width])
    grad_x_norm, _ = rms_back(x_local, gain_one_f, grad_normed_one)
    grad_input = grad_resid + grad_x_norm
    layer_sum = resid + RESIDUAL_SCALE * sum(term.astype(f32) for term in moe_terms)
    grad_experts = grad_experts.astype(f32)
    by_rows = by_heads.transpose(1, 0, 2)
    return (
        layer_sum.astype(bf16)[None],
        grad_input[None],
        sums[:, :, HEAD_PACK].sum(axis=0),
        by_rows[:, :, :PAIR].reshape(own_rows, -1),
        by_rows[:, :, PAIR : PAIR + HEAD_SIZE].reshape(own_rows, -1),
        by_rows[:, :, PAIR + HEAD_SIZE :].reshape(own_rows, -1),
        rest[:, :width],
        rest[:, width + E],
        rest[:, width : width + E],
        grad_experts[:, : 2 * F],
        grad_experts[:, 2 * F :],
    )


def solution(mesh):
    seq, row = mesh.shape["seq"], mesh.shape["row"]
    cut = Mesh(mesh.devices.reshape(GROUPS, seq // GROUPS, row // 2, 2), ALL)
    token_spec = P(("y", "c"), SEQ, None)
    row_spec = P(ALL, None)
    flat_spec = P(ALL)
    in_specs = (
        token_spec,
        token_spec,
        P(("y", "c"), None),
        token_spec,
        flat_spec,
        row_spec,
        row_spec,
        row_spec,
        row_spec,
        flat_spec,
        row_spec,
        row_spec,
        row_spec,
    )
    out_specs = (
        token_spec,
        token_spec,
        flat_spec,
        row_spec,
        row_spec,
        row_spec,
        row_spec,
        flat_spec,
        row_spec,
        row_spec,
        row_spec,
    )
    return jax.shard_map(body, mesh=cut, in_specs=in_specs, out_specs=out_specs, check_vma=False)
```

```python
import functools

import jax
import jax.numpy as jnp
from jax import lax
from jax.experimental import pallas as pl
from jax.experimental.pallas import tpu as pltpu
from jax.sharding import Mesh, PartitionSpec as P

QUERY_HEADS = 16
KEY_VALUE_HEADS = 8
HEAD_SIZE = 64
F = 512
E = 16
GROUPS = 4
EXPERTS_HERE = E // GROUPS
LANES = 128
PAIR = 2 * HEAD_SIZE
HEAD_PACK = 4 * HEAD_SIZE
BLOCK = 256

NORM_EPS = 1e-06
RESIDUAL_SCALE = 0.22
SCALE_OF_SCORES = 0.015625
ROPE_BASE = 10000.0
NEGATIVE_HUGE = -1e30
HIGHEST_DOT = lax.Precision.HIGHEST
VMEM_LIMIT = 60 * 1024 * 1024

PLANE = ("b", "y", "c")
SEQ = ("a", "b")
ALL = ("a", "b", "y", "c")

f32 = jnp.float32
bf16 = jnp.bfloat16


def rotation_tables(positions):
    half = HEAD_SIZE // 2
    freq = jnp.power(ROPE_BASE, -2.0 * jnp.arange(half, dtype=f32) / HEAD_SIZE)
    angle = positions.astype(f32)[:, None] * freq[None, :]
    return jnp.cos(angle), jnp.sin(angle)


def rms_back(values, gain, grad_norm):
    mean_square = jnp.mean(values * values, axis=-1, keepdims=True)
    inverse = lax.rsqrt(mean_square + NORM_EPS)
    scaled_grad = grad_norm * gain
    grad_values = inverse * scaled_grad - values * inverse**3 * jnp.mean(
        values * scaled_grad, axis=-1, keepdims=True
    )
    grad_gain = jnp.sum(grad_norm * values * inverse, axis=0)
    return (grad_values, grad_gain)


def rms_scale(values, gain):
    mean_square = jnp.mean(values * values, axis=-1, keepdims=True)
    return values * lax.rsqrt(mean_square + NORM_EPS) * gain


def contract_rows(left_side, right_side):
    return lax.dot_general(
        left_side, right_side, (((0,), (0,)), ((), ())), preferred_element_type=f32
    )


def contract_cols(left_side, right_side):
    return lax.dot_general(
        left_side, right_side, (((1,), (1,)), ((), ())), preferred_element_type=f32
    )


def gather(x, axes):
    return lax.all_gather(x, axes, axis=0, tiled=True)


def scatter_sum(x, axes):
    return lax.psum_scatter(x, axes, scatter_dimension=0, tiled=True)


def pad_lanes(x, lanes):
    return jnp.pad(x, ((0, 0), (0, lanes - x.shape[1])))


def line_pairs(n, step):
    return [(i, i + step) for i in range(n) if 0 <= i + step < n]


def grid_gather(x):
    n = lax.axis_size("a")

    def cross(block, ends):
        return lax.ppermute(
            block, SEQ, [(2 * i + j, 2 * i + 1 - j) for i in range(n) if ends(i) for j in (0, 1)]
        )

    pieces = [(0, 0, x), (0, 1, cross(x, lambda i: True))]
    up = down = x
    for k in range(1, n):
        up = lax.ppermute(up, "a", line_pairs(n, 1))
        down = lax.ppermute(down, "a", line_pairs(n, -1))
        pieces += [(-k, 0, up), (-k, 1, cross(up, lambda i: i >= k))]
        pieces += [(k, 0, down), (k, 1, cross(down, lambda i: i + k < n))]
    return pieces


def plane_gather(x):
    swap = [(0, 1), (1, 0)]
    half = x.shape[0] // 2
    from_y = lax.ppermute(x, "y", swap)
    from_b = lax.ppermute(x, "b", swap)
    upper = lax.ppermute(from_b[:half], "y", swap)
    lower = lax.ppermute(from_y[half:], "b", swap)
    return [
        (block, lax.ppermute(block, "c", swap)) for block in (x, from_y, from_b, upper, lower)
    ]


def halve_send(v, axis, at):
    me = lax.axis_index(axis)
    other = lax.ppermute(lax.dynamic_index_in_dim(v, 1 - me, at, False), axis, [(0, 1), (1, 0)])
    return lax.dynamic_index_in_dim(v, me, at, False), other


def halve_add(terms):
    own, other = terms
    return (own.astype(f32) + other.astype(f32)).astype(own.dtype)


def rotate_lanes(x, cos, sin):
    width = x.shape[-1]
    lane = lax.broadcasted_iota(jnp.int32, x.shape, x.ndim - 1)
    swapped = jnp.where(
        lane % HEAD_SIZE < HEAD_SIZE // 2,
        pltpu.roll(x, width - HEAD_SIZE // 2, x.ndim - 1),
        pltpu.roll(x, HEAD_SIZE // 2, x.ndim - 1),
    )
    return x * cos + swapped * sin


def spread_tables(cos, sin):
    return jnp.concatenate([cos] * 4, axis=1), jnp.concatenate([-sin, sin, -sin, sin], axis=1)


def key_tables(cos, sin):
    low = lower_lanes(cos.shape)
    return jnp.where(low, cos, 1.0), jnp.where(low, sin, 0.0)


def project_kernel(places, place_ref, *refs):
    count = 1 if places is None else len(places)
    blocks, refs = refs[:count], refs[count:]
    small_ref, w_ref, cos_ref, sin_ref, qkv_ref, normed_ref, x_ref, gain, held, sems = refs
    i = pl.program_id(0)
    slots = held.shape[0]

    @pl.when(i == 0)
    def _():
        if places is None:
            for slot in range(slots):
                pltpu.make_async_copy(blocks[0].at[slot], held.at[slot], sems.at[slot]).start()
        else:
            for (distance, crossed), block in zip(places, blocks):
                at = place_ref[1] + distance
                member = 1 - place_ref[2] if crossed else place_ref[2]

                @pl.when((at >= 0) & (at < slots // 2))
                def _(block=block, slot=2 * at + member):
                    pltpu.make_async_copy(block, held.at[slot], sems.at[slot]).start()

        gain[...] = jnp.transpose(small_ref[...].astype(f32))[E : E + 8, :]

    arrived = blocks[0].at[0] if places is None else blocks[0]
    pltpu.make_async_copy(arrived, held.at[i], sems.at[i]).wait()
    x = held[i]
    x_ref[...] = x
    normed = rms_scale(x.astype(f32), gain[0:1, :]).astype(bf16)
    normed_ref[...] = normed
    pre = jnp.dot(normed, w_ref[...], preferred_element_type=f32)
    cos, sin = spread_tables(cos_ref[...], sin_ref[...])
    qkv_ref[:, :PAIR] = rotate_lanes(pre[:, :PAIR], cos, sin).astype(bf16)
    qkv_ref[:, PAIR:] = rotate_lanes(pre[:, PAIR:], *key_tables(cos, sin)).astype(bf16)


def project(place, places, blocks, rows, packed, cos, sin):
    width = packed.shape[0]
    small_at = packed.shape[1] // LANES - 1
    span = cos.shape[0]
    table = pl.BlockSpec((rows, HEAD_SIZE // 2), lambda i, h: (i, 0))
    token_rows = pl.BlockSpec((rows, width), lambda i, h: (i, 0))
    return pl.pallas_call(
        functools.partial(project_kernel, places),
        grid_spec=pltpu.PrefetchScalarGridSpec(
            num_scalar_prefetch=1,
            grid=(span // rows,),
            in_specs=[pl.BlockSpec(memory_space=pl.ANY)] * len(blocks)
            + [
                pl.BlockSpec((width, LANES), lambda i, h: (0, small_at)),
                pl.BlockSpec((width, HEAD_PACK), lambda i, h: (0, h[0])),
                table,
                table,
            ],
            out_specs=[
                pl.BlockSpec((rows, HEAD_PACK), lambda i, h: (i, 0)),
                token_rows,
                token_rows,
            ],
            scratch_shapes=[
                pltpu.VMEM((8, width), f32),
                pltpu.VMEM((span // rows, rows, width), bf16),
                pltpu.SemaphoreType.DMA((span // rows,)),
            ],
        ),
        out_shape=[
            jax.ShapeDtypeStruct((span, HEAD_PACK), bf16),
            jax.ShapeDtypeStruct((span, width), bf16),
            jax.ShapeDtypeStruct((span, width), bf16),
        ],
        compiler_params=pltpu.CompilerParams(vmem_limit_bytes=VMEM_LIMIT),
        cost_estimate=pl.CostEstimate(
            flops=2 * span * width * HEAD_PACK, bytes_accessed=18 * 2**20, transcendentals=0
        ),
        name="project",
    )(place, *blocks, packed, packed, cos, sin)


def head_grads_kernel(head_ref, x_ref, normed_ref, w_ref, grad_ref, out_ref, acc, gain):
    i = pl.program_id(0)

    @pl.when(i == 0)
    def _():
        acc[...] = jnp.zeros_like(acc)
        gain[...] = jnp.zeros_like(gain)

    grad = grad_ref[...]
    acc[...] += contract_rows(grad, normed_ref[...])
    x = x_ref[...].astype(f32)
    inverse = lax.rsqrt(jnp.mean(x * x, axis=-1, keepdims=True) + NORM_EPS)
    back = contract_cols(grad, w_ref[...]) * (x * inverse)
    gain[...] += jnp.sum(back.reshape(back.shape[0] // 8, 8, back.shape[1]), axis=0)

    @pl.when(i == pl.num_programs(0) - 1)
    def _():
        out_ref[:, :HEAD_PACK] = jnp.transpose(acc[...]).astype(bf16)
        total = jnp.sum(gain[...], axis=0, keepdims=True)
        rows = lax.broadcasted_iota(jnp.int32, (LANES, total.shape[1]), 0)
        out_ref[:, HEAD_PACK:] = jnp.transpose(
            jnp.where(rows == 0, jnp.broadcast_to(total, rows.shape), 0.0)
        ).astype(bf16)


def head_grads(head, x, normed, packed, grads):
    span, width = x.shape
    rows = BLOCK
    token_rows = pl.BlockSpec((rows, width), lambda i, h: (i, 0))
    return pl.pallas_call(
        head_grads_kernel,
        grid_spec=pltpu.PrefetchScalarGridSpec(
            num_scalar_prefetch=1,
            grid=(span // rows,),
            in_specs=[
                token_rows,
                token_rows,
                pl.BlockSpec((width, HEAD_PACK), lambda i, h: (0, h[0])),
                pl.BlockSpec((rows, HEAD_PACK), lambda i, h: (i, 0)),
            ],
            out_specs=pl.BlockSpec((width, HEAD_PACK + LANES), lambda i, h: (0, 0)),
            scratch_shapes=[pltpu.VMEM((HEAD_PACK, width), f32), pltpu.VMEM((8, width), f32)],
        ),
        out_shape=jax.ShapeDtypeStruct((width, HEAD_PACK + LANES), bf16),
        compiler_params=pltpu.CompilerParams(vmem_limit_bytes=VMEM_LIMIT),
        cost_estimate=pl.CostEstimate(
            flops=4 * span * width * HEAD_PACK, bytes_accessed=12 * 2**20, transcendentals=0
        ),
        name="head_grads",
    )(head, x, normed, packed, grads)


def lower_lanes(shape):
    return lax.broadcasted_iota(jnp.int32, shape, len(shape) - 1) < HEAD_SIZE


def both_heads_low(pair):
    low = lower_lanes(pair.shape)
    return jnp.concatenate(
        [jnp.where(low, pair, 0.0), jnp.where(low, pltpu.roll(pair, HEAD_SIZE, 1), 0.0)], axis=0
    )


def both_heads_high(pair):
    low = lower_lanes(pair.shape)
    return jnp.concatenate(
        [jnp.where(low, 0.0, pltpu.roll(pair, HEAD_SIZE, 1)), jnp.where(low, 0.0, pair)], axis=0
    )


def allowed_pairs(shape, query_start, key_start, doc):
    rows = lax.broadcasted_iota(jnp.int32, (shape[0] // 2, 1), 0) + query_start
    rows = jnp.concatenate([rows, rows], axis=0)
    keys = lax.broadcasted_iota(jnp.int32, shape, 1) + key_start
    return (keys >= jnp.concatenate([doc, doc], axis=0)) & (keys <= rows)


def attend_kernel(bounds_ref, q_ref, kv_ref, doc_ref, o_ref, low_ref, lse_ref, kept, top, total, acc):
    i = pl.program_id(0)
    steps = pl.num_programs(0)
    offset = bounds_ref[steps]
    first, last = bounds_ref[i], i + offset + 1
    q = both_heads_low(q_ref[...].astype(f32) * SCALE_OF_SCORES).astype(bf16)
    doc = doc_ref[...]
    top[...] = jnp.full_like(top, NEGATIVE_HUGE)
    total[...] = jnp.zeros_like(total)
    acc[...] = jnp.zeros_like(acc)

    def score(j, carried):
        start = pl.multiple_of(j * BLOCK, BLOCK)
        scores = contract_cols(q, kv_ref[pl.ds(start, BLOCK), :])
        allowed = allowed_pairs(scores.shape, (i + offset) * BLOCK, j * BLOCK, doc)
        scores = jnp.where(allowed, scores, NEGATIVE_HUGE)
        kept[:, pl.ds(start, BLOCK)] = scores
        top[...] = jnp.maximum(top[...], jnp.maximum(scores[:, :LANES], scores[:, LANES:]))
        return carried

    lax.fori_loop(first, last, score, 0)
    highest = jnp.max(top[...], axis=1, keepdims=True)

    def mix(j, carried):
        start = pl.multiple_of(j * BLOCK, BLOCK)
        probs = jnp.exp(kept[:, pl.ds(start, BLOCK)] - highest)
        total[...] += probs[:, :LANES] + probs[:, LANES:]
        acc[...] += jnp.dot(
            probs.astype(bf16), kv_ref[pl.ds(start, BLOCK), :], preferred_element_type=f32
        )
        return carried

    lax.fori_loop(first, last, mix, 0)
    row_total = jnp.sum(total[...], axis=1, keepdims=True)
    mixed = acc[...] / row_total
    first_head, second_head = mixed[:BLOCK], mixed[BLOCK:]
    out = jnp.where(
        lower_lanes(first_head.shape), pltpu.roll(first_head, HEAD_SIZE, 1), second_head
    )
    o_ref[...] = out
    low_ref[...] = out.astype(bf16)
    lse_ref[0] = highest + jnp.log(row_total)


def attend(bounds, qkv, kv, kv_at, doc):
    queries, keys = qkv.shape[0], kv.shape[0]
    steps = queries // BLOCK
    pair = pl.BlockSpec((BLOCK, PAIR), lambda i, s: (i, 0))
    return pl.pallas_call(
        attend_kernel,
        grid_spec=pltpu.PrefetchScalarGridSpec(
            num_scalar_prefetch=1,
            grid=(steps,),
            in_specs=[
                pair,
                pl.BlockSpec((keys, PAIR), lambda i, s: (0, kv_at)),
                pl.BlockSpec((BLOCK, 1), lambda i, s: (i, 0)),
            ],
            out_specs=[pair, pair, pl.BlockSpec((1, 2 * BLOCK, 1), lambda i, s: (i, 0, 0))],
            scratch_shapes=[
                pltpu.VMEM((2 * BLOCK, keys), f32),
                pltpu.VMEM((2 * BLOCK, LANES), f32),
                pltpu.VMEM((2 * BLOCK, LANES), f32),
                pltpu.VMEM((2 * BLOCK, PAIR), f32),
            ],
        ),
        out_shape=[
            jax.ShapeDtypeStruct((queries, PAIR), f32),
            jax.ShapeDtypeStruct((queries, PAIR), bf16),
            jax.ShapeDtypeStruct((steps, 2 * BLOCK, 1), f32),
        ],
        compiler_params=pltpu.CompilerParams(vmem_limit_bytes=VMEM_LIMIT),
        cost_estimate=pl.CostEstimate(
            flops=4 * queries * keys * PAIR, bytes_accessed=6 * 2**20, transcendentals=queries * keys
        ),
        name="attend",
    )(bounds, qkv, kv, doc)


def attend_back_kernel(
    fold, bounds_ref, q_ref, kv_ref, doc_ref, do_ref, o_ref, lse_ref, cos_ref, sin_ref, *refs
):
    if fold:
        out_ref, acc, dkv_ref = refs
    else:
        dq_ref, dkv_ref, acc = refs
    i = pl.program_id(0)
    steps = pl.num_programs(0)
    offset = bounds_ref[steps]

    @pl.when(i == 0)
    def _():
        dkv_ref[...] = jnp.zeros_like(dkv_ref)

    q = both_heads_low(q_ref[...].astype(f32) * SCALE_OF_SCORES).astype(bf16)
    grad = do_ref[...].astype(f32)
    product = grad * o_ref[...]
    low = lower_lanes(product.shape)
    delta = jnp.concatenate(
        [
            jnp.sum(jnp.where(low, product, 0.0), axis=1, keepdims=True),
            jnp.sum(jnp.where(low, 0.0, product), axis=1, keepdims=True),
        ],
        axis=0,
    )
    grad = both_heads_high(grad).astype(bf16)
    sources = jnp.concatenate([q, grad], axis=0)
    doc = doc_ref[...]
    lse = lse_ref[0]
    acc[...] = jnp.zeros_like(acc)

    def step(j, carried):
        start = pl.multiple_of(j * BLOCK, BLOCK)
        kv = kv_ref[pl.ds(start, BLOCK), :]
        scores = contract_cols(q, kv)
        allowed = allowed_pairs(scores.shape, (i + offset) * BLOCK, j * BLOCK, doc)
        probs = jnp.exp(jnp.where(allowed, scores - lse, NEGATIVE_HUGE))
        grad_probs = contract_cols(grad, kv)
        grad_scores = (probs * (grad_probs - delta)).astype(bf16)
        acc[...] += jnp.dot(grad_scores, kv, preferred_element_type=f32)
        both = jnp.concatenate([grad_scores, probs.astype(bf16)], axis=0)
        dkv_ref[pl.ds(start, BLOCK), :] += contract_rows(both, sources)
        return carried

    lax.fori_loop(bounds_ref[i], i + offset + 1, step, 0)
    first, second = acc[:BLOCK], acc[BLOCK:]
    dq = jnp.where(lower_lanes(first.shape), first, pltpu.roll(second, HEAD_SIZE, 1))
    if not fold:
        dq_ref[...] = dq
        return
    mine = pl.ds(pl.multiple_of(i * BLOCK, BLOCK), BLOCK)
    cos, sin = spread_tables(cos_ref[mine, :], sin_ref[mine, :])
    out_ref[mine, :PAIR] = rotate_lanes(dq * SCALE_OF_SCORES, cos, -sin).astype(bf16)

    @pl.when(i == steps - 1)
    def _():
        def finish(j, carried):
            part = pl.ds(pl.multiple_of(j * BLOCK, BLOCK), BLOCK)
            cos, sin = key_tables(*spread_tables(cos_ref[part, :], sin_ref[part, :]))
            out_ref[part, PAIR:] = rotate_lanes(dkv_ref[part, :], cos, -sin).astype(bf16)
            return carried

        lax.fori_loop(0, dkv_ref.shape[0] // BLOCK, finish, 0)


def attend_back(bounds, qkv, kv, kv_at, doc, grad, out, lse, cos, sin, fold):
    queries, keys = qkv.shape[0], kv.shape[0]
    steps = queries // BLOCK
    pair = pl.BlockSpec((BLOCK, PAIR), lambda i, s: (i, 0))
    table = pl.BlockSpec(cos.shape, lambda i, s: (0, 0))
    acc = pltpu.VMEM((2 * BLOCK, PAIR), f32)
    if fold:
        out_specs = pl.BlockSpec((queries, HEAD_PACK), lambda i, s: (0, 0))
        out_shape = jax.ShapeDtypeStruct((queries, HEAD_PACK), bf16)
        scratch = [acc, pltpu.VMEM((keys, PAIR), f32)]
    else:
        out_specs = [pair, pl.BlockSpec((keys, PAIR), lambda i, s: (0, 0))]
        out_shape = [
            jax.ShapeDtypeStruct((queries, PAIR), f32),
            jax.ShapeDtypeStruct((keys, PAIR), f32),
        ]
        scratch = [acc]
    return pl.pallas_call(
        functools.partial(attend_back_kernel, fold),
        grid_spec=pltpu.PrefetchScalarGridSpec(
            num_scalar_prefetch=1,
            grid=(steps,),
            in_specs=[
                pair,
                pl.BlockSpec((keys, PAIR), lambda i, s: (0, kv_at)),
                pl.BlockSpec((BLOCK, 1), lambda i, s: (i, 0)),
                pair,
                pair,
                pl.BlockSpec((1, 2 * BLOCK, 1), lambda i, s: (i, 0, 0)),
                table,
                table,
            ],
            out_specs=out_specs,
            scratch_shapes=scratch,
        ),
        out_shape=out_shape,
        compiler_params=pltpu.CompilerParams(vmem_limit_bytes=VMEM_LIMIT),
        cost_estimate=pl.CostEstimate(
            flops=10 * queries * keys * PAIR,
            bytes_accessed=8 * 2**20,
            transcendentals=queries * keys,
        ),
        name="attend_back",
    )(bounds, qkv, kv, doc, grad, out, lse, cos, sin)


def unrotate_kernel(dq_ref, dkv_ref, cos_ref, sin_ref, out_ref):
    cos, sin = spread_tables(cos_ref[...], sin_ref[...])
    dq = rotate_lanes(dq_ref[...] * SCALE_OF_SCORES, cos, -sin)
    cos, sin = key_tables(cos, sin)
    dkv = rotate_lanes(dkv_ref[...], cos, -sin)
    out_ref[...] = jnp.concatenate([dq, dkv], axis=1).astype(bf16)


def unrotate(dq, dkv, cos, sin):
    rows = dq.shape[0]
    pair = pl.BlockSpec((BLOCK, PAIR), lambda i: (i, 0))
    table = pl.BlockSpec((BLOCK, HEAD_SIZE // 2), lambda i: (i, 0))
    return pl.pallas_call(
        unrotate_kernel,
        grid=(rows // BLOCK,),
        in_specs=[pair, pair, table, table],
        out_specs=pl.BlockSpec((BLOCK, HEAD_PACK), lambda i: (i, 0)),
        out_shape=jax.ShapeDtypeStruct((rows, HEAD_PACK), bf16),
        cost_estimate=pl.CostEstimate(
            flops=rows * HEAD_PACK * 8, bytes_accessed=rows * HEAD_PACK * 14, transcendentals=0
        ),
        name="unrotate",
    )(dq, dkv, cos, sin)


def place_experts_kernel(place_ref, *refs):
    blocks, (ct_ref, w_ref, z_ref, sems) = refs[:10], refs[10:]
    core = place_ref[1]
    rows = w_ref.shape[1] // 2
    half = rows // 2
    sources = [[(0, 0, rows)], [(1, 0, rows)], [(2, 0, rows)], [(3, 0, half), (4, half, half)]]
    for step, parts in enumerate(sources):

        @pl.when(pl.program_id(0) == step)
        def _(parts=parts):
            copies = []
            for source, start, length in parts:
                for other in (0, 1):
                    first = jnp.where(core == other, 0, rows) + start
                    at = pl.ds(pl.multiple_of(first, half), length)
                    copies.append(
                        pltpu.make_async_copy(
                            blocks[2 * source + other], w_ref.at[0, at, :], sems.at[len(copies)]
                        )
                    )
            for copy in copies:
                copy.start()
            for copy in copies:
                copy.wait()

    z_ref[0] = jnp.dot(ct_ref[...], w_ref[0, :, 2 * F :], preferred_element_type=f32)


def place_experts(place, parts, early, width):
    rows = early.shape[0]
    blocks = [block for pair in parts for block in pair]
    return pl.pallas_call(
        place_experts_kernel,
        grid_spec=pltpu.PrefetchScalarGridSpec(
            num_scalar_prefetch=1,
            grid=(EXPERTS_HERE,),
            in_specs=[pl.BlockSpec(memory_space=pl.ANY)] * len(blocks)
            + [pl.BlockSpec((rows, width), lambda r, s: (0, 0))],
            out_specs=[
                pl.BlockSpec((1, width, 3 * F), lambda r, s: (s[0] ^ r, 0, 0)),
                pl.BlockSpec((1, rows, F), lambda r, s: (s[0] ^ r, 0, 0)),
            ],
            scratch_shapes=[pltpu.SemaphoreType.DMA((4,))],
        ),
        out_shape=[
            jax.ShapeDtypeStruct((EXPERTS_HERE, width, 3 * F), bf16),
            jax.ShapeDtypeStruct((EXPERTS_HERE, rows, F), f32),
        ],
        compiler_params=pltpu.CompilerParams(vmem_limit_bytes=VMEM_LIMIT),
        cost_estimate=pl.CostEstimate(
            flops=2 * EXPERTS_HERE * rows * width * F, bytes_accessed=36 * 2**20, transcendentals=0
        ),
        name="place_experts",
    )(place, *blocks, early)


def lane_column(x, at):
    lane = lax.broadcasted_iota(jnp.int32, x.shape, 1)
    return jnp.sum(jnp.where(lane == at, x, 0.0), axis=1, keepdims=True)


def experts_kernel(
    group_ref, n_ref, routed_ref, router_ref, w_ref, z_ref,
    back_ref, gates_ref, hidden_ref, pre_ref, acc, dots,
):
    e = pl.program_id(0)
    own = group_ref[0] * EXPERTS_HERE + e
    rows = n_ref.shape[0]

    @pl.when(e == 0)
    def _():
        logits = jnp.dot(n_ref[...], router_ref[...], preferred_element_type=f32)
        routed = routed_ref[...].astype(f32) > 0.5
        highest = jnp.max(jnp.where(routed, logits, NEGATIVE_HUGE), axis=1, keepdims=True)
        weights = jnp.where(routed, jnp.exp(jnp.where(routed, logits - highest, 0.0)), 0.0)
        gates_ref[...] = weights / jnp.sum(weights, axis=1, keepdims=True)
        acc[...] = jnp.zeros_like(acc)
        dots[...] = jnp.zeros_like(dots)

    w_in = w_ref[0, :, : 2 * F]
    for t in range(rows // BLOCK):
        part = pl.ds(t * BLOCK, BLOCK)
        pre = jnp.dot(n_ref[part, :], w_in, preferred_element_type=f32)
        gate, up = pre[:, :F], pre[:, F:]
        z = z_ref[0, part, :]
        weight = lane_column(gates_ref[part, :], own)
        sig = 1.0 / (1.0 + jnp.exp(-gate))
        act = gate * sig
        hidden = act * up
        hidden_ref[0, part, :] = (weight * hidden).astype(bf16)
        dot = RESIDUAL_SCALE * jnp.sum(hidden.astype(bf16).astype(f32) * z, axis=1, keepdims=True)
        lane = lax.broadcasted_iota(jnp.int32, (BLOCK, LANES), 1)
        dots[part, :] += jnp.where(lane == own, dot, 0.0)
        scaled = (RESIDUAL_SCALE * weight) * z
        pre_ref[0, part, :F] = (scaled * up * (sig + act * (1.0 - sig))).astype(bf16)
        pre_ref[0, part, F:] = (scaled * act).astype(bf16)
        acc[part, :] += contract_cols(pre_ref[0, part, :], w_in)

    @pl.when(e == EXPERTS_HERE - 1)
    def _():
        width = n_ref.shape[1]
        back_ref[:, :width] = acc[...].astype(bf16)
        high = dots[...].astype(bf16)
        low = dots[...] - high.astype(f32)
        back_ref[:, width:] = (high.astype(f32) + pltpu.roll(low, E, 1)).astype(bf16)


def experts(group, normed, early, packed, w_all, z):
    rows, width = normed.shape
    count = w_all.shape[0]
    whole = pl.BlockSpec((rows, width), lambda e, g: (0, 0))
    column = width // LANES
    router_at = packed.shape[1] // LANES - 1
    return pl.pallas_call(
        experts_kernel,
        grid_spec=pltpu.PrefetchScalarGridSpec(
            num_scalar_prefetch=1,
            grid=(count,),
            in_specs=[
                whole,
                pl.BlockSpec((rows, LANES), lambda e, g: (0, column)),
                pl.BlockSpec((width, LANES), lambda e, g: (0, router_at)),
                pl.BlockSpec((1, width, 3 * F), lambda e, g: (e, 0, 0)),
                pl.BlockSpec((1, rows, F), lambda e, g: (e, 0, 0)),
            ],
            out_specs=[
                pl.BlockSpec((rows, width + LANES), lambda e, g: (0, 0)),
                pl.BlockSpec((rows, LANES), lambda e, g: (0, 0)),
                pl.BlockSpec((1, rows, F), lambda e, g: (e, 0, 0)),
                pl.BlockSpec((1, rows, 2 * F), lambda e, g: (e, 0, 0)),
            ],
            scratch_shapes=[pltpu.VMEM((rows, width), f32), pltpu.VMEM((rows, LANES), f32)],
        ),
        out_shape=[
            jax.ShapeDtypeStruct((rows, width + LANES), bf16),
            jax.ShapeDtypeStruct((rows, LANES), f32),
            jax.ShapeDtypeStruct((count, rows, F), bf16),
            jax.ShapeDtypeStruct((count, rows, 2 * F), bf16),
        ],
        compiler_params=pltpu.CompilerParams(vmem_limit_bytes=VMEM_LIMIT),
        cost_estimate=pl.CostEstimate(
            flops=2 * count * rows * width * 4 * F, bytes_accessed=40 * 2**20, transcendentals=0
        ),
        name="experts",
    )(group, normed, early, packed, w_all, z)


def expert_grads_kernel(with_y, half_ref, n_ref, ct_ref, w_ref, hidden_ref, pre_ref, *refs):
    if with_y:
        y_ref, grad_ref, n_t, ct_t, acc = refs
    else:
        grad_ref, n_t, ct_t = refs
    e = pl.program_id(0)

    @pl.when(e == 0)
    def _():
        n_t[...] = jnp.transpose(n_ref[...])
        ct_t[...] = jnp.transpose(ct_ref[...])
        if with_y:
            acc[...] = jnp.zeros_like(acc)

    grad_ref[0, :, : 2 * F] = jnp.dot(n_t[...], pre_ref[0], preferred_element_type=f32).astype(bf16)
    grad_ref[0, :, 2 * F :] = (
        RESIDUAL_SCALE * jnp.dot(ct_t[...], hidden_ref[0], preferred_element_type=f32)
    ).astype(bf16)
    if not with_y:
        return
    acc[...] += contract_cols(hidden_ref[0], w_ref[0, :, 2 * F :])

    @pl.when(e == pl.num_programs(0) - 1)
    def _():
        y_ref[...] = acc[...].astype(bf16)


def expert_grads(half, halves, normed, early, w_all, hidden, pre, with_y):
    rows, width = normed.shape
    count = w_all.shape[0]
    own = width // halves
    feature = pl.BlockSpec((rows, own), lambda e, h: (0, h[0]))
    out_specs = [pl.BlockSpec((1, own, 3 * F), lambda e, h: (e, 0, 0))]
    out_shape = [jax.ShapeDtypeStruct((count, own, 3 * F), bf16)]
    scratch = [pltpu.VMEM((own, rows), bf16), pltpu.VMEM((own, rows), bf16)]
    if with_y:
        out_specs.insert(0, pl.BlockSpec((rows, width), lambda e, h: (0, 0)))
        out_shape.insert(0, jax.ShapeDtypeStruct((rows, width), bf16))
        scratch.append(pltpu.VMEM((rows, width), f32))
    return pl.pallas_call(
        functools.partial(expert_grads_kernel, with_y),
        grid_spec=pltpu.PrefetchScalarGridSpec(
            num_scalar_prefetch=1,
            grid=(count,),
            in_specs=[
                feature,
                feature,
                pl.BlockSpec((1, width, 3 * F), lambda e, h: (e, 0, 0)),
                pl.BlockSpec((1, rows, F), lambda e, h: (e, 0, 0)),
                pl.BlockSpec((1, rows, 2 * F), lambda e, h: (e, 0, 0)),
            ],
            out_specs=out_specs,
            scratch_shapes=scratch,
        ),
        out_shape=out_shape,
        compiler_params=pltpu.CompilerParams(vmem_limit_bytes=VMEM_LIMIT),
        cost_estimate=pl.CostEstimate(
            flops=2 * count * rows * width * 3 * F // halves + 2 * with_y * count * rows * width * F,
            bytes_accessed=30 * 2**20,
            transcendentals=0,
        ),
        name="expert_grads",
    )(half, normed, early, w_all, hidden, pre)


def join_kernel(place_ref, o_ref, w_ref, small_ref, x_ref, normed_ref, resid_ref, own_ref, gain):
    t = pl.program_id(0)
    b = place_ref[2]

    @pl.when(t == 0)
    def _():
        gain[...] = jnp.transpose(small_ref[...].astype(f32))[E : E + 8, :]

    pairs = []
    for a in range(o_ref.shape[0]):
        same, other = o_ref[a, 0, 0], o_ref[a, 1, 0]
        pairs.append(jnp.where(b == 0, same, other))
        pairs.append(jnp.where(b == 0, other, same))
    attended = jnp.concatenate(pairs, axis=1)
    resid = x_ref[...].astype(f32) + RESIDUAL_SCALE * jnp.dot(
        attended, w_ref[...], preferred_element_type=f32
    )
    normed_ref[...] = rms_scale(resid, gain[1:2, :]).astype(bf16)

    @pl.when(t == place_ref[1])
    def _():
        resid_ref[...] = resid
        own_ref[...] = attended


def join(place, outs, packed, weights_at, x):
    width = packed.shape[0]
    lines, _, _, rows, pair = outs.shape
    small_at = packed.shape[1] // LANES - 1
    own = pl.BlockSpec((rows, width), lambda t, s: (0, 0))
    return pl.pallas_call(
        join_kernel,
        grid_spec=pltpu.PrefetchScalarGridSpec(
            num_scalar_prefetch=1,
            grid=(lines,),
            in_specs=[
                pl.BlockSpec((lines, 2, 1, rows, pair), lambda t, s: (0, 0, t, 0, 0)),
                pl.BlockSpec((width, width), lambda t, s: (0, weights_at)),
                pl.BlockSpec((width, LANES), lambda t, s: (0, small_at)),
                pl.BlockSpec((rows, width), lambda t, s: (2 * t + s[2], 0)),
            ],
            out_specs=[pl.BlockSpec((rows, width), lambda t, s: (t, 0)), own, own],
            scratch_shapes=[pltpu.VMEM((8, width), f32)],
        ),
        out_shape=[
            jax.ShapeDtypeStruct((lines * rows, width), bf16),
            jax.ShapeDtypeStruct((rows, width), f32),
            jax.ShapeDtypeStruct((rows, width), bf16),
        ],
        compiler_params=pltpu.CompilerParams(vmem_limit_bytes=VMEM_LIMIT),
        cost_estimate=pl.CostEstimate(
            flops=2 * lines * rows * width * width, bytes_accessed=12 * 2**20, transcendentals=0
        ),
        name="join",
    )(place, outs, packed, packed, x)


def exchange(x, axes):
    return lax.all_to_all(x, axes, 0, 0, tiled=True)


def body(
    tokens,
    cotangent,
    segment_ids,
    routes,
    norm_attn,
    w_query,
    key_weight_matrix,
    value_weight_matrix,
    w_output,
    norm_moe,
    w_router,
    expert_in,
    expert_out,
):
    x_local = tokens[0].astype(f32)
    token_count, width = x_local.shape
    seg_row = segment_ids[0]
    group = lax.axis_index("a")
    head_axes = SEQ if lax.axis_size(SEQ) == KEY_VALUE_HEADS else ("b",)
    whole_rows = head_axes == SEQ
    span = token_count * KEY_VALUE_HEADS
    span_start = 0 if whole_rows else group * span

    def start_of_doc(ids):
        return jnp.sum((seg_row[None, :] < ids[:, None]).astype(jnp.int32), axis=1)

    seg_span = lax.dynamic_slice_in_dim(seg_row, span_start, span)
    doc_span = start_of_doc(seg_span)
    cos_span, sin_span = rotation_tables(
        span_start + jnp.arange(span, dtype=jnp.int32) - doc_span
    )
    bounds = jnp.concatenate(
        [
            doc_span.reshape(-1, BLOCK)[:, 0] // BLOCK,
            jnp.full((1,), span_start // BLOCK, jnp.int32),
        ]
    )
    doc_column = doc_span[:, None]

    own_rows = w_query.shape[0]
    by_head = jnp.concatenate(
        [
            w_query.astype(bf16).reshape(own_rows, KEY_VALUE_HEADS, PAIR),
            key_weight_matrix.astype(bf16).reshape(own_rows, KEY_VALUE_HEADS, HEAD_SIZE),
            value_weight_matrix.astype(bf16).reshape(own_rows, KEY_VALUE_HEADS, HEAD_SIZE),
        ],
        axis=2,
    ).reshape(own_rows, KEY_VALUE_HEADS * HEAD_PACK)
    qkv_width = KEY_VALUE_HEADS * HEAD_PACK
    first_all = gather(
        jnp.concatenate(
            [
                by_head,
                w_output.astype(bf16),
                pad_lanes(
                    jnp.concatenate(
                        [
                            w_router.astype(bf16),
                            norm_attn.astype(bf16)[:, None],
                            norm_moe.astype(bf16)[:, None],
                        ],
                        axis=1,
                    ),
                    LANES,
                ),
            ],
            axis=1,
        ),
        ALL,
    )
    experts_low = jnp.concatenate([expert_in.astype(bf16), expert_out.astype(bf16)], axis=1)
    if whole_rows:
        pieces = grid_gather(tokens[0])
        places = [piece[:2] for piece in pieces]
        blocks = tuple(piece[2] for piece in pieces)
    else:
        places = None
        blocks = (gather(tokens[0], "b").reshape((-1,) + tokens.shape[1:]),)
    first_all, experts_low, blocks, cos_span, sin_span, bounds, doc_column = (
        lax.optimization_barrier(
            (first_all, experts_low, blocks, cos_span, sin_span, bounds, doc_column)
        )
    )
    output_w = first_all[:, qkv_width : qkv_width + width]
    small_at = qkv_width + width
    router_w = first_all[:, small_at : small_at + E]
    gain_one_f = first_all[:, small_at + E].astype(f32)
    gain_two_f = first_all[:, small_at + E + 1].astype(f32)

    expert_ids = jnp.arange(E, dtype=jnp.int32)
    routed_own = jnp.any(routes[0][:, :, None] == expert_ids[None, None, :], axis=1)
    early = jnp.concatenate([cotangent[0], pad_lanes(routed_own.astype(bf16), LANES)], axis=1)
    early, first_all = lax.optimization_barrier((early, first_all))
    early_all = gather(early, "a")
    small_plane = lax.axis_size("b") == 2 and lax.axis_size("y") == 2
    if small_plane:
        parts = plane_gather(experts_low)
    else:
        parts = gather(experts_low, PLANE)

    place = jnp.stack([lax.axis_index(head_axes), group, lax.axis_index("b")])
    qkv, normed_span, x_span = project(
        place, places, blocks, token_count, first_all, cos_span, sin_span
    )
    if whole_rows:
        kv, kv_at = qkv, 1
    else:
        kv, kv_at = gather(qkv[:, PAIR:], "a"), 0
    attention_result, attended, log_total = attend(bounds, qkv, kv, kv_at, doc_column)
    if small_plane:
        member = lax.axis_index("b")
        by_column = attended.reshape(GROUPS, 2, token_count, PAIR)
        other = lax.ppermute(
            lax.dynamic_index_in_dim(by_column, 1 - member, 1, False), "b", [(0, 1), (1, 0)]
        )
        own = lax.dynamic_index_in_dim(by_column, member, 1, False)
        pair, early_all = lax.optimization_barrier((jnp.stack([own, other]), early_all))
        outs = lax.all_gather(pair, "a", axis=0, tiled=False)
        normed_all, resid, attended_low = join(place, outs, first_all, qkv_width // width, x_span)
        normed_two = lax.dynamic_slice_in_dim(normed_all, group * token_count, token_count)
        home = jnp.stack([member * 2 + lax.axis_index("y"), lax.axis_index("c")])
        experts_all, grad_hidden = place_experts(home, parts, early_all, width)
    else:
        attended_low = (
            exchange(attended.reshape(KEY_VALUE_HEADS, token_count, PAIR), head_axes)
            .transpose(1, 0, 2)
            .reshape(token_count, QUERY_HEADS * HEAD_SIZE)
        )
        attn_out = jnp.dot(attended_low, output_w, preferred_element_type=f32)
        resid = x_local + RESIDUAL_SCALE * attn_out
        normed_two = rms_scale(resid, gain_two_f).astype(bf16)
        normed_all = gather(normed_two, "a")
        experts_all = parts.reshape(EXPERTS_HERE, width, 3 * F)
        grad_hidden = jnp.einsum(
            "td,edf->etf",
            early_all[:, :width],
            experts_all[:, :, 2 * F :],
            preferred_element_type=f32,
        )
    back_part, gates_all, gated_hidden, grad_pre = experts(
        group.reshape(1), normed_all, early_all, first_all, experts_all, grad_hidden
    )
    back_own = scatter_sum(back_part, "a").astype(f32)
    inputs = (normed_all, early_all, experts_all, gated_hidden, grad_pre)
    if small_plane:
        core = lax.axis_index("c")
        (send,) = expert_grads((1 - core).reshape(1), 2, *inputs, False)
        arrived = lax.ppermute(send, "c", [(0, 1), (1, 0)])
        moe_part, keep = expert_grads(core.reshape(1), 2, *inputs, True)
        back_own, moe_part, keep = lax.optimization_barrier((back_own, moe_part, keep))
    else:
        moe_part, grad_experts = expert_grads(jnp.zeros((1,), jnp.int32), 1, *inputs, True)
        back_own, moe_part, grad_experts = lax.optimization_barrier(
            (back_own, moe_part, grad_experts)
        )
        grad_experts = scatter_sum(grad_experts.reshape(EXPERTS_HERE * width, 3 * F), PLANE)
    moe_sum = scatter_sum(moe_part, "a")

    grad_out = cotangent[0].astype(f32)
    gates = lax.dynamic_slice_in_dim(gates_all, group * token_count, token_count)[:, :E]
    gate_grads_own = back_own[:, width : width + E] + back_own[:, width + E : width + 2 * E]
    grad_logits = gates * (gate_grads_own - jnp.sum(gates * gate_grads_own, axis=-1, keepdims=True))
    grad_normed_two = back_own[:, :width] + jnp.dot(
        grad_logits, router_w.astype(f32).T, precision=HIGHEST_DOT
    )
    grad_router = jnp.dot(normed_two.astype(f32).T, grad_logits, precision=HIGHEST_DOT)
    grad_resid_norm, grad_gain_two = rms_back(resid, gain_two_f, grad_normed_two)
    grad_resid = grad_out + grad_resid_norm
    grad_attn_low = (RESIDUAL_SCALE * grad_resid).astype(bf16)
    grad_heads = contract_cols(grad_attn_low, output_w).astype(bf16)
    grad_mixed = exchange(
        grad_heads.reshape(token_count, KEY_VALUE_HEADS, PAIR).transpose(1, 0, 2), head_axes
    ).reshape(span, PAIR)
    if small_plane:
        keep, arrived, grad_heads = lax.optimization_barrier((keep, arrived, grad_heads))
        total = keep.astype(f32) + arrived.astype(f32)
        total = total.astype(bf16).reshape((2, 2) + keep.shape[1:])
        total, attended_low, grad_router = lax.optimization_barrier(
            (total, attended_low, grad_router)
        )
        wide = 3 * F // 2
        left, right = halve_send(total[..., :wide], "y", 1), halve_send(total[..., wide:], "b", 0)
    small = jnp.concatenate([grad_router, grad_gain_two[:, None]], axis=1)
    second_part = jnp.concatenate(
        [contract_rows(attended_low, grad_attn_low), pad_lanes(small, LANES)], axis=1
    ).astype(bf16)
    cols = second_part.shape[1]
    second_part = second_part.reshape(GROUPS, -1, own_rows, cols).transpose(1, 0, 2, 3)
    second_part, grad_mixed = lax.optimization_barrier((second_part, grad_mixed))
    rest = scatter_sum(second_part.reshape(-1, cols), PLANE)
    grads = attend_back(
        bounds, qkv, kv, kv_at, doc_column, grad_mixed, attention_result, log_total,
        cos_span, sin_span, whole_rows,
    )
    if whole_rows:
        grad_pack = grads
    else:
        grad_kv = scatter_sum(grads[1].astype(bf16), "a").astype(f32)
        grad_pack = unrotate(grads[0], grad_kv, cos_span, sin_span)
    if small_plane:
        left, right, moe_sum, grad_pack = lax.optimization_barrier(
            (left, right, moe_sum, grad_pack)
        )
        left, right = halve_add(left), halve_add(right)
        left, right = halve_send(left, "b", 0), halve_send(right, "y", 0)
    first_part = head_grads(place, x_span, normed_span, first_all, grad_pack)
    rest, first_part = lax.optimization_barrier((rest, first_part))
    rest = scatter_sum(rest, "a")
    by_tokens = exchange(grad_pack.reshape(KEY_VALUE_HEADS, token_count, HEAD_PACK), head_axes)
    by_tokens, first_part = lax.optimization_barrier((by_tokens, first_part))
    sums = exchange(first_part.reshape(-1, own_rows, first_part.shape[1]), ALL)
    sums, moe_sum, resid = lax.optimization_barrier((sums, moe_sum, resid))
    sums = sums.astype(f32).reshape(lax.axis_size(SEQ), -1, own_rows, first_part.shape[1]).sum(axis=1)
    by_heads = sums[:, :, :HEAD_PACK].reshape(-1, KEY_VALUE_HEADS, own_rows, HEAD_PACK).sum(axis=0)
    rest = rest.astype(f32)
    grad_qkv = by_tokens.transpose(1, 0, 2).reshape(token_count, qkv_width)
    grad_normed_one = contract_cols(grad_qkv, first_all[:, :qkv_width])
    grad_x_norm, _ = rms_back(x_local, gain_one_f, grad_normed_one)
    grad_input = grad_resid + grad_x_norm
    layer_sum = resid + RESIDUAL_SCALE * moe_sum.astype(f32)
    if small_plane:
        grad_experts = jnp.concatenate(
            [own.astype(f32) + other.astype(f32) for own, other in (left, right)], axis=1
        )
    else:
        grad_experts = grad_experts.astype(f32)
    by_rows = by_heads.transpose(1, 0, 2)
    return (
        layer_sum.astype(bf16)[None],
        grad_input[None],
        sums[:, :, HEAD_PACK].sum(axis=0),
        by_rows[:, :, :PAIR].reshape(own_rows, -1),
        by_rows[:, :, PAIR : PAIR + HEAD_SIZE].reshape(own_rows, -1),
        by_rows[:, :, PAIR + HEAD_SIZE :].reshape(own_rows, -1),
        rest[:, :width],
        rest[:, width + E],
        rest[:, width : width + E],
        grad_experts[:, : 2 * F],
        grad_experts[:, 2 * F :],
    )


def solution(mesh):
    seq, row = mesh.shape["seq"], mesh.shape["row"]
    cut = Mesh(mesh.devices.reshape(GROUPS, seq // GROUPS, row // 2, 2), ALL)
    token_spec = P(("y", "c"), SEQ, None)
    row_spec = P(ALL, None)
    flat_spec = P(ALL)
    in_specs = (
        token_spec,
        token_spec,
        P(("y", "c"), None),
        token_spec,
        flat_spec,
        row_spec,
        row_spec,
        row_spec,
        row_spec,
        flat_spec,
        row_spec,
        row_spec,
        row_spec,
    )
    out_specs = (
        token_spec,
        token_spec,
        flat_spec,
        row_spec,
        row_spec,
        row_spec,
        row_spec,
        flat_spec,
        row_spec,
        row_spec,
        row_spec,
    )
    return jax.shard_map(body, mesh=cut, in_specs=in_specs, out_specs=out_specs, check_vma=False)
```

```python
import functools

import jax
import jax.numpy as jnp
from jax import lax
from jax.experimental import pallas as pl
from jax.experimental.pallas import tpu as pltpu
from jax.sharding import Mesh, PartitionSpec as P

QUERY_HEADS = 16
KEY_VALUE_HEADS = 8
HEAD_SIZE = 64
F = 512
E = 16
GROUPS = 4
EXPERTS_HERE = E // GROUPS
LANES = 128
PAIR = 2 * HEAD_SIZE
HEAD_PACK = 4 * HEAD_SIZE
BLOCK = 256
QUERY_BLOCK = 512

NORM_EPS = 1e-06
RESIDUAL_SCALE = 0.22
SCALE_OF_SCORES = 0.015625
ROPE_BASE = 10000.0
NEGATIVE_HUGE = -1e30
HIGHEST_DOT = lax.Precision.HIGHEST
VMEM_LIMIT = 60 * 1024 * 1024

PLANE = ("b", "y", "c")
SEQ = ("a", "b")
ALL = ("a", "b", "y", "c")
SWAP = [(0, 1), (1, 0)]

f32 = jnp.float32
bf16 = jnp.bfloat16


def rotation_tables(positions):
    half = HEAD_SIZE // 2
    freq = jnp.power(ROPE_BASE, -2.0 * jnp.arange(half, dtype=f32) / HEAD_SIZE)
    angle = positions.astype(f32)[:, None] * freq[None, :]
    return jnp.cos(angle), jnp.sin(angle)


def rms_back(values, gain, grad_norm):
    mean_square = jnp.mean(values * values, axis=-1, keepdims=True)
    inverse = lax.rsqrt(mean_square + NORM_EPS)
    scaled_grad = grad_norm * gain
    grad_values = inverse * scaled_grad - values * inverse**3 * jnp.mean(
        values * scaled_grad, axis=-1, keepdims=True
    )
    grad_gain = jnp.sum(grad_norm * values * inverse, axis=0)
    return (grad_values, grad_gain)


def rms_scale(values, gain):
    mean_square = jnp.mean(values * values, axis=-1, keepdims=True)
    return values * lax.rsqrt(mean_square + NORM_EPS) * gain


def contract_rows(left_side, right_side):
    return lax.dot_general(
        left_side, right_side, (((0,), (0,)), ((), ())), preferred_element_type=f32
    )


def contract_cols(left_side, right_side):
    return lax.dot_general(
        left_side, right_side, (((1,), (1,)), ((), ())), preferred_element_type=f32
    )


def gather(x, axes):
    return lax.all_gather(x, axes, axis=0, tiled=True)


def scatter_sum(x, axes):
    return lax.psum_scatter(x, axes, scatter_dimension=0, tiled=True)


def pad_lanes(x, lanes):
    return jnp.pad(x, ((0, 0), (0, lanes - x.shape[1])))


def line_pairs(n, step):
    return [(i, i + step) for i in range(n) if 0 <= i + step < n]


def grid_gather(x):
    n = lax.axis_size("a")

    def cross(block, ends):
        return lax.ppermute(
            block, SEQ, [(2 * i + j, 2 * i + 1 - j) for i in range(n) if ends(i) for j in (0, 1)]
        )

    pieces = [(0, 0, x), (0, 1, cross(x, lambda i: True))]
    up = down = x
    for k in range(1, n):
        up = lax.ppermute(up, "a", line_pairs(n, 1))
        down = lax.ppermute(down, "a", line_pairs(n, -1))
        pieces += [(-k, 0, up), (-k, 1, cross(up, lambda i: i >= k))]
        pieces += [(k, 0, down), (k, 1, cross(down, lambda i: i + k < n))]
    return pieces


def neighbours(x):
    return lax.ppermute(x, "y", SWAP), lax.ppermute(x, "b", SWAP)


def plane_gather(x, from_y, from_b):
    half = x.shape[0] // 2
    upper = lax.ppermute(from_b[:half], "y", SWAP)
    lower = lax.ppermute(from_y[half:], "b", SWAP)
    return [(block, lax.ppermute(block, "c", SWAP)) for block in (x, from_y, from_b, upper, lower)]


def halve_send(v, axis, at):
    me = lax.axis_index(axis)
    other = lax.ppermute(lax.dynamic_index_in_dim(v, 1 - me, at, False), axis, SWAP)
    return lax.dynamic_index_in_dim(v, me, at, False), other


def halve_add(terms):
    own, other = terms
    return (own.astype(f32) + other.astype(f32)).astype(own.dtype)


def rotate_lanes(x, cos, sin):
    width = x.shape[-1]
    lane = lax.broadcasted_iota(jnp.int32, x.shape, x.ndim - 1)
    swapped = jnp.where(
        lane % HEAD_SIZE < HEAD_SIZE // 2,
        pltpu.roll(x, width - HEAD_SIZE // 2, x.ndim - 1),
        pltpu.roll(x, HEAD_SIZE // 2, x.ndim - 1),
    )
    return x * cos + swapped * sin


def spread_tables(cos, sin):
    return jnp.concatenate([cos] * 4, axis=1), jnp.concatenate([-sin, sin, -sin, sin], axis=1)


def key_tables(cos, sin):
    low = lower_lanes(cos.shape)
    return jnp.where(low, cos, 1.0), jnp.where(low, sin, 0.0)


def project_kernel(places, spots, place_ref, *refs):
    count = 1 if places is None else len(places)
    blocks, refs = refs[:count], refs[count:]
    count = 1 if spots is None else len(spots)
    weights, refs = refs[:count], refs[count:]
    cos_ref, sin_ref, qkv_ref, normed_ref, x_ref, w_ref, wide_cos_ref, wide_sin_ref = refs[:8]
    gain, held, sems = refs[8:]
    i = pl.program_id(0)
    slots = held.shape[0]

    @pl.when(i == 0)
    def _():
        copies = []
        if spots is None:
            copies.append(pltpu.make_async_copy(weights[0], w_ref, sems.at[slots]))
        else:
            for at, ((y, c), block) in enumerate(zip(spots, weights)):
                row = 2 * (place_ref[3] ^ y) + (place_ref[4] ^ c)
                copies.append(
                    pltpu.make_async_copy(block, w_ref.at[:, row], sems.at[slots + at])
                )
        for copy in copies:
            copy.start()
        if places is None:
            for slot in range(slots):
                pltpu.make_async_copy(blocks[0].at[slot], held.at[slot], sems.at[slot]).start()
        else:
            for (distance, crossed), block in zip(places, blocks):
                at = place_ref[1] + distance
                member = 1 - place_ref[2] if crossed else place_ref[2]

                @pl.when((at >= 0) & (at < slots // 2))
                def _(block=block, slot=2 * at + member):
                    pltpu.make_async_copy(block, held.at[slot], sems.at[slot]).start()

        for copy in copies:
            copy.wait()
        small = w_ref[..., HEAD_PACK:].reshape(held.shape[2], LANES)
        gain[...] = jnp.transpose(small.astype(f32))[:8, :]

    arrived = blocks[0].at[0] if places is None else blocks[0]
    pltpu.make_async_copy(arrived, held.at[i], sems.at[i]).wait()
    x = held[i]
    x_ref[...] = x
    normed = rms_scale(x.astype(f32), gain[0:1, :]).astype(bf16)
    normed_ref[...] = normed
    w = w_ref[..., :HEAD_PACK].reshape(held.shape[2], HEAD_PACK)
    pre = jnp.dot(normed, w, preferred_element_type=f32)
    cos, sin = spread_tables(cos_ref[...], sin_ref[...])
    wide_cos_ref[...] = cos
    wide_sin_ref[...] = sin
    qkv_ref[:, :PAIR] = rotate_lanes(pre[:, :PAIR], cos, sin).astype(bf16)
    qkv_ref[:, PAIR:] = rotate_lanes(pre[:, PAIR:], *key_tables(cos, sin)).astype(bf16)


def project(place, places, blocks, spots, weights, rows, width, cos, sin):
    span = cos.shape[0]
    table = pl.BlockSpec((rows, HEAD_SIZE // 2), lambda i, h: (i, 0))
    token_rows = pl.BlockSpec((rows, width), lambda i, h: (i, 0))
    cols = HEAD_PACK + LANES
    shape = weights[0].shape if spots is None else (
        weights[0].shape[0], len(spots), weights[0].shape[1], cols
    )
    return pl.pallas_call(
        functools.partial(project_kernel, places, spots),
        grid_spec=pltpu.PrefetchScalarGridSpec(
            num_scalar_prefetch=1,
            grid=(span // rows,),
            in_specs=[pl.BlockSpec(memory_space=pl.ANY)] * (len(blocks) + len(weights))
            + [table, table],
            out_specs=[
                pl.BlockSpec((rows, HEAD_PACK), lambda i, h: (i, 0)),
                token_rows,
                token_rows,
                pl.BlockSpec(shape, lambda i, h: (0,) * len(shape)),
                pl.BlockSpec((rows, PAIR), lambda i, h: (i, 0)),
                pl.BlockSpec((rows, PAIR), lambda i, h: (i, 0)),
            ],
            scratch_shapes=[
                pltpu.VMEM((8, width), f32),
                pltpu.VMEM((span // rows, rows, width), bf16),
                pltpu.SemaphoreType.DMA((span // rows + len(weights),)),
            ],
        ),
        out_shape=[
            jax.ShapeDtypeStruct((span, HEAD_PACK), bf16),
            jax.ShapeDtypeStruct((span, width), bf16),
            jax.ShapeDtypeStruct((span, width), bf16),
            jax.ShapeDtypeStruct(shape, bf16),
            jax.ShapeDtypeStruct((span, PAIR), f32),
            jax.ShapeDtypeStruct((span, PAIR), f32),
        ],
        compiler_params=pltpu.CompilerParams(vmem_limit_bytes=VMEM_LIMIT),
        cost_estimate=pl.CostEstimate(
            flops=2 * span * width * HEAD_PACK, bytes_accessed=18 * 2**20, transcendentals=0
        ),
        name="project",
    )(place, *blocks, *weights, cos, sin)


def head_grads_kernel(x_ref, normed_ref, w_ref, grad_ref, out_ref, acc, gain):
    i = pl.program_id(0)

    @pl.when(i == 0)
    def _():
        acc[...] = jnp.zeros_like(acc)
        gain[...] = jnp.zeros_like(gain)

    grad = grad_ref[...]
    acc[...] += contract_rows(grad, normed_ref[...])
    x = x_ref[...].astype(f32)
    inverse = lax.rsqrt(jnp.mean(x * x, axis=-1, keepdims=True) + NORM_EPS)
    back = contract_cols(grad, w_ref[...]) * (x * inverse)
    gain[...] += jnp.sum(back.reshape(back.shape[0] // 8, 8, back.shape[1]), axis=0)

    @pl.when(i == pl.num_programs(0) - 1)
    def _():
        out_ref[:, :HEAD_PACK] = jnp.transpose(acc[...]).astype(bf16)
        total = jnp.sum(gain[...], axis=0, keepdims=True)
        rows = lax.broadcasted_iota(jnp.int32, (LANES, total.shape[1]), 0)
        out_ref[:, HEAD_PACK:] = jnp.transpose(
            jnp.where(rows == 0, jnp.broadcast_to(total, rows.shape), 0.0)
        ).astype(bf16)


def head_grads(x, normed, weights, grads):
    span, width = x.shape
    rows = 2 * BLOCK
    token_rows = pl.BlockSpec((rows, width), lambda i: (i, 0))
    return pl.pallas_call(
        head_grads_kernel,
        grid=(span // rows,),
        in_specs=[
            token_rows,
            token_rows,
            pl.BlockSpec((width, HEAD_PACK), lambda i: (0, 0)),
            pl.BlockSpec((rows, HEAD_PACK), lambda i: (i, 0)),
        ],
        out_specs=pl.BlockSpec((width, HEAD_PACK + LANES), lambda i: (0, 0)),
        scratch_shapes=[pltpu.VMEM((HEAD_PACK, width), f32), pltpu.VMEM((8, width), f32)],
        out_shape=jax.ShapeDtypeStruct((width, HEAD_PACK + LANES), bf16),
        compiler_params=pltpu.CompilerParams(vmem_limit_bytes=VMEM_LIMIT),
        cost_estimate=pl.CostEstimate(
            flops=4 * span * width * HEAD_PACK, bytes_accessed=12 * 2**20, transcendentals=0
        ),
        name="head_grads",
    )(x, normed, weights, grads)


def lower_lanes(shape):
    return lax.broadcasted_iota(jnp.int32, shape, len(shape) - 1) < HEAD_SIZE


def both_heads_low(pair):
    low = lower_lanes(pair.shape)
    return jnp.concatenate(
        [jnp.where(low, pair, 0.0), jnp.where(low, pltpu.roll(pair, HEAD_SIZE, 1), 0.0)], axis=0
    )


def both_heads_high(pair):
    low = lower_lanes(pair.shape)
    return jnp.concatenate(
        [jnp.where(low, 0.0, pltpu.roll(pair, HEAD_SIZE, 1)), jnp.where(low, 0.0, pair)], axis=0
    )


def block_bounds(bounds_ref):
    i, steps = pl.program_id(0), pl.num_programs(0)
    query_start = (i + bounds_ref[2 * steps]) * QUERY_BLOCK
    diagonal = query_start // BLOCK
    full = jnp.minimum(bounds_ref[steps + i], diagonal)
    return query_start, bounds_ref[i], full, diagonal, diagonal + QUERY_BLOCK // BLOCK


def pair_mask(doc, query_start):
    doc = jnp.concatenate([doc, doc], axis=1)
    queries = lax.broadcasted_iota(jnp.int32, doc.shape, 1) % QUERY_BLOCK + query_start

    def masked(scores, start):
        keys = lax.broadcasted_iota(jnp.int32, scores.shape, 0) + start
        return jnp.where((keys >= doc) & (keys <= queries), scores, NEGATIVE_HUGE)

    return masked


def attend_kernel(bounds_ref, q_ref, kv_ref, doc_ref, o_ref, low_ref, lse_ref, acc):
    query_start, first, full, diagonal, end = block_bounds(bounds_ref)
    q = both_heads_low(q_ref[...].astype(f32) * SCALE_OF_SCORES).astype(bf16)
    masked = pair_mask(doc_ref[0], query_start)
    acc[...] = jnp.zeros_like(acc)

    def step(mask, j, carried):
        top, total = carried
        start = pl.multiple_of(j * BLOCK, BLOCK)
        kv = kv_ref[pl.ds(start, BLOCK), :]
        scores = contract_cols(kv, q)
        if mask:
            scores = masked(scores, start)
        new = jnp.maximum(top, jnp.max(scores, axis=0, keepdims=True))
        probs = jnp.exp(scores - new)
        keep = jnp.exp(top - new)
        acc[...] = acc[...] * keep + contract_rows(kv, probs.astype(bf16))
        return new, total * keep + jnp.sum(probs, axis=0, keepdims=True)

    row = (1, 2 * QUERY_BLOCK)
    carried = (jnp.full(row, NEGATIVE_HUGE, f32), jnp.zeros(row, f32))
    carried = lax.fori_loop(first, full, functools.partial(step, True), carried)
    carried = lax.fori_loop(full, diagonal, functools.partial(step, False), carried)
    top, total = lax.fori_loop(diagonal, end, functools.partial(step, True), carried)
    mixed = jnp.transpose(acc[...] / total)
    one, two = mixed[:QUERY_BLOCK], mixed[QUERY_BLOCK:]
    out = jnp.where(lower_lanes(one.shape), pltpu.roll(one, HEAD_SIZE, 1), two)
    o_ref[...] = out
    low_ref[...] = out.astype(bf16)
    lse_ref[0] = top + jnp.log(total)


def attention_specs(kv_at, keys):
    pair = pl.BlockSpec((QUERY_BLOCK, PAIR), lambda i, s: (i, 0))
    return (
        pair,
        pl.BlockSpec((keys, PAIR), lambda i, s: (0, kv_at)),
        pl.BlockSpec((1, 1, QUERY_BLOCK), lambda i, s: (i, 0, 0)),
        pl.BlockSpec((1, 1, 2 * QUERY_BLOCK), lambda i, s: (i, 0, 0)),
    )


def attend(bounds, qkv, kv, kv_at, doc):
    queries, keys = qkv.shape[0], kv.shape[0]
    steps = queries // QUERY_BLOCK
    pair, whole, doc_row, lse_row = attention_specs(kv_at, keys)
    return pl.pallas_call(
        attend_kernel,
        grid_spec=pltpu.PrefetchScalarGridSpec(
            num_scalar_prefetch=1,
            grid=(steps,),
            in_specs=[pair, whole, doc_row],
            out_specs=[pair, pair, lse_row],
            scratch_shapes=[pltpu.VMEM((PAIR, 2 * QUERY_BLOCK), f32)],
        ),
        out_shape=[
            jax.ShapeDtypeStruct((queries, PAIR), f32),
            jax.ShapeDtypeStruct((queries, PAIR), bf16),
            jax.ShapeDtypeStruct((steps, 1, 2 * QUERY_BLOCK), f32),
        ],
        compiler_params=pltpu.CompilerParams(vmem_limit_bytes=VMEM_LIMIT),
        cost_estimate=pl.CostEstimate(
            flops=4 * queries * keys * PAIR, bytes_accessed=6 * 2**20, transcendentals=queries * keys
        ),
        name="attend",
    )(bounds, qkv, kv, doc)


def attend_back_kernel(
    fold, bounds_ref, q_ref, kv_ref, doc_ref, do_ref, o_ref, lse_ref, cos_ref, sin_ref, *refs
):
    if fold:
        out_ref, acc, dkv_ref = refs
    else:
        dq_ref, dkv_ref, acc = refs
    i = pl.program_id(0)
    query_start, first, full, diagonal, end = block_bounds(bounds_ref)

    @pl.when(i == 0)
    def _():
        dkv_ref[...] = jnp.zeros_like(dkv_ref)

    q = both_heads_low(q_ref[...].astype(f32) * SCALE_OF_SCORES).astype(bf16)
    grad = do_ref[...].astype(f32)
    product = jnp.transpose(grad * o_ref[...])
    delta = jnp.concatenate(
        [
            jnp.sum(product[:HEAD_SIZE], axis=0, keepdims=True),
            jnp.sum(product[HEAD_SIZE:], axis=0, keepdims=True),
        ],
        axis=1,
    )
    grad = both_heads_high(grad).astype(bf16)
    sources = jnp.concatenate([q, grad], axis=0)
    masked = pair_mask(doc_ref[0], query_start)
    lse = lse_ref[0]
    acc[...] = jnp.zeros_like(acc)

    def step(mask, j, carried):
        start = pl.multiple_of(j * BLOCK, BLOCK)
        kv = kv_ref[pl.ds(start, BLOCK), :]
        scores = contract_cols(kv, q) - lse
        if mask:
            scores = masked(scores, start)
        probs = jnp.exp(scores)
        grad_scores = (probs * (contract_cols(kv, grad) - delta)).astype(bf16)
        acc[...] += contract_rows(kv, grad_scores)
        both = jnp.concatenate([grad_scores, probs.astype(bf16)], axis=1)
        dkv_ref[pl.ds(start, BLOCK), :] += jnp.dot(both, sources, preferred_element_type=f32)
        return carried

    lax.fori_loop(first, full, functools.partial(step, True), 0)
    lax.fori_loop(full, diagonal, functools.partial(step, False), 0)
    lax.fori_loop(diagonal, end, functools.partial(step, True), 0)
    dq = jnp.transpose(acc[...])
    one, two = dq[:QUERY_BLOCK], dq[QUERY_BLOCK:]
    dq = jnp.where(lower_lanes(one.shape), one, pltpu.roll(two, HEAD_SIZE, 1))
    if not fold:
        dq_ref[...] = dq
        return
    mine = pl.ds(pl.multiple_of(i * QUERY_BLOCK, QUERY_BLOCK), QUERY_BLOCK)
    out_ref[mine, :PAIR] = rotate_lanes(
        dq * SCALE_OF_SCORES, cos_ref[mine, :], -sin_ref[mine, :]
    ).astype(bf16)

    @pl.when(i == pl.num_programs(0) - 1)
    def _():
        def finish(j, carried):
            part = pl.ds(pl.multiple_of(j * BLOCK, BLOCK), BLOCK)
            cos, sin = key_tables(cos_ref[part, :], sin_ref[part, :])
            out_ref[part, PAIR:] = rotate_lanes(dkv_ref[part, :], cos, -sin).astype(bf16)
            return carried

        lax.fori_loop(0, dkv_ref.shape[0] // BLOCK, finish, 0)


def attend_back(bounds, qkv, kv, kv_at, doc, grad, out, lse, cos, sin, fold):
    queries, keys = qkv.shape[0], kv.shape[0]
    steps = queries // QUERY_BLOCK
    pair, whole, doc_row, lse_row = attention_specs(kv_at, keys)
    table = pl.BlockSpec(cos.shape, lambda i, s: (0, 0))
    acc = pltpu.VMEM((PAIR, 2 * QUERY_BLOCK), f32)
    if fold:
        out_specs = pl.BlockSpec((queries, HEAD_PACK), lambda i, s: (0, 0))
        out_shape = jax.ShapeDtypeStruct((queries, HEAD_PACK), bf16)
        scratch = [acc, pltpu.VMEM((keys, PAIR), f32)]
    else:
        out_specs = [pair, pl.BlockSpec((keys, PAIR), lambda i, s: (0, 0))]
        out_shape = [
            jax.ShapeDtypeStruct((queries, PAIR), f32),
            jax.ShapeDtypeStruct((keys, PAIR), f32),
        ]
        scratch = [acc]
    return pl.pallas_call(
        functools.partial(attend_back_kernel, fold),
        grid_spec=pltpu.PrefetchScalarGridSpec(
            num_scalar_prefetch=1,
            grid=(steps,),
            in_specs=[pair, whole, doc_row, pair, pair, lse_row, table, table],
            out_specs=out_specs,
            scratch_shapes=scratch,
        ),
        out_shape=out_shape,
        compiler_params=pltpu.CompilerParams(vmem_limit_bytes=VMEM_LIMIT),
        cost_estimate=pl.CostEstimate(
            flops=10 * queries * keys * PAIR,
            bytes_accessed=8 * 2**20,
            transcendentals=queries * keys,
        ),
        name="attend_back",
    )(bounds, qkv, kv, doc, grad, out, lse, cos, sin)


def unrotate_kernel(dq_ref, dkv_ref, cos_ref, sin_ref, out_ref):
    cos, sin = cos_ref[...], sin_ref[...]
    dq = rotate_lanes(dq_ref[...] * SCALE_OF_SCORES, cos, -sin)
    cos, sin = key_tables(cos, sin)
    dkv = rotate_lanes(dkv_ref[...], cos, -sin)
    out_ref[...] = jnp.concatenate([dq, dkv], axis=1).astype(bf16)


def unrotate(dq, dkv, cos, sin):
    rows = dq.shape[0]
    pair = pl.BlockSpec((BLOCK, PAIR), lambda i: (i, 0))
    return pl.pallas_call(
        unrotate_kernel,
        grid=(rows // BLOCK,),
        in_specs=[pair, pair, pair, pair],
        out_specs=pl.BlockSpec((BLOCK, HEAD_PACK), lambda i: (i, 0)),
        out_shape=jax.ShapeDtypeStruct((rows, HEAD_PACK), bf16),
        cost_estimate=pl.CostEstimate(
            flops=rows * HEAD_PACK * 8, bytes_accessed=rows * HEAD_PACK * 14, transcendentals=0
        ),
        name="unrotate",
    )(dq, dkv, cos, sin)


def place_experts_kernel(place_ref, *refs):
    blocks, (ct_ref, w_ref, z_ref, sems) = refs[:10], refs[10:]
    core = place_ref[1]
    rows = w_ref.shape[1] // 2
    half = rows // 2
    sources = [[(0, 0, rows)], [(1, 0, rows)], [(2, 0, rows)], [(3, 0, half), (4, half, half)]]
    for step, parts in enumerate(sources):

        @pl.when(pl.program_id(0) == step)
        def _(parts=parts):
            copies = []
            for source, start, length in parts:
                for other in (0, 1):
                    first = jnp.where(core == other, 0, rows) + start
                    at = pl.ds(pl.multiple_of(first, half), length)
                    copies.append(
                        pltpu.make_async_copy(
                            blocks[2 * source + other], w_ref.at[0, at, :], sems.at[len(copies)]
                        )
                    )
            for copy in copies:
                copy.start()
            for copy in copies:
                copy.wait()

    z_ref[0] = jnp.dot(ct_ref[...], w_ref[0, :, 2 * F :], preferred_element_type=f32)


def place_experts(place, parts, early, width):
    rows = early.shape[0]
    blocks = [block for pair in parts for block in pair]
    return pl.pallas_call(
        place_experts_kernel,
        grid_spec=pltpu.PrefetchScalarGridSpec(
            num_scalar_prefetch=1,
            grid=(EXPERTS_HERE,),
            in_specs=[pl.BlockSpec(memory_space=pl.ANY)] * len(blocks)
            + [pl.BlockSpec((rows, width), lambda r, s: (0, 0))],
            out_specs=[
                pl.BlockSpec((1, width, 3 * F), lambda r, s: (s[0] ^ r, 0, 0)),
                pl.BlockSpec((1, rows, F), lambda r, s: (s[0] ^ r, 0, 0)),
            ],
            scratch_shapes=[pltpu.SemaphoreType.DMA((4,))],
        ),
        out_shape=[
            jax.ShapeDtypeStruct((EXPERTS_HERE, width, 3 * F), bf16),
            jax.ShapeDtypeStruct((EXPERTS_HERE, rows, F), f32),
        ],
        compiler_params=pltpu.CompilerParams(vmem_limit_bytes=VMEM_LIMIT),
        cost_estimate=pl.CostEstimate(
            flops=2 * EXPERTS_HERE * rows * width * F, bytes_accessed=36 * 2**20, transcendentals=0
        ),
        name="place_experts",
    )(place, *blocks, early)


def lane_column(x, at):
    lane = lax.broadcasted_iota(jnp.int32, x.shape, 1)
    return jnp.sum(jnp.where(lane == at, x, 0.0), axis=1, keepdims=True)


def experts_kernel(
    group_ref, n_ref, routed_ref, router_ref, w_ref, z_ref,
    back_ref, gates_ref, hidden_ref, pre_ref, acc, dots,
):
    e = pl.program_id(0)
    own = group_ref[0] * EXPERTS_HERE + e
    rows = n_ref.shape[0]

    @pl.when(e == 0)
    def _():
        logits = jnp.dot(n_ref[...], router_ref[...], preferred_element_type=f32)
        routed = routed_ref[...].astype(f32) > 0.5
        highest = jnp.max(jnp.where(routed, logits, NEGATIVE_HUGE), axis=1, keepdims=True)
        weights = jnp.where(routed, jnp.exp(jnp.where(routed, logits - highest, 0.0)), 0.0)
        gates_ref[...] = weights / jnp.sum(weights, axis=1, keepdims=True)
        acc[...] = jnp.zeros_like(acc)
        dots[...] = jnp.zeros_like(dots)

    w_in = w_ref[0, :, : 2 * F]
    for t in range(rows // BLOCK):
        part = pl.ds(t * BLOCK, BLOCK)
        pre = jnp.dot(n_ref[part, :], w_in, preferred_element_type=f32)
        gate, up = pre[:, :F], pre[:, F:]
        z = z_ref[0, part, :]
        weight = lane_column(gates_ref[part, :], own)
        sig = 1.0 / (1.0 + jnp.exp(-gate))
        act = gate * sig
        hidden = act * up
        hidden_ref[0, part, :] = (weight * hidden).astype(bf16)
        dot = RESIDUAL_SCALE * jnp.sum(hidden.astype(bf16).astype(f32) * z, axis=1, keepdims=True)
        lane = lax.broadcasted_iota(jnp.int32, (BLOCK, LANES), 1)
        dots[part, :] += jnp.where(lane == own, dot, 0.0)
        scaled = (RESIDUAL_SCALE * weight) * z
        pre_ref[0, part, :F] = (scaled * up * (sig + act * (1.0 - sig))).astype(bf16)
        pre_ref[0, part, F:] = (scaled * act).astype(bf16)
        acc[part, :] += contract_cols(pre_ref[0, part, :], w_in)

    @pl.when(e == EXPERTS_HERE - 1)
    def _():
        width = n_ref.shape[1]
        back_ref[:, :width] = acc[...].astype(bf16)
        high = dots[...].astype(bf16)
        low = dots[...] - high.astype(f32)
        back_ref[:, width:] = (high.astype(f32) + pltpu.roll(low, E, 1)).astype(bf16)


def experts(group, normed, early, packed, w_all, z):
    rows, width = normed.shape
    count = w_all.shape[0]
    whole = pl.BlockSpec((rows, width), lambda e, g: (0, 0))
    column = width // LANES
    router_at = packed.shape[1] // LANES - 1
    return pl.pallas_call(
        experts_kernel,
        grid_spec=pltpu.PrefetchScalarGridSpec(
            num_scalar_prefetch=1,
            grid=(count,),
            in_specs=[
                whole,
                pl.BlockSpec((rows, LANES), lambda e, g: (0, column)),
                pl.BlockSpec((width, LANES), lambda e, g: (0, router_at)),
                pl.BlockSpec((1, width, 3 * F), lambda e, g: (e, 0, 0)),
                pl.BlockSpec((1, rows, F), lambda e, g: (e, 0, 0)),
            ],
            out_specs=[
                pl.BlockSpec((rows, width + LANES), lambda e, g: (0, 0)),
                pl.BlockSpec((rows, LANES), lambda e, g: (0, 0)),
                pl.BlockSpec((1, rows, F), lambda e, g: (e, 0, 0)),
                pl.BlockSpec((1, rows, 2 * F), lambda e, g: (e, 0, 0)),
            ],
            scratch_shapes=[pltpu.VMEM((rows, width), f32), pltpu.VMEM((rows, LANES), f32)],
        ),
        out_shape=[
            jax.ShapeDtypeStruct((rows, width + LANES), bf16),
            jax.ShapeDtypeStruct((rows, LANES), f32),
            jax.ShapeDtypeStruct((count, rows, F), bf16),
            jax.ShapeDtypeStruct((count, rows, 2 * F), bf16),
        ],
        compiler_params=pltpu.CompilerParams(vmem_limit_bytes=VMEM_LIMIT),
        cost_estimate=pl.CostEstimate(
            flops=2 * count * rows * width * 4 * F, bytes_accessed=40 * 2**20, transcendentals=0
        ),
        name="experts",
    )(group, normed, early, packed, w_all, z)


def expert_grads_kernel(with_y, half_ref, n_ref, ct_ref, w_ref, hidden_ref, pre_ref, *refs):
    if with_y:
        y_ref, grad_ref, n_t, ct_t, acc = refs
    else:
        grad_ref, n_t, ct_t = refs
    e = pl.program_id(0)

    @pl.when(e == 0)
    def _():
        n_t[...] = jnp.transpose(n_ref[...])
        ct_t[...] = jnp.transpose(ct_ref[...])
        if with_y:
            acc[...] = jnp.zeros_like(acc)

    grad_ref[0, :, : 2 * F] = jnp.dot(n_t[...], pre_ref[0], preferred_element_type=f32).astype(bf16)
    grad_ref[0, :, 2 * F :] = (
        RESIDUAL_SCALE * jnp.dot(ct_t[...], hidden_ref[0], preferred_element_type=f32)
    ).astype(bf16)
    if not with_y:
        return
    acc[...] += contract_cols(hidden_ref[0], w_ref[0, :, 2 * F :])

    @pl.when(e == pl.num_programs(0) - 1)
    def _():
        y_ref[...] = acc[...].astype(bf16)


def expert_grads(half, halves, normed, early, w_all, hidden, pre, with_y):
    rows, width = normed.shape
    count = w_all.shape[0]
    own = width // halves
    feature = pl.BlockSpec((rows, own), lambda e, h: (0, h[0]))
    out_specs = [pl.BlockSpec((1, own, 3 * F), lambda e, h: (e, 0, 0))]
    out_shape = [jax.ShapeDtypeStruct((count, own, 3 * F), bf16)]
    scratch = [pltpu.VMEM((own, rows), bf16), pltpu.VMEM((own, rows), bf16)]
    if with_y:
        out_specs.insert(0, pl.BlockSpec((rows, width), lambda e, h: (0, 0)))
        out_shape.insert(0, jax.ShapeDtypeStruct((rows, width), bf16))
        scratch.append(pltpu.VMEM((rows, width), f32))
    return pl.pallas_call(
        functools.partial(expert_grads_kernel, with_y),
        grid_spec=pltpu.PrefetchScalarGridSpec(
            num_scalar_prefetch=1,
            grid=(count,),
            in_specs=[
                feature,
                feature,
                pl.BlockSpec((1, width, 3 * F), lambda e, h: (e, 0, 0)),
                pl.BlockSpec((1, rows, F), lambda e, h: (e, 0, 0)),
                pl.BlockSpec((1, rows, 2 * F), lambda e, h: (e, 0, 0)),
            ],
            out_specs=out_specs,
            scratch_shapes=scratch,
        ),
        out_shape=out_shape,
        compiler_params=pltpu.CompilerParams(vmem_limit_bytes=VMEM_LIMIT),
        cost_estimate=pl.CostEstimate(
            flops=2 * count * rows * width * 3 * F // halves + 2 * with_y * count * rows * width * F,
            bytes_accessed=30 * 2**20,
            transcendentals=0,
        ),
        name="expert_grads",
    )(half, normed, early, w_all, hidden, pre)


def join_kernel(place_ref, o_ref, w_ref, small_ref, x_ref, normed_ref, resid_ref, own_ref, gain):
    t = pl.program_id(0)
    b = place_ref[2]

    @pl.when(t == 0)
    def _():
        gain[...] = jnp.transpose(small_ref[...].astype(f32))[E : E + 8, :]

    pairs = []
    for a in range(o_ref.shape[0]):
        same, other = o_ref[a, 0, 0], o_ref[a, 1, 0]
        pairs.append(jnp.where(b == 0, same, other))
        pairs.append(jnp.where(b == 0, other, same))
    attended = jnp.concatenate(pairs, axis=1)
    resid = x_ref[...].astype(f32) + RESIDUAL_SCALE * jnp.dot(
        attended, w_ref[...], preferred_element_type=f32
    )
    normed_ref[...] = rms_scale(resid, gain[1:2, :]).astype(bf16)

    @pl.when(t == place_ref[1])
    def _():
        resid_ref[...] = resid
        own_ref[...] = attended


def join(place, outs, packed, weights_at, x):
    width = packed.shape[0]
    lines, _, _, rows, pair = outs.shape
    small_at = packed.shape[1] // LANES - 1
    own = pl.BlockSpec((rows, width), lambda t, s: (0, 0))
    return pl.pallas_call(
        join_kernel,
        grid_spec=pltpu.PrefetchScalarGridSpec(
            num_scalar_prefetch=1,
            grid=(lines,),
            in_specs=[
                pl.BlockSpec((lines, 2, 1, rows, pair), lambda t, s: (0, 0, t, 0, 0)),
                pl.BlockSpec((width, width), lambda t, s: (0, weights_at)),
                pl.BlockSpec((width, LANES), lambda t, s: (0, small_at)),
                pl.BlockSpec((rows, width), lambda t, s: (2 * t + s[2], 0)),
            ],
            out_specs=[pl.BlockSpec((rows, width), lambda t, s: (t, 0)), own, own],
            scratch_shapes=[pltpu.VMEM((8, width), f32)],
        ),
        out_shape=[
            jax.ShapeDtypeStruct((lines * rows, width), bf16),
            jax.ShapeDtypeStruct((rows, width), f32),
            jax.ShapeDtypeStruct((rows, width), bf16),
        ],
        compiler_params=pltpu.CompilerParams(vmem_limit_bytes=VMEM_LIMIT),
        cost_estimate=pl.CostEstimate(
            flops=2 * lines * rows * width * width, bytes_accessed=12 * 2**20, transcendentals=0
        ),
        name="join",
    )(place, outs, packed, packed, x)


def token_grads_kernel(grad_ref, w_ref, small_ref, x_ref, resid_ref, out_ref, acc):
    h = pl.program_id(0)
    part = contract_cols(grad_ref[0], w_ref[...])

    @pl.when(h == 0)
    def _():
        acc[...] = part

    @pl.when(h > 0)
    def _():
        acc[...] += part

    @pl.when(h == pl.num_programs(0) - 1)
    def _():
        gain = jnp.transpose(small_ref[...].astype(f32))[E : E + 1, :]
        x = x_ref[...].astype(f32)
        inverse = lax.rsqrt(jnp.mean(x * x, axis=-1, keepdims=True) + NORM_EPS)
        scaled = acc[...] * gain
        mean = jnp.mean(x * scaled, axis=-1, keepdims=True)
        out_ref[...] = resid_ref[...] + (inverse * scaled - x * inverse**3 * mean)


def token_grads(grads, packed, x, resid):
    heads, rows, pack = grads.shape
    width = x.shape[1]
    small_at = packed.shape[1] // LANES - 1
    whole = pl.BlockSpec((rows, width), lambda h: (0, 0))
    return pl.pallas_call(
        token_grads_kernel,
        grid=(heads,),
        in_specs=[
            pl.BlockSpec((1, rows, pack), lambda h: (h, 0, 0)),
            pl.BlockSpec((width, pack), lambda h: (0, h)),
            pl.BlockSpec((width, LANES), lambda h: (0, small_at)),
            whole,
            whole,
        ],
        out_specs=whole,
        out_shape=jax.ShapeDtypeStruct((rows, width), f32),
        scratch_shapes=[pltpu.VMEM((rows, width), f32)],
        compiler_params=pltpu.CompilerParams(vmem_limit_bytes=VMEM_LIMIT),
        cost_estimate=pl.CostEstimate(
            flops=2 * rows * width * heads * pack, bytes_accessed=8 * 2**20, transcendentals=0
        ),
        name="token_grads",
    )(grads, packed, packed, x, resid)


def weight_sums_kernel(sums_ref, q_ref, k_ref, v_ref, gain_ref):
    groups, heads, members = sums_ref.shape[:3]
    gain = jnp.zeros(gain_ref.shape, f32)
    values = []
    for h in range(heads):
        total = jnp.zeros(sums_ref.shape[3:], f32)
        for g in range(groups):
            for member in range(members):
                total += sums_ref[g, h, member].astype(f32)
        values.append(total)
        gain += total[:, HEAD_PACK:]
        q_ref[:, h * PAIR : (h + 1) * PAIR] = total[:, :PAIR]
    gain_ref[...] = gain
    for h in range(0, heads, 2):
        one, two = values[h][:, PAIR:HEAD_PACK], values[h + 1][:, PAIR:HEAD_PACK]
        low = lower_lanes(one.shape)
        at = slice(h // 2 * PAIR, (h // 2 + 1) * PAIR)
        k_ref[:, at] = jnp.where(low, one, pltpu.roll(two, HEAD_SIZE, 1))
        v_ref[:, at] = jnp.where(low, pltpu.roll(one, HEAD_SIZE, 1), two)


def weight_sums(sums):
    rows, heads = sums.shape[3], sums.shape[1]
    return pl.pallas_call(
        weight_sums_kernel,
        out_shape=[
            jax.ShapeDtypeStruct((rows, heads * PAIR), f32),
            jax.ShapeDtypeStruct((rows, heads * HEAD_SIZE), f32),
            jax.ShapeDtypeStruct((rows, heads * HEAD_SIZE), f32),
            jax.ShapeDtypeStruct((rows, LANES), f32),
        ],
        compiler_params=pltpu.CompilerParams(vmem_limit_bytes=VMEM_LIMIT),
        cost_estimate=pl.CostEstimate(flops=2**20, bytes_accessed=2 * 2**20, transcendentals=0),
        name="weight_sums",
    )(sums)


def exchange(x, axes):
    return lax.all_to_all(x, axes, 0, 0, tiled=True)


def body(
    tokens,
    cotangent,
    segment_ids,
    routes,
    norm_attn,
    w_query,
    key_weight_matrix,
    value_weight_matrix,
    w_output,
    norm_moe,
    w_router,
    expert_in,
    expert_out,
):
    x_local = tokens[0].astype(f32)
    token_count, width = x_local.shape
    seg_row = segment_ids[0]
    group = lax.axis_index("a")
    head_axes = SEQ if lax.axis_size(SEQ) == KEY_VALUE_HEADS else ("b",)
    whole_rows = head_axes == SEQ
    span = token_count * KEY_VALUE_HEADS
    span_start = 0 if whole_rows else group * span

    def start_of_doc(ids):
        return jnp.sum((seg_row[None, :] < ids[:, None]).astype(jnp.int32), axis=1)

    seg_span = lax.dynamic_slice_in_dim(seg_row, span_start, span)
    doc_span = start_of_doc(seg_span)
    cos_span, sin_span = rotation_tables(
        span_start + jnp.arange(span, dtype=jnp.int32) - doc_span
    )
    by_block = doc_span.reshape(-1, QUERY_BLOCK)
    bounds = jnp.concatenate(
        [
            by_block[:, 0] // BLOCK,
            (by_block[:, -1] + BLOCK - 1) // BLOCK,
            jnp.full((1,), span_start // QUERY_BLOCK, jnp.int32),
        ]
    )
    doc_rows = by_block[:, None, :]

    own_rows = w_query.shape[0]
    by_head = jnp.concatenate(
        [
            w_query.astype(bf16).reshape(own_rows, KEY_VALUE_HEADS, PAIR),
            key_weight_matrix.astype(bf16).reshape(own_rows, KEY_VALUE_HEADS, HEAD_SIZE),
            value_weight_matrix.astype(bf16).reshape(own_rows, KEY_VALUE_HEADS, HEAD_SIZE),
        ],
        axis=2,
    ).reshape(own_rows, KEY_VALUE_HEADS * HEAD_PACK)
    qkv_width = KEY_VALUE_HEADS * HEAD_PACK
    first_all = gather(
        jnp.concatenate(
            [
                by_head,
                w_output.astype(bf16),
                pad_lanes(
                    jnp.concatenate(
                        [
                            w_router.astype(bf16),
                            norm_attn.astype(bf16)[:, None],
                            norm_moe.astype(bf16)[:, None],
                        ],
                        axis=1,
                    ),
                    LANES,
                ),
            ],
            axis=1,
        ),
        ALL,
    )
    experts_low = jnp.concatenate([expert_in.astype(bf16), expert_out.astype(bf16)], axis=1)
    small_plane = lax.axis_size("b") == 2 and lax.axis_size("y") == 2 and lax.axis_size("c") == 2
    if small_plane:
        gains = jnp.broadcast_to(
            pad_lanes(norm_attn.astype(bf16)[:, None], LANES), (KEY_VALUE_HEADS, own_rows, LANES)
        )
        columns = exchange(
            jnp.concatenate(
                [by_head.reshape(own_rows, KEY_VALUE_HEADS, HEAD_PACK).transpose(1, 0, 2), gains],
                axis=2,
            ),
            SEQ,
        )
        from_y = lax.ppermute(columns, "y", SWAP)
        spots = ((0, 0), (0, 1), (1, 0), (1, 1))
        weights = (
            columns, lax.ppermute(columns, "c", SWAP), from_y, lax.ppermute(from_y, "c", SWAP)
        )
    else:
        spots = None
        at = lax.axis_index(head_axes) * HEAD_PACK
        gain_at = qkv_width + width + E
        weights = (
            jnp.concatenate(
                [
                    lax.dynamic_slice_in_dim(first_all, at, HEAD_PACK, 1),
                    pad_lanes(first_all[:, gain_at : gain_at + 1], LANES),
                ],
                axis=1,
            ),
        )
    if whole_rows:
        pieces = grid_gather(tokens[0])
        places = [piece[:2] for piece in pieces]
        blocks = tuple(piece[2] for piece in pieces)
    else:
        places = None
        blocks = (gather(tokens[0], "b").reshape((-1,) + tokens.shape[1:]),)
    experts_low, blocks, weights, cos_span, sin_span, bounds, doc_rows = (
        lax.optimization_barrier(
            (experts_low, blocks, weights, cos_span, sin_span, bounds, doc_rows)
        )
    )
    output_w = first_all[:, qkv_width : qkv_width + width]
    small_at = qkv_width + width
    router_w = first_all[:, small_at : small_at + E]
    gain_two_f = first_all[:, small_at + E + 1].astype(f32)

    expert_ids = jnp.arange(E, dtype=jnp.int32)
    routed_own = jnp.any(routes[0][:, :, None] == expert_ids[None, None, :], axis=1)
    early = jnp.concatenate([cotangent[0], pad_lanes(routed_own.astype(bf16), LANES)], axis=1)
    early_all = gather(early, "a")
    if small_plane:
        beside = neighbours(experts_low)
    else:
        parts = gather(experts_low, PLANE)

    place = jnp.stack(
        [lax.axis_index(axis) for axis in (head_axes, "a", "b", "y", "c")]
    )
    qkv, normed_span, x_span, own_weights, wide_cos, wide_sin = project(
        place, places, blocks, spots, weights, token_count, width, cos_span, sin_span
    )
    own_weights = own_weights.reshape(width, HEAD_PACK + LANES)
    if whole_rows:
        kv, kv_at = qkv, 1
    else:
        kv, kv_at = gather(qkv[:, PAIR:], "a"), 0
    attention_result, attended, log_total = attend(bounds, qkv, kv, kv_at, doc_rows)
    if small_plane:
        member = lax.axis_index("b")
        attended, beside, first_all = lax.optimization_barrier((attended, beside, first_all))
        parts = plane_gather(experts_low, *beside)
        by_column = attended.reshape(GROUPS, 2, token_count, PAIR)
        other = lax.ppermute(
            lax.dynamic_index_in_dim(by_column, 1 - member, 1, False), "b", SWAP
        )
        own = lax.dynamic_index_in_dim(by_column, member, 1, False)
        pair, early_all = lax.optimization_barrier((jnp.stack([own, other]), early_all))
        outs = lax.all_gather(pair, "a", axis=0, tiled=False)
        normed_all, resid, attended_low = join(place, outs, first_all, qkv_width // width, x_span)
        normed_two = lax.dynamic_slice_in_dim(normed_all, group * token_count, token_count)
        home = jnp.stack([member * 2 + lax.axis_index("y"), lax.axis_index("c")])
        experts_all, grad_hidden = place_experts(home, parts, early_all, width)
    else:
        attended_low = (
            exchange(attended.reshape(KEY_VALUE_HEADS, token_count, PAIR), head_axes)
            .transpose(1, 0, 2)
            .reshape(token_count, QUERY_HEADS * HEAD_SIZE)
        )
        attn_out = jnp.dot(attended_low, output_w, preferred_element_type=f32)
        resid = x_local + RESIDUAL_SCALE * attn_out
        normed_two = rms_scale(resid, gain_two_f).astype(bf16)
        normed_all = gather(normed_two, "a")
        experts_all = parts.reshape(EXPERTS_HERE, width, 3 * F)
        grad_hidden = jnp.einsum(
            "td,edf->etf",
            early_all[:, :width],
            experts_all[:, :, 2 * F :],
            preferred_element_type=f32,
        )
    back_part, gates_all, gated_hidden, grad_pre = experts(
        group.reshape(1), normed_all, early_all, first_all, experts_all, grad_hidden
    )
    back_own = scatter_sum(back_part, "a").astype(f32)
    inputs = (normed_all, early_all, experts_all, gated_hidden, grad_pre)
    if small_plane:
        core = lax.axis_index("c")
        (send,) = expert_grads((1 - core).reshape(1), 2, *inputs, False)
        arrived = lax.ppermute(send, "c", SWAP)
        moe_part, keep = expert_grads(core.reshape(1), 2, *inputs, True)
        back_own, moe_part, keep = lax.optimization_barrier((back_own, moe_part, keep))
    else:
        moe_part, grad_experts = expert_grads(jnp.zeros((1,), jnp.int32), 1, *inputs, True)
        back_own, moe_part, grad_experts = lax.optimization_barrier(
            (back_own, moe_part, grad_experts)
        )
        grad_experts = scatter_sum(grad_experts.reshape(EXPERTS_HERE * width, 3 * F), PLANE)
    moe_sum = scatter_sum(moe_part, "a")

    grad_out = cotangent[0].astype(f32)
    gates = lax.dynamic_slice_in_dim(gates_all, group * token_count, token_count)[:, :E]
    gate_grads_own = back_own[:, width : width + E] + back_own[:, width + E : width + 2 * E]
    grad_logits = gates * (gate_grads_own - jnp.sum(gates * gate_grads_own, axis=-1, keepdims=True))
    grad_normed_two = back_own[:, :width] + jnp.dot(
        grad_logits, router_w.astype(f32).T, precision=HIGHEST_DOT
    )
    grad_router = jnp.dot(normed_two.astype(f32).T, grad_logits, precision=HIGHEST_DOT)
    grad_resid_norm, grad_gain_two = rms_back(resid, gain_two_f, grad_normed_two)
    grad_resid = grad_out + grad_resid_norm
    grad_attn_low = (RESIDUAL_SCALE * grad_resid).astype(bf16)
    grad_heads = contract_cols(grad_attn_low, output_w).astype(bf16)
    grad_mixed = exchange(
        grad_heads.reshape(token_count, KEY_VALUE_HEADS, PAIR).transpose(1, 0, 2), head_axes
    ).reshape(span, PAIR)
    if small_plane:
        keep, arrived, grad_heads = lax.optimization_barrier((keep, arrived, grad_heads))
        total = keep.astype(f32) + arrived.astype(f32)
        total = total.astype(bf16).reshape((2, 2) + keep.shape[1:])
        total, attended_low, grad_router = lax.optimization_barrier(
            (total, attended_low, grad_router)
        )
        wide = 3 * F // 2
        left, right = halve_send(total[..., :wide], "y", 1), halve_send(total[..., wide:], "b", 0)
    small = jnp.concatenate([grad_router, grad_gain_two[:, None]], axis=1)
    second_part = jnp.concatenate(
        [contract_rows(attended_low, grad_attn_low), pad_lanes(small, LANES)], axis=1
    ).astype(bf16)
    cols = second_part.shape[1]
    second_part = second_part.reshape(GROUPS, -1, own_rows, cols).transpose(1, 0, 2, 3)
    second_part, grad_mixed = lax.optimization_barrier((second_part, grad_mixed))
    rest = scatter_sum(second_part.reshape(-1, cols), PLANE)
    grads = attend_back(
        bounds, qkv, kv, kv_at, doc_rows, grad_mixed, attention_result, log_total,
        wide_cos, wide_sin, whole_rows,
    )
    if whole_rows:
        grad_pack = grads
    else:
        grad_kv = scatter_sum(grads[1].astype(bf16), "a").astype(f32)
        grad_pack = unrotate(grads[0], grad_kv, wide_cos, wide_sin)
    if small_plane:
        left, right, moe_sum, grad_pack = lax.optimization_barrier(
            (left, right, moe_sum, grad_pack)
        )
        left, right = halve_add(left), halve_add(right)
        left, right = halve_send(left, "b", 0), halve_send(right, "y", 0)
    first_part = head_grads(x_span, normed_span, own_weights, grad_pack)
    rest, first_part = lax.optimization_barrier((rest, first_part))
    rest = scatter_sum(rest, "a")
    by_tokens = exchange(grad_pack.reshape(KEY_VALUE_HEADS, token_count, HEAD_PACK), head_axes)
    by_tokens, first_part = lax.optimization_barrier((by_tokens, first_part))
    sums = exchange(first_part.reshape(-1, own_rows, first_part.shape[1]), ALL)
    sums, moe_sum, resid = lax.optimization_barrier((sums, moe_sum, resid))
    grad_q_w, grad_k_w, grad_v_w, grad_gain_one = weight_sums(
        sums.reshape(-1, KEY_VALUE_HEADS, lax.axis_size(("y", "c")), own_rows, first_part.shape[1])
    )
    rest = rest.astype(f32)
    grad_input = token_grads(by_tokens, first_all, tokens[0], grad_resid)
    layer_sum = resid + RESIDUAL_SCALE * moe_sum.astype(f32)
    if small_plane:
        grad_experts = jnp.concatenate(
            [own.astype(f32) + other.astype(f32) for own, other in (left, right)], axis=1
        )
    else:
        grad_experts = grad_experts.astype(f32)
    return (
        layer_sum.astype(bf16)[None],
        grad_input[None],
        grad_gain_one[:, 0],
        grad_q_w,
        grad_k_w,
        grad_v_w,
        rest[:, :width],
        rest[:, width + E],
        rest[:, width : width + E],
        grad_experts[:, : 2 * F],
        grad_experts[:, 2 * F :],
    )


def solution(mesh):
    seq, row = mesh.shape["seq"], mesh.shape["row"]
    cut = Mesh(mesh.devices.reshape(GROUPS, seq // GROUPS, row // 2, 2), ALL)
    token_spec = P(("y", "c"), SEQ, None)
    row_spec = P(ALL, None)
    flat_spec = P(ALL)
    in_specs = (
        token_spec,
        token_spec,
        P(("y", "c"), None),
        token_spec,
        flat_spec,
        row_spec,
        row_spec,
        row_spec,
        row_spec,
        flat_spec,
        row_spec,
        row_spec,
        row_spec,
    )
    out_specs = (
        token_spec,
        token_spec,
        flat_spec,
        row_spec,
        row_spec,
        row_spec,
        row_spec,
        flat_spec,
        row_spec,
        row_spec,
        row_spec,
    )
    return jax.shard_map(body, mesh=cut, in_specs=in_specs, out_specs=out_specs, check_vma=False)
```

```python
import functools

import jax
import jax.numpy as jnp
from jax import lax
from jax.experimental import pallas as pl
from jax.experimental.pallas import tpu as pltpu
from jax.sharding import Mesh, PartitionSpec as P

QUERY_HEADS = 16
KEY_VALUE_HEADS = 8
HEAD_SIZE = 64
F = 512
E = 16
GROUPS = 4
EXPERTS_HERE = E // GROUPS
LANES = 128
PAIR = 2 * HEAD_SIZE
HEAD_PACK = 4 * HEAD_SIZE
BLOCK = 256
QUERY_BLOCK = 512

NORM_EPS = 1e-06
RESIDUAL_SCALE = 0.22
SCALE_OF_SCORES = 0.015625
ROPE_BASE = 10000.0
NEGATIVE_HUGE = -1e30
HIGHEST_DOT = lax.Precision.HIGHEST
VMEM_LIMIT = 60 * 1024 * 1024

PLANE = ("b", "y", "c")
SEQ = ("a", "b")
ALL = ("a", "b", "y", "c")
SWAP = [(0, 1), (1, 0)]

f32 = jnp.float32
bf16 = jnp.bfloat16


def rotation_tables(positions):
    half = HEAD_SIZE // 2
    freq = jnp.power(ROPE_BASE, -2.0 * jnp.arange(half, dtype=f32) / HEAD_SIZE)
    angle = positions.astype(f32)[:, None] * freq[None, :]
    return jnp.cos(angle), jnp.sin(angle)


def rms_back(values, gain, grad_norm):
    mean_square = jnp.mean(values * values, axis=-1, keepdims=True)
    inverse = lax.rsqrt(mean_square + NORM_EPS)
    scaled_grad = grad_norm * gain
    grad_values = inverse * scaled_grad - values * inverse**3 * jnp.mean(
        values * scaled_grad, axis=-1, keepdims=True
    )
    grad_gain = jnp.sum(grad_norm * values * inverse, axis=0)
    return (grad_values, grad_gain)


def rms_scale(values, gain):
    mean_square = jnp.mean(values * values, axis=-1, keepdims=True)
    return values * lax.rsqrt(mean_square + NORM_EPS) * gain


def contract_rows(left_side, right_side):
    return lax.dot_general(
        left_side, right_side, (((0,), (0,)), ((), ())), preferred_element_type=f32
    )


def contract_cols(left_side, right_side):
    return lax.dot_general(
        left_side, right_side, (((1,), (1,)), ((), ())), preferred_element_type=f32
    )


def gather(x, axes):
    return lax.all_gather(x, axes, axis=0, tiled=True)


def scatter_sum(x, axes):
    return lax.psum_scatter(x, axes, scatter_dimension=0, tiled=True)


def pad_lanes(x, lanes):
    return jnp.pad(x, ((0, 0), (0, lanes - x.shape[1])))


def line_pairs(n, step):
    return [(i, i + step) for i in range(n) if 0 <= i + step < n]


def line_gather(x, axis):
    n = lax.axis_size(axis)
    pieces = [(0, x)]
    up = down = x
    for k in range(1, n):
        up = lax.ppermute(up, axis, line_pairs(n, 1))
        down = lax.ppermute(down, axis, line_pairs(n, -1))
        pieces += [(-k, up), (k, down)]
    return pieces


def by_columns(own, other, member):
    first, second = jnp.where(member == 0, own, other), jnp.where(member == 0, other, own)
    return jnp.stack([first, second], axis=1)


def neighbours(x):
    return lax.ppermute(x, "y", SWAP), lax.ppermute(x, "b", SWAP)


def plane_gather(x, from_y, from_b):
    half = x.shape[0] // 2
    upper = lax.ppermute(from_b[:half], "y", SWAP)
    lower = lax.ppermute(from_y[half:], "b", SWAP)
    return [(block, lax.ppermute(block, "c", SWAP)) for block in (x, from_y, from_b, upper, lower)]


def halve_send(v, axis, at):
    me = lax.axis_index(axis)
    other = lax.ppermute(lax.dynamic_index_in_dim(v, 1 - me, at, False), axis, SWAP)
    return lax.dynamic_index_in_dim(v, me, at, False), other


def halve_add(terms):
    own, other = terms
    return (own.astype(f32) + other.astype(f32)).astype(own.dtype)


def rotate_lanes(x, cos, sin):
    width = x.shape[-1]
    lane = lax.broadcasted_iota(jnp.int32, x.shape, x.ndim - 1)
    swapped = jnp.where(
        lane % HEAD_SIZE < HEAD_SIZE // 2,
        pltpu.roll(x, width - HEAD_SIZE // 2, x.ndim - 1),
        pltpu.roll(x, HEAD_SIZE // 2, x.ndim - 1),
    )
    return x * cos + swapped * sin


def spread_tables(cos, sin):
    return jnp.concatenate([cos] * 4, axis=1), jnp.concatenate([-sin, sin, -sin, sin], axis=1)


def key_tables(cos, sin):
    low = lower_lanes(cos.shape)
    return jnp.where(low, cos, 1.0), jnp.where(low, sin, 0.0)


def project_kernel(places, spots, place_ref, *refs):
    count = 1 if places is None else len(places)
    blocks, refs = refs[:count], refs[count:]
    count = 1 if spots is None else len(spots)
    weights, refs = refs[:count], refs[count:]
    cos_ref, sin_ref, q_ref, kv_ref, x_ref, w_ref, gain, held, sems = refs
    i = pl.program_id(0)
    slots, _, width = held.shape
    heads = q_ref.shape[1] // PAIR

    @pl.when(i == 0)
    def _():
        copies = []
        if spots is None:
            copies.append(pltpu.make_async_copy(weights[0], w_ref, sems.at[slots]))
        else:
            for at, ((y, c), block) in enumerate(zip(spots, weights)):
                row = 2 * (place_ref[2] ^ y) + (place_ref[3] ^ c)
                copies.append(
                    pltpu.make_async_copy(block, w_ref.at[:, row], sems.at[slots + at])
                )
        for copy in copies:
            copy.start()
        if places is None:
            for slot in range(slots):
                pltpu.make_async_copy(blocks[0].at[slot], held.at[slot], sems.at[slot]).start()
        else:
            for distance, block in zip(places, blocks):
                slot = place_ref[0] + distance

                @pl.when((slot >= 0) & (slot < slots))
                def _(block=block, slot=slot):
                    pltpu.make_async_copy(block, held.at[slot], sems.at[slot]).start()

        for copy in copies:
            copy.wait()
        small = w_ref[..., heads * HEAD_PACK :].reshape(width, LANES)
        gain[...] = jnp.transpose(small.astype(f32))[:8, :]

    arrived = blocks[0].at[0] if places is None else blocks[0]
    pltpu.make_async_copy(arrived, held.at[i], sems.at[i]).wait()
    x = held[i]
    x_ref[...] = x
    normed = rms_scale(x.astype(f32), gain[0:1, :]).astype(bf16)
    w = w_ref[..., : heads * HEAD_PACK].reshape(width, heads * HEAD_PACK)
    pre = jnp.dot(normed, w, preferred_element_type=f32)
    cos, sin = spread_tables(cos_ref[...], sin_ref[...])
    key_cos, key_sin = key_tables(cos, sin)
    for h in range(heads):
        out, at = slice(h * PAIR, (h + 1) * PAIR), h * HEAD_PACK
        q_ref[:, out] = rotate_lanes(pre[:, at : at + PAIR], cos, sin).astype(bf16)
        kv_ref[:, out] = rotate_lanes(
            pre[:, at + PAIR : at + HEAD_PACK], key_cos, key_sin
        ).astype(bf16)


def project(place, places, blocks, spots, weights, rows, width, cos, sin):
    span = cos.shape[0]
    cols = weights[0].shape[-1]
    heads = (cols - LANES) // HEAD_PACK
    table = pl.BlockSpec((rows, HEAD_SIZE // 2), lambda i, h: (i, 0))
    token_rows = pl.BlockSpec((rows, width), lambda i, h: (i, 0))
    head_rows = pl.BlockSpec((rows, heads * PAIR), lambda i, h: (i, 0))
    shape = weights[0].shape if spots is None else (
        weights[0].shape[0], len(spots), weights[0].shape[1], cols
    )
    return pl.pallas_call(
        functools.partial(project_kernel, places, spots),
        grid_spec=pltpu.PrefetchScalarGridSpec(
            num_scalar_prefetch=1,
            grid=(span // rows,),
            in_specs=[pl.BlockSpec(memory_space=pl.ANY)] * (len(blocks) + len(weights))
            + [table, table],
            out_specs=[
                head_rows,
                head_rows,
                token_rows,
                pl.BlockSpec(shape, lambda i, h: (0,) * len(shape)),
            ],
            scratch_shapes=[
                pltpu.VMEM((8, width), f32),
                pltpu.VMEM((span // rows, rows, width), bf16),
                pltpu.SemaphoreType.DMA((span // rows + len(weights),)),
            ],
        ),
        out_shape=[
            jax.ShapeDtypeStruct((span, heads * PAIR), bf16),
            jax.ShapeDtypeStruct((span, heads * PAIR), bf16),
            jax.ShapeDtypeStruct((span, width), bf16),
            jax.ShapeDtypeStruct(shape, bf16),
        ],
        compiler_params=pltpu.CompilerParams(vmem_limit_bytes=VMEM_LIMIT),
        cost_estimate=pl.CostEstimate(
            flops=2 * span * width * heads * HEAD_PACK, bytes_accessed=8 * 2**20, transcendentals=0
        ),
        name="project",
    )(place, *blocks, *weights, cos, sin)


def spread_kernel(cos_ref, sin_ref, wide_cos_ref, wide_sin_ref):
    wide_cos_ref[...], wide_sin_ref[...] = spread_tables(cos_ref[...], sin_ref[...])


def spread(cos, sin):
    rows = cos.shape[0]
    wide = jax.ShapeDtypeStruct((rows, PAIR), f32)
    return pl.pallas_call(
        spread_kernel,
        grid=(4,),
        in_specs=[pl.BlockSpec((rows // 4, HEAD_SIZE // 2), lambda i: (i, 0))] * 2,
        out_specs=[pl.BlockSpec((rows // 4, PAIR), lambda i: (i, 0))] * 2,
        out_shape=[wide, wide],
        cost_estimate=pl.CostEstimate(flops=2**20, bytes_accessed=4 * 2**20, transcendentals=0),
        name="spread",
    )(cos, sin)


def head_grads_kernel(place_ref, own_ref, other_ref, w_ref, small_ref, grad_ref, out_ref, acc, sums, gain):
    i = pl.program_id(0)
    half = pl.num_programs(0) // 2

    @pl.when(i == 0)
    def _():
        acc[...] = jnp.zeros_like(acc)
        sums[...] = jnp.zeros_like(sums)
        gain[...] = jnp.transpose(small_ref[...].astype(f32))[:8, :]

    grad = grad_ref[...]
    x = jnp.where(i < half, own_ref[...], other_ref[...]).astype(f32)
    inverse = lax.rsqrt(jnp.mean(x * x, axis=-1, keepdims=True) + NORM_EPS)
    x = x * inverse
    acc[...] += contract_rows(grad, (x * gain[0:1, :]).astype(bf16))
    back = contract_cols(grad, w_ref[...]) * x
    sums[...] += jnp.sum(back.reshape(back.shape[0] // 8, 8, back.shape[1]), axis=0)

    @pl.when(i == pl.num_programs(0) - 1)
    def _():
        out_ref[:, :HEAD_PACK] = jnp.transpose(acc[...]).astype(bf16)
        total = jnp.sum(sums[...], axis=0, keepdims=True)
        rows = lax.broadcasted_iota(jnp.int32, (LANES, total.shape[1]), 0)
        out_ref[:, HEAD_PACK:] = jnp.transpose(
            jnp.where(rows == 0, jnp.broadcast_to(total, rows.shape), 0.0)
        ).astype(bf16)


def head_grads(own, other, first, second, stride, head_at, weights, grads):
    span, pack = grads.shape
    width = own.shape[1]
    rows = BLOCK
    half = span // rows // 2
    small_at = weights.shape[1] // LANES - 1

    def grads_at(i, s):
        return (jnp.where(i < half, s[0] + stride * i, s[1] + stride * (i - half)), 0)

    return pl.pallas_call(
        head_grads_kernel,
        grid_spec=pltpu.PrefetchScalarGridSpec(
            num_scalar_prefetch=1,
            grid=(span // rows,),
            in_specs=[
                pl.BlockSpec((rows, width), lambda i, s: (jnp.minimum(i, half - 1), 0)),
                pl.BlockSpec((rows, width), lambda i, s: (jnp.maximum(i - half, 0), 0)),
                pl.BlockSpec((width, pack), lambda i, s: (0, s[2])),
                pl.BlockSpec((width, LANES), lambda i, s: (0, small_at)),
                pl.BlockSpec((rows, pack), grads_at),
            ],
            out_specs=pl.BlockSpec((width, pack + LANES), lambda i, s: (0, 0)),
            scratch_shapes=[
                pltpu.VMEM((pack, width), f32),
                pltpu.VMEM((8, width), f32),
                pltpu.VMEM((8, width), f32),
            ],
        ),
        out_shape=jax.ShapeDtypeStruct((width, pack + LANES), bf16),
        compiler_params=pltpu.CompilerParams(vmem_limit_bytes=VMEM_LIMIT),
        cost_estimate=pl.CostEstimate(
            flops=4 * span * width * pack, bytes_accessed=8 * 2**20, transcendentals=0
        ),
        name="head_grads",
    )(jnp.stack([first, second, head_at]), own, other, weights, weights, grads)


def lower_lanes(shape):
    return lax.broadcasted_iota(jnp.int32, shape, len(shape) - 1) < HEAD_SIZE


def both_heads_low(pair):
    low = lower_lanes(pair.shape)
    return jnp.concatenate(
        [jnp.where(low, pair, 0.0), jnp.where(low, pltpu.roll(pair, HEAD_SIZE, 1), 0.0)], axis=0
    )


def both_heads_high(pair):
    low = lower_lanes(pair.shape)
    return jnp.concatenate(
        [jnp.where(low, 0.0, pltpu.roll(pair, HEAD_SIZE, 1)), jnp.where(low, 0.0, pair)], axis=0
    )


def block_bounds(bounds_ref, tile, tiles, stride):
    place = bounds_ref[2 * tiles] + stride * (QUERY_BLOCK // BLOCK) * tile
    full = jnp.minimum(bounds_ref[tiles + tile], place)
    return place, bounds_ref[tile], full, place + stride * (QUERY_BLOCK // BLOCK - 1) + 1


def pair_mask(doc, place, stride):
    doc = jnp.concatenate([doc, doc], axis=1)
    lane = lax.broadcasted_iota(jnp.int32, doc.shape, 1) % QUERY_BLOCK
    queries = (place + stride * (lane // BLOCK)) * BLOCK + lane % BLOCK

    def masked(scores, start):
        keys = lax.broadcasted_iota(jnp.int32, scores.shape, 0) + start
        return jnp.where((keys >= doc) & (keys <= queries), scores, NEGATIVE_HUGE)

    return masked


def attend_kernel(stride, bounds_ref, q_ref, kv_ref, doc_ref, o_ref, low_ref, lse_ref, acc):
    place, first, full, end = block_bounds(
        bounds_ref, pl.program_id(1), pl.num_programs(1), stride
    )
    q = both_heads_low(q_ref[...].astype(f32) * SCALE_OF_SCORES).astype(bf16)
    masked = pair_mask(doc_ref[0], place, stride)
    acc[...] = jnp.zeros_like(acc)

    def step(mask, j, carried):
        top, total = carried
        start = pl.multiple_of(j * BLOCK, BLOCK)
        kv = kv_ref[pl.ds(start, BLOCK), :]
        scores = contract_cols(kv, q)
        if mask:
            scores = masked(scores, start)
        new = jnp.maximum(top, jnp.max(scores, axis=0, keepdims=True))
        probs = jnp.exp(scores - new)
        keep = jnp.exp(top - new)
        acc[...] = acc[...] * keep + contract_rows(kv, probs.astype(bf16))
        return new, total * keep + jnp.sum(probs, axis=0, keepdims=True)

    row = (1, 2 * QUERY_BLOCK)
    carried = (jnp.full(row, NEGATIVE_HUGE, f32), jnp.zeros(row, f32))
    carried = lax.fori_loop(first, full, functools.partial(step, True), carried)
    carried = lax.fori_loop(full, place, functools.partial(step, False), carried)
    top, total = lax.fori_loop(place, end, functools.partial(step, True), carried)
    mixed = jnp.transpose(acc[...] / total)
    one, two = mixed[:QUERY_BLOCK], mixed[QUERY_BLOCK:]
    out = jnp.where(lower_lanes(one.shape), pltpu.roll(one, HEAD_SIZE, 1), two)
    o_ref[...] = out
    low_ref[...] = out.astype(bf16)
    lse_ref[0, 0] = top + jnp.log(total)


def attend(bounds, q, kv, doc, stride):
    (queries, cols), keys = q.shape, kv.shape[0]
    heads, tiles = cols // PAIR, queries // QUERY_BLOCK
    pair = pl.BlockSpec((QUERY_BLOCK, PAIR), lambda h, i, s: (i, h))
    return pl.pallas_call(
        functools.partial(attend_kernel, stride),
        grid_spec=pltpu.PrefetchScalarGridSpec(
            num_scalar_prefetch=1,
            grid=(heads, tiles),
            in_specs=[
                pair,
                pl.BlockSpec((keys, PAIR), lambda h, i, s: (0, h)),
                pl.BlockSpec((1, 1, QUERY_BLOCK), lambda h, i, s: (i, 0, 0)),
            ],
            out_specs=[
                pair,
                pair,
                pl.BlockSpec((1, 1, 1, 2 * QUERY_BLOCK), lambda h, i, s: (h, i, 0, 0)),
            ],
            scratch_shapes=[pltpu.VMEM((PAIR, 2 * QUERY_BLOCK), f32)],
        ),
        out_shape=[
            jax.ShapeDtypeStruct((queries, cols), f32),
            jax.ShapeDtypeStruct((queries, cols), bf16),
            jax.ShapeDtypeStruct((heads, tiles, 1, 2 * QUERY_BLOCK), f32),
        ],
        compiler_params=pltpu.CompilerParams(vmem_limit_bytes=VMEM_LIMIT),
        cost_estimate=pl.CostEstimate(
            flops=4 * queries * keys * cols,
            bytes_accessed=6 * 2**20,
            transcendentals=queries * keys * heads,
        ),
        name="attend",
    )(bounds, q, kv, doc)


def attend_back_kernel(
    fold, bounds_ref, q_ref, kv_ref, doc_ref, do_ref, o_ref, lse_ref, cos_ref, sin_ref, *refs
):
    if fold:
        out_ref, acc, dkv_ref = refs
    else:
        dq_ref, dkv_ref, acc = refs
    i = pl.program_id(0)
    place, first, full, end = block_bounds(bounds_ref, i, pl.num_programs(0), 1)

    @pl.when(i == 0)
    def _():
        dkv_ref[...] = jnp.zeros_like(dkv_ref)

    q = both_heads_low(q_ref[...].astype(f32) * SCALE_OF_SCORES).astype(bf16)
    grad = do_ref[...].astype(f32)
    product = jnp.transpose(grad * o_ref[...])
    delta = jnp.concatenate(
        [
            jnp.sum(product[:HEAD_SIZE], axis=0, keepdims=True),
            jnp.sum(product[HEAD_SIZE:], axis=0, keepdims=True),
        ],
        axis=1,
    )
    grad = both_heads_high(grad).astype(bf16)
    sources = jnp.concatenate([q, grad], axis=0)
    masked = pair_mask(doc_ref[0], place, 1)
    lse = lse_ref[0]
    acc[...] = jnp.zeros_like(acc)

    def step(mask, j, carried):
        start = pl.multiple_of(j * BLOCK, BLOCK)
        kv = kv_ref[pl.ds(start, BLOCK), :]
        scores = contract_cols(kv, q) - lse
        if mask:
            scores = masked(scores, start)
        probs = jnp.exp(scores)
        grad_scores = (probs * (contract_cols(kv, grad) - delta)).astype(bf16)
        acc[...] += contract_rows(kv, grad_scores)
        both = jnp.concatenate([grad_scores, probs.astype(bf16)], axis=1)
        dkv_ref[pl.ds(start, BLOCK), :] += jnp.dot(both, sources, preferred_element_type=f32)
        return carried

    lax.fori_loop(first, full, functools.partial(step, True), 0)
    lax.fori_loop(full, place, functools.partial(step, False), 0)
    lax.fori_loop(place, end, functools.partial(step, True), 0)
    dq = jnp.transpose(acc[...])
    one, two = dq[:QUERY_BLOCK], dq[QUERY_BLOCK:]
    dq = jnp.where(lower_lanes(one.shape), one, pltpu.roll(two, HEAD_SIZE, 1))
    if not fold:
        dq_ref[...] = dq
        return
    mine = pl.ds(pl.multiple_of(i * QUERY_BLOCK, QUERY_BLOCK), QUERY_BLOCK)
    out_ref[mine, :PAIR] = rotate_lanes(
        dq * SCALE_OF_SCORES, cos_ref[mine, :], -sin_ref[mine, :]
    ).astype(bf16)

    @pl.when(i == pl.num_programs(0) - 1)
    def _():
        def finish(j, carried):
            part = pl.ds(pl.multiple_of(j * BLOCK, BLOCK), BLOCK)
            cos, sin = key_tables(cos_ref[part, :], sin_ref[part, :])
            out_ref[part, PAIR:] = rotate_lanes(dkv_ref[part, :], cos, -sin).astype(bf16)
            return carried

        lax.fori_loop(0, dkv_ref.shape[0] // BLOCK, finish, 0)


def attend_back(bounds, q, kv, doc, grad, out, lse, cos, sin, fold):
    queries, keys = q.shape[0], kv.shape[0]
    steps = queries // QUERY_BLOCK
    pair = pl.BlockSpec((QUERY_BLOCK, PAIR), lambda i, s: (i, 0))
    whole = pl.BlockSpec((keys, PAIR), lambda i, s: (0, s[2 * steps + 1]))
    doc_row = pl.BlockSpec((1, 1, QUERY_BLOCK), lambda i, s: (i, 0, 0))
    lse_row = pl.BlockSpec((1, 1, 2 * QUERY_BLOCK), lambda i, s: (i, 0, 0))
    table = pl.BlockSpec(cos.shape, lambda i, s: (0, 0))
    acc = pltpu.VMEM((PAIR, 2 * QUERY_BLOCK), f32)
    if fold:
        out_specs = pl.BlockSpec((queries, HEAD_PACK), lambda i, s: (0, 0))
        out_shape = jax.ShapeDtypeStruct((queries, HEAD_PACK), bf16)
        scratch = [acc, pltpu.VMEM((keys, PAIR), f32)]
    else:
        out_specs = [pair, pl.BlockSpec((keys, PAIR), lambda i, s: (0, 0))]
        out_shape = [
            jax.ShapeDtypeStruct((queries, PAIR), f32),
            jax.ShapeDtypeStruct((keys, PAIR), f32),
        ]
        scratch = [acc]
    return pl.pallas_call(
        functools.partial(attend_back_kernel, fold),
        grid_spec=pltpu.PrefetchScalarGridSpec(
            num_scalar_prefetch=1,
            grid=(steps,),
            in_specs=[pair, whole, doc_row, pair, pair, lse_row, table, table],
            out_specs=out_specs,
            scratch_shapes=scratch,
        ),
        out_shape=out_shape,
        compiler_params=pltpu.CompilerParams(vmem_limit_bytes=VMEM_LIMIT),
        cost_estimate=pl.CostEstimate(
            flops=10 * queries * keys * PAIR,
            bytes_accessed=8 * 2**20,
            transcendentals=queries * keys,
        ),
        name="attend_back",
    )(bounds, q, kv, doc, grad, out, lse, cos, sin)


def unrotate_kernel(dq_ref, dkv_ref, cos_ref, sin_ref, out_ref):
    cos, sin = cos_ref[...], sin_ref[...]
    dq = rotate_lanes(dq_ref[...] * SCALE_OF_SCORES, cos, -sin)
    cos, sin = key_tables(cos, sin)
    dkv = rotate_lanes(dkv_ref[...], cos, -sin)
    out_ref[...] = jnp.concatenate([dq, dkv], axis=1).astype(bf16)


def unrotate(dq, dkv, cos, sin):
    rows = dq.shape[0]
    pair = pl.BlockSpec((BLOCK, PAIR), lambda i: (i, 0))
    return pl.pallas_call(
        unrotate_kernel,
        grid=(rows // BLOCK,),
        in_specs=[pair, pair, pair, pair],
        out_specs=pl.BlockSpec((BLOCK, HEAD_PACK), lambda i: (i, 0)),
        out_shape=jax.ShapeDtypeStruct((rows, HEAD_PACK), bf16),
        cost_estimate=pl.CostEstimate(
            flops=rows * HEAD_PACK * 8, bytes_accessed=rows * HEAD_PACK * 14, transcendentals=0
        ),
        name="unrotate",
    )(dq, dkv, cos, sin)


def place_experts_kernel(place_ref, *refs):
    blocks, (ct_ref, w_ref, z_ref, sems) = refs[:10], refs[10:]
    core = place_ref[1]
    rows = w_ref.shape[1] // 2
    half = rows // 2
    sources = [[(0, 0, rows)], [(1, 0, rows)], [(2, 0, rows)], [(3, 0, half), (4, half, half)]]
    for step, parts in enumerate(sources):

        @pl.when(pl.program_id(0) == step)
        def _(parts=parts):
            copies = []
            for source, start, length in parts:
                for other in (0, 1):
                    first = jnp.where(core == other, 0, rows) + start
                    at = pl.ds(pl.multiple_of(first, half), length)
                    copies.append(
                        pltpu.make_async_copy(
                            blocks[2 * source + other], w_ref.at[0, at, :], sems.at[len(copies)]
                        )
                    )
            for copy in copies:
                copy.start()
            for copy in copies:
                copy.wait()

    z_ref[0] = jnp.dot(ct_ref[...], w_ref[0, :, 2 * F :], preferred_element_type=f32)


def place_experts(place, parts, early, width):
    rows = early.shape[0]
    blocks = [block for pair in parts for block in pair]
    return pl.pallas_call(
        place_experts_kernel,
        grid_spec=pltpu.PrefetchScalarGridSpec(
            num_scalar_prefetch=1,
            grid=(EXPERTS_HERE,),
            in_specs=[pl.BlockSpec(memory_space=pl.ANY)] * len(blocks)
            + [pl.BlockSpec((rows, width), lambda r, s: (0, 0))],
            out_specs=[
                pl.BlockSpec((1, width, 3 * F), lambda r, s: (s[0] ^ r, 0, 0)),
                pl.BlockSpec((1, rows, F), lambda r, s: (s[0] ^ r, 0, 0)),
            ],
            scratch_shapes=[pltpu.SemaphoreType.DMA((4,))],
        ),
        out_shape=[
            jax.ShapeDtypeStruct((EXPERTS_HERE, width, 3 * F), bf16),
            jax.ShapeDtypeStruct((EXPERTS_HERE, rows, F), f32),
        ],
        compiler_params=pltpu.CompilerParams(vmem_limit_bytes=VMEM_LIMIT),
        cost_estimate=pl.CostEstimate(
            flops=2 * EXPERTS_HERE * rows * width * F, bytes_accessed=36 * 2**20, transcendentals=0
        ),
        name="place_experts",
    )(place, *blocks, early)


def lane_column(x, at):
    lane = lax.broadcasted_iota(jnp.int32, x.shape, 1)
    return jnp.sum(jnp.where(lane == at, x, 0.0), axis=1, keepdims=True)


def experts_kernel(
    group_ref, n_ref, routed_ref, router_ref, w_ref, z_ref,
    back_ref, gates_ref, hidden_ref, pre_ref, acc, dots,
):
    e = pl.program_id(0)
    own = group_ref[0] * EXPERTS_HERE + e
    rows = n_ref.shape[0]

    @pl.when(e == 0)
    def _():
        logits = jnp.dot(n_ref[...], router_ref[...], preferred_element_type=f32)
        routed = routed_ref[...].astype(f32) > 0.5
        highest = jnp.max(jnp.where(routed, logits, NEGATIVE_HUGE), axis=1, keepdims=True)
        weights = jnp.where(routed, jnp.exp(jnp.where(routed, logits - highest, 0.0)), 0.0)
        gates_ref[...] = weights / jnp.sum(weights, axis=1, keepdims=True)
        acc[...] = jnp.zeros_like(acc)
        dots[...] = jnp.zeros_like(dots)

    w_in = w_ref[0, :, : 2 * F]
    for t in range(rows // BLOCK):
        part = pl.ds(t * BLOCK, BLOCK)
        pre = jnp.dot(n_ref[part, :], w_in, preferred_element_type=f32)
        gate, up = pre[:, :F], pre[:, F:]
        z = z_ref[0, part, :]
        weight = lane_column(gates_ref[part, :], own)
        sig = 1.0 / (1.0 + jnp.exp(-gate))
        act = gate * sig
        hidden = act * up
        hidden_ref[0, part, :] = (weight * hidden).astype(bf16)
        dot = RESIDUAL_SCALE * jnp.sum(hidden.astype(bf16).astype(f32) * z, axis=1, keepdims=True)
        lane = lax.broadcasted_iota(jnp.int32, (BLOCK, LANES), 1)
        dots[part, :] += jnp.where(lane == own, dot, 0.0)
        scaled = (RESIDUAL_SCALE * weight) * z
        pre_ref[0, part, :F] = (scaled * up * (sig + act * (1.0 - sig))).astype(bf16)
        pre_ref[0, part, F:] = (scaled * act).astype(bf16)
        acc[part, :] += contract_cols(pre_ref[0, part, :], w_in)

    @pl.when(e == EXPERTS_HERE - 1)
    def _():
        width = n_ref.shape[1]
        back_ref[:, :width] = acc[...].astype(bf16)
        high = dots[...].astype(bf16)
        low = dots[...] - high.astype(f32)
        back_ref[:, width:] = (high.astype(f32) + pltpu.roll(low, E, 1)).astype(bf16)


def experts(group, normed, early, packed, w_all, z):
    rows, width = normed.shape
    count = w_all.shape[0]
    whole = pl.BlockSpec((rows, width), lambda e, g: (0, 0))
    column = width // LANES
    router_at = packed.shape[1] // LANES - 1
    return pl.pallas_call(
        experts_kernel,
        grid_spec=pltpu.PrefetchScalarGridSpec(
            num_scalar_prefetch=1,
            grid=(count,),
            in_specs=[
                whole,
                pl.BlockSpec((rows, LANES), lambda e, g: (0, column)),
                pl.BlockSpec((width, LANES), lambda e, g: (0, router_at)),
                pl.BlockSpec((1, width, 3 * F), lambda e, g: (e, 0, 0)),
                pl.BlockSpec((1, rows, F), lambda e, g: (e, 0, 0)),
            ],
            out_specs=[
                pl.BlockSpec((rows, width + LANES), lambda e, g: (0, 0)),
                pl.BlockSpec((rows, LANES), lambda e, g: (0, 0)),
                pl.BlockSpec((1, rows, F), lambda e, g: (e, 0, 0)),
                pl.BlockSpec((1, rows, 2 * F), lambda e, g: (e, 0, 0)),
            ],
            scratch_shapes=[pltpu.VMEM((rows, width), f32), pltpu.VMEM((rows, LANES), f32)],
        ),
        out_shape=[
            jax.ShapeDtypeStruct((rows, width + LANES), bf16),
            jax.ShapeDtypeStruct((rows, LANES), f32),
            jax.ShapeDtypeStruct((count, rows, F), bf16),
            jax.ShapeDtypeStruct((count, rows, 2 * F), bf16),
        ],
        compiler_params=pltpu.CompilerParams(vmem_limit_bytes=VMEM_LIMIT),
        cost_estimate=pl.CostEstimate(
            flops=2 * count * rows * width * 4 * F, bytes_accessed=40 * 2**20, transcendentals=0
        ),
        name="experts",
    )(group, normed, early, packed, w_all, z)


def expert_grads_kernel(half_ref, n_ref, ct_ref, w_ref, hidden_ref, pre_ref, y_ref, *refs):
    grad_refs, (n_t, ct_t, acc) = refs[:-3], refs[-3:]
    e = pl.program_id(0)

    @pl.when(e == 0)
    def _():
        n_t[...] = jnp.transpose(n_ref[...])
        ct_t[...] = jnp.transpose(ct_ref[...])
        acc[...] = jnp.zeros_like(acc)

    for part in range(len(grad_refs) // 2):
        left_ref, right_ref = grad_refs[2 * part : 2 * part + 2]
        rows, cut = left_ref.shape[1:]
        at = pl.ds(pl.multiple_of((half_ref[0] ^ part) * rows, rows), rows)
        grads = jnp.dot(n_t[at, :], pre_ref[0], preferred_element_type=f32).astype(bf16)
        left_ref[0] = grads[:, :cut]
        right_ref[0, :, : 2 * F - cut] = grads[:, cut:]
        right_ref[0, :, 2 * F - cut :] = (
            RESIDUAL_SCALE * jnp.dot(ct_t[at, :], hidden_ref[0], preferred_element_type=f32)
        ).astype(bf16)
    acc[...] += contract_cols(hidden_ref[0], w_ref[0, :, 2 * F :])

    @pl.when(e == pl.num_programs(0) - 1)
    def _():
        y_ref[...] = acc[...].astype(bf16)


def expert_grads(half, parts, normed, early, w_all, hidden, pre):
    rows, width = normed.shape
    count = w_all.shape[0]
    own, cut = width // parts, 3 * F // 2
    whole = pl.BlockSpec((rows, width), lambda e, h: (0, 0))
    return pl.pallas_call(
        expert_grads_kernel,
        grid_spec=pltpu.PrefetchScalarGridSpec(
            num_scalar_prefetch=1,
            grid=(count,),
            in_specs=[
                whole,
                whole,
                pl.BlockSpec((1, width, 3 * F), lambda e, h: (e, 0, 0)),
                pl.BlockSpec((1, rows, F), lambda e, h: (e, 0, 0)),
                pl.BlockSpec((1, rows, 2 * F), lambda e, h: (e, 0, 0)),
            ],
            out_specs=[whole] + [pl.BlockSpec((1, own, cut), lambda e, h: (e, 0, 0))] * (2 * parts),
            scratch_shapes=[
                pltpu.VMEM((width, rows), bf16),
                pltpu.VMEM((width, rows), bf16),
                pltpu.VMEM((rows, width), f32),
            ],
        ),
        out_shape=[jax.ShapeDtypeStruct((rows, width), bf16)]
        + [jax.ShapeDtypeStruct((count, own, cut), bf16)] * (2 * parts),
        compiler_params=pltpu.CompilerParams(vmem_limit_bytes=VMEM_LIMIT),
        cost_estimate=pl.CostEstimate(
            flops=2 * count * rows * width * 4 * F, bytes_accessed=40 * 2**20, transcendentals=0
        ),
        name="expert_grads",
    )(half, normed, early, w_all, hidden, pre)


def join_kernel(place_ref, o_ref, w_ref, small_ref, x_ref, normed_ref, resid_ref, own_ref, gain):
    t = pl.program_id(0)

    @pl.when(t == 0)
    def _():
        gain[...] = jnp.transpose(small_ref[...].astype(f32))[E : E + 8, :]

    attended = jnp.concatenate([o_ref[a] for a in range(o_ref.shape[0])], axis=1)
    resid = x_ref[...].astype(f32) + RESIDUAL_SCALE * jnp.dot(
        attended, w_ref[...], preferred_element_type=f32
    )
    normed_ref[...] = rms_scale(resid, gain[1:2, :]).astype(bf16)

    @pl.when(t == place_ref[0])
    def _():
        resid_ref[...] = resid
        own_ref[...] = attended


def join(place, outs, packed, weights_at, x):
    width = packed.shape[0]
    lines, tokens, cols = outs.shape
    rows = tokens // lines
    small_at = packed.shape[1] // LANES - 1
    own = pl.BlockSpec((rows, width), lambda t, s: (0, 0))
    return pl.pallas_call(
        join_kernel,
        grid_spec=pltpu.PrefetchScalarGridSpec(
            num_scalar_prefetch=1,
            grid=(lines,),
            in_specs=[
                pl.BlockSpec((lines, rows, cols), lambda t, s: (0, t, 0)),
                pl.BlockSpec((width, width), lambda t, s: (0, weights_at)),
                pl.BlockSpec((width, LANES), lambda t, s: (0, small_at)),
                pl.BlockSpec((rows, width), lambda t, s: (t, 0)),
            ],
            out_specs=[pl.BlockSpec((rows, width), lambda t, s: (t, 0)), own, own],
            scratch_shapes=[pltpu.VMEM((8, width), f32)],
        ),
        out_shape=[
            jax.ShapeDtypeStruct((lines * rows, width), bf16),
            jax.ShapeDtypeStruct((rows, width), f32),
            jax.ShapeDtypeStruct((rows, width), bf16),
        ],
        compiler_params=pltpu.CompilerParams(vmem_limit_bytes=VMEM_LIMIT),
        cost_estimate=pl.CostEstimate(
            flops=2 * lines * rows * width * width, bytes_accessed=12 * 2**20, transcendentals=0
        ),
        name="join",
    )(place, outs, packed, packed, x)


def token_grads_kernel(grad_ref, w_ref, small_ref, x_ref, resid_ref, out_ref, acc):
    h = pl.program_id(0)
    part = contract_cols(grad_ref[0], w_ref[...])

    @pl.when(h == 0)
    def _():
        acc[...] = part

    @pl.when(h > 0)
    def _():
        acc[...] += part

    @pl.when(h == pl.num_programs(0) - 1)
    def _():
        gain = jnp.transpose(small_ref[...].astype(f32))[E : E + 1, :]
        x = x_ref[...].astype(f32)
        inverse = lax.rsqrt(jnp.mean(x * x, axis=-1, keepdims=True) + NORM_EPS)
        scaled = acc[...] * gain
        mean = jnp.mean(x * scaled, axis=-1, keepdims=True)
        out_ref[...] = resid_ref[...] + (inverse * scaled - x * inverse**3 * mean)


def token_grads(grads, packed, x, resid):
    heads, rows, pack = grads.shape
    width = x.shape[1]
    small_at = packed.shape[1] // LANES - 1
    whole = pl.BlockSpec((rows, width), lambda h: (0, 0))
    return pl.pallas_call(
        token_grads_kernel,
        grid=(heads,),
        in_specs=[
            pl.BlockSpec((1, rows, pack), lambda h: (h, 0, 0)),
            pl.BlockSpec((width, pack), lambda h: (0, h)),
            pl.BlockSpec((width, LANES), lambda h: (0, small_at)),
            whole,
            whole,
        ],
        out_specs=whole,
        out_shape=jax.ShapeDtypeStruct((rows, width), f32),
        scratch_shapes=[pltpu.VMEM((rows, width), f32)],
        compiler_params=pltpu.CompilerParams(vmem_limit_bytes=VMEM_LIMIT),
        cost_estimate=pl.CostEstimate(
            flops=2 * rows * width * heads * pack, bytes_accessed=8 * 2**20, transcendentals=0
        ),
        name="token_grads",
    )(grads, packed, packed, x, resid)


def weight_sums_kernel(sums_ref, q_ref, k_ref, v_ref, gain_ref):
    groups, heads, members = sums_ref.shape[:3]
    gain = jnp.zeros(gain_ref.shape, f32)
    values = []
    for h in range(heads):
        total = jnp.zeros(sums_ref.shape[3:], f32)
        for g in range(groups):
            for member in range(members):
                total += sums_ref[g, h, member].astype(f32)
        values.append(total)
        gain += total[:, HEAD_PACK:]
        q_ref[:, h * PAIR : (h + 1) * PAIR] = total[:, :PAIR]
    gain_ref[...] = gain
    for h in range(0, heads, 2):
        one, two = values[h][:, PAIR:HEAD_PACK], values[h + 1][:, PAIR:HEAD_PACK]
        low = lower_lanes(one.shape)
        at = slice(h // 2 * PAIR, (h // 2 + 1) * PAIR)
        k_ref[:, at] = jnp.where(low, one, pltpu.roll(two, HEAD_SIZE, 1))
        v_ref[:, at] = jnp.where(low, pltpu.roll(one, HEAD_SIZE, 1), two)


def weight_sums(sums):
    rows, heads = sums.shape[3], sums.shape[1]
    return pl.pallas_call(
        weight_sums_kernel,
        out_shape=[
            jax.ShapeDtypeStruct((rows, heads * PAIR), f32),
            jax.ShapeDtypeStruct((rows, heads * HEAD_SIZE), f32),
            jax.ShapeDtypeStruct((rows, heads * HEAD_SIZE), f32),
            jax.ShapeDtypeStruct((rows, LANES), f32),
        ],
        compiler_params=pltpu.CompilerParams(vmem_limit_bytes=VMEM_LIMIT),
        cost_estimate=pl.CostEstimate(flops=2**20, bytes_accessed=2 * 2**20, transcendentals=0),
        name="weight_sums",
    )(sums)


def exchange(x, axes):
    return lax.all_to_all(x, axes, 0, 0, tiled=True)


def body(
    tokens,
    cotangent,
    segment_ids,
    routes,
    norm_attn,
    w_query,
    key_weight_matrix,
    value_weight_matrix,
    w_output,
    norm_moe,
    w_router,
    expert_in,
    expert_out,
):
    x_local = tokens[0].astype(f32)
    token_count, width = x_local.shape
    seg_row = segment_ids[0]
    group, member = lax.axis_index("a"), lax.axis_index("b")
    by_column = all(lax.axis_size(axis) == 2 for axis in PLANE)
    by_column = by_column and lax.axis_size(SEQ) == KEY_VALUE_HEADS
    head_axes = SEQ if by_column else ("b",)
    span = token_count * KEY_VALUE_HEADS
    span_start = 0 if by_column else group * span

    def start_of_doc(ids):
        return jnp.sum((seg_row[None, :] < ids[:, None]).astype(jnp.int32), axis=1)

    def tile_bounds(docs, place):
        tiles = docs.reshape(-1, QUERY_BLOCK)
        ends = (tiles[:, 0] // BLOCK, (tiles[:, -1] + BLOCK - 1) // BLOCK, jnp.stack(place))
        return jnp.concatenate(ends).astype(jnp.int32), tiles[:, None, :]

    def own_column(x):
        x = x.reshape((GROUPS, 2, token_count) + x.shape[1:])
        x = lax.dynamic_index_in_dim(x, member, 1, False)
        return x.reshape((GROUPS * token_count,) + x.shape[2:])

    doc_span = start_of_doc(lax.dynamic_slice_in_dim(seg_row, span_start, span))
    cos_span, sin_span = rotation_tables(span_start + jnp.arange(span, dtype=jnp.int32) - doc_span)
    zero = jnp.zeros_like(member)
    head_of_two = member if by_column else zero
    bounds, doc_rows = tile_bounds(doc_span, (zero + span_start // BLOCK, head_of_two))
    wide_cos, wide_sin = spread(cos_span, sin_span)
    if by_column:
        cos_ahead, sin_ahead = own_column(cos_span), own_column(sin_span)
        bounds_ahead, docs_ahead = tile_bounds(own_column(doc_span), (member,))
    else:
        cos_ahead, sin_ahead, bounds_ahead, docs_ahead = cos_span, sin_span, bounds, doc_rows

    own_rows = w_query.shape[0]
    by_head = jnp.concatenate(
        [
            w_query.astype(bf16).reshape(own_rows, KEY_VALUE_HEADS, PAIR),
            key_weight_matrix.astype(bf16).reshape(own_rows, KEY_VALUE_HEADS, HEAD_SIZE),
            value_weight_matrix.astype(bf16).reshape(own_rows, KEY_VALUE_HEADS, HEAD_SIZE),
        ],
        axis=2,
    ).reshape(own_rows, KEY_VALUE_HEADS * HEAD_PACK)
    qkv_width = KEY_VALUE_HEADS * HEAD_PACK
    first_all = gather(
        jnp.concatenate(
            [
                by_head,
                w_output.astype(bf16),
                pad_lanes(
                    jnp.concatenate(
                        [
                            w_router.astype(bf16),
                            norm_attn.astype(bf16)[:, None],
                            norm_moe.astype(bf16)[:, None],
                        ],
                        axis=1,
                    ),
                    LANES,
                ),
            ],
            axis=1,
        ),
        ALL,
    )
    experts_low = jnp.concatenate([expert_in.astype(bf16), expert_out.astype(bf16)], axis=1)
    if by_column:
        two = by_head.reshape(own_rows, GROUPS, 2 * HEAD_PACK).transpose(1, 0, 2)
        gains = pad_lanes(norm_attn.astype(bf16)[:, None], LANES)
        gains = jnp.broadcast_to(gains, (GROUPS, own_rows, LANES))
        columns = exchange(jnp.repeat(jnp.concatenate([two, gains], axis=2), 2, axis=0), SEQ)
        from_y = lax.ppermute(columns, "y", SWAP)
        spots = ((0, 0), (0, 1), (1, 0), (1, 1))
        weights = (
            columns, lax.ppermute(columns, "c", SWAP), from_y, lax.ppermute(from_y, "c", SWAP)
        )
        pieces = line_gather(tokens[0], "a")
        places = [piece[0] for piece in pieces]
        blocks = tuple(piece[1] for piece in pieces)
    else:
        at = lax.axis_index(head_axes) * HEAD_PACK
        gain_at = qkv_width + width + E
        gains = pad_lanes(first_all[:, gain_at : gain_at + 1], LANES)
        spots, places = None, None
        weights = (
            jnp.concatenate(
                [lax.dynamic_slice_in_dim(first_all, at, HEAD_PACK, 1), gains], axis=1
            ),
        )
        blocks = (gather(tokens[0], "b").reshape((-1,) + tokens.shape[1:]),)
    experts_low, blocks, weights, cos_ahead, sin_ahead, bounds_ahead, docs_ahead, wide_cos, wide_sin = (
        lax.optimization_barrier(
            (
                experts_low, blocks, weights, cos_ahead, sin_ahead, bounds_ahead, docs_ahead,
                wide_cos, wide_sin,
            )
        )
    )
    output_w = first_all[:, qkv_width : qkv_width + width]
    small_at = qkv_width + width
    router_w = first_all[:, small_at : small_at + E]
    gain_two_f = first_all[:, small_at + E + 1].astype(f32)

    expert_ids = jnp.arange(E, dtype=jnp.int32)
    routed_own = jnp.any(routes[0][:, :, None] == expert_ids[None, None, :], axis=1)
    early = jnp.concatenate([cotangent[0], pad_lanes(routed_own.astype(bf16), LANES)], axis=1)
    early_all = gather(early, "a")
    if by_column:
        beside = neighbours(experts_low)
    else:
        parts = gather(experts_low, PLANE)

    place = jnp.stack([lax.axis_index(axis) for axis in ALL])
    q, kv, x_span, own_weights = project(
        place, places, blocks, spots, weights, token_count, width, cos_ahead, sin_ahead
    )
    own_weights = own_weights.reshape(width, own_weights.shape[-1])
    if by_column:
        columns = (GROUPS, token_count)

        def in_row(own, other, shape):
            return by_columns(own.reshape(shape), other.reshape(shape), member)

        kv_other = lax.ppermute(kv, "b", SWAP)
        kv = in_row(kv, kv_other, columns + (2 * PAIR,)).reshape(span, 2 * PAIR)
    else:
        kv = gather(kv, "a")
    attention_result, attended, log_total = attend(
        bounds_ahead, q, kv, docs_ahead, 2 if by_column else 1
    )
    if by_column:
        attended, first_all = lax.optimization_barrier((attended, first_all))
        attended, early_all = lax.optimization_barrier((attended, early_all))
        outs = lax.all_gather(attended, "a", axis=0, tiled=False)
        parts = plane_gather(experts_low, *beside)

        def heads_apart(x, axis):
            mine = lax.dynamic_index_in_dim(x, member, axis, False)
            return mine, lax.dynamic_index_in_dim(x, 1 - member, axis, False)

        q, q_sent = heads_apart(q.reshape(-1, 2, PAIR), 1)
        attention_result, out_sent = heads_apart(attention_result.reshape(-1, 2, PAIR), 1)
        log_total, log_sent = heads_apart(log_total, 0)
        q_other, out_other, log_other = (
            lax.ppermute(x, "b", SWAP) for x in (q_sent, out_sent, log_sent)
        )
        cut = 2 * token_count
        x_other = [lax.ppermute(x_span[:cut], "b", SWAP)]
        home = jnp.stack([member * 2 + lax.axis_index("y"), lax.axis_index("c")])
        experts_all, grad_hidden = place_experts(home, parts, early_all, width)
        outs, experts_all, x_other[0], q_other, out_other, log_other = lax.optimization_barrier(
            (outs, experts_all, x_other[0], q_other, out_other, log_other)
        )
        normed_all, resid, attended_low = join(place, outs, first_all, qkv_width // width, x_span)
        normed_two = lax.dynamic_slice_in_dim(normed_all, group * token_count, token_count)
    else:
        attended_low = (
            exchange(attended.reshape(KEY_VALUE_HEADS, token_count, PAIR), head_axes)
            .transpose(1, 0, 2)
            .reshape(token_count, QUERY_HEADS * HEAD_SIZE)
        )
        attn_out = jnp.dot(attended_low, output_w, preferred_element_type=f32)
        resid = x_local + RESIDUAL_SCALE * attn_out
        normed_two = rms_scale(resid, gain_two_f).astype(bf16)
        normed_all = gather(normed_two, "a")
        experts_all = parts.reshape(EXPERTS_HERE, width, 3 * F)
        grad_hidden = jnp.einsum(
            "td,edf->etf",
            early_all[:, :width],
            experts_all[:, :, 2 * F :],
            preferred_element_type=f32,
        )
    back_part, gates_all, gated_hidden, grad_pre = experts(
        group.reshape(1), normed_all, early_all, first_all, experts_all, grad_hidden
    )
    if by_column:
        q = in_row(q, q_other, columns + (PAIR,)).reshape(span, PAIR)
        attention_result = in_row(attention_result, out_other, columns + (PAIR,)).reshape(span, PAIR)

        def by_block(x):
            x = x.reshape(-1, 2, QUERY_BLOCK // BLOCK, BLOCK).transpose(0, 2, 1, 3)
            return x.reshape(GROUPS, 2, BLOCK)

        log_total = in_row(by_block(log_total), by_block(log_other), (GROUPS, 2, BLOCK))
        log_total = log_total.transpose(0, 2, 1, 3)
    log_total = log_total.reshape(-1, 1, 2 * QUERY_BLOCK)
    back_own = scatter_sum(back_part, "a")
    inputs = (normed_all, early_all, experts_all, gated_hidden, grad_pre)
    if by_column:
        core = lax.axis_index("c")
        x_other.append(lax.ppermute(x_span[cut:], "b", SWAP))
        moe_part, *keep, send_left, send_right = expert_grads(core.reshape(1), 2, *inputs)
        arrived = [lax.ppermute(x, "c", SWAP) for x in (send_left, send_right)]
        back_own, moe_part, keep = lax.optimization_barrier((back_own, moe_part, keep))
    else:
        moe_part, *grads = expert_grads(jnp.zeros((1,), jnp.int32), 1, *inputs)
        grad_experts = jnp.concatenate(grads, axis=2)
        back_own, moe_part, grad_experts = lax.optimization_barrier(
            (back_own, moe_part, grad_experts)
        )
        grad_experts = scatter_sum(grad_experts.reshape(EXPERTS_HERE * width, 3 * F), PLANE)
    back_own = back_own.astype(f32)
    moe_sum = scatter_sum(moe_part, "a")

    grad_out = cotangent[0].astype(f32)
    gates = lax.dynamic_slice_in_dim(gates_all, group * token_count, token_count)[:, :E]
    gate_grads_own = back_own[:, width : width + E] + back_own[:, width + E : width + 2 * E]
    grad_logits = gates * (gate_grads_own - jnp.sum(gates * gate_grads_own, axis=-1, keepdims=True))
    grad_normed_two = back_own[:, :width] + jnp.dot(
        grad_logits, router_w.astype(f32).T, precision=HIGHEST_DOT
    )
    grad_router = jnp.dot(normed_two.astype(f32).T, grad_logits, precision=HIGHEST_DOT)
    grad_resid_norm, grad_gain_two = rms_back(resid, gain_two_f, grad_normed_two)
    grad_resid = grad_out + grad_resid_norm
    grad_attn_low = (RESIDUAL_SCALE * grad_resid).astype(bf16)
    grad_heads = contract_cols(grad_attn_low, output_w).astype(bf16)
    grad_mixed = exchange(
        grad_heads.reshape(token_count, KEY_VALUE_HEADS, PAIR).transpose(1, 0, 2), head_axes
    ).reshape(span, PAIR)
    if by_column:
        keep, arrived, x_other, grad_heads = lax.optimization_barrier(
            (keep, arrived, tuple(x_other), grad_heads)
        )
        x_other = jnp.concatenate(x_other)
        left, right = (
            halve_add(terms).reshape((2, 2) + terms[0].shape[1:]) for terms in zip(keep, arrived)
        )
        left, right = halve_send(left, "y", 1), halve_send(right, "b", 0)
    small = jnp.concatenate([grad_router, grad_gain_two[:, None]], axis=1)
    second_part = jnp.concatenate(
        [contract_rows(attended_low, grad_attn_low), pad_lanes(small, LANES)], axis=1
    ).astype(bf16)
    cols = second_part.shape[1]
    second_part = second_part.reshape(GROUPS, -1, own_rows, cols).transpose(1, 0, 2, 3)
    if by_column:
        left, right = halve_add(left), halve_add(right)
        second_part, left, right, grad_mixed = lax.optimization_barrier(
            (second_part, left, right, grad_mixed)
        )
        left, right = halve_send(left, "b", 0), halve_send(right, "y", 0)
    rest = scatter_sum(second_part.reshape(-1, cols), PLANE)
    grads = attend_back(
        bounds, q, kv, doc_rows, grad_mixed, attention_result, log_total, wide_cos, wide_sin,
        by_column,
    )
    if by_column:
        left, right, moe_sum, grad_pack = lax.optimization_barrier((left, right, moe_sum, grads))
        first_part = head_grads(
            x_span, x_other, member, 1 - member, 2, member, own_weights, grad_pack
        )
    else:
        grad_kv = scatter_sum(grads[1].astype(bf16), "a").astype(f32)
        grad_pack = unrotate(grads[0], grad_kv, wide_cos, wide_sin)
        half = span // 2
        first_part = head_grads(
            x_span[:half], x_span[half:], zero, zero + half // BLOCK, 1, zero, own_weights, grad_pack
        )
    rest, first_part = lax.optimization_barrier((rest, first_part))
    rest = scatter_sum(rest, "a")
    by_tokens = exchange(grad_pack.reshape(KEY_VALUE_HEADS, token_count, HEAD_PACK), head_axes)
    by_tokens, first_part = lax.optimization_barrier((by_tokens, first_part))
    sums = exchange(first_part.reshape(-1, own_rows, first_part.shape[1]), ALL)
    sums, moe_sum, resid = lax.optimization_barrier((sums, moe_sum, resid))
    grad_q_w, grad_k_w, grad_v_w, grad_gain_one = weight_sums(
        sums.reshape(-1, KEY_VALUE_HEADS, lax.axis_size(("y", "c")), own_rows, first_part.shape[1])
    )
    rest = rest.astype(f32)
    grad_input = token_grads(by_tokens, first_all, tokens[0], grad_resid)
    layer_sum = resid + RESIDUAL_SCALE * moe_sum.astype(f32)
    if by_column:
        grad_experts = jnp.concatenate(
            [own.astype(f32) + other.astype(f32) for own, other in (left, right)], axis=1
        )
    else:
        grad_experts = grad_experts.astype(f32)
    return (
        layer_sum.astype(bf16)[None],
        grad_input[None],
        grad_gain_one[:, 0],
        grad_q_w,
        grad_k_w,
        grad_v_w,
        rest[:, :width],
        rest[:, width + E],
        rest[:, width : width + E],
        grad_experts[:, : 2 * F],
        grad_experts[:, 2 * F :],
    )


def solution(mesh):
    seq, row = mesh.shape["seq"], mesh.shape["row"]
    cut = Mesh(mesh.devices.reshape(GROUPS, seq // GROUPS, row // 2, 2), ALL)
    token_spec = P(("y", "c"), SEQ, None)
    row_spec = P(ALL, None)
    flat_spec = P(ALL)
    in_specs = (
        token_spec,
        token_spec,
        P(("y", "c"), None),
        token_spec,
        flat_spec,
        row_spec,
        row_spec,
        row_spec,
        row_spec,
        flat_spec,
        row_spec,
        row_spec,
        row_spec,
    )
    out_specs = (
        token_spec,
        token_spec,
        flat_spec,
        row_spec,
        row_spec,
        row_spec,
        row_spec,
        flat_spec,
        row_spec,
        row_spec,
        row_spec,
    )
    return jax.shard_map(body, mesh=cut, in_specs=in_specs, out_specs=out_specs, check_vma=False)
```

```python
import functools

import jax
import jax.numpy as jnp
from jax import lax
from jax.experimental import pallas as pl
from jax.experimental.pallas import tpu as pltpu
from jax.sharding import Mesh, PartitionSpec as P

QUERY_HEADS = 16
KEY_VALUE_HEADS = 8
HEAD_SIZE = 64
F = 512
E = 16
GROUPS = 4
EXPERTS_HERE = E // GROUPS
LANES = 128
PAIR = 2 * HEAD_SIZE
HEAD_PACK = 4 * HEAD_SIZE
BLOCK = 256
QUERY_BLOCK = 512

NORM_EPS = 1e-06
RESIDUAL_SCALE = 0.22
SCALE_OF_SCORES = 0.015625
ROPE_BASE = 10000.0
NEGATIVE_HUGE = -1e30
HIGHEST_DOT = lax.Precision.HIGHEST
VMEM_LIMIT = 60 * 1024 * 1024

PLANE = ("b", "y", "c")
SEQ = ("a", "b")
ALL = ("a", "b", "y", "c")
SWAP = [(0, 1), (1, 0)]

f32 = jnp.float32
bf16 = jnp.bfloat16


def rotation_tables(positions):
    half = HEAD_SIZE // 2
    freq = jnp.power(ROPE_BASE, -2.0 * jnp.arange(half, dtype=f32) / HEAD_SIZE)
    angle = positions.astype(f32)[:, None] * freq[None, :]
    return jnp.cos(angle), jnp.sin(angle)


def rms_back(values, gain, grad_norm):
    mean_square = jnp.mean(values * values, axis=-1, keepdims=True)
    inverse = lax.rsqrt(mean_square + NORM_EPS)
    scaled_grad = grad_norm * gain
    grad_values = inverse * scaled_grad - values * inverse**3 * jnp.mean(
        values * scaled_grad, axis=-1, keepdims=True
    )
    grad_gain = jnp.sum(grad_norm * values * inverse, axis=0)
    return (grad_values, grad_gain)


def rms_scale(values, gain):
    mean_square = jnp.mean(values * values, axis=-1, keepdims=True)
    return values * lax.rsqrt(mean_square + NORM_EPS) * gain


def contract_rows(left_side, right_side):
    return lax.dot_general(
        left_side, right_side, (((0,), (0,)), ((), ())), preferred_element_type=f32
    )


def contract_cols(left_side, right_side):
    return lax.dot_general(
        left_side, right_side, (((1,), (1,)), ((), ())), preferred_element_type=f32
    )


def gather(x, axes):
    return lax.all_gather(x, axes, axis=0, tiled=True)


def scatter_sum(x, axes):
    return lax.psum_scatter(x, axes, scatter_dimension=0, tiled=True)


def pad_lanes(x, lanes):
    return jnp.pad(x, ((0, 0), (0, lanes - x.shape[1])))


def line_pairs(n, step):
    return [(i, i + step) for i in range(n) if 0 <= i + step < n]


def hop(up, down):
    n = lax.axis_size("a")
    return lax.ppermute(up, "a", line_pairs(n, 1)), lax.ppermute(down, "a", line_pairs(n, -1))


def line_gather(x):
    pieces = [(0, x)]
    up = down = x
    for k in range(1, lax.axis_size("a")):
        up, down = hop(up, down)
        pieces += [(-k, up), (k, down)]
    return pieces


def in_line(own, ups, downs, me):
    n = lax.axis_size("a")
    out = jnp.zeros((n,) + own.shape, own.dtype)
    out = lax.dynamic_update_index_in_dim(out, own, me, 0)
    for k in range(1, n):
        piece = jnp.where(me >= k, ups[k - 1], downs[n - k - 1])
        out = lax.dynamic_update_index_in_dim(out, piece, (me - k) % n, 0)
    return out.reshape((n * own.shape[0],) + own.shape[1:])


def by_columns(own, other, member):
    first, second = jnp.where(member == 0, own, other), jnp.where(member == 0, other, own)
    return jnp.stack([first, second], axis=1)


def neighbours(x):
    return lax.ppermute(x, "y", SWAP), lax.ppermute(x, "b", SWAP)


def plane_gather(x, from_y, from_b):
    half = x.shape[0] // 2
    upper = lax.ppermute(from_b[:half], "y", SWAP)
    lower = lax.ppermute(from_y[half:], "b", SWAP)
    return [(block, lax.ppermute(block, "c", SWAP)) for block in (x, from_y, from_b, upper, lower)]


def halve_send(v, axis, at):
    me = lax.axis_index(axis)
    other = lax.ppermute(lax.dynamic_index_in_dim(v, 1 - me, at, False), axis, SWAP)
    return lax.dynamic_index_in_dim(v, me, at, False), other


def halve_add(terms):
    own, other = terms
    return (own.astype(f32) + other.astype(f32)).astype(own.dtype)


def rotate_lanes(x, cos, sin):
    width = x.shape[-1]
    lane = lax.broadcasted_iota(jnp.int32, x.shape, x.ndim - 1)
    swapped = jnp.where(
        lane % HEAD_SIZE < HEAD_SIZE // 2,
        pltpu.roll(x, width - HEAD_SIZE // 2, x.ndim - 1),
        pltpu.roll(x, HEAD_SIZE // 2, x.ndim - 1),
    )
    return x * cos + swapped * sin


def spread_tables(cos, sin):
    return jnp.concatenate([cos] * 4, axis=1), jnp.concatenate([-sin, sin, -sin, sin], axis=1)


def key_tables(cos, sin):
    low = lower_lanes(cos.shape)
    return jnp.where(low, cos, 1.0), jnp.where(low, sin, 0.0)


def project_kernel(places, spots, place_ref, *refs):
    count = 1 if places is None else len(places)
    blocks, refs = refs[:count], refs[count:]
    count = 1 if spots is None else len(spots)
    weights, refs = refs[:count], refs[count:]
    cos_ref, sin_ref, q_ref, kv_ref, x_ref, w_ref, gain, held, sems = refs
    i = pl.program_id(0)
    slots, _, width = held.shape
    heads = q_ref.shape[1] // PAIR

    @pl.when(i == 0)
    def _():
        copies = []
        if spots is None:
            copies.append(pltpu.make_async_copy(weights[0], w_ref, sems.at[slots]))
        else:
            for at, ((y, c), block) in enumerate(zip(spots, weights)):
                row = 2 * (place_ref[2] ^ y) + (place_ref[3] ^ c)
                copies.append(
                    pltpu.make_async_copy(block, w_ref.at[:, row], sems.at[slots + at])
                )
        for copy in copies:
            copy.start()
        if places is None:
            for slot in range(slots):
                pltpu.make_async_copy(blocks[0].at[slot], held.at[slot], sems.at[slot]).start()
        else:
            for distance, block in zip(places, blocks):
                slot = place_ref[0] + distance

                @pl.when((slot >= 0) & (slot < slots))
                def _(block=block, slot=slot):
                    pltpu.make_async_copy(block, held.at[slot], sems.at[slot]).start()

        for copy in copies:
            copy.wait()
        small = w_ref[..., heads * HEAD_PACK :].reshape(width, LANES)
        gain[...] = jnp.transpose(small.astype(f32))[:8, :]

    arrived = blocks[0].at[0] if places is None else blocks[0]
    pltpu.make_async_copy(arrived, held.at[i], sems.at[i]).wait()
    x = held[i]
    x_ref[...] = x
    normed = rms_scale(x.astype(f32), gain[0:1, :]).astype(bf16)
    w = w_ref[..., : heads * HEAD_PACK].reshape(width, heads * HEAD_PACK)
    pre = jnp.dot(normed, w, preferred_element_type=f32)
    cos, sin = spread_tables(cos_ref[...], sin_ref[...])
    key_cos, key_sin = key_tables(cos, sin)
    for h in range(heads):
        out, at = slice(h * PAIR, (h + 1) * PAIR), h * HEAD_PACK
        q_ref[:, out] = rotate_lanes(pre[:, at : at + PAIR], cos, sin).astype(bf16)
        kv_ref[:, out] = rotate_lanes(
            pre[:, at + PAIR : at + HEAD_PACK], key_cos, key_sin
        ).astype(bf16)


def project(place, places, blocks, spots, weights, rows, width, cos, sin):
    span = cos.shape[0]
    cols = weights[0].shape[-1]
    heads = (cols - LANES) // HEAD_PACK
    table = pl.BlockSpec((rows, HEAD_SIZE // 2), lambda i, h: (i, 0))
    token_rows = pl.BlockSpec((rows, width), lambda i, h: (i, 0))
    head_rows = pl.BlockSpec((rows, heads * PAIR), lambda i, h: (i, 0))
    shape = weights[0].shape if spots is None else (
        weights[0].shape[0], len(spots), weights[0].shape[1], cols
    )
    return pl.pallas_call(
        functools.partial(project_kernel, places, spots),
        grid_spec=pltpu.PrefetchScalarGridSpec(
            num_scalar_prefetch=1,
            grid=(span // rows,),
            in_specs=[pl.BlockSpec(memory_space=pl.ANY)] * (len(blocks) + len(weights))
            + [table, table],
            out_specs=[
                head_rows,
                head_rows,
                token_rows,
                pl.BlockSpec(shape, lambda i, h: (0,) * len(shape)),
            ],
            scratch_shapes=[
                pltpu.VMEM((8, width), f32),
                pltpu.VMEM((span // rows, rows, width), bf16),
                pltpu.SemaphoreType.DMA((span // rows + len(weights),)),
            ],
        ),
        out_shape=[
            jax.ShapeDtypeStruct((span, heads * PAIR), bf16),
            jax.ShapeDtypeStruct((span, heads * PAIR), bf16),
            jax.ShapeDtypeStruct((span, width), bf16),
            jax.ShapeDtypeStruct(shape, bf16),
        ],
        compiler_params=pltpu.CompilerParams(vmem_limit_bytes=VMEM_LIMIT),
        cost_estimate=pl.CostEstimate(
            flops=2 * span * width * heads * HEAD_PACK, bytes_accessed=8 * 2**20, transcendentals=0
        ),
        name="project",
    )(place, *blocks, *weights, cos, sin)


def spread_kernel(cos_ref, sin_ref, wide_cos_ref, wide_sin_ref):
    wide_cos_ref[...], wide_sin_ref[...] = spread_tables(cos_ref[...], sin_ref[...])


def spread(cos, sin):
    rows = cos.shape[0]
    wide = jax.ShapeDtypeStruct((rows, PAIR), f32)
    return pl.pallas_call(
        spread_kernel,
        grid=(4,),
        in_specs=[pl.BlockSpec((rows // 4, HEAD_SIZE // 2), lambda i: (i, 0))] * 2,
        out_specs=[pl.BlockSpec((rows // 4, PAIR), lambda i: (i, 0))] * 2,
        out_shape=[wide, wide],
        cost_estimate=pl.CostEstimate(flops=2**20, bytes_accessed=4 * 2**20, transcendentals=0),
        name="spread",
    )(cos, sin)


def head_grads_kernel(place_ref, own_ref, other_ref, w_ref, small_ref, grad_ref, out_ref, acc, sums, gain):
    i = pl.program_id(0)
    half = pl.num_programs(0) // 2

    @pl.when(i == 0)
    def _():
        acc[...] = jnp.zeros_like(acc)
        sums[...] = jnp.zeros_like(sums)
        gain[...] = jnp.transpose(small_ref[...].astype(f32))[:8, :]

    grad = grad_ref[...]
    x = jnp.where(i < half, own_ref[...], other_ref[...]).astype(f32)
    inverse = lax.rsqrt(jnp.mean(x * x, axis=-1, keepdims=True) + NORM_EPS)
    x = x * inverse
    acc[...] += contract_rows(grad, (x * gain[0:1, :]).astype(bf16))
    back = contract_cols(grad, w_ref[...]) * x
    sums[...] += jnp.sum(back.reshape(back.shape[0] // 8, 8, back.shape[1]), axis=0)

    @pl.when(i == pl.num_programs(0) - 1)
    def _():
        out_ref[:, :HEAD_PACK] = jnp.transpose(acc[...]).astype(bf16)
        total = jnp.sum(sums[...], axis=0, keepdims=True)
        rows = lax.broadcasted_iota(jnp.int32, (LANES, total.shape[1]), 0)
        out_ref[:, HEAD_PACK:] = jnp.transpose(
            jnp.where(rows == 0, jnp.broadcast_to(total, rows.shape), 0.0)
        ).astype(bf16)


def head_grads(own, other, first, second, stride, head_at, weights, grads):
    span, pack = grads.shape
    width = own.shape[1]
    rows = BLOCK
    half = span // rows // 2
    small_at = weights.shape[1] // LANES - 1

    def grads_at(i, s):
        return (jnp.where(i < half, s[0] + stride * i, s[1] + stride * (i - half)), 0)

    return pl.pallas_call(
        head_grads_kernel,
        grid_spec=pltpu.PrefetchScalarGridSpec(
            num_scalar_prefetch=1,
            grid=(span // rows,),
            in_specs=[
                pl.BlockSpec((rows, width), lambda i, s: (jnp.minimum(i, half - 1), 0)),
                pl.BlockSpec((rows, width), lambda i, s: (jnp.maximum(i - half, 0), 0)),
                pl.BlockSpec((width, pack), lambda i, s: (0, s[2])),
                pl.BlockSpec((width, LANES), lambda i, s: (0, small_at)),
                pl.BlockSpec((rows, pack), grads_at),
            ],
            out_specs=pl.BlockSpec((width, pack + LANES), lambda i, s: (0, 0)),
            scratch_shapes=[
                pltpu.VMEM((pack, width), f32),
                pltpu.VMEM((8, width), f32),
                pltpu.VMEM((8, width), f32),
            ],
        ),
        out_shape=jax.ShapeDtypeStruct((width, pack + LANES), bf16),
        compiler_params=pltpu.CompilerParams(vmem_limit_bytes=VMEM_LIMIT),
        cost_estimate=pl.CostEstimate(
            flops=4 * span * width * pack, bytes_accessed=8 * 2**20, transcendentals=0
        ),
        name="head_grads",
    )(jnp.stack([first, second, head_at]), own, other, weights, weights, grads)


def lower_lanes(shape):
    return lax.broadcasted_iota(jnp.int32, shape, len(shape) - 1) < HEAD_SIZE


def both_heads_low(pair):
    low = lower_lanes(pair.shape)
    return jnp.concatenate(
        [jnp.where(low, pair, 0.0), jnp.where(low, pltpu.roll(pair, HEAD_SIZE, 1), 0.0)], axis=0
    )


def both_heads_high(pair):
    low = lower_lanes(pair.shape)
    return jnp.concatenate(
        [jnp.where(low, 0.0, pltpu.roll(pair, HEAD_SIZE, 1)), jnp.where(low, 0.0, pair)], axis=0
    )


def block_bounds(bounds_ref, tile, tiles, stride):
    place = bounds_ref[2 * tiles] + stride * (QUERY_BLOCK // BLOCK) * tile
    full = jnp.minimum(bounds_ref[tiles + tile], place)
    return place, bounds_ref[tile], full, place + stride * (QUERY_BLOCK // BLOCK - 1) + 1


def pair_mask(doc, place, stride):
    doc = jnp.concatenate([doc, doc], axis=1)
    lane = lax.broadcasted_iota(jnp.int32, doc.shape, 1) % QUERY_BLOCK
    queries = (place + stride * (lane // BLOCK)) * BLOCK + lane % BLOCK

    def masked(scores, start):
        keys = lax.broadcasted_iota(jnp.int32, scores.shape, 0) + start
        return jnp.where((keys >= doc) & (keys <= queries), scores, NEGATIVE_HUGE)

    return masked


def attend_kernel(stride, bounds_ref, q_ref, kv_ref, doc_ref, o_ref, low_ref, lse_ref, acc):
    place, first, full, end = block_bounds(
        bounds_ref, pl.program_id(1), pl.num_programs(1), stride
    )
    q = both_heads_low(q_ref[...].astype(f32) * SCALE_OF_SCORES).astype(bf16)
    masked = pair_mask(doc_ref[0], place, stride)
    acc[...] = jnp.zeros_like(acc)

    def step(mask, j, carried):
        top, total = carried
        start = pl.multiple_of(j * BLOCK, BLOCK)
        kv = kv_ref[pl.ds(start, BLOCK), :]
        scores = contract_cols(kv, q)
        if mask:
            scores = masked(scores, start)
        new = jnp.maximum(top, jnp.max(scores, axis=0, keepdims=True))
        probs = jnp.exp(scores - new)
        keep = jnp.exp(top - new)
        acc[...] = acc[...] * keep + contract_rows(kv, probs.astype(bf16))
        return new, total * keep + jnp.sum(probs, axis=0, keepdims=True)

    row = (1, 2 * QUERY_BLOCK)
    carried = (jnp.full(row, NEGATIVE_HUGE, f32), jnp.zeros(row, f32))
    carried = lax.fori_loop(first, full, functools.partial(step, True), carried)
    carried = lax.fori_loop(full, place, functools.partial(step, False), carried)
    top, total = lax.fori_loop(place, end, functools.partial(step, True), carried)
    mixed = jnp.transpose(acc[...] / total)
    one, two = mixed[:QUERY_BLOCK], mixed[QUERY_BLOCK:]
    out = jnp.where(lower_lanes(one.shape), pltpu.roll(one, HEAD_SIZE, 1), two)
    o_ref[...] = out
    low_ref[...] = out.astype(bf16)
    lse_ref[0, 0] = top + jnp.log(total)


def attend(bounds, q, kv, doc, stride):
    (queries, cols), keys = q.shape, kv.shape[0]
    heads, tiles = cols // PAIR, queries // QUERY_BLOCK
    pair = pl.BlockSpec((QUERY_BLOCK, PAIR), lambda h, i, s: (i, h))
    return pl.pallas_call(
        functools.partial(attend_kernel, stride),
        grid_spec=pltpu.PrefetchScalarGridSpec(
            num_scalar_prefetch=1,
            grid=(heads, tiles),
            in_specs=[
                pair,
                pl.BlockSpec((keys, PAIR), lambda h, i, s: (0, h)),
                pl.BlockSpec((1, 1, QUERY_BLOCK), lambda h, i, s: (i, 0, 0)),
            ],
            out_specs=[
                pair,
                pair,
                pl.BlockSpec((1, 1, 1, 2 * QUERY_BLOCK), lambda h, i, s: (h, i, 0, 0)),
            ],
            scratch_shapes=[pltpu.VMEM((PAIR, 2 * QUERY_BLOCK), f32)],
        ),
        out_shape=[
            jax.ShapeDtypeStruct((queries, cols), f32),
            jax.ShapeDtypeStruct((queries, cols), bf16),
            jax.ShapeDtypeStruct((heads, tiles, 1, 2 * QUERY_BLOCK), f32),
        ],
        compiler_params=pltpu.CompilerParams(vmem_limit_bytes=VMEM_LIMIT),
        cost_estimate=pl.CostEstimate(
            flops=4 * queries * keys * cols,
            bytes_accessed=6 * 2**20,
            transcendentals=queries * keys * heads,
        ),
        name="attend",
    )(bounds, q, kv, doc)


def attend_back_kernel(
    fold, bounds_ref, q_ref, kv_ref, doc_ref, do_ref, o_ref, lse_ref, cos_ref, sin_ref, *refs
):
    if fold:
        out_ref, acc, dkv_ref = refs
    else:
        dq_ref, dkv_ref, acc = refs
    i = pl.program_id(0)
    place, first, full, end = block_bounds(bounds_ref, i, pl.num_programs(0), 1)

    @pl.when(i == 0)
    def _():
        dkv_ref[...] = jnp.zeros_like(dkv_ref)

    q = both_heads_low(q_ref[...].astype(f32) * SCALE_OF_SCORES).astype(bf16)
    grad = do_ref[...].astype(f32)
    product = jnp.transpose(grad * o_ref[...])
    delta = jnp.concatenate(
        [
            jnp.sum(product[:HEAD_SIZE], axis=0, keepdims=True),
            jnp.sum(product[HEAD_SIZE:], axis=0, keepdims=True),
        ],
        axis=1,
    )
    grad = both_heads_high(grad).astype(bf16)
    sources = jnp.concatenate([q, grad], axis=0)
    masked = pair_mask(doc_ref[0], place, 1)
    lse = lse_ref[0]
    acc[...] = jnp.zeros_like(acc)

    def step(mask, j, carried):
        start = pl.multiple_of(j * BLOCK, BLOCK)
        kv = kv_ref[pl.ds(start, BLOCK), :]
        scores = contract_cols(kv, q) - lse
        if mask:
            scores = masked(scores, start)
        probs = jnp.exp(scores)
        grad_scores = (probs * (contract_cols(kv, grad) - delta)).astype(bf16)
        acc[...] += contract_rows(kv, grad_scores)
        both = jnp.concatenate([grad_scores, probs.astype(bf16)], axis=1)
        dkv_ref[pl.ds(start, BLOCK), :] += jnp.dot(both, sources, preferred_element_type=f32)
        return carried

    lax.fori_loop(first, full, functools.partial(step, True), 0)
    lax.fori_loop(full, place, functools.partial(step, False), 0)
    lax.fori_loop(place, end, functools.partial(step, True), 0)
    dq = jnp.transpose(acc[...])
    one, two = dq[:QUERY_BLOCK], dq[QUERY_BLOCK:]
    dq = jnp.where(lower_lanes(one.shape), one, pltpu.roll(two, HEAD_SIZE, 1))
    if not fold:
        dq_ref[...] = dq
        return
    mine = pl.ds(pl.multiple_of(i * QUERY_BLOCK, QUERY_BLOCK), QUERY_BLOCK)
    out_ref[mine, :PAIR] = rotate_lanes(
        dq * SCALE_OF_SCORES, cos_ref[mine, :], -sin_ref[mine, :]
    ).astype(bf16)

    @pl.when(i == pl.num_programs(0) - 1)
    def _():
        def finish(j, carried):
            part = pl.ds(pl.multiple_of(j * BLOCK, BLOCK), BLOCK)
            cos, sin = key_tables(cos_ref[part, :], sin_ref[part, :])
            out_ref[part, PAIR:] = rotate_lanes(dkv_ref[part, :], cos, -sin).astype(bf16)
            return carried

        lax.fori_loop(0, dkv_ref.shape[0] // BLOCK, finish, 0)


def attend_back(bounds, q, kv, doc, grad, out, lse, cos, sin, fold):
    queries, keys = q.shape[0], kv.shape[0]
    steps = queries // QUERY_BLOCK
    pair = pl.BlockSpec((QUERY_BLOCK, PAIR), lambda i, s: (i, 0))
    whole = pl.BlockSpec((keys, PAIR), lambda i, s: (0, s[2 * steps + 1]))
    doc_row = pl.BlockSpec((1, 1, QUERY_BLOCK), lambda i, s: (i, 0, 0))
    lse_row = pl.BlockSpec((1, 1, 2 * QUERY_BLOCK), lambda i, s: (i, 0, 0))
    table = pl.BlockSpec(cos.shape, lambda i, s: (0, 0))
    acc = pltpu.VMEM((PAIR, 2 * QUERY_BLOCK), f32)
    if fold:
        out_specs = pl.BlockSpec((queries, HEAD_PACK), lambda i, s: (0, 0))
        out_shape = jax.ShapeDtypeStruct((queries, HEAD_PACK), bf16)
        scratch = [acc, pltpu.VMEM((keys, PAIR), f32)]
    else:
        out_specs = [pair, pl.BlockSpec((keys, PAIR), lambda i, s: (0, 0))]
        out_shape = [
            jax.ShapeDtypeStruct((queries, PAIR), f32),
            jax.ShapeDtypeStruct((keys, PAIR), f32),
        ]
        scratch = [acc]
    return pl.pallas_call(
        functools.partial(attend_back_kernel, fold),
        grid_spec=pltpu.PrefetchScalarGridSpec(
            num_scalar_prefetch=1,
            grid=(steps,),
            in_specs=[pair, whole, doc_row, pair, pair, lse_row, table, table],
            out_specs=out_specs,
            scratch_shapes=scratch,
        ),
        out_shape=out_shape,
        compiler_params=pltpu.CompilerParams(vmem_limit_bytes=VMEM_LIMIT),
        cost_estimate=pl.CostEstimate(
            flops=10 * queries * keys * PAIR,
            bytes_accessed=8 * 2**20,
            transcendentals=queries * keys,
        ),
        name="attend_back",
    )(bounds, q, kv, doc, grad, out, lse, cos, sin)


def unrotate_kernel(dq_ref, dkv_ref, cos_ref, sin_ref, out_ref):
    cos, sin = cos_ref[...], sin_ref[...]
    dq = rotate_lanes(dq_ref[...] * SCALE_OF_SCORES, cos, -sin)
    cos, sin = key_tables(cos, sin)
    dkv = rotate_lanes(dkv_ref[...], cos, -sin)
    out_ref[...] = jnp.concatenate([dq, dkv], axis=1).astype(bf16)


def unrotate(dq, dkv, cos, sin):
    rows = dq.shape[0]
    pair = pl.BlockSpec((BLOCK, PAIR), lambda i: (i, 0))
    return pl.pallas_call(
        unrotate_kernel,
        grid=(rows // BLOCK,),
        in_specs=[pair, pair, pair, pair],
        out_specs=pl.BlockSpec((BLOCK, HEAD_PACK), lambda i: (i, 0)),
        out_shape=jax.ShapeDtypeStruct((rows, HEAD_PACK), bf16),
        cost_estimate=pl.CostEstimate(
            flops=rows * HEAD_PACK * 8, bytes_accessed=rows * HEAD_PACK * 14, transcendentals=0
        ),
        name="unrotate",
    )(dq, dkv, cos, sin)


def place_experts_kernel(place_ref, *refs):
    blocks, (ct_ref, w_ref, z_ref, sems) = refs[:10], refs[10:]
    core = place_ref[1]
    rows = w_ref.shape[1] // 2
    half = rows // 2
    sources = [[(0, 0, rows)], [(1, 0, rows)], [(2, 0, rows)], [(3, 0, half), (4, half, half)]]
    for step, parts in enumerate(sources):

        @pl.when(pl.program_id(0) == step)
        def _(parts=parts):
            copies = []
            for source, start, length in parts:
                for other in (0, 1):
                    first = jnp.where(core == other, 0, rows) + start
                    at = pl.ds(pl.multiple_of(first, half), length)
                    copies.append(
                        pltpu.make_async_copy(
                            blocks[2 * source + other], w_ref.at[0, at, :], sems.at[len(copies)]
                        )
                    )
            for copy in copies:
                copy.start()
            for copy in copies:
                copy.wait()

    z_ref[0] = jnp.dot(ct_ref[...], w_ref[0, :, 2 * F :], preferred_element_type=f32)


def place_experts(place, parts, early, width):
    rows = early.shape[0]
    blocks = [block for pair in parts for block in pair]
    return pl.pallas_call(
        place_experts_kernel,
        grid_spec=pltpu.PrefetchScalarGridSpec(
            num_scalar_prefetch=1,
            grid=(EXPERTS_HERE,),
            in_specs=[pl.BlockSpec(memory_space=pl.ANY)] * len(blocks)
            + [pl.BlockSpec((rows, width), lambda r, s: (0, 0))],
            out_specs=[
                pl.BlockSpec((1, width, 3 * F), lambda r, s: (s[0] ^ r, 0, 0)),
                pl.BlockSpec((1, rows, F), lambda r, s: (s[0] ^ r, 0, 0)),
            ],
            scratch_shapes=[pltpu.SemaphoreType.DMA((4,))],
        ),
        out_shape=[
            jax.ShapeDtypeStruct((EXPERTS_HERE, width, 3 * F), bf16),
            jax.ShapeDtypeStruct((EXPERTS_HERE, rows, F), f32),
        ],
        compiler_params=pltpu.CompilerParams(vmem_limit_bytes=VMEM_LIMIT),
        cost_estimate=pl.CostEstimate(
            flops=2 * EXPERTS_HERE * rows * width * F, bytes_accessed=36 * 2**20, transcendentals=0
        ),
        name="place_experts",
    )(place, *blocks, early)


def lane_column(x, at):
    lane = lax.broadcasted_iota(jnp.int32, x.shape, 1)
    return jnp.sum(jnp.where(lane == at, x, 0.0), axis=1, keepdims=True)


def experts_kernel(
    group_ref, n_ref, routed_ref, router_ref, w_ref, z_ref,
    back_ref, gates_ref, hidden_ref, pre_ref, acc, dots,
):
    e = pl.program_id(0)
    own = group_ref[0] * EXPERTS_HERE + e
    rows = n_ref.shape[0]

    @pl.when(e == 0)
    def _():
        logits = jnp.dot(n_ref[...], router_ref[...], preferred_element_type=f32)
        routed = routed_ref[...].astype(f32) > 0.5
        highest = jnp.max(jnp.where(routed, logits, NEGATIVE_HUGE), axis=1, keepdims=True)
        weights = jnp.where(routed, jnp.exp(jnp.where(routed, logits - highest, 0.0)), 0.0)
        gates_ref[...] = weights / jnp.sum(weights, axis=1, keepdims=True)
        acc[...] = jnp.zeros_like(acc)
        dots[...] = jnp.zeros_like(dots)

    w_in = w_ref[0, :, : 2 * F]
    for t in range(rows // BLOCK):
        part = pl.ds(t * BLOCK, BLOCK)
        pre = jnp.dot(n_ref[part, :], w_in, preferred_element_type=f32)
        gate, up = pre[:, :F], pre[:, F:]
        z = z_ref[0, part, :]
        weight = lane_column(gates_ref[part, :], own)
        sig = 1.0 / (1.0 + jnp.exp(-gate))
        act = gate * sig
        hidden = act * up
        hidden_ref[0, part, :] = (weight * hidden).astype(bf16)
        dot = RESIDUAL_SCALE * jnp.sum(hidden.astype(bf16).astype(f32) * z, axis=1, keepdims=True)
        lane = lax.broadcasted_iota(jnp.int32, (BLOCK, LANES), 1)
        dots[part, :] += jnp.where(lane == own, dot, 0.0)
        scaled = (RESIDUAL_SCALE * weight) * z
        pre_ref[0, part, :F] = (scaled * up * (sig + act * (1.0 - sig))).astype(bf16)
        pre_ref[0, part, F:] = (scaled * act).astype(bf16)
        acc[part, :] += contract_cols(pre_ref[0, part, :], w_in)

    @pl.when(e == EXPERTS_HERE - 1)
    def _():
        width = n_ref.shape[1]
        back_ref[:, :width] = acc[...].astype(bf16)
        high = dots[...].astype(bf16)
        low = dots[...] - high.astype(f32)
        back_ref[:, width:] = (high.astype(f32) + pltpu.roll(low, E, 1)).astype(bf16)


def experts(group, normed, early, packed, w_all, z):
    rows, width = normed.shape
    count = w_all.shape[0]
    whole = pl.BlockSpec((rows, width), lambda e, g: (0, 0))
    column = width // LANES
    router_at = packed.shape[1] // LANES - 1
    return pl.pallas_call(
        experts_kernel,
        grid_spec=pltpu.PrefetchScalarGridSpec(
            num_scalar_prefetch=1,
            grid=(count,),
            in_specs=[
                whole,
                pl.BlockSpec((rows, LANES), lambda e, g: (0, column)),
                pl.BlockSpec((width, LANES), lambda e, g: (0, router_at)),
                pl.BlockSpec((1, width, 3 * F), lambda e, g: (e, 0, 0)),
                pl.BlockSpec((1, rows, F), lambda e, g: (e, 0, 0)),
            ],
            out_specs=[
                pl.BlockSpec((rows, width + LANES), lambda e, g: (0, 0)),
                pl.BlockSpec((rows, LANES), lambda e, g: (0, 0)),
                pl.BlockSpec((1, rows, F), lambda e, g: (e, 0, 0)),
                pl.BlockSpec((1, rows, 2 * F), lambda e, g: (e, 0, 0)),
            ],
            scratch_shapes=[pltpu.VMEM((rows, width), f32), pltpu.VMEM((rows, LANES), f32)],
        ),
        out_shape=[
            jax.ShapeDtypeStruct((rows, width + LANES), bf16),
            jax.ShapeDtypeStruct((rows, LANES), f32),
            jax.ShapeDtypeStruct((count, rows, F), bf16),
            jax.ShapeDtypeStruct((count, rows, 2 * F), bf16),
        ],
        compiler_params=pltpu.CompilerParams(vmem_limit_bytes=VMEM_LIMIT),
        cost_estimate=pl.CostEstimate(
            flops=2 * count * rows * width * 4 * F, bytes_accessed=40 * 2**20, transcendentals=0
        ),
        name="experts",
    )(group, normed, early, packed, w_all, z)


def expert_grads_kernel(half_ref, n_ref, ct_ref, w_ref, hidden_ref, pre_ref, y_ref, *refs):
    grad_refs, (n_t, ct_t, acc) = refs[:-3], refs[-3:]
    e = pl.program_id(0)

    @pl.when(e == 0)
    def _():
        n_t[...] = jnp.transpose(n_ref[...])
        ct_t[...] = jnp.transpose(ct_ref[...])
        acc[...] = jnp.zeros_like(acc)

    for part in range(len(grad_refs) // 2):
        left_ref, right_ref = grad_refs[2 * part : 2 * part + 2]
        rows, cut = left_ref.shape[1:]
        at = pl.ds(pl.multiple_of((half_ref[0] ^ part) * rows, rows), rows)
        grads = jnp.dot(n_t[at, :], pre_ref[0], preferred_element_type=f32).astype(bf16)
        left_ref[0] = grads[:, :cut]
        right_ref[0, :, : 2 * F - cut] = grads[:, cut:]
        right_ref[0, :, 2 * F - cut :] = (
            RESIDUAL_SCALE * jnp.dot(ct_t[at, :], hidden_ref[0], preferred_element_type=f32)
        ).astype(bf16)
    acc[...] += contract_cols(hidden_ref[0], w_ref[0, :, 2 * F :])

    @pl.when(e == pl.num_programs(0) - 1)
    def _():
        y_ref[...] = acc[...].astype(bf16)


def expert_grads(half, parts, normed, early, w_all, hidden, pre):
    rows, width = normed.shape
    count = w_all.shape[0]
    own, cut = width // parts, 3 * F // 2
    whole = pl.BlockSpec((rows, width), lambda e, h: (0, 0))
    return pl.pallas_call(
        expert_grads_kernel,
        grid_spec=pltpu.PrefetchScalarGridSpec(
            num_scalar_prefetch=1,
            grid=(count,),
            in_specs=[
                whole,
                whole,
                pl.BlockSpec((1, width, 3 * F), lambda e, h: (e, 0, 0)),
                pl.BlockSpec((1, rows, F), lambda e, h: (e, 0, 0)),
                pl.BlockSpec((1, rows, 2 * F), lambda e, h: (e, 0, 0)),
            ],
            out_specs=[whole] + [pl.BlockSpec((1, own, cut), lambda e, h: (e, 0, 0))] * (2 * parts),
            scratch_shapes=[
                pltpu.VMEM((width, rows), bf16),
                pltpu.VMEM((width, rows), bf16),
                pltpu.VMEM((rows, width), f32),
            ],
        ),
        out_shape=[jax.ShapeDtypeStruct((rows, width), bf16)]
        + [jax.ShapeDtypeStruct((count, own, cut), bf16)] * (2 * parts),
        compiler_params=pltpu.CompilerParams(vmem_limit_bytes=VMEM_LIMIT),
        cost_estimate=pl.CostEstimate(
            flops=2 * count * rows * width * 4 * F, bytes_accessed=40 * 2**20, transcendentals=0
        ),
        name="expert_grads",
    )(half, normed, early, w_all, hidden, pre)


def join_kernel(place_ref, o_ref, w_ref, small_ref, x_ref, normed_ref, resid_ref, own_ref, gain):
    t = pl.program_id(0)

    @pl.when(t == 0)
    def _():
        gain[...] = jnp.transpose(small_ref[...].astype(f32))[E : E + 8, :]

    attended = jnp.concatenate([o_ref[a] for a in range(o_ref.shape[0])], axis=1)
    resid = x_ref[...].astype(f32) + RESIDUAL_SCALE * jnp.dot(
        attended, w_ref[...], preferred_element_type=f32
    )
    normed_ref[...] = rms_scale(resid, gain[1:2, :]).astype(bf16)

    @pl.when(t == place_ref[0])
    def _():
        resid_ref[...] = resid
        own_ref[...] = attended


def join(place, outs, packed, weights_at, x):
    width = packed.shape[0]
    lines, tokens, cols = outs.shape
    rows = tokens // lines
    small_at = packed.shape[1] // LANES - 1
    own = pl.BlockSpec((rows, width), lambda t, s: (0, 0))
    return pl.pallas_call(
        join_kernel,
        grid_spec=pltpu.PrefetchScalarGridSpec(
            num_scalar_prefetch=1,
            grid=(lines,),
            in_specs=[
                pl.BlockSpec((lines, rows, cols), lambda t, s: (0, t, 0)),
                pl.BlockSpec((width, width), lambda t, s: (0, weights_at)),
                pl.BlockSpec((width, LANES), lambda t, s: (0, small_at)),
                pl.BlockSpec((rows, width), lambda t, s: (t, 0)),
            ],
            out_specs=[pl.BlockSpec((rows, width), lambda t, s: (t, 0)), own, own],
            scratch_shapes=[pltpu.VMEM((8, width), f32)],
        ),
        out_shape=[
            jax.ShapeDtypeStruct((lines * rows, width), bf16),
            jax.ShapeDtypeStruct((rows, width), f32),
            jax.ShapeDtypeStruct((rows, width), bf16),
        ],
        compiler_params=pltpu.CompilerParams(vmem_limit_bytes=VMEM_LIMIT),
        cost_estimate=pl.CostEstimate(
            flops=2 * lines * rows * width * width, bytes_accessed=12 * 2**20, transcendentals=0
        ),
        name="join",
    )(place, outs, packed, packed, x)


def token_grads_kernel(grad_ref, w_ref, small_ref, x_ref, resid_ref, out_ref, acc):
    h = pl.program_id(0)
    part = contract_cols(grad_ref[0], w_ref[...])

    @pl.when(h == 0)
    def _():
        acc[...] = part

    @pl.when(h > 0)
    def _():
        acc[...] += part

    @pl.when(h == pl.num_programs(0) - 1)
    def _():
        gain = jnp.transpose(small_ref[...].astype(f32))[E : E + 1, :]
        x = x_ref[...].astype(f32)
        inverse = lax.rsqrt(jnp.mean(x * x, axis=-1, keepdims=True) + NORM_EPS)
        scaled = acc[...] * gain
        mean = jnp.mean(x * scaled, axis=-1, keepdims=True)
        out_ref[...] = resid_ref[...] + (inverse * scaled - x * inverse**3 * mean)


def token_grads(grads, weights, packed, x, resid):
    heads, rows, pack = grads.shape
    width = x.shape[1]
    small_at = packed.shape[1] // LANES - 1
    whole = pl.BlockSpec((rows, width), lambda h: (0, 0))
    return pl.pallas_call(
        token_grads_kernel,
        grid=(heads,),
        in_specs=[
            pl.BlockSpec((1, rows, pack), lambda h: (h, 0, 0)),
            pl.BlockSpec((width, pack), lambda h: (0, h)),
            pl.BlockSpec((width, LANES), lambda h: (0, small_at)),
            whole,
            whole,
        ],
        out_specs=whole,
        out_shape=jax.ShapeDtypeStruct((rows, width), f32),
        scratch_shapes=[pltpu.VMEM((rows, width), f32)],
        compiler_params=pltpu.CompilerParams(vmem_limit_bytes=VMEM_LIMIT),
        cost_estimate=pl.CostEstimate(
            flops=2 * rows * width * heads * pack, bytes_accessed=8 * 2**20, transcendentals=0
        ),
        name="token_grads",
    )(grads, weights, packed, x, resid)


def weight_sums_kernel(sums_ref, q_ref, k_ref, v_ref, gain_ref):
    groups, heads, members = sums_ref.shape[:3]
    gain = jnp.zeros(gain_ref.shape, f32)
    values = []
    for h in range(heads):
        total = jnp.zeros(sums_ref.shape[3:], f32)
        for g in range(groups):
            for member in range(members):
                total += sums_ref[g, h, member].astype(f32)
        values.append(total)
        gain += total[:, HEAD_PACK:]
        q_ref[:, h * PAIR : (h + 1) * PAIR] = total[:, :PAIR]
    gain_ref[...] = gain
    for h in range(0, heads, 2):
        one, two = values[h][:, PAIR:HEAD_PACK], values[h + 1][:, PAIR:HEAD_PACK]
        low = lower_lanes(one.shape)
        at = slice(h // 2 * PAIR, (h // 2 + 1) * PAIR)
        k_ref[:, at] = jnp.where(low, one, pltpu.roll(two, HEAD_SIZE, 1))
        v_ref[:, at] = jnp.where(low, pltpu.roll(one, HEAD_SIZE, 1), two)


def weight_sums(sums):
    rows, heads = sums.shape[3], sums.shape[1]
    return pl.pallas_call(
        weight_sums_kernel,
        out_shape=[
            jax.ShapeDtypeStruct((rows, heads * PAIR), f32),
            jax.ShapeDtypeStruct((rows, heads * HEAD_SIZE), f32),
            jax.ShapeDtypeStruct((rows, heads * HEAD_SIZE), f32),
            jax.ShapeDtypeStruct((rows, LANES), f32),
        ],
        compiler_params=pltpu.CompilerParams(vmem_limit_bytes=VMEM_LIMIT),
        cost_estimate=pl.CostEstimate(flops=2**20, bytes_accessed=2 * 2**20, transcendentals=0),
        name="weight_sums",
    )(sums)


def exchange(x, axes):
    return lax.all_to_all(x, axes, 0, 0, tiled=True)


def body(
    tokens,
    cotangent,
    segment_ids,
    routes,
    norm_attn,
    w_query,
    key_weight_matrix,
    value_weight_matrix,
    w_output,
    norm_moe,
    w_router,
    expert_in,
    expert_out,
):
    x_local = tokens[0].astype(f32)
    token_count, width = x_local.shape
    seg_row = segment_ids[0]
    group, member = lax.axis_index("a"), lax.axis_index("b")
    by_column = all(lax.axis_size(axis) == 2 for axis in PLANE)
    by_column = by_column and lax.axis_size(SEQ) == KEY_VALUE_HEADS
    head_axes = SEQ if by_column else ("b",)
    span = token_count * KEY_VALUE_HEADS
    span_start = 0 if by_column else group * span

    def start_of_doc(ids):
        return jnp.sum((seg_row[None, :] < ids[:, None]).astype(jnp.int32), axis=1)

    def tile_bounds(docs, place):
        tiles = docs.reshape(-1, QUERY_BLOCK)
        ends = (tiles[:, 0] // BLOCK, (tiles[:, -1] + BLOCK - 1) // BLOCK, jnp.stack(place))
        return jnp.concatenate(ends).astype(jnp.int32), tiles[:, None, :]

    def own_column(x):
        x = x.reshape((GROUPS, 2, token_count) + x.shape[1:])
        x = lax.dynamic_index_in_dim(x, member, 1, False)
        return x.reshape((GROUPS * token_count,) + x.shape[2:])

    doc_span = start_of_doc(lax.dynamic_slice_in_dim(seg_row, span_start, span))
    cos_span, sin_span = rotation_tables(span_start + jnp.arange(span, dtype=jnp.int32) - doc_span)
    zero = jnp.zeros_like(member)
    head_of_two = member if by_column else zero
    bounds, doc_rows = tile_bounds(doc_span, (zero + span_start // BLOCK, head_of_two))
    wide_cos, wide_sin = spread(cos_span, sin_span)
    if by_column:
        cos_ahead, sin_ahead = own_column(cos_span), own_column(sin_span)
        bounds_ahead, docs_ahead = tile_bounds(own_column(doc_span), (member,))
    else:
        cos_ahead, sin_ahead, bounds_ahead, docs_ahead = cos_span, sin_span, bounds, doc_rows

    own_rows = w_query.shape[0]
    by_head = jnp.concatenate(
        [
            w_query.astype(bf16).reshape(own_rows, KEY_VALUE_HEADS, PAIR),
            key_weight_matrix.astype(bf16).reshape(own_rows, KEY_VALUE_HEADS, HEAD_SIZE),
            value_weight_matrix.astype(bf16).reshape(own_rows, KEY_VALUE_HEADS, HEAD_SIZE),
        ],
        axis=2,
    ).reshape(own_rows, KEY_VALUE_HEADS * HEAD_PACK)
    qkv_width = KEY_VALUE_HEADS * HEAD_PACK
    second_all = gather(
        jnp.concatenate(
            [
                w_output.astype(bf16),
                pad_lanes(
                    jnp.concatenate(
                        [
                            w_router.astype(bf16),
                            norm_attn.astype(bf16)[:, None],
                            norm_moe.astype(bf16)[:, None],
                        ],
                        axis=1,
                    ),
                    LANES,
                ),
            ],
            axis=1,
        ),
        ALL,
    )
    qkv_all = gather(by_head, ALL)
    experts_low = jnp.concatenate([expert_in.astype(bf16), expert_out.astype(bf16)], axis=1)
    if by_column:
        two = by_head.reshape(own_rows, GROUPS, 2 * HEAD_PACK).transpose(1, 0, 2)
        gains = pad_lanes(norm_attn.astype(bf16)[:, None], LANES)
        gains = jnp.broadcast_to(gains, (GROUPS, own_rows, LANES))
        columns = exchange(jnp.repeat(jnp.concatenate([two, gains], axis=2), 2, axis=0), SEQ)
        from_y = lax.ppermute(columns, "y", SWAP)
        spots = ((0, 0), (0, 1), (1, 0), (1, 1))
        weights = (
            columns, lax.ppermute(columns, "c", SWAP), from_y, lax.ppermute(from_y, "c", SWAP)
        )
        pieces = line_gather(tokens[0])
        places = [piece[0] for piece in pieces]
        blocks = tuple(piece[1] for piece in pieces)
    else:
        at = lax.axis_index(head_axes) * HEAD_PACK
        gains = pad_lanes(second_all[:, width + E : width + E + 1], LANES)
        spots, places = None, None
        weights = (
            jnp.concatenate(
                [lax.dynamic_slice_in_dim(qkv_all, at, HEAD_PACK, 1), gains], axis=1
            ),
        )
        blocks = (gather(tokens[0], "b").reshape((-1,) + tokens.shape[1:]),)
    experts_low, blocks, weights, cos_ahead, sin_ahead, bounds_ahead, docs_ahead, wide_cos, wide_sin = (
        lax.optimization_barrier(
            (
                experts_low, blocks, weights, cos_ahead, sin_ahead, bounds_ahead, docs_ahead,
                wide_cos, wide_sin,
            )
        )
    )
    expert_ids = jnp.arange(E, dtype=jnp.int32)
    routed_own = jnp.any(routes[0][:, :, None] == expert_ids[None, None, :], axis=1)
    early = jnp.concatenate([cotangent[0], pad_lanes(routed_own.astype(bf16), LANES)], axis=1)
    if by_column:
        beside = neighbours(experts_low)
    else:
        parts = gather(experts_low, PLANE)

    place = jnp.stack([lax.axis_index(axis) for axis in ALL])
    q, kv, x_span, own_weights = project(
        place, places, blocks, spots, weights, token_count, width, cos_ahead, sin_ahead
    )
    own_weights = own_weights.reshape(width, own_weights.shape[-1])
    if by_column:
        columns = (GROUPS, token_count)
        early, q = lax.optimization_barrier((early, q))
        up, down = hop(early, early)
        ups, downs = [up], [down]

        def in_row(own, other, shape):
            return by_columns(own.reshape(shape), other.reshape(shape), member)

        kv_other = lax.ppermute(kv, "b", SWAP)
        kv = in_row(kv, kv_other, columns + (2 * PAIR,)).reshape(span, 2 * PAIR)
        kv, up, down = lax.optimization_barrier((kv, up, down))
        up, down = hop(up, down)
        ups, downs = ups + [up], downs + [down]
    else:
        kv = gather(kv, "a")
        early_all = gather(early, "a")
    attention_result, attended, log_total = attend(
        bounds_ahead, q, kv, docs_ahead, 2 if by_column else 1
    )
    if by_column:
        attended, second_all, up, down = lax.optimization_barrier((attended, second_all, up, down))
        up, down = hop(up, down)
        early_all = in_line(early, ups + [up], downs + [down], group)
        attended, qkv_all = lax.optimization_barrier((attended, qkv_all))
        outs = lax.all_gather(attended, "a", axis=0, tiled=False)
        parts = plane_gather(experts_low, *beside)

        def heads_apart(x, axis):
            mine = lax.dynamic_index_in_dim(x, member, axis, False)
            return mine, lax.dynamic_index_in_dim(x, 1 - member, axis, False)

        q, q_sent = heads_apart(q.reshape(-1, 2, PAIR), 1)
        attention_result, out_sent = heads_apart(attention_result.reshape(-1, 2, PAIR), 1)
        log_total, log_sent = heads_apart(log_total, 0)
        q_other, out_other, log_other = (
            lax.ppermute(x, "b", SWAP) for x in (q_sent, out_sent, log_sent)
        )
        home = jnp.stack([member * 2 + lax.axis_index("y"), lax.axis_index("c")])
        experts_all, grad_hidden = place_experts(home, parts, early_all, width)
        outs, experts_all, q_other, out_other, log_other = lax.optimization_barrier(
            (outs, experts_all, q_other, out_other, log_other)
        )
        normed_all, resid, attended_low = join(place, outs, second_all, 0, x_span)
        normed_two = lax.dynamic_slice_in_dim(normed_all, group * token_count, token_count)
    else:
        attended_low = (
            exchange(attended.reshape(KEY_VALUE_HEADS, token_count, PAIR), head_axes)
            .transpose(1, 0, 2)
            .reshape(token_count, QUERY_HEADS * HEAD_SIZE)
        )
        attn_out = jnp.dot(attended_low, second_all[:, :width], preferred_element_type=f32)
        resid = x_local + RESIDUAL_SCALE * attn_out
        gain_two = second_all[:, width + E + 1].astype(f32)
        normed_two = rms_scale(resid, gain_two).astype(bf16)
        normed_all = gather(normed_two, "a")
        experts_all = parts.reshape(EXPERTS_HERE, width, 3 * F)
        grad_hidden = jnp.einsum(
            "td,edf->etf",
            early_all[:, :width],
            experts_all[:, :, 2 * F :],
            preferred_element_type=f32,
        )
    back_part, gates_all, gated_hidden, grad_pre = experts(
        group.reshape(1), normed_all, early_all, second_all, experts_all, grad_hidden
    )
    if by_column:
        q = in_row(q, q_other, columns + (PAIR,)).reshape(span, PAIR)
        attention_result = in_row(attention_result, out_other, columns + (PAIR,)).reshape(span, PAIR)

        def by_block(x):
            x = x.reshape(-1, 2, QUERY_BLOCK // BLOCK, BLOCK).transpose(0, 2, 1, 3)
            return x.reshape(GROUPS, 2, BLOCK)

        log_total = in_row(by_block(log_total), by_block(log_other), (GROUPS, 2, BLOCK))
        log_total = log_total.transpose(0, 2, 1, 3)
    log_total = log_total.reshape(-1, 1, 2 * QUERY_BLOCK)
    back_own = scatter_sum(back_part, "a")
    inputs = (normed_all, early_all, experts_all, gated_hidden, grad_pre)
    if by_column:
        core = lax.axis_index("c")
        x_other = lax.ppermute(x_span, "b", SWAP)
        moe_part, *keep, send_left, send_right = expert_grads(core.reshape(1), 2, *inputs)
        arrived = [lax.ppermute(x, "c", SWAP) for x in (send_left, send_right)]
        back_own, moe_part, keep, x_other = lax.optimization_barrier(
            (back_own, moe_part, keep, x_other)
        )
    else:
        moe_part, *grads = expert_grads(jnp.zeros((1,), jnp.int32), 1, *inputs)
        grad_experts = jnp.concatenate(grads, axis=2)
        back_own, moe_part, grad_experts = lax.optimization_barrier(
            (back_own, moe_part, grad_experts)
        )
        grad_experts = scatter_sum(grad_experts.reshape(EXPERTS_HERE * width, 3 * F), PLANE)
    back_own = back_own.astype(f32)
    moe_sum = scatter_sum(moe_part, "a")

    output_w = second_all[:, :width]
    router_w = second_all[:, width : width + E]
    gain_two_f = second_all[:, width + E + 1].astype(f32)
    grad_out = cotangent[0].astype(f32)
    gates = lax.dynamic_slice_in_dim(gates_all, group * token_count, token_count)[:, :E]
    gate_grads_own = back_own[:, width : width + E] + back_own[:, width + E : width + 2 * E]
    grad_logits = gates * (gate_grads_own - jnp.sum(gates * gate_grads_own, axis=-1, keepdims=True))
    grad_normed_two = back_own[:, :width] + jnp.dot(
        grad_logits, router_w.astype(f32).T, precision=HIGHEST_DOT
    )
    grad_router = jnp.dot(normed_two.astype(f32).T, grad_logits, precision=HIGHEST_DOT)
    grad_resid_norm, grad_gain_two = rms_back(resid, gain_two_f, grad_normed_two)
    grad_resid = grad_out + grad_resid_norm
    grad_attn_low = (RESIDUAL_SCALE * grad_resid).astype(bf16)
    grad_heads = contract_cols(grad_attn_low, output_w).astype(bf16)
    grad_mixed = exchange(
        grad_heads.reshape(token_count, KEY_VALUE_HEADS, PAIR).transpose(1, 0, 2), head_axes
    ).reshape(span, PAIR)
    small = jnp.concatenate([grad_router, grad_gain_two[:, None]], axis=1)
    second_part = jnp.concatenate(
        [contract_rows(attended_low, grad_attn_low), pad_lanes(small, LANES)], axis=1
    ).astype(bf16)
    cols = second_part.shape[1]
    if by_column:
        keep, arrived, second_part = lax.optimization_barrier((keep, arrived, second_part))
        left, right = (
            halve_add(terms).reshape((2, 2) + terms[0].shape[1:]) for terms in zip(keep, arrived)
        )
        left, right = halve_send(left, "y", 1), halve_send(right, "b", 0)
    second_part = second_part.reshape(GROUPS, -1, own_rows, cols).transpose(1, 0, 2, 3)
    if by_column:
        second_part, grad_mixed = lax.optimization_barrier((second_part, grad_mixed))
    rest = scatter_sum(second_part.reshape(-1, cols), PLANE)
    grads = attend_back(
        bounds, q, kv, doc_rows, grad_mixed, attention_result, log_total, wide_cos, wide_sin,
        by_column,
    )
    if by_column:
        left, right, moe_sum, grad_pack = lax.optimization_barrier((left, right, moe_sum, grads))
        left, right = halve_add(left), halve_add(right)
        left, right = halve_send(left, "b", 0), halve_send(right, "y", 0)
        first_part = head_grads(
            x_span, x_other, member, 1 - member, 2, member, own_weights, grad_pack
        )
    else:
        grad_kv = scatter_sum(grads[1].astype(bf16), "a").astype(f32)
        grad_pack = unrotate(grads[0], grad_kv, wide_cos, wide_sin)
        half = span // 2
        first_part = head_grads(
            x_span[:half], x_span[half:], zero, zero + half // BLOCK, 1, zero, own_weights, grad_pack
        )
    rest, first_part = lax.optimization_barrier((rest, first_part))
    rest = scatter_sum(rest, "a")
    by_tokens = exchange(grad_pack.reshape(KEY_VALUE_HEADS, token_count, HEAD_PACK), head_axes)
    by_tokens, first_part, rest = lax.optimization_barrier((by_tokens, first_part, rest))
    sums = exchange(first_part.reshape(-1, own_rows, first_part.shape[1]), ALL)
    grad_input = token_grads(by_tokens, qkv_all, second_all, tokens[0], grad_resid)
    sums, moe_sum, resid, grad_input = lax.optimization_barrier((sums, moe_sum, resid, grad_input))
    grad_q_w, grad_k_w, grad_v_w, grad_gain_one = weight_sums(
        sums.reshape(-1, KEY_VALUE_HEADS, lax.axis_size(("y", "c")), own_rows, first_part.shape[1])
    )
    rest = rest.astype(f32)
    layer_sum = resid + RESIDUAL_SCALE * moe_sum.astype(f32)
    if by_column:
        grad_experts = jnp.concatenate(
            [own.astype(f32) + other.astype(f32) for own, other in (left, right)], axis=1
        )
    else:
        grad_experts = grad_experts.astype(f32)
    return (
        layer_sum.astype(bf16)[None],
        grad_input[None],
        grad_gain_one[:, 0],
        grad_q_w,
        grad_k_w,
        grad_v_w,
        rest[:, :width],
        rest[:, width + E],
        rest[:, width : width + E],
        grad_experts[:, : 2 * F],
        grad_experts[:, 2 * F :],
    )


def solution(mesh):
    seq, row = mesh.shape["seq"], mesh.shape["row"]
    cut = Mesh(mesh.devices.reshape(GROUPS, seq // GROUPS, row // 2, 2), ALL)
    token_spec = P(("y", "c"), SEQ, None)
    row_spec = P(ALL, None)
    flat_spec = P(ALL)
    in_specs = (
        token_spec,
        token_spec,
        P(("y", "c"), None),
        token_spec,
        flat_spec,
        row_spec,
        row_spec,
        row_spec,
        row_spec,
        flat_spec,
        row_spec,
        row_spec,
        row_spec,
    )
    out_specs = (
        token_spec,
        token_spec,
        flat_spec,
        row_spec,
        row_spec,
        row_spec,
        row_spec,
        flat_spec,
        row_spec,
        row_spec,
        row_spec,
    )
    return jax.shard_map(body, mesh=cut, in_specs=in_specs, out_specs=out_specs, check_vma=False)
```

```python
import functools

import jax
import jax.numpy as jnp
from jax import lax
from jax.experimental import pallas as pl
from jax.experimental.pallas import tpu as pltpu
from jax.sharding import Mesh, PartitionSpec as P

QUERY_HEADS = 16
KEY_VALUE_HEADS = 8
HEAD_SIZE = 64
F = 512
E = 16
GROUPS = 4
EXPERTS_HERE = E // GROUPS
LANES = 128
PAIR = 2 * HEAD_SIZE
HEAD_PACK = 4 * HEAD_SIZE
BLOCK = 256
QUERY_BLOCK = 512

NORM_EPS = 1e-06
RESIDUAL_SCALE = 0.22
SCALE_OF_SCORES = 0.015625
ROPE_BASE = 10000.0
NEGATIVE_HUGE = -1e30
HIGHEST_DOT = lax.Precision.HIGHEST
VMEM_LIMIT = 60 * 1024 * 1024

PLANE = ("b", "y", "c")
SEQ = ("a", "b")
ALL = ("a", "b", "y", "c")
SWAP = [(0, 1), (1, 0)]

f32 = jnp.float32
bf16 = jnp.bfloat16


def rotation_tables(positions):
    half = HEAD_SIZE // 2
    freq = jnp.power(ROPE_BASE, -2.0 * jnp.arange(half, dtype=f32) / HEAD_SIZE)
    angle = positions.astype(f32)[:, None] * freq[None, :]
    return jnp.cos(angle), jnp.sin(angle)


def rms_back(values, gain, grad_norm):
    mean_square = jnp.mean(values * values, axis=-1, keepdims=True)
    inverse = lax.rsqrt(mean_square + NORM_EPS)
    scaled_grad = grad_norm * gain
    grad_values = inverse * scaled_grad - values * inverse**3 * jnp.mean(
        values * scaled_grad, axis=-1, keepdims=True
    )
    grad_gain = jnp.sum(grad_norm * values * inverse, axis=0)
    return (grad_values, grad_gain)


def rms_scale(values, gain):
    mean_square = jnp.mean(values * values, axis=-1, keepdims=True)
    return values * lax.rsqrt(mean_square + NORM_EPS) * gain


def contract_rows(left_side, right_side):
    return lax.dot_general(
        left_side, right_side, (((0,), (0,)), ((), ())), preferred_element_type=f32
    )


def contract_cols(left_side, right_side):
    return lax.dot_general(
        left_side, right_side, (((1,), (1,)), ((), ())), preferred_element_type=f32
    )


def gather(x, axes):
    return lax.all_gather(x, axes, axis=0, tiled=True)


def scatter_sum(x, axes):
    return lax.psum_scatter(x, axes, scatter_dimension=0, tiled=True)


def pad_lanes(x, lanes):
    return jnp.pad(x, ((0, 0), (0, lanes - x.shape[1])))


def line_pairs(n, step):
    return [(i, i + step) for i in range(n) if 0 <= i + step < n]


def hop(up, down):
    n = lax.axis_size("a")
    return lax.ppermute(up, "a", line_pairs(n, 1)), lax.ppermute(down, "a", line_pairs(n, -1))


def line_gather(x):
    pieces = [(0, x)]
    up = down = x
    for k in range(1, lax.axis_size("a")):
        up, down = hop(up, down)
        pieces += [(-k, up), (k, down)]
    return pieces


def by_columns(own, other, member):
    first, second = jnp.where(member == 0, own, other), jnp.where(member == 0, other, own)
    return jnp.stack([first, second], axis=1)


def neighbours(x):
    return lax.ppermute(x, "y", SWAP), lax.ppermute(x, "b", SWAP)


def plane_gather(x, from_y, from_b):
    half = x.shape[0] // 2
    upper = lax.ppermute(from_b[:half], "y", SWAP)
    lower = lax.ppermute(from_y[half:], "b", SWAP)
    return [(block, lax.ppermute(block, "c", SWAP)) for block in (x, from_y, from_b, upper, lower)]


def halve_send(v, axis, at):
    me = lax.axis_index(axis)
    other = lax.ppermute(lax.dynamic_index_in_dim(v, 1 - me, at, False), axis, SWAP)
    return lax.dynamic_index_in_dim(v, me, at, False), other


def halve_add(terms):
    own, other = terms
    return (own.astype(f32) + other.astype(f32)).astype(own.dtype)


def rotate_lanes(x, cos, sin):
    width = x.shape[-1]
    lane = lax.broadcasted_iota(jnp.int32, x.shape, x.ndim - 1)
    swapped = jnp.where(
        lane % HEAD_SIZE < HEAD_SIZE // 2,
        pltpu.roll(x, width - HEAD_SIZE // 2, x.ndim - 1),
        pltpu.roll(x, HEAD_SIZE // 2, x.ndim - 1),
    )
    return x * cos + swapped * sin


def spread_tables(cos, sin):
    return jnp.concatenate([cos] * 4, axis=1), jnp.concatenate([-sin, sin, -sin, sin], axis=1)


def key_tables(cos, sin):
    low = lower_lanes(cos.shape)
    return jnp.where(low, cos, 1.0), jnp.where(low, sin, 0.0)


def project_kernel(places, spots, place_ref, *refs):
    count = 1 if places is None else len(places)
    blocks, refs = refs[:count], refs[count:]
    count = 1 if spots is None else len(spots)
    weights, refs = refs[:count], refs[count:]
    cos_ref, sin_ref, q_ref, kv_ref, x_ref, w_ref, gain, held, sems = refs
    i = pl.program_id(0)
    slots, _, width = held.shape
    heads = q_ref.shape[1] // PAIR

    @pl.when(i == 0)
    def _():
        copies = []
        if spots is None:
            copies.append(pltpu.make_async_copy(weights[0], w_ref, sems.at[slots]))
        else:
            for at, ((y, c), block) in enumerate(zip(spots, weights)):
                row = 2 * (place_ref[2] ^ y) + (place_ref[3] ^ c)
                copies.append(
                    pltpu.make_async_copy(block, w_ref.at[:, row], sems.at[slots + at])
                )
        for copy in copies:
            copy.start()
        if places is None:
            for slot in range(slots):
                pltpu.make_async_copy(blocks[0].at[slot], held.at[slot], sems.at[slot]).start()
        else:
            for distance, block in zip(places, blocks):
                slot = place_ref[0] + distance

                @pl.when((slot >= 0) & (slot < slots))
                def _(block=block, slot=slot):
                    pltpu.make_async_copy(block, held.at[slot], sems.at[slot]).start()

        for copy in copies:
            copy.wait()
        small = w_ref[..., heads * HEAD_PACK :].reshape(width, LANES)
        gain[...] = jnp.transpose(small.astype(f32))[:8, :]

    arrived = blocks[0].at[0] if places is None else blocks[0]
    pltpu.make_async_copy(arrived, held.at[i], sems.at[i]).wait()
    x = held[i]
    x_ref[...] = x
    normed = rms_scale(x.astype(f32), gain[0:1, :]).astype(bf16)
    w = w_ref[..., : heads * HEAD_PACK].reshape(width, heads * HEAD_PACK)
    pre = jnp.dot(normed, w, preferred_element_type=f32)
    cos, sin = spread_tables(cos_ref[...], sin_ref[...])
    key_cos, key_sin = key_tables(cos, sin)
    for h in range(heads):
        out, at = slice(h * PAIR, (h + 1) * PAIR), h * HEAD_PACK
        q_ref[:, out] = rotate_lanes(pre[:, at : at + PAIR], cos, sin).astype(bf16)
        kv_ref[:, out] = rotate_lanes(
            pre[:, at + PAIR : at + HEAD_PACK], key_cos, key_sin
        ).astype(bf16)


def project(place, places, blocks, spots, weights, rows, width, cos, sin):
    span = cos.shape[0]
    cols = weights[0].shape[-1]
    heads = (cols - LANES) // HEAD_PACK
    table = pl.BlockSpec((rows, HEAD_SIZE // 2), lambda i, h: (i, 0))
    token_rows = pl.BlockSpec((rows, width), lambda i, h: (i, 0))
    head_rows = pl.BlockSpec((rows, heads * PAIR), lambda i, h: (i, 0))
    shape = weights[0].shape if spots is None else (
        weights[0].shape[0], len(spots), weights[0].shape[1], cols
    )
    return pl.pallas_call(
        functools.partial(project_kernel, places, spots),
        grid_spec=pltpu.PrefetchScalarGridSpec(
            num_scalar_prefetch=1,
            grid=(span // rows,),
            in_specs=[pl.BlockSpec(memory_space=pl.ANY)] * (len(blocks) + len(weights))
            + [table, table],
            out_specs=[
                head_rows,
                head_rows,
                token_rows,
                pl.BlockSpec(shape, lambda i, h: (0,) * len(shape)),
            ],
            scratch_shapes=[
                pltpu.VMEM((8, width), f32),
                pltpu.VMEM((span // rows, rows, width), bf16),
                pltpu.SemaphoreType.DMA((span // rows + len(weights),)),
            ],
        ),
        out_shape=[
            jax.ShapeDtypeStruct((span, heads * PAIR), bf16),
            jax.ShapeDtypeStruct((span, heads * PAIR), bf16),
            jax.ShapeDtypeStruct((span, width), bf16),
            jax.ShapeDtypeStruct(shape, bf16),
        ],
        compiler_params=pltpu.CompilerParams(vmem_limit_bytes=VMEM_LIMIT),
        cost_estimate=pl.CostEstimate(
            flops=2 * span * width * heads * HEAD_PACK, bytes_accessed=8 * 2**20, transcendentals=0
        ),
        name="project",
    )(place, *blocks, *weights, cos, sin)


def spread_kernel(cos_ref, sin_ref, wide_cos_ref, wide_sin_ref):
    wide_cos_ref[...], wide_sin_ref[...] = spread_tables(cos_ref[...], sin_ref[...])


def spread(cos, sin):
    rows = cos.shape[0]
    wide = jax.ShapeDtypeStruct((rows, PAIR), f32)
    return pl.pallas_call(
        spread_kernel,
        grid=(4,),
        in_specs=[pl.BlockSpec((rows // 4, HEAD_SIZE // 2), lambda i: (i, 0))] * 2,
        out_specs=[pl.BlockSpec((rows // 4, PAIR), lambda i: (i, 0))] * 2,
        out_shape=[wide, wide],
        cost_estimate=pl.CostEstimate(flops=2**20, bytes_accessed=4 * 2**20, transcendentals=0),
        name="spread",
    )(cos, sin)


def head_grads_kernel(place_ref, own_ref, other_ref, w_ref, small_ref, grad_ref, out_ref, acc, sums, gain):
    i = pl.program_id(0)
    half = pl.num_programs(0) // 2

    @pl.when(i == 0)
    def _():
        acc[...] = jnp.zeros_like(acc)
        sums[...] = jnp.zeros_like(sums)
        gain[...] = jnp.transpose(small_ref[...].astype(f32))[:8, :]

    grad = grad_ref[...]
    x = jnp.where(i < half, own_ref[...], other_ref[...]).astype(f32)
    inverse = lax.rsqrt(jnp.mean(x * x, axis=-1, keepdims=True) + NORM_EPS)
    x = x * inverse
    acc[...] += contract_rows(grad, (x * gain[0:1, :]).astype(bf16))
    back = contract_cols(grad, w_ref[...]) * x
    sums[...] += jnp.sum(back.reshape(back.shape[0] // 8, 8, back.shape[1]), axis=0)

    @pl.when(i == pl.num_programs(0) - 1)
    def _():
        out_ref[:, :HEAD_PACK] = jnp.transpose(acc[...]).astype(bf16)
        total = jnp.sum(sums[...], axis=0, keepdims=True)
        rows = lax.broadcasted_iota(jnp.int32, (LANES, total.shape[1]), 0)
        out_ref[:, HEAD_PACK:] = jnp.transpose(
            jnp.where(rows == 0, jnp.broadcast_to(total, rows.shape), 0.0)
        ).astype(bf16)


def head_grads(own, other, first, second, stride, head_at, weights, grads):
    span, pack = grads.shape
    width = own.shape[1]
    rows = BLOCK
    half = span // rows // 2
    small_at = weights.shape[1] // LANES - 1

    def grads_at(i, s):
        return (jnp.where(i < half, s[0] + stride * i, s[1] + stride * (i - half)), 0)

    return pl.pallas_call(
        head_grads_kernel,
        grid_spec=pltpu.PrefetchScalarGridSpec(
            num_scalar_prefetch=1,
            grid=(span // rows,),
            in_specs=[
                pl.BlockSpec((rows, width), lambda i, s: (jnp.minimum(i, half - 1), 0)),
                pl.BlockSpec((rows, width), lambda i, s: (jnp.maximum(i - half, 0), 0)),
                pl.BlockSpec((width, pack), lambda i, s: (0, s[2])),
                pl.BlockSpec((width, LANES), lambda i, s: (0, small_at)),
                pl.BlockSpec((rows, pack), grads_at),
            ],
            out_specs=pl.BlockSpec((width, pack + LANES), lambda i, s: (0, 0)),
            scratch_shapes=[
                pltpu.VMEM((pack, width), f32),
                pltpu.VMEM((8, width), f32),
                pltpu.VMEM((8, width), f32),
            ],
        ),
        out_shape=jax.ShapeDtypeStruct((width, pack + LANES), bf16),
        compiler_params=pltpu.CompilerParams(vmem_limit_bytes=VMEM_LIMIT),
        cost_estimate=pl.CostEstimate(
            flops=4 * span * width * pack, bytes_accessed=8 * 2**20, transcendentals=0
        ),
        name="head_grads",
    )(jnp.stack([first, second, head_at]), own, other, weights, weights, grads)


def lower_lanes(shape):
    return lax.broadcasted_iota(jnp.int32, shape, len(shape) - 1) < HEAD_SIZE


def both_heads_low(pair):
    low = lower_lanes(pair.shape)
    return jnp.concatenate(
        [jnp.where(low, pair, 0.0), jnp.where(low, pltpu.roll(pair, HEAD_SIZE, 1), 0.0)], axis=0
    )


def both_heads_high(pair):
    low = lower_lanes(pair.shape)
    return jnp.concatenate(
        [jnp.where(low, 0.0, pltpu.roll(pair, HEAD_SIZE, 1)), jnp.where(low, 0.0, pair)], axis=0
    )


def block_bounds(bounds_ref, tile, tiles, stride):
    place = bounds_ref[2 * tiles] + stride * (QUERY_BLOCK // BLOCK) * tile
    full = jnp.minimum(bounds_ref[tiles + tile], place)
    return place, bounds_ref[tile], full, place + stride * (QUERY_BLOCK // BLOCK - 1) + 1


def pair_mask(doc, place, stride):
    doc = jnp.concatenate([doc, doc], axis=1)
    lane = lax.broadcasted_iota(jnp.int32, doc.shape, 1) % QUERY_BLOCK
    queries = (place + stride * (lane // BLOCK)) * BLOCK + lane % BLOCK

    def masked(scores, start):
        keys = lax.broadcasted_iota(jnp.int32, scores.shape, 0) + start
        return jnp.where((keys >= doc) & (keys <= queries), scores, NEGATIVE_HUGE)

    return masked


def attend_kernel(stride, bounds_ref, q_ref, kv_ref, doc_ref, o_ref, low_ref, lse_ref, acc):
    place, first, full, end = block_bounds(
        bounds_ref, pl.program_id(1), pl.num_programs(1), stride
    )
    q = both_heads_low(q_ref[...].astype(f32) * SCALE_OF_SCORES).astype(bf16)
    masked = pair_mask(doc_ref[0], place, stride)
    acc[...] = jnp.zeros_like(acc)

    def step(mask, j, carried):
        top, total = carried
        start = pl.multiple_of(j * BLOCK, BLOCK)
        kv = kv_ref[pl.ds(start, BLOCK), :]
        scores = contract_cols(kv, q)
        if mask:
            scores = masked(scores, start)
        new = jnp.maximum(top, jnp.max(scores, axis=0, keepdims=True))
        probs = jnp.exp(scores - new)
        keep = jnp.exp(top - new)
        acc[...] = acc[...] * keep + contract_rows(kv, probs.astype(bf16))
        return new, total * keep + jnp.sum(probs, axis=0, keepdims=True)

    row = (1, 2 * QUERY_BLOCK)
    carried = (jnp.full(row, NEGATIVE_HUGE, f32), jnp.zeros(row, f32))
    carried = lax.fori_loop(first, full, functools.partial(step, True), carried)
    carried = lax.fori_loop(full, place, functools.partial(step, False), carried)
    top, total = lax.fori_loop(place, end, functools.partial(step, True), carried)
    mixed = jnp.transpose(acc[...] / total)
    one, two = mixed[:QUERY_BLOCK], mixed[QUERY_BLOCK:]
    out = jnp.where(lower_lanes(one.shape), pltpu.roll(one, HEAD_SIZE, 1), two)
    o_ref[...] = out
    low_ref[...] = out.astype(bf16)
    lse_ref[0, 0] = top + jnp.log(total)


def attend(bounds, q, kv, doc, stride):
    (queries, cols), keys = q.shape, kv.shape[0]
    heads, tiles = cols // PAIR, queries // QUERY_BLOCK
    pair = pl.BlockSpec((QUERY_BLOCK, PAIR), lambda h, i, s: (i, h))
    return pl.pallas_call(
        functools.partial(attend_kernel, stride),
        grid_spec=pltpu.PrefetchScalarGridSpec(
            num_scalar_prefetch=1,
            grid=(heads, tiles),
            in_specs=[
                pair,
                pl.BlockSpec((keys, PAIR), lambda h, i, s: (0, h)),
                pl.BlockSpec((1, 1, QUERY_BLOCK), lambda h, i, s: (i, 0, 0)),
            ],
            out_specs=[
                pair,
                pair,
                pl.BlockSpec((1, 1, 1, 2 * QUERY_BLOCK), lambda h, i, s: (h, i, 0, 0)),
            ],
            scratch_shapes=[pltpu.VMEM((PAIR, 2 * QUERY_BLOCK), f32)],
        ),
        out_shape=[
            jax.ShapeDtypeStruct((queries, cols), f32),
            jax.ShapeDtypeStruct((queries, cols), bf16),
            jax.ShapeDtypeStruct((heads, tiles, 1, 2 * QUERY_BLOCK), f32),
        ],
        compiler_params=pltpu.CompilerParams(vmem_limit_bytes=VMEM_LIMIT),
        cost_estimate=pl.CostEstimate(
            flops=4 * queries * keys * cols,
            bytes_accessed=6 * 2**20,
            transcendentals=queries * keys * heads,
        ),
        name="attend",
    )(bounds, q, kv, doc)


def attend_back_kernel(
    fold, bounds_ref, q_ref, kv_ref, doc_ref, do_ref, o_ref, lse_ref, cos_ref, sin_ref, *refs
):
    if fold:
        out_ref, acc, dkv_ref = refs
    else:
        dq_ref, dkv_ref, acc = refs
    i = pl.program_id(0)
    place, first, full, end = block_bounds(bounds_ref, i, pl.num_programs(0), 1)

    @pl.when(i == 0)
    def _():
        dkv_ref[...] = jnp.zeros_like(dkv_ref)

    q = both_heads_low(q_ref[...].astype(f32) * SCALE_OF_SCORES).astype(bf16)
    grad = do_ref[...].astype(f32)
    product = jnp.transpose(grad * o_ref[...])
    delta = jnp.concatenate(
        [
            jnp.sum(product[:HEAD_SIZE], axis=0, keepdims=True),
            jnp.sum(product[HEAD_SIZE:], axis=0, keepdims=True),
        ],
        axis=1,
    )
    grad = both_heads_high(grad).astype(bf16)
    sources = jnp.concatenate([q, grad], axis=0)
    masked = pair_mask(doc_ref[0], place, 1)
    lse = lse_ref[0]
    acc[...] = jnp.zeros_like(acc)

    def step(mask, j, carried):
        start = pl.multiple_of(j * BLOCK, BLOCK)
        kv = kv_ref[pl.ds(start, BLOCK), :]
        scores = contract_cols(kv, q) - lse
        if mask:
            scores = masked(scores, start)
        probs = jnp.exp(scores)
        grad_scores = (probs * (contract_cols(kv, grad) - delta)).astype(bf16)
        acc[...] += contract_rows(kv, grad_scores)
        both = jnp.concatenate([grad_scores, probs.astype(bf16)], axis=1)
        dkv_ref[pl.ds(start, BLOCK), :] += jnp.dot(both, sources, preferred_element_type=f32)
        return carried

    lax.fori_loop(first, full, functools.partial(step, True), 0)
    lax.fori_loop(full, place, functools.partial(step, False), 0)
    lax.fori_loop(place, end, functools.partial(step, True), 0)
    dq = jnp.transpose(acc[...])
    one, two = dq[:QUERY_BLOCK], dq[QUERY_BLOCK:]
    dq = jnp.where(lower_lanes(one.shape), one, pltpu.roll(two, HEAD_SIZE, 1))
    if not fold:
        dq_ref[...] = dq
        return
    mine = pl.ds(pl.multiple_of(i * QUERY_BLOCK, QUERY_BLOCK), QUERY_BLOCK)
    out_ref[mine, :PAIR] = rotate_lanes(
        dq * SCALE_OF_SCORES, cos_ref[mine, :], -sin_ref[mine, :]
    ).astype(bf16)

    @pl.when(i == pl.num_programs(0) - 1)
    def _():
        def finish(j, carried):
            part = pl.ds(pl.multiple_of(j * BLOCK, BLOCK), BLOCK)
            cos, sin = key_tables(cos_ref[part, :], sin_ref[part, :])
            out_ref[part, PAIR:] = rotate_lanes(dkv_ref[part, :], cos, -sin).astype(bf16)
            return carried

        lax.fori_loop(0, dkv_ref.shape[0] // BLOCK, finish, 0)


def attend_back(bounds, q, kv, doc, grad, out, lse, cos, sin, fold):
    queries, keys = q.shape[0], kv.shape[0]
    steps = queries // QUERY_BLOCK
    pair = pl.BlockSpec((QUERY_BLOCK, PAIR), lambda i, s: (i, 0))
    whole = pl.BlockSpec((keys, PAIR), lambda i, s: (0, s[2 * steps + 1]))
    doc_row = pl.BlockSpec((1, 1, QUERY_BLOCK), lambda i, s: (i, 0, 0))
    lse_row = pl.BlockSpec((1, 1, 2 * QUERY_BLOCK), lambda i, s: (i, 0, 0))
    table = pl.BlockSpec(cos.shape, lambda i, s: (0, 0))
    acc = pltpu.VMEM((PAIR, 2 * QUERY_BLOCK), f32)
    if fold:
        out_specs = pl.BlockSpec((queries, HEAD_PACK), lambda i, s: (0, 0))
        out_shape = jax.ShapeDtypeStruct((queries, HEAD_PACK), bf16)
        scratch = [acc, pltpu.VMEM((keys, PAIR), f32)]
    else:
        out_specs = [pair, pl.BlockSpec((keys, PAIR), lambda i, s: (0, 0))]
        out_shape = [
            jax.ShapeDtypeStruct((queries, PAIR), f32),
            jax.ShapeDtypeStruct((keys, PAIR), f32),
        ]
        scratch = [acc]
    return pl.pallas_call(
        functools.partial(attend_back_kernel, fold),
        grid_spec=pltpu.PrefetchScalarGridSpec(
            num_scalar_prefetch=1,
            grid=(steps,),
            in_specs=[pair, whole, doc_row, pair, pair, lse_row, table, table],
            out_specs=out_specs,
            scratch_shapes=scratch,
        ),
        out_shape=out_shape,
        compiler_params=pltpu.CompilerParams(vmem_limit_bytes=VMEM_LIMIT),
        cost_estimate=pl.CostEstimate(
            flops=10 * queries * keys * PAIR,
            bytes_accessed=8 * 2**20,
            transcendentals=queries * keys,
        ),
        name="attend_back",
    )(bounds, q, kv, doc, grad, out, lse, cos, sin)


def unrotate_kernel(dq_ref, dkv_ref, cos_ref, sin_ref, out_ref):
    cos, sin = cos_ref[...], sin_ref[...]
    dq = rotate_lanes(dq_ref[...] * SCALE_OF_SCORES, cos, -sin)
    cos, sin = key_tables(cos, sin)
    dkv = rotate_lanes(dkv_ref[...], cos, -sin)
    out_ref[...] = jnp.concatenate([dq, dkv], axis=1).astype(bf16)


def unrotate(dq, dkv, cos, sin):
    rows = dq.shape[0]
    pair = pl.BlockSpec((BLOCK, PAIR), lambda i: (i, 0))
    return pl.pallas_call(
        unrotate_kernel,
        grid=(rows // BLOCK,),
        in_specs=[pair, pair, pair, pair],
        out_specs=pl.BlockSpec((BLOCK, HEAD_PACK), lambda i: (i, 0)),
        out_shape=jax.ShapeDtypeStruct((rows, HEAD_PACK), bf16),
        cost_estimate=pl.CostEstimate(
            flops=rows * HEAD_PACK * 8, bytes_accessed=rows * HEAD_PACK * 14, transcendentals=0
        ),
        name="unrotate",
    )(dq, dkv, cos, sin)


def place_experts_kernel(place_ref, *refs):
    blocks, (ct_ref, w_ref, z_ref, sems) = refs[:10], refs[10:]
    core = place_ref[1]
    rows = w_ref.shape[1] // 2
    half = rows // 2
    sources = [[(0, 0, rows)], [(1, 0, rows)], [(2, 0, rows)], [(3, 0, half), (4, half, half)]]
    for step, parts in enumerate(sources):

        @pl.when(pl.program_id(0) == step)
        def _(parts=parts):
            copies = []
            for source, start, length in parts:
                for other in (0, 1):
                    first = jnp.where(core == other, 0, rows) + start
                    at = pl.ds(pl.multiple_of(first, half), length)
                    copies.append(
                        pltpu.make_async_copy(
                            blocks[2 * source + other], w_ref.at[0, at, :], sems.at[len(copies)]
                        )
                    )
            for copy in copies:
                copy.start()
            for copy in copies:
                copy.wait()

    z_ref[0] = jnp.dot(ct_ref[...], w_ref[0, :, 2 * F :], preferred_element_type=f32)


def place_experts(place, parts, early, width):
    rows = early.shape[0]
    blocks = [block for pair in parts for block in pair]
    return pl.pallas_call(
        place_experts_kernel,
        grid_spec=pltpu.PrefetchScalarGridSpec(
            num_scalar_prefetch=1,
            grid=(EXPERTS_HERE,),
            in_specs=[pl.BlockSpec(memory_space=pl.ANY)] * len(blocks)
            + [pl.BlockSpec((rows, width), lambda r, s: (0, 0))],
            out_specs=[
                pl.BlockSpec((1, width, 3 * F), lambda r, s: (s[0] ^ r, 0, 0)),
                pl.BlockSpec((1, rows, F), lambda r, s: (s[0] ^ r, 0, 0)),
            ],
            scratch_shapes=[pltpu.SemaphoreType.DMA((4,))],
        ),
        out_shape=[
            jax.ShapeDtypeStruct((EXPERTS_HERE, width, 3 * F), bf16),
            jax.ShapeDtypeStruct((EXPERTS_HERE, rows, F), f32),
        ],
        compiler_params=pltpu.CompilerParams(vmem_limit_bytes=VMEM_LIMIT),
        cost_estimate=pl.CostEstimate(
            flops=2 * EXPERTS_HERE * rows * width * F, bytes_accessed=36 * 2**20, transcendentals=0
        ),
        name="place_experts",
    )(place, *blocks, early)


def lane_column(x, at):
    lane = lax.broadcasted_iota(jnp.int32, x.shape, 1)
    return jnp.sum(jnp.where(lane == at, x, 0.0), axis=1, keepdims=True)


def experts_kernel(
    group_ref, n_ref, routed_ref, router_ref, w_ref, z_ref,
    back_ref, gates_ref, hidden_ref, pre_ref, acc, dots,
):
    e = pl.program_id(0)
    own = group_ref[0] * EXPERTS_HERE + e
    rows = n_ref.shape[0]

    @pl.when(e == 0)
    def _():
        logits = jnp.dot(n_ref[...], router_ref[...], preferred_element_type=f32)
        routed = routed_ref[...].astype(f32) > 0.5
        highest = jnp.max(jnp.where(routed, logits, NEGATIVE_HUGE), axis=1, keepdims=True)
        weights = jnp.where(routed, jnp.exp(jnp.where(routed, logits - highest, 0.0)), 0.0)
        gates_ref[...] = weights / jnp.sum(weights, axis=1, keepdims=True)
        acc[...] = jnp.zeros_like(acc)
        dots[...] = jnp.zeros_like(dots)

    w_in = w_ref[0, :, : 2 * F]
    for t in range(rows // BLOCK):
        part = pl.ds(t * BLOCK, BLOCK)
        pre = jnp.dot(n_ref[part, :], w_in, preferred_element_type=f32)
        gate, up = pre[:, :F], pre[:, F:]
        z = z_ref[0, part, :]
        weight = lane_column(gates_ref[part, :], own)
        sig = 1.0 / (1.0 + jnp.exp(-gate))
        act = gate * sig
        hidden = act * up
        hidden_ref[0, part, :] = (weight * hidden).astype(bf16)
        dot = RESIDUAL_SCALE * jnp.sum(hidden.astype(bf16).astype(f32) * z, axis=1, keepdims=True)
        lane = lax.broadcasted_iota(jnp.int32, (BLOCK, LANES), 1)
        dots[part, :] += jnp.where(lane == own, dot, 0.0)
        scaled = (RESIDUAL_SCALE * weight) * z
        pre_ref[0, part, :F] = (scaled * up * (sig + act * (1.0 - sig))).astype(bf16)
        pre_ref[0, part, F:] = (scaled * act).astype(bf16)
        acc[part, :] += contract_cols(pre_ref[0, part, :], w_in)

    @pl.when(e == EXPERTS_HERE - 1)
    def _():
        width = n_ref.shape[1]
        back_ref[:, :width] = acc[...].astype(bf16)
        high = dots[...].astype(bf16)
        low = dots[...] - high.astype(f32)
        back_ref[:, width:] = (high.astype(f32) + pltpu.roll(low, E, 1)).astype(bf16)


def experts(group, normed, early, packed, w_all, z):
    rows, width = normed.shape
    count = w_all.shape[0]
    whole = pl.BlockSpec((rows, width), lambda e, g: (0, 0))
    column = width // LANES
    router_at = packed.shape[1] // LANES - 1
    return pl.pallas_call(
        experts_kernel,
        grid_spec=pltpu.PrefetchScalarGridSpec(
            num_scalar_prefetch=1,
            grid=(count,),
            in_specs=[
                whole,
                pl.BlockSpec((rows, LANES), lambda e, g: (0, column)),
                pl.BlockSpec((width, LANES), lambda e, g: (0, router_at)),
                pl.BlockSpec((1, width, 3 * F), lambda e, g: (e, 0, 0)),
                pl.BlockSpec((1, rows, F), lambda e, g: (e, 0, 0)),
            ],
            out_specs=[
                pl.BlockSpec((rows, width + LANES), lambda e, g: (0, 0)),
                pl.BlockSpec((rows, LANES), lambda e, g: (0, 0)),
                pl.BlockSpec((1, rows, F), lambda e, g: (e, 0, 0)),
                pl.BlockSpec((1, rows, 2 * F), lambda e, g: (e, 0, 0)),
            ],
            scratch_shapes=[pltpu.VMEM((rows, width), f32), pltpu.VMEM((rows, LANES), f32)],
        ),
        out_shape=[
            jax.ShapeDtypeStruct((rows, width + LANES), bf16),
            jax.ShapeDtypeStruct((rows, LANES), f32),
            jax.ShapeDtypeStruct((count, rows, F), bf16),
            jax.ShapeDtypeStruct((count, rows, 2 * F), bf16),
        ],
        compiler_params=pltpu.CompilerParams(vmem_limit_bytes=VMEM_LIMIT),
        cost_estimate=pl.CostEstimate(
            flops=2 * count * rows * width * 4 * F, bytes_accessed=40 * 2**20, transcendentals=0
        ),
        name="experts",
    )(group, normed, early, packed, w_all, z)


def expert_grads_kernel(with_y, half_ref, n_ref, ct_ref, w_ref, hidden_ref, pre_ref, *refs):
    if with_y:
        left_ref, right_ref, y_ref, n_t, ct_t, acc = refs
    else:
        left_ref, right_ref, n_t, ct_t = refs
    e = pl.program_id(0)
    cut = left_ref.shape[2]

    @pl.when(e == 0)
    def _():
        n_t[...] = jnp.transpose(n_ref[...])
        ct_t[...] = jnp.transpose(ct_ref[...])
        if with_y:
            acc[...] = jnp.zeros_like(acc)

    grads = jnp.dot(n_t[...], pre_ref[0], preferred_element_type=f32).astype(bf16)
    left_ref[0] = grads[:, :cut]
    right_ref[0, :, : 2 * F - cut] = grads[:, cut:]
    right_ref[0, :, 2 * F - cut :] = (
        RESIDUAL_SCALE * jnp.dot(ct_t[...], hidden_ref[0], preferred_element_type=f32)
    ).astype(bf16)
    if not with_y:
        return
    acc[...] += contract_cols(hidden_ref[0], w_ref[0, :, 2 * F :])

    @pl.when(e == pl.num_programs(0) - 1)
    def _():
        y_ref[...] = acc[...].astype(bf16)


def expert_grads(half, halves, normed, early, w_all, hidden, pre, with_y):
    rows, width = normed.shape
    count = w_all.shape[0]
    own, cut = width // halves, 3 * F // 2
    feature = pl.BlockSpec((rows, own), lambda e, h: (0, h[0]))
    out_specs = [pl.BlockSpec((1, own, cut), lambda e, h: (e, 0, 0))] * 2
    out_shape = [jax.ShapeDtypeStruct((count, own, cut), bf16)] * 2
    scratch = [pltpu.VMEM((own, rows), bf16), pltpu.VMEM((own, rows), bf16)]
    if with_y:
        out_specs.append(pl.BlockSpec((rows, width), lambda e, h: (0, 0)))
        out_shape.append(jax.ShapeDtypeStruct((rows, width), bf16))
        scratch.append(pltpu.VMEM((rows, width), f32))
    return pl.pallas_call(
        functools.partial(expert_grads_kernel, with_y),
        grid_spec=pltpu.PrefetchScalarGridSpec(
            num_scalar_prefetch=1,
            grid=(count,),
            in_specs=[
                feature,
                feature,
                pl.BlockSpec((1, width, 3 * F), lambda e, h: (e, 0, 0)),
                pl.BlockSpec((1, rows, F), lambda e, h: (e, 0, 0)),
                pl.BlockSpec((1, rows, 2 * F), lambda e, h: (e, 0, 0)),
            ],
            out_specs=out_specs,
            scratch_shapes=scratch,
        ),
        out_shape=out_shape,
        compiler_params=pltpu.CompilerParams(vmem_limit_bytes=VMEM_LIMIT),
        cost_estimate=pl.CostEstimate(
            flops=2 * count * rows * width * 3 * F // halves + 2 * with_y * count * rows * width * F,
            bytes_accessed=30 * 2**20,
            transcendentals=0,
        ),
        name="expert_grads",
    )(half, normed, early, w_all, hidden, pre)


def join_kernel(place_ref, o_ref, w_ref, small_ref, x_ref, normed_ref, resid_ref, own_ref, gain):
    t = pl.program_id(0)

    @pl.when(t == 0)
    def _():
        gain[...] = jnp.transpose(small_ref[...].astype(f32))[E : E + 8, :]

    attended = jnp.concatenate([o_ref[a] for a in range(o_ref.shape[0])], axis=1)
    resid = x_ref[...].astype(f32) + RESIDUAL_SCALE * jnp.dot(
        attended, w_ref[...], preferred_element_type=f32
    )
    normed_ref[...] = rms_scale(resid, gain[1:2, :]).astype(bf16)

    @pl.when(t == place_ref[0])
    def _():
        resid_ref[...] = resid
        own_ref[...] = attended


def join(place, outs, packed, weights_at, x):
    width = packed.shape[0]
    lines, tokens, cols = outs.shape
    rows = tokens // lines
    small_at = packed.shape[1] // LANES - 1
    own = pl.BlockSpec((rows, width), lambda t, s: (0, 0))
    return pl.pallas_call(
        join_kernel,
        grid_spec=pltpu.PrefetchScalarGridSpec(
            num_scalar_prefetch=1,
            grid=(lines,),
            in_specs=[
                pl.BlockSpec((lines, rows, cols), lambda t, s: (0, t, 0)),
                pl.BlockSpec((width, width), lambda t, s: (0, weights_at)),
                pl.BlockSpec((width, LANES), lambda t, s: (0, small_at)),
                pl.BlockSpec((rows, width), lambda t, s: (t, 0)),
            ],
            out_specs=[pl.BlockSpec((rows, width), lambda t, s: (t, 0)), own, own],
            scratch_shapes=[pltpu.VMEM((8, width), f32)],
        ),
        out_shape=[
            jax.ShapeDtypeStruct((lines * rows, width), bf16),
            jax.ShapeDtypeStruct((rows, width), f32),
            jax.ShapeDtypeStruct((rows, width), bf16),
        ],
        compiler_params=pltpu.CompilerParams(vmem_limit_bytes=VMEM_LIMIT),
        cost_estimate=pl.CostEstimate(
            flops=2 * lines * rows * width * width, bytes_accessed=12 * 2**20, transcendentals=0
        ),
        name="join",
    )(place, outs, packed, packed, x)


def token_grads_kernel(grad_ref, w_ref, small_ref, x_ref, resid_ref, out_ref, acc):
    h = pl.program_id(0)
    part = contract_cols(grad_ref[0], w_ref[...])

    @pl.when(h == 0)
    def _():
        acc[...] = part

    @pl.when(h > 0)
    def _():
        acc[...] += part

    @pl.when(h == pl.num_programs(0) - 1)
    def _():
        gain = jnp.transpose(small_ref[...].astype(f32))[E : E + 1, :]
        x = x_ref[...].astype(f32)
        inverse = lax.rsqrt(jnp.mean(x * x, axis=-1, keepdims=True) + NORM_EPS)
        scaled = acc[...] * gain
        mean = jnp.mean(x * scaled, axis=-1, keepdims=True)
        out_ref[...] = resid_ref[...] + (inverse * scaled - x * inverse**3 * mean)


def token_grads(grads, weights, packed, x, resid):
    heads, rows, pack = grads.shape
    width = x.shape[1]
    small_at = packed.shape[1] // LANES - 1
    whole = pl.BlockSpec((rows, width), lambda h: (0, 0))
    return pl.pallas_call(
        token_grads_kernel,
        grid=(heads,),
        in_specs=[
            pl.BlockSpec((1, rows, pack), lambda h: (h, 0, 0)),
            pl.BlockSpec((width, pack), lambda h: (0, h)),
            pl.BlockSpec((width, LANES), lambda h: (0, small_at)),
            whole,
            whole,
        ],
        out_specs=whole,
        out_shape=jax.ShapeDtypeStruct((rows, width), f32),
        scratch_shapes=[pltpu.VMEM((rows, width), f32)],
        compiler_params=pltpu.CompilerParams(vmem_limit_bytes=VMEM_LIMIT),
        cost_estimate=pl.CostEstimate(
            flops=2 * rows * width * heads * pack, bytes_accessed=8 * 2**20, transcendentals=0
        ),
        name="token_grads",
    )(grads, weights, packed, x, resid)


def weight_sums_kernel(sums_ref, q_ref, k_ref, v_ref, gain_ref):
    groups, heads, members = sums_ref.shape[:3]
    gain = jnp.zeros(gain_ref.shape, f32)
    values = []
    for h in range(heads):
        total = jnp.zeros(sums_ref.shape[3:], f32)
        for g in range(groups):
            for member in range(members):
                total += sums_ref[g, h, member].astype(f32)
        values.append(total)
        gain += total[:, HEAD_PACK:]
        q_ref[:, h * PAIR : (h + 1) * PAIR] = total[:, :PAIR]
    gain_ref[...] = gain
    for h in range(0, heads, 2):
        one, two = values[h][:, PAIR:HEAD_PACK], values[h + 1][:, PAIR:HEAD_PACK]
        low = lower_lanes(one.shape)
        at = slice(h // 2 * PAIR, (h // 2 + 1) * PAIR)
        k_ref[:, at] = jnp.where(low, one, pltpu.roll(two, HEAD_SIZE, 1))
        v_ref[:, at] = jnp.where(low, pltpu.roll(one, HEAD_SIZE, 1), two)


def weight_sums(sums):
    rows, heads = sums.shape[3], sums.shape[1]
    return pl.pallas_call(
        weight_sums_kernel,
        out_shape=[
            jax.ShapeDtypeStruct((rows, heads * PAIR), f32),
            jax.ShapeDtypeStruct((rows, heads * HEAD_SIZE), f32),
            jax.ShapeDtypeStruct((rows, heads * HEAD_SIZE), f32),
            jax.ShapeDtypeStruct((rows, LANES), f32),
        ],
        compiler_params=pltpu.CompilerParams(vmem_limit_bytes=VMEM_LIMIT),
        cost_estimate=pl.CostEstimate(flops=2**20, bytes_accessed=2 * 2**20, transcendentals=0),
        name="weight_sums",
    )(sums)


def exchange(x, axes):
    return lax.all_to_all(x, axes, 0, 0, tiled=True)


def body(
    tokens,
    cotangent,
    segment_ids,
    routes,
    norm_attn,
    w_query,
    key_weight_matrix,
    value_weight_matrix,
    w_output,
    norm_moe,
    w_router,
    expert_in,
    expert_out,
):
    x_local = tokens[0].astype(f32)
    token_count, width = x_local.shape
    seg_row = segment_ids[0]
    group, member = lax.axis_index("a"), lax.axis_index("b")
    by_column = all(lax.axis_size(axis) == 2 for axis in PLANE)
    by_column = by_column and lax.axis_size(SEQ) == KEY_VALUE_HEADS
    head_axes = SEQ if by_column else ("b",)
    span = token_count * KEY_VALUE_HEADS
    span_start = 0 if by_column else group * span

    def start_of_doc(ids):
        return jnp.sum((seg_row[None, :] < ids[:, None]).astype(jnp.int32), axis=1)

    def tile_bounds(docs, place):
        tiles = docs.reshape(-1, QUERY_BLOCK)
        ends = (tiles[:, 0] // BLOCK, (tiles[:, -1] + BLOCK - 1) // BLOCK, jnp.stack(place))
        return jnp.concatenate(ends).astype(jnp.int32), tiles[:, None, :]

    def own_column(x):
        x = x.reshape((GROUPS, 2, token_count) + x.shape[1:])
        x = lax.dynamic_index_in_dim(x, member, 1, False)
        return x.reshape((GROUPS * token_count,) + x.shape[2:])

    doc_span = start_of_doc(lax.dynamic_slice_in_dim(seg_row, span_start, span))
    cos_span, sin_span = rotation_tables(span_start + jnp.arange(span, dtype=jnp.int32) - doc_span)
    zero = jnp.zeros_like(member)
    head_of_two = member if by_column else zero
    bounds, doc_rows = tile_bounds(doc_span, (zero + span_start // BLOCK, head_of_two))
    wide_cos, wide_sin = spread(cos_span, sin_span)
    if by_column:
        cos_ahead, sin_ahead = own_column(cos_span), own_column(sin_span)
        bounds_ahead, docs_ahead = tile_bounds(own_column(doc_span), (member,))
    else:
        cos_ahead, sin_ahead, bounds_ahead, docs_ahead = cos_span, sin_span, bounds, doc_rows

    own_rows = w_query.shape[0]
    by_head = jnp.concatenate(
        [
            w_query.astype(bf16).reshape(own_rows, KEY_VALUE_HEADS, PAIR),
            key_weight_matrix.astype(bf16).reshape(own_rows, KEY_VALUE_HEADS, HEAD_SIZE),
            value_weight_matrix.astype(bf16).reshape(own_rows, KEY_VALUE_HEADS, HEAD_SIZE),
        ],
        axis=2,
    ).reshape(own_rows, KEY_VALUE_HEADS * HEAD_PACK)
    qkv_width = KEY_VALUE_HEADS * HEAD_PACK
    expert_ids = jnp.arange(E, dtype=jnp.int32)
    routed_own = jnp.any(routes[0][:, :, None] == expert_ids[None, None, :], axis=1)
    small = jnp.concatenate(
        [
            w_router.astype(bf16),
            norm_attn.astype(bf16)[:, None],
            norm_moe.astype(bf16)[:, None],
        ],
        axis=1,
    )
    wide = width + LANES
    packed = (
        jnp.concatenate([cotangent[0], pad_lanes(routed_own.astype(bf16), LANES)], axis=1),
        jnp.concatenate([w_output.astype(bf16), pad_lanes(small, LANES)], axis=1),
        by_head[:, :wide],
        pad_lanes(by_head[:, wide:], wide),
    )
    lines = gather(jnp.concatenate(packed), "a").reshape(GROUPS, -1, wide)
    if by_column:
        two = by_head.reshape(own_rows, GROUPS, 2 * HEAD_PACK).transpose(1, 0, 2)
        gains = pad_lanes(norm_attn.astype(bf16)[:, None], LANES)
        gains = jnp.broadcast_to(gains, (GROUPS, own_rows, LANES))
        columns = exchange(jnp.repeat(jnp.concatenate([two, gains], axis=2), 2, axis=0), SEQ)
        from_y = lax.ppermute(columns, "y", SWAP)
        spots = ((0, 0), (0, 1), (1, 0), (1, 1))
        weights = (
            columns, lax.ppermute(columns, "c", SWAP), from_y, lax.ppermute(from_y, "c", SWAP)
        )
        pieces = line_gather(tokens[0])
        places = [piece[0] for piece in pieces]
        blocks = tuple(piece[1] for piece in pieces)
        lines, blocks, weights = lax.optimization_barrier((lines, blocks, weights))
    ends = [token_count + k * own_rows for k in range(4)]
    early_all = lines[:, : ends[0]].reshape(-1, wide)

    def across(x):
        x = gather(x.reshape(-1, x.shape[2]), PLANE).reshape(-1, GROUPS, own_rows, x.shape[2])
        return x.transpose(1, 0, 2, 3).reshape(-1, x.shape[3])

    second_all = across(lines[:, ends[0] : ends[1]])
    qkv_lines = jnp.concatenate(
        [lines[:, ends[1] : ends[2]], lines[:, ends[2] : ends[3], : qkv_width - wide]], axis=2
    )
    experts_low = jnp.concatenate([expert_in.astype(bf16), expert_out.astype(bf16)], axis=1)
    if not by_column:
        at = lax.axis_index(head_axes) * HEAD_PACK
        gains = pad_lanes(second_all[:, width + E : width + E + 1], LANES)
        spots, places = None, None
        weights = (
            jnp.concatenate(
                [lax.dynamic_slice_in_dim(across(qkv_lines), at, HEAD_PACK, 1), gains], axis=1
            ),
        )
        blocks = (gather(tokens[0], "b").reshape((-1,) + tokens.shape[1:]),)
    experts_low, blocks, weights, cos_ahead, sin_ahead, bounds_ahead, docs_ahead, wide_cos, wide_sin = (
        lax.optimization_barrier(
            (
                experts_low, blocks, weights, cos_ahead, sin_ahead, bounds_ahead, docs_ahead,
                wide_cos, wide_sin,
            )
        )
    )
    if by_column:
        beside = neighbours(experts_low)
    else:
        parts = gather(experts_low, PLANE)

    place = jnp.stack([lax.axis_index(axis) for axis in ALL])
    q, kv, x_span, own_weights = project(
        place, places, blocks, spots, weights, token_count, width, cos_ahead, sin_ahead
    )
    own_weights = own_weights.reshape(width, own_weights.shape[-1])
    if by_column:
        columns = (GROUPS, token_count)

        def in_row(own, other, shape):
            return by_columns(own.reshape(shape), other.reshape(shape), member)

        kv_other = lax.ppermute(kv, "b", SWAP)
        kv = in_row(kv, kv_other, columns + (2 * PAIR,)).reshape(span, 2 * PAIR)
    else:
        kv = gather(kv, "a")
    attention_result, attended, log_total = attend(
        bounds_ahead, q, kv, docs_ahead, 2 if by_column else 1
    )
    if by_column:
        attended, second_all = lax.optimization_barrier((attended, second_all))
        attended, early_all = lax.optimization_barrier((attended, early_all))
        outs = lax.all_gather(attended, "a", axis=0, tiled=False)
        parts = plane_gather(experts_low, *beside)

        def heads_apart(x, axis):
            mine = lax.dynamic_index_in_dim(x, member, axis, False)
            return mine, lax.dynamic_index_in_dim(x, 1 - member, axis, False)

        q, q_sent = heads_apart(q.reshape(-1, 2, PAIR), 1)
        attention_result, out_sent = heads_apart(attention_result.reshape(-1, 2, PAIR), 1)
        log_total, log_sent = heads_apart(log_total, 0)
        q_other, out_other, log_other = (
            lax.ppermute(x, "b", SWAP) for x in (q_sent, out_sent, log_sent)
        )
        home = jnp.stack([member * 2 + lax.axis_index("y"), lax.axis_index("c")])
        experts_all, grad_hidden = place_experts(home, parts, early_all, width)
        outs, experts_all, q_other, out_other, log_other = lax.optimization_barrier(
            (outs, experts_all, q_other, out_other, log_other)
        )
        normed_all, resid, attended_low = join(place, outs, second_all, 0, x_span)
        qkv_lines, outs = lax.optimization_barrier((qkv_lines, outs))
        normed_two = lax.dynamic_slice_in_dim(normed_all, group * token_count, token_count)
    else:
        attended_low = (
            exchange(attended.reshape(KEY_VALUE_HEADS, token_count, PAIR), head_axes)
            .transpose(1, 0, 2)
            .reshape(token_count, QUERY_HEADS * HEAD_SIZE)
        )
        attn_out = jnp.dot(attended_low, second_all[:, :width], preferred_element_type=f32)
        resid = x_local + RESIDUAL_SCALE * attn_out
        gain_two = second_all[:, width + E + 1].astype(f32)
        normed_two = rms_scale(resid, gain_two).astype(bf16)
        normed_all = gather(normed_two, "a")
        experts_all = parts.reshape(EXPERTS_HERE, width, 3 * F)
        grad_hidden = jnp.einsum(
            "td,edf->etf",
            early_all[:, :width],
            experts_all[:, :, 2 * F :],
            preferred_element_type=f32,
        )
    back_part, gates_all, gated_hidden, grad_pre = experts(
        group.reshape(1), normed_all, early_all, second_all, experts_all, grad_hidden
    )
    if by_column:
        q = in_row(q, q_other, columns + (PAIR,)).reshape(span, PAIR)
        attention_result = in_row(attention_result, out_other, columns + (PAIR,)).reshape(span, PAIR)

        def by_block(x):
            x = x.reshape(-1, 2, QUERY_BLOCK // BLOCK, BLOCK).transpose(0, 2, 1, 3)
            return x.reshape(GROUPS, 2, BLOCK)

        log_total = in_row(by_block(log_total), by_block(log_other), (GROUPS, 2, BLOCK))
        log_total = log_total.transpose(0, 2, 1, 3)
    log_total = log_total.reshape(-1, 1, 2 * QUERY_BLOCK)
    qkv_all = across(qkv_lines)
    if by_column:
        back_part, qkv_all = lax.optimization_barrier((back_part, qkv_all))
    back_own = scatter_sum(back_part, "a")
    inputs = (normed_all, early_all, experts_all, gated_hidden, grad_pre)
    if by_column:
        core = lax.axis_index("c")
        x_other = lax.ppermute(x_span, "b", SWAP)
        send = expert_grads((1 - core).reshape(1), 2, *inputs, False)
        arrived = [lax.ppermute(x, "c", SWAP) for x in send]
        *keep, moe_part = expert_grads(core.reshape(1), 2, *inputs, True)
        left, right = (
            halve_add(terms).reshape((2, 2) + terms[0].shape[1:]) for terms in zip(keep, arrived)
        )
        back_own, moe_part, left, right, x_other = lax.optimization_barrier(
            (back_own, moe_part, left, right, x_other)
        )
        left, right = halve_send(left, "y", 1), halve_send(right, "b", 0)
    else:
        *grads, moe_part = expert_grads(jnp.zeros((1,), jnp.int32), 1, *inputs, True)
        grad_experts = jnp.concatenate(grads, axis=2)
        back_own, moe_part, grad_experts = lax.optimization_barrier(
            (back_own, moe_part, grad_experts)
        )
        grad_experts = scatter_sum(grad_experts.reshape(EXPERTS_HERE * width, 3 * F), PLANE)
    back_own = back_own.astype(f32)
    moe_sum = scatter_sum(moe_part, "a")

    output_w = second_all[:, :width]
    router_w = second_all[:, width : width + E]
    gain_two_f = second_all[:, width + E + 1].astype(f32)
    grad_out = cotangent[0].astype(f32)
    gates = lax.dynamic_slice_in_dim(gates_all, group * token_count, token_count)[:, :E]
    gate_grads_own = back_own[:, width : width + E] + back_own[:, width + E : width + 2 * E]
    grad_logits = gates * (gate_grads_own - jnp.sum(gates * gate_grads_own, axis=-1, keepdims=True))
    grad_normed_two = back_own[:, :width] + jnp.dot(
        grad_logits, router_w.astype(f32).T, precision=HIGHEST_DOT
    )
    grad_router = jnp.dot(normed_two.astype(f32).T, grad_logits, precision=HIGHEST_DOT)
    grad_resid_norm, grad_gain_two = rms_back(resid, gain_two_f, grad_normed_two)
    grad_resid = grad_out + grad_resid_norm
    grad_attn_low = (RESIDUAL_SCALE * grad_resid).astype(bf16)
    grad_heads = contract_cols(grad_attn_low, output_w).astype(bf16)
    grad_mixed = exchange(
        grad_heads.reshape(token_count, KEY_VALUE_HEADS, PAIR).transpose(1, 0, 2), head_axes
    ).reshape(span, PAIR)
    small = jnp.concatenate([grad_router, grad_gain_two[:, None]], axis=1)
    second_part = jnp.concatenate(
        [contract_rows(attended_low, grad_attn_low), pad_lanes(small, LANES)], axis=1
    ).astype(bf16)
    cols = second_part.shape[1]
    second_part = second_part.reshape(GROUPS, -1, own_rows, cols).transpose(1, 0, 2, 3)
    if by_column:
        left, right = halve_add(left), halve_add(right)
        second_part, left, right, grad_mixed = lax.optimization_barrier(
            (second_part, left, right, grad_mixed)
        )
        left, right = halve_send(left, "b", 0), halve_send(right, "y", 0)
    rest = scatter_sum(second_part.reshape(-1, cols), PLANE)
    grads = attend_back(
        bounds, q, kv, doc_rows, grad_mixed, attention_result, log_total, wide_cos, wide_sin,
        by_column,
    )
    if by_column:
        left, right, moe_sum, grad_pack = lax.optimization_barrier((left, right, moe_sum, grads))
        first_part = head_grads(
            x_span, x_other, member, 1 - member, 2, member, own_weights, grad_pack
        )
    else:
        grad_kv = scatter_sum(grads[1].astype(bf16), "a").astype(f32)
        grad_pack = unrotate(grads[0], grad_kv, wide_cos, wide_sin)
        half = span // 2
        first_part = head_grads(
            x_span[:half], x_span[half:], zero, zero + half // BLOCK, 1, zero, own_weights, grad_pack
        )
    rest, first_part = lax.optimization_barrier((rest, first_part))
    rest = scatter_sum(rest, "a")
    by_tokens = exchange(grad_pack.reshape(KEY_VALUE_HEADS, token_count, HEAD_PACK), head_axes)
    by_tokens, first_part = lax.optimization_barrier((by_tokens, first_part))
    sums = exchange(first_part.reshape(-1, own_rows, first_part.shape[1]), ALL)
    grad_input = token_grads(by_tokens, qkv_all, second_all, tokens[0], grad_resid)
    sums, moe_sum, resid, grad_input = lax.optimization_barrier((sums, moe_sum, resid, grad_input))
    grad_q_w, grad_k_w, grad_v_w, grad_gain_one = weight_sums(
        sums.reshape(-1, KEY_VALUE_HEADS, lax.axis_size(("y", "c")), own_rows, first_part.shape[1])
    )
    rest = rest.astype(f32)
    layer_sum = resid + RESIDUAL_SCALE * moe_sum.astype(f32)
    if by_column:
        grad_experts = jnp.concatenate(
            [own.astype(f32) + other.astype(f32) for own, other in (left, right)], axis=1
        )
    else:
        grad_experts = grad_experts.astype(f32)
    return (
        layer_sum.astype(bf16)[None],
        grad_input[None],
        grad_gain_one[:, 0],
        grad_q_w,
        grad_k_w,
        grad_v_w,
        rest[:, :width],
        rest[:, width + E],
        rest[:, width : width + E],
        grad_experts[:, : 2 * F],
        grad_experts[:, 2 * F :],
    )


def solution(mesh):
    seq, row = mesh.shape["seq"], mesh.shape["row"]
    cut = Mesh(mesh.devices.reshape(GROUPS, seq // GROUPS, row // 2, 2), ALL)
    token_spec = P(("y", "c"), SEQ, None)
    row_spec = P(ALL, None)
    flat_spec = P(ALL)
    in_specs = (
        token_spec,
        token_spec,
        P(("y", "c"), None),
        token_spec,
        flat_spec,
        row_spec,
        row_spec,
        row_spec,
        row_spec,
        flat_spec,
        row_spec,
        row_spec,
        row_spec,
    )
    out_specs = (
        token_spec,
        token_spec,
        flat_spec,
        row_spec,
        row_spec,
        row_spec,
        row_spec,
        flat_spec,
        row_spec,
        row_spec,
        row_spec,
    )
    return jax.shard_map(body, mesh=cut, in_specs=in_specs, out_specs=out_specs, check_vma=False)
```

```python
import functools

import jax
import jax.numpy as jnp
from jax import lax
from jax.experimental import pallas as pl
from jax.experimental.pallas import tpu as pltpu
from jax.sharding import Mesh, PartitionSpec as P

QUERY_HEADS = 16
KEY_VALUE_HEADS = 8
HEAD_SIZE = 64
F = 512
E = 16
GROUPS = 4
EXPERTS_HERE = E // GROUPS
LANES = 128
PAIR = 2 * HEAD_SIZE
HEAD_PACK = 4 * HEAD_SIZE
BLOCK = 256
QUERY_BLOCK = 512

NORM_EPS = 1e-06
RESIDUAL_SCALE = 0.22
SCALE_OF_SCORES = 0.015625
ROPE_BASE = 10000.0
NEGATIVE_HUGE = -1e30
HIGHEST_DOT = lax.Precision.HIGHEST
VMEM_LIMIT = 60 * 1024 * 1024

PLANE = ("b", "y", "c")
SEQ = ("a", "b")
ALL = ("a", "b", "y", "c")

f32 = jnp.float32
bf16 = jnp.bfloat16


def rotation_tables(positions):
    half = HEAD_SIZE // 2
    freq = jnp.power(ROPE_BASE, -2.0 * jnp.arange(half, dtype=f32) / HEAD_SIZE)
    angle = positions.astype(f32)[:, None] * freq[None, :]
    return jnp.cos(angle), jnp.sin(angle)


def rms_back(values, gain, grad_norm):
    mean_square = jnp.mean(values * values, axis=-1, keepdims=True)
    inverse = lax.rsqrt(mean_square + NORM_EPS)
    scaled_grad = grad_norm * gain
    grad_values = inverse * scaled_grad - values * inverse**3 * jnp.mean(
        values * scaled_grad, axis=-1, keepdims=True
    )
    grad_gain = jnp.sum(grad_norm * values * inverse, axis=0)
    return (grad_values, grad_gain)


def rms_scale(values, gain):
    mean_square = jnp.mean(values * values, axis=-1, keepdims=True)
    return values * lax.rsqrt(mean_square + NORM_EPS) * gain


def contract_rows(left_side, right_side):
    return lax.dot_general(
        left_side, right_side, (((0,), (0,)), ((), ())), preferred_element_type=f32
    )


def contract_cols(left_side, right_side):
    return lax.dot_general(
        left_side, right_side, (((1,), (1,)), ((), ())), preferred_element_type=f32
    )


def gather(x, axes):
    return lax.all_gather(x, axes, axis=0, tiled=True)


def scatter_sum(x, axes):
    return lax.psum_scatter(x, axes, scatter_dimension=0, tiled=True)


def pad_lanes(x, lanes):
    return jnp.pad(x, ((0, 0), (0, lanes - x.shape[1])))


def line_pairs(n, step):
    return [(i, i + step) for i in range(n) if 0 <= i + step < n]


def grid_gather(x):
    n = lax.axis_size("a")

    def cross(block, ends):
        return lax.ppermute(
            block, SEQ, [(2 * i + j, 2 * i + 1 - j) for i in range(n) if ends(i) for j in (0, 1)]
        )

    pieces = [(0, 0, x), (0, 1, cross(x, lambda i: True))]
    up = down = x
    for k in range(1, n):
        up = lax.ppermute(up, "a", line_pairs(n, 1))
        down = lax.ppermute(down, "a", line_pairs(n, -1))
        pieces += [(-k, 0, up), (-k, 1, cross(up, lambda i: i >= k))]
        pieces += [(k, 0, down), (k, 1, cross(down, lambda i: i + k < n))]
    return pieces


def plane_gather(x):
    swap = [(0, 1), (1, 0)]
    half = x.shape[0] // 2
    from_y = lax.ppermute(x, "y", swap)
    from_b = lax.ppermute(x, "b", swap)
    upper = lax.ppermute(from_b[:half], "y", swap)
    lower = lax.ppermute(from_y[half:], "b", swap)
    return [
        (block, lax.ppermute(block, "c", swap)) for block in (x, from_y, from_b, upper, lower)
    ]


def halve_send(v, axis, at):
    me = lax.axis_index(axis)
    other = lax.ppermute(lax.dynamic_index_in_dim(v, 1 - me, at, False), axis, [(0, 1), (1, 0)])
    return lax.dynamic_index_in_dim(v, me, at, False), other


def halve_add(terms):
    own, other = terms
    return (own.astype(f32) + other.astype(f32)).astype(own.dtype)


def rotate_lanes(x, cos, sin):
    width = x.shape[-1]
    lane = lax.broadcasted_iota(jnp.int32, x.shape, x.ndim - 1)
    swapped = jnp.where(
        lane % HEAD_SIZE < HEAD_SIZE // 2,
        pltpu.roll(x, width - HEAD_SIZE // 2, x.ndim - 1),
        pltpu.roll(x, HEAD_SIZE // 2, x.ndim - 1),
    )
    return x * cos + swapped * sin


def spread_tables(cos, sin):
    return jnp.concatenate([cos] * 4, axis=1), jnp.concatenate([-sin, sin, -sin, sin], axis=1)


def key_tables(cos, sin):
    low = lower_lanes(cos.shape)
    return jnp.where(low, cos, 1.0), jnp.where(low, sin, 0.0)


def project_kernel(places, place_ref, *refs):
    count = 1 if places is None else len(places)
    blocks, refs = refs[:count], refs[count:]
    small_ref, w_ref, cos_ref, sin_ref, qkv_ref, normed_ref, x_ref = refs[:7]
    wide_cos_ref, wide_sin_ref, gain, held, sems = refs[7:]
    i = pl.program_id(0)
    slots = held.shape[0]

    @pl.when(i == 0)
    def _():
        if places is None:
            for slot in range(slots):
                pltpu.make_async_copy(blocks[0].at[slot], held.at[slot], sems.at[slot]).start()
        else:
            for (distance, crossed), block in zip(places, blocks):
                at = place_ref[1] + distance
                member = 1 - place_ref[2] if crossed else place_ref[2]

                @pl.when((at >= 0) & (at < slots // 2))
                def _(block=block, slot=2 * at + member):
                    pltpu.make_async_copy(block, held.at[slot], sems.at[slot]).start()

        gain[...] = jnp.transpose(small_ref[...].astype(f32))[E : E + 8, :]

    arrived = blocks[0].at[0] if places is None else blocks[0]
    pltpu.make_async_copy(arrived, held.at[i], sems.at[i]).wait()
    x = held[i]
    x_ref[...] = x
    normed = rms_scale(x.astype(f32), gain[0:1, :]).astype(bf16)
    normed_ref[...] = normed
    pre = jnp.dot(normed, w_ref[...], preferred_element_type=f32)
    cos, sin = spread_tables(cos_ref[...], sin_ref[...])
    wide_cos_ref[...] = cos
    wide_sin_ref[...] = sin
    qkv_ref[:, :PAIR] = rotate_lanes(pre[:, :PAIR], cos, sin).astype(bf16)
    qkv_ref[:, PAIR:] = rotate_lanes(pre[:, PAIR:], *key_tables(cos, sin)).astype(bf16)


def project(place, places, blocks, rows, packed, cos, sin):
    width = packed.shape[0]
    small_at = packed.shape[1] // LANES - 1
    span = cos.shape[0]
    table = pl.BlockSpec((rows, HEAD_SIZE // 2), lambda i, h: (i, 0))
    token_rows = pl.BlockSpec((rows, width), lambda i, h: (i, 0))
    return pl.pallas_call(
        functools.partial(project_kernel, places),
        grid_spec=pltpu.PrefetchScalarGridSpec(
            num_scalar_prefetch=1,
            grid=(span // rows,),
            in_specs=[pl.BlockSpec(memory_space=pl.ANY)] * len(blocks)
            + [
                pl.BlockSpec((width, LANES), lambda i, h: (0, small_at)),
                pl.BlockSpec((width, HEAD_PACK), lambda i, h: (0, h[0])),
                table,
                table,
            ],
            out_specs=[
                pl.BlockSpec((rows, HEAD_PACK), lambda i, h: (i, 0)),
                token_rows,
                token_rows,
                pl.BlockSpec((rows, PAIR), lambda i, h: (i, 0)),
                pl.BlockSpec((rows, PAIR), lambda i, h: (i, 0)),
            ],
            scratch_shapes=[
                pltpu.VMEM((8, width), f32),
                pltpu.VMEM((span // rows, rows, width), bf16),
                pltpu.SemaphoreType.DMA((span // rows,)),
            ],
        ),
        out_shape=[
            jax.ShapeDtypeStruct((span, HEAD_PACK), bf16),
            jax.ShapeDtypeStruct((span, width), bf16),
            jax.ShapeDtypeStruct((span, width), bf16),
            jax.ShapeDtypeStruct((span, PAIR), f32),
            jax.ShapeDtypeStruct((span, PAIR), f32),
        ],
        compiler_params=pltpu.CompilerParams(vmem_limit_bytes=VMEM_LIMIT),
        cost_estimate=pl.CostEstimate(
            flops=2 * span * width * HEAD_PACK, bytes_accessed=18 * 2**20, transcendentals=0
        ),
        name="project",
    )(place, *blocks, packed, packed, cos, sin)


def head_grads_kernel(head_ref, x_ref, normed_ref, w_ref, grad_ref, out_ref, acc, gain):
    i = pl.program_id(0)

    @pl.when(i == 0)
    def _():
        acc[...] = jnp.zeros_like(acc)
        gain[...] = jnp.zeros_like(gain)

    grad = grad_ref[...]
    acc[...] += contract_rows(grad, normed_ref[...])
    x = x_ref[...].astype(f32)
    inverse = lax.rsqrt(jnp.mean(x * x, axis=-1, keepdims=True) + NORM_EPS)
    back = contract_cols(grad, w_ref[...]) * (x * inverse)
    gain[...] += jnp.sum(back.reshape(back.shape[0] // 8, 8, back.shape[1]), axis=0)

    @pl.when(i == pl.num_programs(0) - 1)
    def _():
        out_ref[:, :HEAD_PACK] = jnp.transpose(acc[...]).astype(bf16)
        total = jnp.sum(gain[...], axis=0, keepdims=True)
        rows = lax.broadcasted_iota(jnp.int32, (LANES, total.shape[1]), 0)
        out_ref[:, HEAD_PACK:] = jnp.transpose(
            jnp.where(rows == 0, jnp.broadcast_to(total, rows.shape), 0.0)
        ).astype(bf16)


def head_grads(head, x, normed, packed, grads):
    span, width = x.shape
    rows = 2 * BLOCK
    token_rows = pl.BlockSpec((rows, width), lambda i, h: (i, 0))
    return pl.pallas_call(
        head_grads_kernel,
        grid_spec=pltpu.PrefetchScalarGridSpec(
            num_scalar_prefetch=1,
            grid=(span // rows,),
            in_specs=[
                token_rows,
                token_rows,
                pl.BlockSpec((width, HEAD_PACK), lambda i, h: (0, h[0])),
                pl.BlockSpec((rows, HEAD_PACK), lambda i, h: (i, 0)),
            ],
            out_specs=pl.BlockSpec((width, HEAD_PACK + LANES), lambda i, h: (0, 0)),
            scratch_shapes=[pltpu.VMEM((HEAD_PACK, width), f32), pltpu.VMEM((8, width), f32)],
        ),
        out_shape=jax.ShapeDtypeStruct((width, HEAD_PACK + LANES), bf16),
        compiler_params=pltpu.CompilerParams(vmem_limit_bytes=VMEM_LIMIT),
        cost_estimate=pl.CostEstimate(
            flops=4 * span * width * HEAD_PACK, bytes_accessed=12 * 2**20, transcendentals=0
        ),
        name="head_grads",
    )(head, x, normed, packed, grads)


def lower_lanes(shape):
    return lax.broadcasted_iota(jnp.int32, shape, len(shape) - 1) < HEAD_SIZE


def both_heads_low(pair):
    low = lower_lanes(pair.shape)
    return jnp.concatenate(
        [jnp.where(low, pair, 0.0), jnp.where(low, pltpu.roll(pair, HEAD_SIZE, 1), 0.0)], axis=0
    )


def both_heads_high(pair):
    low = lower_lanes(pair.shape)
    return jnp.concatenate(
        [jnp.where(low, 0.0, pltpu.roll(pair, HEAD_SIZE, 1)), jnp.where(low, 0.0, pair)], axis=0
    )


def block_bounds(bounds_ref):
    i, steps = pl.program_id(0), pl.num_programs(0)
    query_start = (i + bounds_ref[2 * steps]) * QUERY_BLOCK
    diagonal = query_start // BLOCK
    full = jnp.minimum(bounds_ref[steps + i], diagonal)
    return query_start, bounds_ref[i], full, diagonal, diagonal + QUERY_BLOCK // BLOCK


def pair_mask(doc, query_start):
    doc = jnp.concatenate([doc, doc], axis=1)
    queries = lax.broadcasted_iota(jnp.int32, doc.shape, 1) % QUERY_BLOCK + query_start

    def masked(scores, start):
        keys = lax.broadcasted_iota(jnp.int32, scores.shape, 0) + start
        return jnp.where((keys >= doc) & (keys <= queries), scores, NEGATIVE_HUGE)

    return masked


def attend_kernel(bounds_ref, q_ref, kv_ref, doc_ref, o_ref, low_ref, lse_ref, acc):
    query_start, first, full, diagonal, end = block_bounds(bounds_ref)
    q = both_heads_low(q_ref[...].astype(f32) * SCALE_OF_SCORES).astype(bf16)
    masked = pair_mask(doc_ref[0], query_start)
    acc[...] = jnp.zeros_like(acc)

    def step(mask, j, carried):
        top, total = carried
        start = pl.multiple_of(j * BLOCK, BLOCK)
        kv = kv_ref[pl.ds(start, BLOCK), :]
        scores = contract_cols(kv, q)
        if mask:
            scores = masked(scores, start)
        new = jnp.maximum(top, jnp.max(scores, axis=0, keepdims=True))
        probs = jnp.exp(scores - new)
        keep = jnp.exp(top - new)
        acc[...] = acc[...] * keep + contract_rows(kv, probs.astype(bf16))
        return new, total * keep + jnp.sum(probs, axis=0, keepdims=True)

    row = (1, 2 * QUERY_BLOCK)
    carried = (jnp.full(row, NEGATIVE_HUGE, f32), jnp.zeros(row, f32))
    carried = lax.fori_loop(first, full, functools.partial(step, True), carried)
    carried = lax.fori_loop(full, diagonal, functools.partial(step, False), carried)
    top, total = lax.fori_loop(diagonal, end, functools.partial(step, True), carried)
    mixed = jnp.transpose(acc[...] / total)
    one, two = mixed[:QUERY_BLOCK], mixed[QUERY_BLOCK:]
    out = jnp.where(lower_lanes(one.shape), pltpu.roll(one, HEAD_SIZE, 1), two)
    o_ref[...] = out
    low_ref[...] = out.astype(bf16)
    lse_ref[0] = top + jnp.log(total)


def attention_specs(kv_at, keys):
    pair = pl.BlockSpec((QUERY_BLOCK, PAIR), lambda i, s: (i, 0))
    return (
        pair,
        pl.BlockSpec((keys, PAIR), lambda i, s: (0, kv_at)),
        pl.BlockSpec((1, 1, QUERY_BLOCK), lambda i, s: (i, 0, 0)),
        pl.BlockSpec((1, 1, 2 * QUERY_BLOCK), lambda i, s: (i, 0, 0)),
    )


def attend(bounds, qkv, kv, kv_at, doc):
    queries, keys = qkv.shape[0], kv.shape[0]
    steps = queries // QUERY_BLOCK
    pair, whole, doc_row, lse_row = attention_specs(kv_at, keys)
    return pl.pallas_call(
        attend_kernel,
        grid_spec=pltpu.PrefetchScalarGridSpec(
            num_scalar_prefetch=1,
            grid=(steps,),
            in_specs=[pair, whole, doc_row],
            out_specs=[pair, pair, lse_row],
            scratch_shapes=[pltpu.VMEM((PAIR, 2 * QUERY_BLOCK), f32)],
        ),
        out_shape=[
            jax.ShapeDtypeStruct((queries, PAIR), f32),
            jax.ShapeDtypeStruct((queries, PAIR), bf16),
            jax.ShapeDtypeStruct((steps, 1, 2 * QUERY_BLOCK), f32),
        ],
        compiler_params=pltpu.CompilerParams(vmem_limit_bytes=VMEM_LIMIT),
        cost_estimate=pl.CostEstimate(
            flops=4 * queries * keys * PAIR, bytes_accessed=6 * 2**20, transcendentals=queries * keys
        ),
        name="attend",
    )(bounds, qkv, kv, doc)


def attend_back_kernel(
    fold, bounds_ref, q_ref, kv_ref, doc_ref, do_ref, o_ref, lse_ref, cos_ref, sin_ref, *refs
):
    if fold:
        out_ref, acc, dkv_ref = refs
    else:
        dq_ref, dkv_ref, acc = refs
    i = pl.program_id(0)
    query_start, first, full, diagonal, end = block_bounds(bounds_ref)

    @pl.when(i == 0)
    def _():
        dkv_ref[...] = jnp.zeros_like(dkv_ref)

    q = both_heads_low(q_ref[...].astype(f32) * SCALE_OF_SCORES).astype(bf16)
    grad = do_ref[...].astype(f32)
    product = jnp.transpose(grad * o_ref[...])
    delta = jnp.concatenate(
        [
            jnp.sum(product[:HEAD_SIZE], axis=0, keepdims=True),
            jnp.sum(product[HEAD_SIZE:], axis=0, keepdims=True),
        ],
        axis=1,
    )
    grad = both_heads_high(grad).astype(bf16)
    sources = jnp.concatenate([q, grad], axis=0)
    masked = pair_mask(doc_ref[0], query_start)
    lse = lse_ref[0]
    acc[...] = jnp.zeros_like(acc)

    def step(mask, j, carried):
        start = pl.multiple_of(j * BLOCK, BLOCK)
        kv = kv_ref[pl.ds(start, BLOCK), :]
        scores = contract_cols(kv, q) - lse
        if mask:
            scores = masked(scores, start)
        probs = jnp.exp(scores)
        grad_scores = (probs * (contract_cols(kv, grad) - delta)).astype(bf16)
        acc[...] += contract_rows(kv, grad_scores)
        both = jnp.concatenate([grad_scores, probs.astype(bf16)], axis=1)
        dkv_ref[pl.ds(start, BLOCK), :] += jnp.dot(both, sources, preferred_element_type=f32)
        return carried

    lax.fori_loop(first, full, functools.partial(step, True), 0)
    lax.fori_loop(full, diagonal, functools.partial(step, False), 0)
    lax.fori_loop(diagonal, end, functools.partial(step, True), 0)
    dq = jnp.transpose(acc[...])
    one, two = dq[:QUERY_BLOCK], dq[QUERY_BLOCK:]
    dq = jnp.where(lower_lanes(one.shape), one, pltpu.roll(two, HEAD_SIZE, 1))
    if not fold:
        dq_ref[...] = dq
        return
    mine = pl.ds(pl.multiple_of(i * QUERY_BLOCK, QUERY_BLOCK), QUERY_BLOCK)
    out_ref[mine, :PAIR] = rotate_lanes(
        dq * SCALE_OF_SCORES, cos_ref[mine, :], -sin_ref[mine, :]
    ).astype(bf16)

    @pl.when(i == pl.num_programs(0) - 1)
    def _():
        def finish(j, carried):
            part = pl.ds(pl.multiple_of(j * BLOCK, BLOCK), BLOCK)
            cos, sin = key_tables(cos_ref[part, :], sin_ref[part, :])
            out_ref[part, PAIR:] = rotate_lanes(dkv_ref[part, :], cos, -sin).astype(bf16)
            return carried

        lax.fori_loop(0, dkv_ref.shape[0] // BLOCK, finish, 0)


def attend_back(bounds, qkv, kv, kv_at, doc, grad, out, lse, cos, sin, fold):
    queries, keys = qkv.shape[0], kv.shape[0]
    steps = queries // QUERY_BLOCK
    pair, whole, doc_row, lse_row = attention_specs(kv_at, keys)
    table = pl.BlockSpec(cos.shape, lambda i, s: (0, 0))
    acc = pltpu.VMEM((PAIR, 2 * QUERY_BLOCK), f32)
    if fold:
        out_specs = pl.BlockSpec((queries, HEAD_PACK), lambda i, s: (0, 0))
        out_shape = jax.ShapeDtypeStruct((queries, HEAD_PACK), bf16)
        scratch = [acc, pltpu.VMEM((keys, PAIR), f32)]
    else:
        out_specs = [pair, pl.BlockSpec((keys, PAIR), lambda i, s: (0, 0))]
        out_shape = [
            jax.ShapeDtypeStruct((queries, PAIR), f32),
            jax.ShapeDtypeStruct((keys, PAIR), f32),
        ]
        scratch = [acc]
    return pl.pallas_call(
        functools.partial(attend_back_kernel, fold),
        grid_spec=pltpu.PrefetchScalarGridSpec(
            num_scalar_prefetch=1,
            grid=(steps,),
            in_specs=[pair, whole, doc_row, pair, pair, lse_row, table, table],
            out_specs=out_specs,
            scratch_shapes=scratch,
        ),
        out_shape=out_shape,
        compiler_params=pltpu.CompilerParams(vmem_limit_bytes=VMEM_LIMIT),
        cost_estimate=pl.CostEstimate(
            flops=10 * queries * keys * PAIR,
            bytes_accessed=8 * 2**20,
            transcendentals=queries * keys,
        ),
        name="attend_back",
    )(bounds, qkv, kv, doc, grad, out, lse, cos, sin)


def unrotate_kernel(dq_ref, dkv_ref, cos_ref, sin_ref, out_ref):
    cos, sin = cos_ref[...], sin_ref[...]
    dq = rotate_lanes(dq_ref[...] * SCALE_OF_SCORES, cos, -sin)
    cos, sin = key_tables(cos, sin)
    dkv = rotate_lanes(dkv_ref[...], cos, -sin)
    out_ref[...] = jnp.concatenate([dq, dkv], axis=1).astype(bf16)


def unrotate(dq, dkv, cos, sin):
    rows = dq.shape[0]
    pair = pl.BlockSpec((BLOCK, PAIR), lambda i: (i, 0))
    return pl.pallas_call(
        unrotate_kernel,
        grid=(rows // BLOCK,),
        in_specs=[pair, pair, pair, pair],
        out_specs=pl.BlockSpec((BLOCK, HEAD_PACK), lambda i: (i, 0)),
        out_shape=jax.ShapeDtypeStruct((rows, HEAD_PACK), bf16),
        cost_estimate=pl.CostEstimate(
            flops=rows * HEAD_PACK * 8, bytes_accessed=rows * HEAD_PACK * 14, transcendentals=0
        ),
        name="unrotate",
    )(dq, dkv, cos, sin)


def place_experts_kernel(place_ref, *refs):
    blocks, (ct_ref, w_ref, z_ref, sems) = refs[:10], refs[10:]
    core = place_ref[1]
    rows = w_ref.shape[1] // 2
    half = rows // 2
    sources = [[(0, 0, rows)], [(1, 0, rows)], [(2, 0, rows)], [(3, 0, half), (4, half, half)]]
    for step, parts in enumerate(sources):

        @pl.when(pl.program_id(0) == step)
        def _(parts=parts):
            copies = []
            for source, start, length in parts:
                for other in (0, 1):
                    first = jnp.where(core == other, 0, rows) + start
                    at = pl.ds(pl.multiple_of(first, half), length)
                    copies.append(
                        pltpu.make_async_copy(
                            blocks[2 * source + other], w_ref.at[0, at, :], sems.at[len(copies)]
                        )
                    )
            for copy in copies:
                copy.start()
            for copy in copies:
                copy.wait()

    z_ref[0] = jnp.dot(ct_ref[...], w_ref[0, :, 2 * F :], preferred_element_type=f32)


def place_experts(place, parts, early, width):
    rows = early.shape[0]
    blocks = [block for pair in parts for block in pair]
    return pl.pallas_call(
        place_experts_kernel,
        grid_spec=pltpu.PrefetchScalarGridSpec(
            num_scalar_prefetch=1,
            grid=(EXPERTS_HERE,),
            in_specs=[pl.BlockSpec(memory_space=pl.ANY)] * len(blocks)
            + [pl.BlockSpec((rows, width), lambda r, s: (0, 0))],
            out_specs=[
                pl.BlockSpec((1, width, 3 * F), lambda r, s: (s[0] ^ r, 0, 0)),
                pl.BlockSpec((1, rows, F), lambda r, s: (s[0] ^ r, 0, 0)),
            ],
            scratch_shapes=[pltpu.SemaphoreType.DMA((4,))],
        ),
        out_shape=[
            jax.ShapeDtypeStruct((EXPERTS_HERE, width, 3 * F), bf16),
            jax.ShapeDtypeStruct((EXPERTS_HERE, rows, F), f32),
        ],
        compiler_params=pltpu.CompilerParams(vmem_limit_bytes=VMEM_LIMIT),
        cost_estimate=pl.CostEstimate(
            flops=2 * EXPERTS_HERE * rows * width * F, bytes_accessed=36 * 2**20, transcendentals=0
        ),
        name="place_experts",
    )(place, *blocks, early)


def lane_column(x, at):
    lane = lax.broadcasted_iota(jnp.int32, x.shape, 1)
    return jnp.sum(jnp.where(lane == at, x, 0.0), axis=1, keepdims=True)


def experts_kernel(
    group_ref, n_ref, routed_ref, router_ref, w_ref, z_ref,
    back_ref, gates_ref, hidden_ref, pre_ref, acc, dots,
):
    e = pl.program_id(0)
    own = group_ref[0] * EXPERTS_HERE + e
    rows = n_ref.shape[0]

    @pl.when(e == 0)
    def _():
        logits = jnp.dot(n_ref[...], router_ref[...], preferred_element_type=f32)
        routed = routed_ref[...].astype(f32) > 0.5
        highest = jnp.max(jnp.where(routed, logits, NEGATIVE_HUGE), axis=1, keepdims=True)
        weights = jnp.where(routed, jnp.exp(jnp.where(routed, logits - highest, 0.0)), 0.0)
        gates_ref[...] = weights / jnp.sum(weights, axis=1, keepdims=True)
        acc[...] = jnp.zeros_like(acc)
        dots[...] = jnp.zeros_like(dots)

    w_in = w_ref[0, :, : 2 * F]
    for t in range(rows // BLOCK):
        part = pl.ds(t * BLOCK, BLOCK)
        pre = jnp.dot(n_ref[part, :], w_in, preferred_element_type=f32)
        gate, up = pre[:, :F], pre[:, F:]
        z = z_ref[0, part, :]
        weight = lane_column(gates_ref[part, :], own)
        sig = 1.0 / (1.0 + jnp.exp(-gate))
        act = gate * sig
        hidden = act * up
        hidden_ref[0, part, :] = (weight * hidden).astype(bf16)
        dot = RESIDUAL_SCALE * jnp.sum(hidden.astype(bf16).astype(f32) * z, axis=1, keepdims=True)
        lane = lax.broadcasted_iota(jnp.int32, (BLOCK, LANES), 1)
        dots[part, :] += jnp.where(lane == own, dot, 0.0)
        scaled = (RESIDUAL_SCALE * weight) * z
        pre_ref[0, part, :F] = (scaled * up * (sig + act * (1.0 - sig))).astype(bf16)
        pre_ref[0, part, F:] = (scaled * act).astype(bf16)
        acc[part, :] += contract_cols(pre_ref[0, part, :], w_in)

    @pl.when(e == EXPERTS_HERE - 1)
    def _():
        width = n_ref.shape[1]
        back_ref[:, :width] = acc[...].astype(bf16)
        high = dots[...].astype(bf16)
        low = dots[...] - high.astype(f32)
        back_ref[:, width:] = (high.astype(f32) + pltpu.roll(low, E, 1)).astype(bf16)


def experts(group, normed, early, packed, w_all, z):
    rows, width = normed.shape
    count = w_all.shape[0]
    whole = pl.BlockSpec((rows, width), lambda e, g: (0, 0))
    column = width // LANES
    router_at = packed.shape[1] // LANES - 1
    return pl.pallas_call(
        experts_kernel,
        grid_spec=pltpu.PrefetchScalarGridSpec(
            num_scalar_prefetch=1,
            grid=(count,),
            in_specs=[
                whole,
                pl.BlockSpec((rows, LANES), lambda e, g: (0, column)),
                pl.BlockSpec((width, LANES), lambda e, g: (0, router_at)),
                pl.BlockSpec((1, width, 3 * F), lambda e, g: (e, 0, 0)),
                pl.BlockSpec((1, rows, F), lambda e, g: (e, 0, 0)),
            ],
            out_specs=[
                pl.BlockSpec((rows, width + LANES), lambda e, g: (0, 0)),
                pl.BlockSpec((rows, LANES), lambda e, g: (0, 0)),
                pl.BlockSpec((1, rows, F), lambda e, g: (e, 0, 0)),
                pl.BlockSpec((1, rows, 2 * F), lambda e, g: (e, 0, 0)),
            ],
            scratch_shapes=[pltpu.VMEM((rows, width), f32), pltpu.VMEM((rows, LANES), f32)],
        ),
        out_shape=[
            jax.ShapeDtypeStruct((rows, width + LANES), bf16),
            jax.ShapeDtypeStruct((rows, LANES), f32),
            jax.ShapeDtypeStruct((count, rows, F), bf16),
            jax.ShapeDtypeStruct((count, rows, 2 * F), bf16),
        ],
        compiler_params=pltpu.CompilerParams(vmem_limit_bytes=VMEM_LIMIT),
        cost_estimate=pl.CostEstimate(
            flops=2 * count * rows * width * 4 * F, bytes_accessed=40 * 2**20, transcendentals=0
        ),
        name="experts",
    )(group, normed, early, packed, w_all, z)


def expert_grads_kernel(with_y, half_ref, n_ref, ct_ref, w_ref, hidden_ref, pre_ref, *refs):
    if with_y:
        y_ref, grad_ref, n_t, ct_t, acc = refs
    else:
        grad_ref, n_t, ct_t = refs
    e = pl.program_id(0)

    @pl.when(e == 0)
    def _():
        n_t[...] = jnp.transpose(n_ref[...])
        ct_t[...] = jnp.transpose(ct_ref[...])
        if with_y:
            acc[...] = jnp.zeros_like(acc)

    grad_ref[0, :, : 2 * F] = jnp.dot(n_t[...], pre_ref[0], preferred_element_type=f32).astype(bf16)
    grad_ref[0, :, 2 * F :] = (
        RESIDUAL_SCALE * jnp.dot(ct_t[...], hidden_ref[0], preferred_element_type=f32)
    ).astype(bf16)
    if not with_y:
        return
    acc[...] += contract_cols(hidden_ref[0], w_ref[0, :, 2 * F :])

    @pl.when(e == pl.num_programs(0) - 1)
    def _():
        y_ref[...] = acc[...].astype(bf16)


def expert_grads(half, halves, normed, early, w_all, hidden, pre, with_y):
    rows, width = normed.shape
    count = w_all.shape[0]
    own = width // halves
    feature = pl.BlockSpec((rows, own), lambda e, h: (0, h[0]))
    out_specs = [pl.BlockSpec((1, own, 3 * F), lambda e, h: (e, 0, 0))]
    out_shape = [jax.ShapeDtypeStruct((count, own, 3 * F), bf16)]
    scratch = [pltpu.VMEM((own, rows), bf16), pltpu.VMEM((own, rows), bf16)]
    if with_y:
        out_specs.insert(0, pl.BlockSpec((rows, width), lambda e, h: (0, 0)))
        out_shape.insert(0, jax.ShapeDtypeStruct((rows, width), bf16))
        scratch.append(pltpu.VMEM((rows, width), f32))
    return pl.pallas_call(
        functools.partial(expert_grads_kernel, with_y),
        grid_spec=pltpu.PrefetchScalarGridSpec(
            num_scalar_prefetch=1,
            grid=(count,),
            in_specs=[
                feature,
                feature,
                pl.BlockSpec((1, width, 3 * F), lambda e, h: (e, 0, 0)),
                pl.BlockSpec((1, rows, F), lambda e, h: (e, 0, 0)),
                pl.BlockSpec((1, rows, 2 * F), lambda e, h: (e, 0, 0)),
            ],
            out_specs=out_specs,
            scratch_shapes=scratch,
        ),
        out_shape=out_shape,
        compiler_params=pltpu.CompilerParams(vmem_limit_bytes=VMEM_LIMIT),
        cost_estimate=pl.CostEstimate(
            flops=2 * count * rows * width * 3 * F // halves + 2 * with_y * count * rows * width * F,
            bytes_accessed=30 * 2**20,
            transcendentals=0,
        ),
        name="expert_grads",
    )(half, normed, early, w_all, hidden, pre)


def join_kernel(place_ref, o_ref, w_ref, small_ref, x_ref, normed_ref, resid_ref, own_ref, gain):
    t = pl.program_id(0)
    b = place_ref[2]

    @pl.when(t == 0)
    def _():
        gain[...] = jnp.transpose(small_ref[...].astype(f32))[E : E + 8, :]

    pairs = []
    for a in range(o_ref.shape[0]):
        same, other = o_ref[a, 0, 0], o_ref[a, 1, 0]
        pairs.append(jnp.where(b == 0, same, other))
        pairs.append(jnp.where(b == 0, other, same))
    attended = jnp.concatenate(pairs, axis=1)
    resid = x_ref[...].astype(f32) + RESIDUAL_SCALE * jnp.dot(
        attended, w_ref[...], preferred_element_type=f32
    )
    normed_ref[...] = rms_scale(resid, gain[1:2, :]).astype(bf16)

    @pl.when(t == place_ref[1])
    def _():
        resid_ref[...] = resid
        own_ref[...] = attended


def join(place, outs, packed, weights_at, x):
    width = packed.shape[0]
    lines, _, _, rows, pair = outs.shape
    small_at = packed.shape[1] // LANES - 1
    own = pl.BlockSpec((rows, width), lambda t, s: (0, 0))
    return pl.pallas_call(
        join_kernel,
        grid_spec=pltpu.PrefetchScalarGridSpec(
            num_scalar_prefetch=1,
            grid=(lines,),
            in_specs=[
                pl.BlockSpec((lines, 2, 1, rows, pair), lambda t, s: (0, 0, t, 0, 0)),
                pl.BlockSpec((width, width), lambda t, s: (0, weights_at)),
                pl.BlockSpec((width, LANES), lambda t, s: (0, small_at)),
                pl.BlockSpec((rows, width), lambda t, s: (2 * t + s[2], 0)),
            ],
            out_specs=[pl.BlockSpec((rows, width), lambda t, s: (t, 0)), own, own],
            scratch_shapes=[pltpu.VMEM((8, width), f32)],
        ),
        out_shape=[
            jax.ShapeDtypeStruct((lines * rows, width), bf16),
            jax.ShapeDtypeStruct((rows, width), f32),
            jax.ShapeDtypeStruct((rows, width), bf16),
        ],
        compiler_params=pltpu.CompilerParams(vmem_limit_bytes=VMEM_LIMIT),
        cost_estimate=pl.CostEstimate(
            flops=2 * lines * rows * width * width, bytes_accessed=12 * 2**20, transcendentals=0
        ),
        name="join",
    )(place, outs, packed, packed, x)


def weight_sums_kernel(sums_ref, q_ref, k_ref, v_ref, gain_ref):
    groups, heads, members = sums_ref.shape[:3]
    gain = jnp.zeros(gain_ref.shape, f32)
    values = []
    for h in range(heads):
        total = jnp.zeros(sums_ref.shape[3:], f32)
        for g in range(groups):
            for member in range(members):
                total += sums_ref[g, h, member].astype(f32)
        values.append(total)
        gain += total[:, HEAD_PACK:]
        q_ref[:, h * PAIR : (h + 1) * PAIR] = total[:, :PAIR]
    gain_ref[...] = gain
    for h in range(0, heads, 2):
        one, two = values[h][:, PAIR:HEAD_PACK], values[h + 1][:, PAIR:HEAD_PACK]
        low = lower_lanes(one.shape)
        at = slice(h // 2 * PAIR, (h // 2 + 1) * PAIR)
        k_ref[:, at] = jnp.where(low, one, pltpu.roll(two, HEAD_SIZE, 1))
        v_ref[:, at] = jnp.where(low, pltpu.roll(one, HEAD_SIZE, 1), two)


def weight_sums(sums):
    rows, heads = sums.shape[3], sums.shape[1]
    return pl.pallas_call(
        weight_sums_kernel,
        out_shape=[
            jax.ShapeDtypeStruct((rows, heads * PAIR), f32),
            jax.ShapeDtypeStruct((rows, heads * HEAD_SIZE), f32),
            jax.ShapeDtypeStruct((rows, heads * HEAD_SIZE), f32),
            jax.ShapeDtypeStruct((rows, LANES), f32),
        ],
        compiler_params=pltpu.CompilerParams(vmem_limit_bytes=VMEM_LIMIT),
        cost_estimate=pl.CostEstimate(flops=2**20, bytes_accessed=2 * 2**20, transcendentals=0),
        name="weight_sums",
    )(sums)


def exchange(x, axes):
    return lax.all_to_all(x, axes, 0, 0, tiled=True)


def body(
    tokens,
    cotangent,
    segment_ids,
    routes,
    norm_attn,
    w_query,
    key_weight_matrix,
    value_weight_matrix,
    w_output,
    norm_moe,
    w_router,
    expert_in,
    expert_out,
):
    x_local = tokens[0].astype(f32)
    token_count, width = x_local.shape
    seg_row = segment_ids[0]
    group = lax.axis_index("a")
    head_axes = SEQ if lax.axis_size(SEQ) == KEY_VALUE_HEADS else ("b",)
    whole_rows = head_axes == SEQ
    span = token_count * KEY_VALUE_HEADS
    span_start = 0 if whole_rows else group * span

    def start_of_doc(ids):
        return jnp.sum((seg_row[None, :] < ids[:, None]).astype(jnp.int32), axis=1)

    seg_span = lax.dynamic_slice_in_dim(seg_row, span_start, span)
    doc_span = start_of_doc(seg_span)
    cos_span, sin_span = rotation_tables(
        span_start + jnp.arange(span, dtype=jnp.int32) - doc_span
    )
    by_block = doc_span.reshape(-1, QUERY_BLOCK)
    bounds = jnp.concatenate(
        [
            by_block[:, 0] // BLOCK,
            (by_block[:, -1] + BLOCK - 1) // BLOCK,
            jnp.full((1,), span_start // QUERY_BLOCK, jnp.int32),
        ]
    )
    doc_rows = by_block[:, None, :]

    own_rows = w_query.shape[0]
    by_head = jnp.concatenate(
        [
            w_query.astype(bf16).reshape(own_rows, KEY_VALUE_HEADS, PAIR),
            key_weight_matrix.astype(bf16).reshape(own_rows, KEY_VALUE_HEADS, HEAD_SIZE),
            value_weight_matrix.astype(bf16).reshape(own_rows, KEY_VALUE_HEADS, HEAD_SIZE),
        ],
        axis=2,
    ).reshape(own_rows, KEY_VALUE_HEADS * HEAD_PACK)
    qkv_width = KEY_VALUE_HEADS * HEAD_PACK
    first_all = gather(
        jnp.concatenate(
            [
                by_head,
                w_output.astype(bf16),
                pad_lanes(
                    jnp.concatenate(
                        [
                            w_router.astype(bf16),
                            norm_attn.astype(bf16)[:, None],
                            norm_moe.astype(bf16)[:, None],
                        ],
                        axis=1,
                    ),
                    LANES,
                ),
            ],
            axis=1,
        ),
        ALL,
    )
    experts_low = jnp.concatenate([expert_in.astype(bf16), expert_out.astype(bf16)], axis=1)
    if whole_rows:
        pieces = grid_gather(tokens[0])
        places = [piece[:2] for piece in pieces]
        blocks = tuple(piece[2] for piece in pieces)
    else:
        places = None
        blocks = (gather(tokens[0], "b").reshape((-1,) + tokens.shape[1:]),)
    first_all, experts_low, blocks, cos_span, sin_span, bounds, doc_rows = (
        lax.optimization_barrier(
            (first_all, experts_low, blocks, cos_span, sin_span, bounds, doc_rows)
        )
    )
    output_w = first_all[:, qkv_width : qkv_width + width]
    small_at = qkv_width + width
    router_w = first_all[:, small_at : small_at + E]
    gain_one_f = first_all[:, small_at + E].astype(f32)
    gain_two_f = first_all[:, small_at + E + 1].astype(f32)

    expert_ids = jnp.arange(E, dtype=jnp.int32)
    routed_own = jnp.any(routes[0][:, :, None] == expert_ids[None, None, :], axis=1)
    early = jnp.concatenate([cotangent[0], pad_lanes(routed_own.astype(bf16), LANES)], axis=1)
    early, first_all = lax.optimization_barrier((early, first_all))
    early_all = gather(early, "a")
    small_plane = lax.axis_size("b") == 2 and lax.axis_size("y") == 2
    if small_plane:
        parts = plane_gather(experts_low)
    else:
        parts = gather(experts_low, PLANE)

    place = jnp.stack([lax.axis_index(head_axes), group, lax.axis_index("b")])
    qkv, normed_span, x_span, wide_cos, wide_sin = project(
        place, places, blocks, token_count, first_all, cos_span, sin_span
    )
    if whole_rows:
        kv, kv_at = qkv, 1
    else:
        kv, kv_at = gather(qkv[:, PAIR:], "a"), 0
    attention_result, attended, log_total = attend(bounds, qkv, kv, kv_at, doc_rows)
    if small_plane:
        member = lax.axis_index("b")
        by_column = attended.reshape(GROUPS, 2, token_count, PAIR)
        other = lax.ppermute(
            lax.dynamic_index_in_dim(by_column, 1 - member, 1, False), "b", [(0, 1), (1, 0)]
        )
        own = lax.dynamic_index_in_dim(by_column, member, 1, False)
        pair, early_all = lax.optimization_barrier((jnp.stack([own, other]), early_all))
        outs = lax.all_gather(pair, "a", axis=0, tiled=False)
        normed_all, resid, attended_low = join(place, outs, first_all, qkv_width // width, x_span)
        normed_two = lax.dynamic_slice_in_dim(normed_all, group * token_count, token_count)
        home = jnp.stack([member * 2 + lax.axis_index("y"), lax.axis_index("c")])
        experts_all, grad_hidden = place_experts(home, parts, early_all, width)
    else:
        attended_low = (
            exchange(attended.reshape(KEY_VALUE_HEADS, token_count, PAIR), head_axes)
            .transpose(1, 0, 2)
            .reshape(token_count, QUERY_HEADS * HEAD_SIZE)
        )
        attn_out = jnp.dot(attended_low, output_w, preferred_element_type=f32)
        resid = x_local + RESIDUAL_SCALE * attn_out
        normed_two = rms_scale(resid, gain_two_f).astype(bf16)
        normed_all = gather(normed_two, "a")
        experts_all = parts.reshape(EXPERTS_HERE, width, 3 * F)
        grad_hidden = jnp.einsum(
            "td,edf->etf",
            early_all[:, :width],
            experts_all[:, :, 2 * F :],
            preferred_element_type=f32,
        )
    back_part, gates_all, gated_hidden, grad_pre = experts(
        group.reshape(1), normed_all, early_all, first_all, experts_all, grad_hidden
    )
    back_own = scatter_sum(back_part, "a").astype(f32)
    inputs = (normed_all, early_all, experts_all, gated_hidden, grad_pre)
    if small_plane:
        core = lax.axis_index("c")
        (send,) = expert_grads((1 - core).reshape(1), 2, *inputs, False)
        arrived = lax.ppermute(send, "c", [(0, 1), (1, 0)])
        moe_part, keep = expert_grads(core.reshape(1), 2, *inputs, True)
        back_own, moe_part, keep = lax.optimization_barrier((back_own, moe_part, keep))
    else:
        moe_part, grad_experts = expert_grads(jnp.zeros((1,), jnp.int32), 1, *inputs, True)
        back_own, moe_part, grad_experts = lax.optimization_barrier(
            (back_own, moe_part, grad_experts)
        )
        grad_experts = scatter_sum(grad_experts.reshape(EXPERTS_HERE * width, 3 * F), PLANE)
    moe_sum = scatter_sum(moe_part, "a")

    grad_out = cotangent[0].astype(f32)
    gates = lax.dynamic_slice_in_dim(gates_all, group * token_count, token_count)[:, :E]
    gate_grads_own = back_own[:, width : width + E] + back_own[:, width + E : width + 2 * E]
    grad_logits = gates * (gate_grads_own - jnp.sum(gates * gate_grads_own, axis=-1, keepdims=True))
    grad_normed_two = back_own[:, :width] + jnp.dot(
        grad_logits, router_w.astype(f32).T, precision=HIGHEST_DOT
    )
    grad_router = jnp.dot(normed_two.astype(f32).T, grad_logits, precision=HIGHEST_DOT)
    grad_resid_norm, grad_gain_two = rms_back(resid, gain_two_f, grad_normed_two)
    grad_resid = grad_out + grad_resid_norm
    grad_attn_low = (RESIDUAL_SCALE * grad_resid).astype(bf16)
    grad_heads = contract_cols(grad_attn_low, output_w).astype(bf16)
    grad_mixed = exchange(
        grad_heads.reshape(token_count, KEY_VALUE_HEADS, PAIR).transpose(1, 0, 2), head_axes
    ).reshape(span, PAIR)
    if small_plane:
        keep, arrived, grad_heads = lax.optimization_barrier((keep, arrived, grad_heads))
        total = keep.astype(f32) + arrived.astype(f32)
        total = total.astype(bf16).reshape((2, 2) + keep.shape[1:])
        total, attended_low, grad_router = lax.optimization_barrier(
            (total, attended_low, grad_router)
        )
        wide = 3 * F // 2
        left, right = halve_send(total[..., :wide], "y", 1), halve_send(total[..., wide:], "b", 0)
    small = jnp.concatenate([grad_router, grad_gain_two[:, None]], axis=1)
    second_part = jnp.concatenate(
        [contract_rows(attended_low, grad_attn_low), pad_lanes(small, LANES)], axis=1
    ).astype(bf16)
    cols = second_part.shape[1]
    second_part = second_part.reshape(GROUPS, -1, own_rows, cols).transpose(1, 0, 2, 3)
    second_part, grad_mixed = lax.optimization_barrier((second_part, grad_mixed))
    rest = scatter_sum(second_part.reshape(-1, cols), PLANE)
    grads = attend_back(
        bounds, qkv, kv, kv_at, doc_rows, grad_mixed, attention_result, log_total,
        wide_cos, wide_sin, whole_rows,
    )
    if whole_rows:
        grad_pack = grads
    else:
        grad_kv = scatter_sum(grads[1].astype(bf16), "a").astype(f32)
        grad_pack = unrotate(grads[0], grad_kv, wide_cos, wide_sin)
    if small_plane:
        left, right, moe_sum, grad_pack = lax.optimization_barrier(
            (left, right, moe_sum, grad_pack)
        )
        left, right = halve_add(left), halve_add(right)
        left, right = halve_send(left, "b", 0), halve_send(right, "y", 0)
    first_part = head_grads(place, x_span, normed_span, first_all, grad_pack)
    rest, first_part = lax.optimization_barrier((rest, first_part))
    rest = scatter_sum(rest, "a")
    by_tokens = exchange(grad_pack.reshape(KEY_VALUE_HEADS, token_count, HEAD_PACK), head_axes)
    by_tokens, first_part = lax.optimization_barrier((by_tokens, first_part))
    sums = exchange(first_part.reshape(-1, own_rows, first_part.shape[1]), ALL)
    sums, moe_sum, resid = lax.optimization_barrier((sums, moe_sum, resid))
    grad_q_w, grad_k_w, grad_v_w, grad_gain_one = weight_sums(
        sums.reshape(-1, KEY_VALUE_HEADS, lax.axis_size(("y", "c")), own_rows, first_part.shape[1])
    )
    rest = rest.astype(f32)
    grad_qkv = by_tokens.transpose(1, 0, 2).reshape(token_count, qkv_width)
    grad_normed_one = contract_cols(grad_qkv, first_all[:, :qkv_width])
    grad_x_norm, _ = rms_back(x_local, gain_one_f, grad_normed_one)
    grad_input = grad_resid + grad_x_norm
    layer_sum = resid + RESIDUAL_SCALE * moe_sum.astype(f32)
    if small_plane:
        grad_experts = jnp.concatenate(
            [own.astype(f32) + other.astype(f32) for own, other in (left, right)], axis=1
        )
    else:
        grad_experts = grad_experts.astype(f32)
    return (
        layer_sum.astype(bf16)[None],
        grad_input[None],
        grad_gain_one[:, 0],
        grad_q_w,
        grad_k_w,
        grad_v_w,
        rest[:, :width],
        rest[:, width + E],
        rest[:, width : width + E],
        grad_experts[:, : 2 * F],
        grad_experts[:, 2 * F :],
    )


def solution(mesh):
    seq, row = mesh.shape["seq"], mesh.shape["row"]
    cut = Mesh(mesh.devices.reshape(GROUPS, seq // GROUPS, row // 2, 2), ALL)
    token_spec = P(("y", "c"), SEQ, None)
    row_spec = P(ALL, None)
    flat_spec = P(ALL)
    in_specs = (
        token_spec,
        token_spec,
        P(("y", "c"), None),
        token_spec,
        flat_spec,
        row_spec,
        row_spec,
        row_spec,
        row_spec,
        flat_spec,
        row_spec,
        row_spec,
        row_spec,
    )
    out_specs = (
        token_spec,
        token_spec,
        flat_spec,
        row_spec,
        row_spec,
        row_spec,
        row_spec,
        flat_spec,
        row_spec,
        row_spec,
        row_spec,
    )
    return jax.shard_map(body, mesh=cut, in_specs=in_specs, out_specs=out_specs, check_vma=False)
```

```python
import functools

import jax
import jax.numpy as jnp
from jax import lax
from jax.experimental import pallas as pl
from jax.experimental.pallas import tpu as pltpu
from jax.sharding import Mesh, PartitionSpec as P

QUERY_HEADS = 16
KEY_VALUE_HEADS = 8
HEAD_SIZE = 64
F = 512
E = 16
GROUPS = 4
EXPERTS_HERE = E // GROUPS
LANES = 128
PAIR = 2 * HEAD_SIZE
HEAD_PACK = 4 * HEAD_SIZE
BLOCK = 256
QUERY_BLOCK = 512

NORM_EPS = 1e-06
RESIDUAL_SCALE = 0.22
SCALE_OF_SCORES = 0.015625
ROPE_BASE = 10000.0
NEGATIVE_HUGE = -1e30
HIGHEST_DOT = lax.Precision.HIGHEST
VMEM_LIMIT = 60 * 1024 * 1024

PLANE = ("b", "y", "c")
SEQ = ("a", "b")
ALL = ("a", "b", "y", "c")
SWAP = [(0, 1), (1, 0)]

f32 = jnp.float32
bf16 = jnp.bfloat16


def rotation_tables(positions):
    half = HEAD_SIZE // 2
    freq = jnp.power(ROPE_BASE, -2.0 * jnp.arange(half, dtype=f32) / HEAD_SIZE)
    angle = positions.astype(f32)[:, None] * freq[None, :]
    return jnp.cos(angle), jnp.sin(angle)


def rms_back(values, gain, grad_norm):
    mean_square = jnp.mean(values * values, axis=-1, keepdims=True)
    inverse = lax.rsqrt(mean_square + NORM_EPS)
    scaled_grad = grad_norm * gain
    grad_values = inverse * scaled_grad - values * inverse**3 * jnp.mean(
        values * scaled_grad, axis=-1, keepdims=True
    )
    grad_gain = jnp.sum(grad_norm * values * inverse, axis=0)
    return (grad_values, grad_gain)


def rms_scale(values, gain):
    mean_square = jnp.mean(values * values, axis=-1, keepdims=True)
    return values * lax.rsqrt(mean_square + NORM_EPS) * gain


def contract_rows(left_side, right_side):
    return lax.dot_general(
        left_side, right_side, (((0,), (0,)), ((), ())), preferred_element_type=f32
    )


def contract_cols(left_side, right_side):
    return lax.dot_general(
        left_side, right_side, (((1,), (1,)), ((), ())), preferred_element_type=f32
    )


def gather(x, axes):
    return lax.all_gather(x, axes, axis=0, tiled=True)


def scatter_sum(x, axes):
    return lax.psum_scatter(x, axes, scatter_dimension=0, tiled=True)


def pad_lanes(x, lanes):
    return jnp.pad(x, ((0, 0), (0, lanes - x.shape[1])))


def line_pairs(n, step):
    return [(i, i + step) for i in range(n) if 0 <= i + step < n]


def grid_gather(x):
    n = lax.axis_size("a")

    def cross(block, ends):
        return lax.ppermute(
            block, SEQ, [(2 * i + j, 2 * i + 1 - j) for i in range(n) if ends(i) for j in (0, 1)]
        )

    pieces = [(0, 0, x), (0, 1, cross(x, lambda i: True))]
    up = down = x
    for k in range(1, n):
        up = lax.ppermute(up, "a", line_pairs(n, 1))
        down = lax.ppermute(down, "a", line_pairs(n, -1))
        pieces += [(-k, 0, up), (-k, 1, cross(up, lambda i: i >= k))]
        pieces += [(k, 0, down), (k, 1, cross(down, lambda i: i + k < n))]
    return pieces


def plane_gather(x):
    swap = SWAP
    half = x.shape[0] // 2
    from_y = lax.ppermute(x, "y", SWAP)
    from_b = lax.ppermute(x, "b", SWAP)
    upper = lax.ppermute(from_b[:half], "y", SWAP)
    lower = lax.ppermute(from_y[half:], "b", SWAP)
    return [
        (block, lax.ppermute(block, "c", SWAP)) for block in (x, from_y, from_b, upper, lower)
    ]


def halve_send(v, axis, at):
    me = lax.axis_index(axis)
    other = lax.ppermute(lax.dynamic_index_in_dim(v, 1 - me, at, False), axis, SWAP)
    return lax.dynamic_index_in_dim(v, me, at, False), other


def halve_add(terms):
    own, other = terms
    return (own.astype(f32) + other.astype(f32)).astype(own.dtype)


def rotate_lanes(x, cos, sin):
    width = x.shape[-1]
    lane = lax.broadcasted_iota(jnp.int32, x.shape, x.ndim - 1)
    swapped = jnp.where(
        lane % HEAD_SIZE < HEAD_SIZE // 2,
        pltpu.roll(x, width - HEAD_SIZE // 2, x.ndim - 1),
        pltpu.roll(x, HEAD_SIZE // 2, x.ndim - 1),
    )
    return x * cos + swapped * sin


def spread_tables(cos, sin):
    return jnp.concatenate([cos] * 4, axis=1), jnp.concatenate([-sin, sin, -sin, sin], axis=1)


def key_tables(cos, sin):
    low = lower_lanes(cos.shape)
    return jnp.where(low, cos, 1.0), jnp.where(low, sin, 0.0)


def project_kernel(places, place_ref, *refs):
    count = 1 if places is None else len(places)
    blocks, refs = refs[:count], refs[count:]
    small_ref, w_ref, cos_ref, sin_ref, qkv_ref, normed_ref, x_ref = refs[:7]
    wide_cos_ref, wide_sin_ref, gain, held, sems = refs[7:]
    i = pl.program_id(0)
    slots = held.shape[0]

    @pl.when(i == 0)
    def _():
        if places is None:
            for slot in range(slots):
                pltpu.make_async_copy(blocks[0].at[slot], held.at[slot], sems.at[slot]).start()
        else:
            for (distance, crossed), block in zip(places, blocks):
                at = place_ref[1] + distance
                member = 1 - place_ref[2] if crossed else place_ref[2]

                @pl.when((at >= 0) & (at < slots // 2))
                def _(block=block, slot=2 * at + member):
                    pltpu.make_async_copy(block, held.at[slot], sems.at[slot]).start()

        gain[...] = jnp.transpose(small_ref[...].astype(f32))[E : E + 8, :]

    arrived = blocks[0].at[0] if places is None else blocks[0]
    pltpu.make_async_copy(arrived, held.at[i], sems.at[i]).wait()
    x = held[i]
    x_ref[...] = x
    normed = rms_scale(x.astype(f32), gain[0:1, :]).astype(bf16)
    normed_ref[...] = normed
    pre = jnp.dot(normed, w_ref[...], preferred_element_type=f32)
    cos, sin = spread_tables(cos_ref[...], sin_ref[...])
    wide_cos_ref[...] = cos
    wide_sin_ref[...] = sin
    qkv_ref[:, :PAIR] = rotate_lanes(pre[:, :PAIR], cos, sin).astype(bf16)
    qkv_ref[:, PAIR:] = rotate_lanes(pre[:, PAIR:], *key_tables(cos, sin)).astype(bf16)


def project(place, places, blocks, rows, packed, cos, sin):
    width = packed.shape[0]
    small_at = packed.shape[1] // LANES - 1
    span = cos.shape[0]
    table = pl.BlockSpec((rows, HEAD_SIZE // 2), lambda i, h: (i, 0))
    token_rows = pl.BlockSpec((rows, width), lambda i, h: (i, 0))
    return pl.pallas_call(
        functools.partial(project_kernel, places),
        grid_spec=pltpu.PrefetchScalarGridSpec(
            num_scalar_prefetch=1,
            grid=(span // rows,),
            in_specs=[pl.BlockSpec(memory_space=pl.ANY)] * len(blocks)
            + [
                pl.BlockSpec((width, LANES), lambda i, h: (0, small_at)),
                pl.BlockSpec((width, HEAD_PACK), lambda i, h: (0, h[0])),
                table,
                table,
            ],
            out_specs=[
                pl.BlockSpec((rows, HEAD_PACK), lambda i, h: (i, 0)),
                token_rows,
                token_rows,
                pl.BlockSpec((rows, PAIR), lambda i, h: (i, 0)),
                pl.BlockSpec((rows, PAIR), lambda i, h: (i, 0)),
            ],
            scratch_shapes=[
                pltpu.VMEM((8, width), f32),
                pltpu.VMEM((span // rows, rows, width), bf16),
                pltpu.SemaphoreType.DMA((span // rows,)),
            ],
        ),
        out_shape=[
            jax.ShapeDtypeStruct((span, HEAD_PACK), bf16),
            jax.ShapeDtypeStruct((span, width), bf16),
            jax.ShapeDtypeStruct((span, width), bf16),
            jax.ShapeDtypeStruct((span, PAIR), f32),
            jax.ShapeDtypeStruct((span, PAIR), f32),
        ],
        compiler_params=pltpu.CompilerParams(vmem_limit_bytes=VMEM_LIMIT),
        cost_estimate=pl.CostEstimate(
            flops=2 * span * width * HEAD_PACK, bytes_accessed=18 * 2**20, transcendentals=0
        ),
        name="project",
    )(place, *blocks, packed, packed, cos, sin)


def head_grads_kernel(head_ref, x_ref, normed_ref, w_ref, grad_ref, out_ref, acc, gain):
    i = pl.program_id(0)

    @pl.when(i == 0)
    def _():
        acc[...] = jnp.zeros_like(acc)
        gain[...] = jnp.zeros_like(gain)

    grad = grad_ref[...]
    acc[...] += contract_rows(grad, normed_ref[...])
    x = x_ref[...].astype(f32)
    inverse = lax.rsqrt(jnp.mean(x * x, axis=-1, keepdims=True) + NORM_EPS)
    back = contract_cols(grad, w_ref[...]) * (x * inverse)
    gain[...] += jnp.sum(back.reshape(back.shape[0] // 8, 8, back.shape[1]), axis=0)

    @pl.when(i == pl.num_programs(0) - 1)
    def _():
        out_ref[:, :HEAD_PACK] = jnp.transpose(acc[...]).astype(bf16)
        total = jnp.sum(gain[...], axis=0, keepdims=True)
        rows = lax.broadcasted_iota(jnp.int32, (LANES, total.shape[1]), 0)
        out_ref[:, HEAD_PACK:] = jnp.transpose(
            jnp.where(rows == 0, jnp.broadcast_to(total, rows.shape), 0.0)
        ).astype(bf16)


def head_grads(head, x, normed, packed, grads):
    span, width = x.shape
    rows = 2 * BLOCK
    token_rows = pl.BlockSpec((rows, width), lambda i, h: (i, 0))
    return pl.pallas_call(
        head_grads_kernel,
        grid_spec=pltpu.PrefetchScalarGridSpec(
            num_scalar_prefetch=1,
            grid=(span // rows,),
            in_specs=[
                token_rows,
                token_rows,
                pl.BlockSpec((width, HEAD_PACK), lambda i, h: (0, h[0])),
                pl.BlockSpec((rows, HEAD_PACK), lambda i, h: (i, 0)),
            ],
            out_specs=pl.BlockSpec((width, HEAD_PACK + LANES), lambda i, h: (0, 0)),
            scratch_shapes=[pltpu.VMEM((HEAD_PACK, width), f32), pltpu.VMEM((8, width), f32)],
        ),
        out_shape=jax.ShapeDtypeStruct((width, HEAD_PACK + LANES), bf16),
        compiler_params=pltpu.CompilerParams(vmem_limit_bytes=VMEM_LIMIT),
        cost_estimate=pl.CostEstimate(
            flops=4 * span * width * HEAD_PACK, bytes_accessed=12 * 2**20, transcendentals=0
        ),
        name="head_grads",
    )(head, x, normed, packed, grads)


def lower_lanes(shape):
    return lax.broadcasted_iota(jnp.int32, shape, len(shape) - 1) < HEAD_SIZE


def both_heads_low(pair):
    low = lower_lanes(pair.shape)
    return jnp.concatenate(
        [jnp.where(low, pair, 0.0), jnp.where(low, pltpu.roll(pair, HEAD_SIZE, 1), 0.0)], axis=0
    )


def both_heads_high(pair):
    low = lower_lanes(pair.shape)
    return jnp.concatenate(
        [jnp.where(low, 0.0, pltpu.roll(pair, HEAD_SIZE, 1)), jnp.where(low, 0.0, pair)], axis=0
    )


def block_bounds(bounds_ref):
    i, steps = pl.program_id(0), pl.num_programs(0)
    query_start = (i + bounds_ref[2 * steps]) * QUERY_BLOCK
    diagonal = query_start // BLOCK
    full = jnp.minimum(bounds_ref[steps + i], diagonal)
    return query_start, bounds_ref[i], full, diagonal, diagonal + QUERY_BLOCK // BLOCK


def pair_mask(doc, query_start):
    doc = jnp.concatenate([doc, doc], axis=1)
    queries = lax.broadcasted_iota(jnp.int32, doc.shape, 1) % QUERY_BLOCK + query_start

    def masked(scores, start):
        keys = lax.broadcasted_iota(jnp.int32, scores.shape, 0) + start
        return jnp.where((keys >= doc) & (keys <= queries), scores, NEGATIVE_HUGE)

    return masked


def attend_kernel(bounds_ref, q_ref, kv_ref, doc_ref, o_ref, low_ref, lse_ref, acc):
    query_start, first, full, diagonal, end = block_bounds(bounds_ref)
    q = both_heads_low(q_ref[...].astype(f32) * SCALE_OF_SCORES).astype(bf16)
    masked = pair_mask(doc_ref[0], query_start)
    acc[...] = jnp.zeros_like(acc)

    def step(mask, j, carried):
        top, total = carried
        start = pl.multiple_of(j * BLOCK, BLOCK)
        kv = kv_ref[pl.ds(start, BLOCK), :]
        scores = contract_cols(kv, q)
        if mask:
            scores = masked(scores, start)
        new = jnp.maximum(top, jnp.max(scores, axis=0, keepdims=True))
        probs = jnp.exp(scores - new)
        keep = jnp.exp(top - new)
        acc[...] = acc[...] * keep + contract_rows(kv, probs.astype(bf16))
        return new, total * keep + jnp.sum(probs, axis=0, keepdims=True)

    row = (1, 2 * QUERY_BLOCK)
    carried = (jnp.full(row, NEGATIVE_HUGE, f32), jnp.zeros(row, f32))
    carried = lax.fori_loop(first, full, functools.partial(step, True), carried)
    carried = lax.fori_loop(full, diagonal, functools.partial(step, False), carried)
    top, total = lax.fori_loop(diagonal, end, functools.partial(step, True), carried)
    mixed = jnp.transpose(acc[...] / total)
    one, two = mixed[:QUERY_BLOCK], mixed[QUERY_BLOCK:]
    out = jnp.where(lower_lanes(one.shape), pltpu.roll(one, HEAD_SIZE, 1), two)
    o_ref[...] = out
    low_ref[...] = out.astype(bf16)
    lse_ref[0] = top + jnp.log(total)


def attention_specs(kv_at, keys):
    pair = pl.BlockSpec((QUERY_BLOCK, PAIR), lambda i, s: (i, 0))
    return (
        pair,
        pl.BlockSpec((keys, PAIR), lambda i, s: (0, kv_at)),
        pl.BlockSpec((1, 1, QUERY_BLOCK), lambda i, s: (i, 0, 0)),
        pl.BlockSpec((1, 1, 2 * QUERY_BLOCK), lambda i, s: (i, 0, 0)),
    )


def attend(bounds, qkv, kv, kv_at, doc):
    queries, keys = qkv.shape[0], kv.shape[0]
    steps = queries // QUERY_BLOCK
    pair, whole, doc_row, lse_row = attention_specs(kv_at, keys)
    return pl.pallas_call(
        attend_kernel,
        grid_spec=pltpu.PrefetchScalarGridSpec(
            num_scalar_prefetch=1,
            grid=(steps,),
            in_specs=[pair, whole, doc_row],
            out_specs=[pair, pair, lse_row],
            scratch_shapes=[pltpu.VMEM((PAIR, 2 * QUERY_BLOCK), f32)],
        ),
        out_shape=[
            jax.ShapeDtypeStruct((queries, PAIR), f32),
            jax.ShapeDtypeStruct((queries, PAIR), bf16),
            jax.ShapeDtypeStruct((steps, 1, 2 * QUERY_BLOCK), f32),
        ],
        compiler_params=pltpu.CompilerParams(vmem_limit_bytes=VMEM_LIMIT),
        cost_estimate=pl.CostEstimate(
            flops=4 * queries * keys * PAIR, bytes_accessed=6 * 2**20, transcendentals=queries * keys
        ),
        name="attend",
    )(bounds, qkv, kv, doc)


def attend_back_kernel(
    fold, bounds_ref, q_ref, kv_ref, doc_ref, do_ref, o_ref, lse_ref, cos_ref, sin_ref, *refs
):
    if fold:
        out_ref, acc, dkv_ref = refs
    else:
        dq_ref, dkv_ref, acc = refs
    i = pl.program_id(0)
    query_start, first, full, diagonal, end = block_bounds(bounds_ref)

    @pl.when(i == 0)
    def _():
        dkv_ref[...] = jnp.zeros_like(dkv_ref)

    q = both_heads_low(q_ref[...].astype(f32) * SCALE_OF_SCORES).astype(bf16)
    grad = do_ref[...].astype(f32)
    product = jnp.transpose(grad * o_ref[...])
    delta = jnp.concatenate(
        [
            jnp.sum(product[:HEAD_SIZE], axis=0, keepdims=True),
            jnp.sum(product[HEAD_SIZE:], axis=0, keepdims=True),
        ],
        axis=1,
    )
    grad = both_heads_high(grad).astype(bf16)
    sources = jnp.concatenate([q, grad], axis=0)
    masked = pair_mask(doc_ref[0], query_start)
    lse = lse_ref[0]
    acc[...] = jnp.zeros_like(acc)

    def step(mask, j, carried):
        start = pl.multiple_of(j * BLOCK, BLOCK)
        kv = kv_ref[pl.ds(start, BLOCK), :]
        scores = contract_cols(kv, q) - lse
        if mask:
            scores = masked(scores, start)
        probs = jnp.exp(scores)
        grad_scores = (probs * (contract_cols(kv, grad) - delta)).astype(bf16)
        acc[...] += contract_rows(kv, grad_scores)
        both = jnp.concatenate([grad_scores, probs.astype(bf16)], axis=1)
        dkv_ref[pl.ds(start, BLOCK), :] += jnp.dot(both, sources, preferred_element_type=f32)
        return carried

    lax.fori_loop(first, full, functools.partial(step, True), 0)
    lax.fori_loop(full, diagonal, functools.partial(step, False), 0)
    lax.fori_loop(diagonal, end, functools.partial(step, True), 0)
    dq = jnp.transpose(acc[...])
    one, two = dq[:QUERY_BLOCK], dq[QUERY_BLOCK:]
    dq = jnp.where(lower_lanes(one.shape), one, pltpu.roll(two, HEAD_SIZE, 1))
    if not fold:
        dq_ref[...] = dq
        return
    mine = pl.ds(pl.multiple_of(i * QUERY_BLOCK, QUERY_BLOCK), QUERY_BLOCK)
    out_ref[mine, :PAIR] = rotate_lanes(
        dq * SCALE_OF_SCORES, cos_ref[mine, :], -sin_ref[mine, :]
    ).astype(bf16)

    @pl.when(i == pl.num_programs(0) - 1)
    def _():
        def finish(j, carried):
            part = pl.ds(pl.multiple_of(j * BLOCK, BLOCK), BLOCK)
            cos, sin = key_tables(cos_ref[part, :], sin_ref[part, :])
            out_ref[part, PAIR:] = rotate_lanes(dkv_ref[part, :], cos, -sin).astype(bf16)
            return carried

        lax.fori_loop(0, dkv_ref.shape[0] // BLOCK, finish, 0)


def attend_back(bounds, qkv, kv, kv_at, doc, grad, out, lse, cos, sin, fold):
    queries, keys = qkv.shape[0], kv.shape[0]
    steps = queries // QUERY_BLOCK
    pair, whole, doc_row, lse_row = attention_specs(kv_at, keys)
    table = pl.BlockSpec(cos.shape, lambda i, s: (0, 0))
    acc = pltpu.VMEM((PAIR, 2 * QUERY_BLOCK), f32)
    if fold:
        out_specs = pl.BlockSpec((queries, HEAD_PACK), lambda i, s: (0, 0))
        out_shape = jax.ShapeDtypeStruct((queries, HEAD_PACK), bf16)
        scratch = [acc, pltpu.VMEM((keys, PAIR), f32)]
    else:
        out_specs = [pair, pl.BlockSpec((keys, PAIR), lambda i, s: (0, 0))]
        out_shape = [
            jax.ShapeDtypeStruct((queries, PAIR), f32),
            jax.ShapeDtypeStruct((keys, PAIR), f32),
        ]
        scratch = [acc]
    return pl.pallas_call(
        functools.partial(attend_back_kernel, fold),
        grid_spec=pltpu.PrefetchScalarGridSpec(
            num_scalar_prefetch=1,
            grid=(steps,),
            in_specs=[pair, whole, doc_row, pair, pair, lse_row, table, table],
            out_specs=out_specs,
            scratch_shapes=scratch,
        ),
        out_shape=out_shape,
        compiler_params=pltpu.CompilerParams(vmem_limit_bytes=VMEM_LIMIT),
        cost_estimate=pl.CostEstimate(
            flops=10 * queries * keys * PAIR,
            bytes_accessed=8 * 2**20,
            transcendentals=queries * keys,
        ),
        name="attend_back",
    )(bounds, qkv, kv, doc, grad, out, lse, cos, sin)


def unrotate_kernel(dq_ref, dkv_ref, cos_ref, sin_ref, out_ref):
    cos, sin = cos_ref[...], sin_ref[...]
    dq = rotate_lanes(dq_ref[...] * SCALE_OF_SCORES, cos, -sin)
    cos, sin = key_tables(cos, sin)
    dkv = rotate_lanes(dkv_ref[...], cos, -sin)
    out_ref[...] = jnp.concatenate([dq, dkv], axis=1).astype(bf16)


def unrotate(dq, dkv, cos, sin):
    rows = dq.shape[0]
    pair = pl.BlockSpec((BLOCK, PAIR), lambda i: (i, 0))
    return pl.pallas_call(
        unrotate_kernel,
        grid=(rows // BLOCK,),
        in_specs=[pair, pair, pair, pair],
        out_specs=pl.BlockSpec((BLOCK, HEAD_PACK), lambda i: (i, 0)),
        out_shape=jax.ShapeDtypeStruct((rows, HEAD_PACK), bf16),
        cost_estimate=pl.CostEstimate(
            flops=rows * HEAD_PACK * 8, bytes_accessed=rows * HEAD_PACK * 14, transcendentals=0
        ),
        name="unrotate",
    )(dq, dkv, cos, sin)


def place_experts_kernel(place_ref, *refs):
    blocks, (ct_ref, w_ref, z_ref, sems) = refs[:10], refs[10:]
    core = place_ref[1]
    rows = w_ref.shape[1] // 2
    half = rows // 2
    sources = [[(0, 0, rows)], [(1, 0, rows)], [(2, 0, rows)], [(3, 0, half), (4, half, half)]]
    for step, parts in enumerate(sources):

        @pl.when(pl.program_id(0) == step)
        def _(parts=parts):
            copies = []
            for source, start, length in parts:
                for other in (0, 1):
                    first = jnp.where(core == other, 0, rows) + start
                    at = pl.ds(pl.multiple_of(first, half), length)
                    copies.append(
                        pltpu.make_async_copy(
                            blocks[2 * source + other], w_ref.at[0, at, :], sems.at[len(copies)]
                        )
                    )
            for copy in copies:
                copy.start()
            for copy in copies:
                copy.wait()

    z_ref[0] = jnp.dot(ct_ref[...], w_ref[0, :, 2 * F :], preferred_element_type=f32)


def place_experts(place, parts, early, width):
    rows = early.shape[0]
    blocks = [block for pair in parts for block in pair]
    return pl.pallas_call(
        place_experts_kernel,
        grid_spec=pltpu.PrefetchScalarGridSpec(
            num_scalar_prefetch=1,
            grid=(EXPERTS_HERE,),
            in_specs=[pl.BlockSpec(memory_space=pl.ANY)] * len(blocks)
            + [pl.BlockSpec((rows, width), lambda r, s: (0, 0))],
            out_specs=[
                pl.BlockSpec((1, width, 3 * F), lambda r, s: (s[0] ^ r, 0, 0)),
                pl.BlockSpec((1, rows, F), lambda r, s: (s[0] ^ r, 0, 0)),
            ],
            scratch_shapes=[pltpu.SemaphoreType.DMA((4,))],
        ),
        out_shape=[
            jax.ShapeDtypeStruct((EXPERTS_HERE, width, 3 * F), bf16),
            jax.ShapeDtypeStruct((EXPERTS_HERE, rows, F), f32),
        ],
        compiler_params=pltpu.CompilerParams(vmem_limit_bytes=VMEM_LIMIT),
        cost_estimate=pl.CostEstimate(
            flops=2 * EXPERTS_HERE * rows * width * F, bytes_accessed=36 * 2**20, transcendentals=0
        ),
        name="place_experts",
    )(place, *blocks, early)


def lane_column(x, at):
    lane = lax.broadcasted_iota(jnp.int32, x.shape, 1)
    return jnp.sum(jnp.where(lane == at, x, 0.0), axis=1, keepdims=True)


def experts_kernel(
    group_ref, n_ref, routed_ref, router_ref, w_ref, z_ref,
    back_ref, gates_ref, hidden_ref, pre_ref, acc, dots,
):
    e = pl.program_id(0)
    own = group_ref[0] * EXPERTS_HERE + e
    rows = n_ref.shape[0]

    @pl.when(e == 0)
    def _():
        logits = jnp.dot(n_ref[...], router_ref[...], preferred_element_type=f32)
        routed = routed_ref[...].astype(f32) > 0.5
        highest = jnp.max(jnp.where(routed, logits, NEGATIVE_HUGE), axis=1, keepdims=True)
        weights = jnp.where(routed, jnp.exp(jnp.where(routed, logits - highest, 0.0)), 0.0)
        gates_ref[...] = weights / jnp.sum(weights, axis=1, keepdims=True)
        acc[...] = jnp.zeros_like(acc)
        dots[...] = jnp.zeros_like(dots)

    w_in = w_ref[0, :, : 2 * F]
    for t in range(rows // BLOCK):
        part = pl.ds(t * BLOCK, BLOCK)
        pre = jnp.dot(n_ref[part, :], w_in, preferred_element_type=f32)
        gate, up = pre[:, :F], pre[:, F:]
        z = z_ref[0, part, :]
        weight = lane_column(gates_ref[part, :], own)
        sig = 1.0 / (1.0 + jnp.exp(-gate))
        act = gate * sig
        hidden = act * up
        hidden_ref[0, part, :] = (weight * hidden).astype(bf16)
        dot = RESIDUAL_SCALE * jnp.sum(hidden.astype(bf16).astype(f32) * z, axis=1, keepdims=True)
        lane = lax.broadcasted_iota(jnp.int32, (BLOCK, LANES), 1)
        dots[part, :] += jnp.where(lane == own, dot, 0.0)
        scaled = (RESIDUAL_SCALE * weight) * z
        pre_ref[0, part, :F] = (scaled * up * (sig + act * (1.0 - sig))).astype(bf16)
        pre_ref[0, part, F:] = (scaled * act).astype(bf16)
        acc[part, :] += contract_cols(pre_ref[0, part, :], w_in)

    @pl.when(e == EXPERTS_HERE - 1)
    def _():
        width = n_ref.shape[1]
        back_ref[:, :width] = acc[...].astype(bf16)
        high = dots[...].astype(bf16)
        low = dots[...] - high.astype(f32)
        back_ref[:, width:] = (high.astype(f32) + pltpu.roll(low, E, 1)).astype(bf16)


def experts(group, normed, early, packed, w_all, z):
    rows, width = normed.shape
    count = w_all.shape[0]
    whole = pl.BlockSpec((rows, width), lambda e, g: (0, 0))
    column = width // LANES
    router_at = packed.shape[1] // LANES - 1
    return pl.pallas_call(
        experts_kernel,
        grid_spec=pltpu.PrefetchScalarGridSpec(
            num_scalar_prefetch=1,
            grid=(count,),
            in_specs=[
                whole,
                pl.BlockSpec((rows, LANES), lambda e, g: (0, column)),
                pl.BlockSpec((width, LANES), lambda e, g: (0, router_at)),
                pl.BlockSpec((1, width, 3 * F), lambda e, g: (e, 0, 0)),
                pl.BlockSpec((1, rows, F), lambda e, g: (e, 0, 0)),
            ],
            out_specs=[
                pl.BlockSpec((rows, width + LANES), lambda e, g: (0, 0)),
                pl.BlockSpec((rows, LANES), lambda e, g: (0, 0)),
                pl.BlockSpec((1, rows, F), lambda e, g: (e, 0, 0)),
                pl.BlockSpec((1, rows, 2 * F), lambda e, g: (e, 0, 0)),
            ],
            scratch_shapes=[pltpu.VMEM((rows, width), f32), pltpu.VMEM((rows, LANES), f32)],
        ),
        out_shape=[
            jax.ShapeDtypeStruct((rows, width + LANES), bf16),
            jax.ShapeDtypeStruct((rows, LANES), f32),
            jax.ShapeDtypeStruct((count, rows, F), bf16),
            jax.ShapeDtypeStruct((count, rows, 2 * F), bf16),
        ],
        compiler_params=pltpu.CompilerParams(vmem_limit_bytes=VMEM_LIMIT),
        cost_estimate=pl.CostEstimate(
            flops=2 * count * rows * width * 4 * F, bytes_accessed=40 * 2**20, transcendentals=0
        ),
        name="experts",
    )(group, normed, early, packed, w_all, z)


def expert_grads_kernel(with_y, half_ref, n_ref, ct_ref, w_ref, hidden_ref, pre_ref, *refs):
    if with_y:
        left_ref, right_ref, y_ref, n_t, ct_t, acc = refs
    else:
        left_ref, right_ref, n_t, ct_t = refs
    e = pl.program_id(0)
    cut = left_ref.shape[2]

    @pl.when(e == 0)
    def _():
        n_t[...] = jnp.transpose(n_ref[...])
        ct_t[...] = jnp.transpose(ct_ref[...])
        if with_y:
            acc[...] = jnp.zeros_like(acc)

    grads = jnp.dot(n_t[...], pre_ref[0], preferred_element_type=f32).astype(bf16)
    left_ref[0] = grads[:, :cut]
    right_ref[0, :, : 2 * F - cut] = grads[:, cut:]
    right_ref[0, :, 2 * F - cut :] = (
        RESIDUAL_SCALE * jnp.dot(ct_t[...], hidden_ref[0], preferred_element_type=f32)
    ).astype(bf16)
    if not with_y:
        return
    acc[...] += contract_cols(hidden_ref[0], w_ref[0, :, 2 * F :])

    @pl.when(e == pl.num_programs(0) - 1)
    def _():
        y_ref[...] = acc[...].astype(bf16)


def expert_grads(half, halves, normed, early, w_all, hidden, pre, with_y):
    rows, width = normed.shape
    count = w_all.shape[0]
    own, cut = width // halves, 3 * F // 2
    feature = pl.BlockSpec((rows, own), lambda e, h: (0, h[0]))
    out_specs = [pl.BlockSpec((1, own, cut), lambda e, h: (e, 0, 0))] * 2
    out_shape = [jax.ShapeDtypeStruct((count, own, cut), bf16)] * 2
    scratch = [pltpu.VMEM((own, rows), bf16), pltpu.VMEM((own, rows), bf16)]
    if with_y:
        out_specs.append(pl.BlockSpec((rows, width), lambda e, h: (0, 0)))
        out_shape.append(jax.ShapeDtypeStruct((rows, width), bf16))
        scratch.append(pltpu.VMEM((rows, width), f32))
    return pl.pallas_call(
        functools.partial(expert_grads_kernel, with_y),
        grid_spec=pltpu.PrefetchScalarGridSpec(
            num_scalar_prefetch=1,
            grid=(count,),
            in_specs=[
                feature,
                feature,
                pl.BlockSpec((1, width, 3 * F), lambda e, h: (e, 0, 0)),
                pl.BlockSpec((1, rows, F), lambda e, h: (e, 0, 0)),
                pl.BlockSpec((1, rows, 2 * F), lambda e, h: (e, 0, 0)),
            ],
            out_specs=out_specs,
            scratch_shapes=scratch,
        ),
        out_shape=out_shape,
        compiler_params=pltpu.CompilerParams(vmem_limit_bytes=VMEM_LIMIT),
        cost_estimate=pl.CostEstimate(
            flops=2 * count * rows * width * 3 * F // halves + 2 * with_y * count * rows * width * F,
            bytes_accessed=30 * 2**20,
            transcendentals=0,
        ),
        name="expert_grads",
    )(half, normed, early, w_all, hidden, pre)


def join_kernel(place_ref, o_ref, w_ref, small_ref, x_ref, normed_ref, resid_ref, own_ref, gain):
    t = pl.program_id(0)
    b = place_ref[2]

    @pl.when(t == 0)
    def _():
        gain[...] = jnp.transpose(small_ref[...].astype(f32))[E : E + 8, :]

    pairs = []
    for a in range(o_ref.shape[0]):
        same, other = o_ref[a, 0, 0], o_ref[a, 1, 0]
        pairs.append(jnp.where(b == 0, same, other))
        pairs.append(jnp.where(b == 0, other, same))
    attended = jnp.concatenate(pairs, axis=1)
    resid = x_ref[...].astype(f32) + RESIDUAL_SCALE * jnp.dot(
        attended, w_ref[...], preferred_element_type=f32
    )
    normed_ref[...] = rms_scale(resid, gain[1:2, :]).astype(bf16)

    @pl.when(t == place_ref[1])
    def _():
        resid_ref[...] = resid
        own_ref[...] = attended


def join(place, outs, packed, weights_at, x):
    width = packed.shape[0]
    lines, _, _, rows, pair = outs.shape
    small_at = packed.shape[1] // LANES - 1
    own = pl.BlockSpec((rows, width), lambda t, s: (0, 0))
    return pl.pallas_call(
        join_kernel,
        grid_spec=pltpu.PrefetchScalarGridSpec(
            num_scalar_prefetch=1,
            grid=(lines,),
            in_specs=[
                pl.BlockSpec((lines, 2, 1, rows, pair), lambda t, s: (0, 0, t, 0, 0)),
                pl.BlockSpec((width, width), lambda t, s: (0, weights_at)),
                pl.BlockSpec((width, LANES), lambda t, s: (0, small_at)),
                pl.BlockSpec((rows, width), lambda t, s: (2 * t + s[2], 0)),
            ],
            out_specs=[pl.BlockSpec((rows, width), lambda t, s: (t, 0)), own, own],
            scratch_shapes=[pltpu.VMEM((8, width), f32)],
        ),
        out_shape=[
            jax.ShapeDtypeStruct((lines * rows, width), bf16),
            jax.ShapeDtypeStruct((rows, width), f32),
            jax.ShapeDtypeStruct((rows, width), bf16),
        ],
        compiler_params=pltpu.CompilerParams(vmem_limit_bytes=VMEM_LIMIT),
        cost_estimate=pl.CostEstimate(
            flops=2 * lines * rows * width * width, bytes_accessed=12 * 2**20, transcendentals=0
        ),
        name="join",
    )(place, outs, packed, packed, x)


def weight_sums_kernel(sums_ref, q_ref, k_ref, v_ref, gain_ref):
    groups, heads, members = sums_ref.shape[:3]
    gain = jnp.zeros(gain_ref.shape, f32)
    values = []
    for h in range(heads):
        total = jnp.zeros(sums_ref.shape[3:], f32)
        for g in range(groups):
            for member in range(members):
                total += sums_ref[g, h, member].astype(f32)
        values.append(total)
        gain += total[:, HEAD_PACK:]
        q_ref[:, h * PAIR : (h + 1) * PAIR] = total[:, :PAIR]
    gain_ref[...] = gain
    for h in range(0, heads, 2):
        one, two = values[h][:, PAIR:HEAD_PACK], values[h + 1][:, PAIR:HEAD_PACK]
        low = lower_lanes(one.shape)
        at = slice(h // 2 * PAIR, (h // 2 + 1) * PAIR)
        k_ref[:, at] = jnp.where(low, one, pltpu.roll(two, HEAD_SIZE, 1))
        v_ref[:, at] = jnp.where(low, pltpu.roll(one, HEAD_SIZE, 1), two)


def weight_sums(sums):
    rows, heads = sums.shape[3], sums.shape[1]
    return pl.pallas_call(
        weight_sums_kernel,
        out_shape=[
            jax.ShapeDtypeStruct((rows, heads * PAIR), f32),
            jax.ShapeDtypeStruct((rows, heads * HEAD_SIZE), f32),
            jax.ShapeDtypeStruct((rows, heads * HEAD_SIZE), f32),
            jax.ShapeDtypeStruct((rows, LANES), f32),
        ],
        compiler_params=pltpu.CompilerParams(vmem_limit_bytes=VMEM_LIMIT),
        cost_estimate=pl.CostEstimate(flops=2**20, bytes_accessed=2 * 2**20, transcendentals=0),
        name="weight_sums",
    )(sums)


def exchange(x, axes):
    return lax.all_to_all(x, axes, 0, 0, tiled=True)


def body(
    tokens,
    cotangent,
    segment_ids,
    routes,
    norm_attn,
    w_query,
    key_weight_matrix,
    value_weight_matrix,
    w_output,
    norm_moe,
    w_router,
    expert_in,
    expert_out,
):
    x_local = tokens[0].astype(f32)
    token_count, width = x_local.shape
    seg_row = segment_ids[0]
    group = lax.axis_index("a")
    head_axes = SEQ if lax.axis_size(SEQ) == KEY_VALUE_HEADS else ("b",)
    whole_rows = head_axes == SEQ
    span = token_count * KEY_VALUE_HEADS
    span_start = 0 if whole_rows else group * span

    def start_of_doc(ids):
        return jnp.sum((seg_row[None, :] < ids[:, None]).astype(jnp.int32), axis=1)

    seg_span = lax.dynamic_slice_in_dim(seg_row, span_start, span)
    doc_span = start_of_doc(seg_span)
    cos_span, sin_span = rotation_tables(
        span_start + jnp.arange(span, dtype=jnp.int32) - doc_span
    )
    by_block = doc_span.reshape(-1, QUERY_BLOCK)
    bounds = jnp.concatenate(
        [
            by_block[:, 0] // BLOCK,
            (by_block[:, -1] + BLOCK - 1) // BLOCK,
            jnp.full((1,), span_start // QUERY_BLOCK, jnp.int32),
        ]
    )
    doc_rows = by_block[:, None, :]

    own_rows = w_query.shape[0]
    by_head = jnp.concatenate(
        [
            w_query.astype(bf16).reshape(own_rows, KEY_VALUE_HEADS, PAIR),
            key_weight_matrix.astype(bf16).reshape(own_rows, KEY_VALUE_HEADS, HEAD_SIZE),
            value_weight_matrix.astype(bf16).reshape(own_rows, KEY_VALUE_HEADS, HEAD_SIZE),
        ],
        axis=2,
    ).reshape(own_rows, KEY_VALUE_HEADS * HEAD_PACK)
    qkv_width = KEY_VALUE_HEADS * HEAD_PACK
    first_all = gather(
        jnp.concatenate(
            [
                by_head,
                w_output.astype(bf16),
                pad_lanes(
                    jnp.concatenate(
                        [
                            w_router.astype(bf16),
                            norm_attn.astype(bf16)[:, None],
                            norm_moe.astype(bf16)[:, None],
                        ],
                        axis=1,
                    ),
                    LANES,
                ),
            ],
            axis=1,
        ),
        ALL,
    )
    experts_low = jnp.concatenate([expert_in.astype(bf16), expert_out.astype(bf16)], axis=1)
    if whole_rows:
        pieces = grid_gather(tokens[0])
        places = [piece[:2] for piece in pieces]
        blocks = tuple(piece[2] for piece in pieces)
    else:
        places = None
        blocks = (gather(tokens[0], "b").reshape((-1,) + tokens.shape[1:]),)
    first_all, experts_low, blocks, cos_span, sin_span, bounds, doc_rows = (
        lax.optimization_barrier(
            (first_all, experts_low, blocks, cos_span, sin_span, bounds, doc_rows)
        )
    )
    output_w = first_all[:, qkv_width : qkv_width + width]
    small_at = qkv_width + width
    router_w = first_all[:, small_at : small_at + E]
    gain_one_f = first_all[:, small_at + E].astype(f32)
    gain_two_f = first_all[:, small_at + E + 1].astype(f32)

    expert_ids = jnp.arange(E, dtype=jnp.int32)
    routed_own = jnp.any(routes[0][:, :, None] == expert_ids[None, None, :], axis=1)
    early = jnp.concatenate([cotangent[0], pad_lanes(routed_own.astype(bf16), LANES)], axis=1)
    early, first_all = lax.optimization_barrier((early, first_all))
    early_all = gather(early, "a")
    small_plane = lax.axis_size("b") == 2 and lax.axis_size("y") == 2
    if small_plane:
        parts = plane_gather(experts_low)
    else:
        parts = gather(experts_low, PLANE)

    place = jnp.stack([lax.axis_index(head_axes), group, lax.axis_index("b")])
    qkv, normed_span, x_span, wide_cos, wide_sin = project(
        place, places, blocks, token_count, first_all, cos_span, sin_span
    )
    if whole_rows:
        kv, kv_at = qkv, 1
    else:
        kv, kv_at = gather(qkv[:, PAIR:], "a"), 0
    attention_result, attended, log_total = attend(bounds, qkv, kv, kv_at, doc_rows)
    if small_plane:
        member = lax.axis_index("b")
        by_column = attended.reshape(GROUPS, 2, token_count, PAIR)
        other = lax.ppermute(
            lax.dynamic_index_in_dim(by_column, 1 - member, 1, False), "b", SWAP
        )
        own = lax.dynamic_index_in_dim(by_column, member, 1, False)
        pair, early_all = lax.optimization_barrier((jnp.stack([own, other]), early_all))
        outs = lax.all_gather(pair, "a", axis=0, tiled=False)
        normed_all, resid, attended_low = join(place, outs, first_all, qkv_width // width, x_span)
        normed_two = lax.dynamic_slice_in_dim(normed_all, group * token_count, token_count)
        home = jnp.stack([member * 2 + lax.axis_index("y"), lax.axis_index("c")])
        experts_all, grad_hidden = place_experts(home, parts, early_all, width)
    else:
        attended_low = (
            exchange(attended.reshape(KEY_VALUE_HEADS, token_count, PAIR), head_axes)
            .transpose(1, 0, 2)
            .reshape(token_count, QUERY_HEADS * HEAD_SIZE)
        )
        attn_out = jnp.dot(attended_low, output_w, preferred_element_type=f32)
        resid = x_local + RESIDUAL_SCALE * attn_out
        normed_two = rms_scale(resid, gain_two_f).astype(bf16)
        normed_all = gather(normed_two, "a")
        experts_all = parts.reshape(EXPERTS_HERE, width, 3 * F)
        grad_hidden = jnp.einsum(
            "td,edf->etf",
            early_all[:, :width],
            experts_all[:, :, 2 * F :],
            preferred_element_type=f32,
        )
    back_part, gates_all, gated_hidden, grad_pre = experts(
        group.reshape(1), normed_all, early_all, first_all, experts_all, grad_hidden
    )
    back_own = scatter_sum(back_part, "a").astype(f32)
    inputs = (normed_all, early_all, experts_all, gated_hidden, grad_pre)
    if small_plane:
        core = lax.axis_index("c")
        send = expert_grads((1 - core).reshape(1), 2, *inputs, False)
        arrived = [lax.ppermute(x, "c", SWAP) for x in send]
        *keep, moe_part = expert_grads(core.reshape(1), 2, *inputs, True)
        left, right = (
            halve_add(terms).reshape((2, 2) + terms[0].shape[1:]) for terms in zip(keep, arrived)
        )
        back_own, moe_part, left, right = lax.optimization_barrier(
            (back_own, moe_part, left, right)
        )
        left, right = halve_send(left, "y", 1), halve_send(right, "b", 0)
    else:
        *grads, moe_part = expert_grads(jnp.zeros((1,), jnp.int32), 1, *inputs, True)
        grad_experts = jnp.concatenate(grads, axis=2)
        back_own, moe_part, grad_experts = lax.optimization_barrier(
            (back_own, moe_part, grad_experts)
        )
        grad_experts = scatter_sum(grad_experts.reshape(EXPERTS_HERE * width, 3 * F), PLANE)
    moe_sum = scatter_sum(moe_part, "a")

    grad_out = cotangent[0].astype(f32)
    gates = lax.dynamic_slice_in_dim(gates_all, group * token_count, token_count)[:, :E]
    gate_grads_own = back_own[:, width : width + E] + back_own[:, width + E : width + 2 * E]
    grad_logits = gates * (gate_grads_own - jnp.sum(gates * gate_grads_own, axis=-1, keepdims=True))
    grad_normed_two = back_own[:, :width] + jnp.dot(
        grad_logits, router_w.astype(f32).T, precision=HIGHEST_DOT
    )
    grad_router = jnp.dot(normed_two.astype(f32).T, grad_logits, precision=HIGHEST_DOT)
    grad_resid_norm, grad_gain_two = rms_back(resid, gain_two_f, grad_normed_two)
    grad_resid = grad_out + grad_resid_norm
    grad_attn_low = (RESIDUAL_SCALE * grad_resid).astype(bf16)
    grad_heads = contract_cols(grad_attn_low, output_w).astype(bf16)
    grad_mixed = exchange(
        grad_heads.reshape(token_count, KEY_VALUE_HEADS, PAIR).transpose(1, 0, 2), head_axes
    ).reshape(span, PAIR)
    small = jnp.concatenate([grad_router, grad_gain_two[:, None]], axis=1)
    second_part = jnp.concatenate(
        [contract_rows(attended_low, grad_attn_low), pad_lanes(small, LANES)], axis=1
    ).astype(bf16)
    cols = second_part.shape[1]
    second_part = second_part.reshape(GROUPS, -1, own_rows, cols).transpose(1, 0, 2, 3)
    if small_plane:
        left, right = halve_add(left), halve_add(right)
        second_part, left, right, grad_mixed = lax.optimization_barrier(
            (second_part, left, right, grad_mixed)
        )
        left, right = halve_send(left, "b", 0), halve_send(right, "y", 0)
    rest = scatter_sum(second_part.reshape(-1, cols), PLANE)
    grads = attend_back(
        bounds, qkv, kv, kv_at, doc_rows, grad_mixed, attention_result, log_total,
        wide_cos, wide_sin, whole_rows,
    )
    if whole_rows:
        grad_pack = grads
    else:
        grad_kv = scatter_sum(grads[1].astype(bf16), "a").astype(f32)
        grad_pack = unrotate(grads[0], grad_kv, wide_cos, wide_sin)
    if small_plane:
        left, right, moe_sum, grad_pack = lax.optimization_barrier(
            (left, right, moe_sum, grad_pack)
        )
    first_part = head_grads(place, x_span, normed_span, first_all, grad_pack)
    rest, first_part = lax.optimization_barrier((rest, first_part))
    rest = scatter_sum(rest, "a")
    by_tokens = exchange(grad_pack.reshape(KEY_VALUE_HEADS, token_count, HEAD_PACK), head_axes)
    by_tokens, first_part = lax.optimization_barrier((by_tokens, first_part))
    sums = exchange(first_part.reshape(-1, own_rows, first_part.shape[1]), ALL)
    sums, moe_sum, resid = lax.optimization_barrier((sums, moe_sum, resid))
    grad_q_w, grad_k_w, grad_v_w, grad_gain_one = weight_sums(
        sums.reshape(-1, KEY_VALUE_HEADS, lax.axis_size(("y", "c")), own_rows, first_part.shape[1])
    )
    rest = rest.astype(f32)
    grad_qkv = by_tokens.transpose(1, 0, 2).reshape(token_count, qkv_width)
    grad_normed_one = contract_cols(grad_qkv, first_all[:, :qkv_width])
    grad_x_norm, _ = rms_back(x_local, gain_one_f, grad_normed_one)
    grad_input = grad_resid + grad_x_norm
    layer_sum = resid + RESIDUAL_SCALE * moe_sum.astype(f32)
    if small_plane:
        grad_experts = jnp.concatenate(
            [own.astype(f32) + other.astype(f32) for own, other in (left, right)], axis=1
        )
    else:
        grad_experts = grad_experts.astype(f32)
    return (
        layer_sum.astype(bf16)[None],
        grad_input[None],
        grad_gain_one[:, 0],
        grad_q_w,
        grad_k_w,
        grad_v_w,
        rest[:, :width],
        rest[:, width + E],
        rest[:, width : width + E],
        grad_experts[:, : 2 * F],
        grad_experts[:, 2 * F :],
    )


def solution(mesh):
    seq, row = mesh.shape["seq"], mesh.shape["row"]
    cut = Mesh(mesh.devices.reshape(GROUPS, seq // GROUPS, row // 2, 2), ALL)
    token_spec = P(("y", "c"), SEQ, None)
    row_spec = P(ALL, None)
    flat_spec = P(ALL)
    in_specs = (
        token_spec,
        token_spec,
        P(("y", "c"), None),
        token_spec,
        flat_spec,
        row_spec,
        row_spec,
        row_spec,
        row_spec,
        flat_spec,
        row_spec,
        row_spec,
        row_spec,
    )
    out_specs = (
        token_spec,
        token_spec,
        flat_spec,
        row_spec,
        row_spec,
        row_spec,
        row_spec,
        flat_spec,
        row_spec,
        row_spec,
        row_spec,
    )
    return jax.shard_map(body, mesh=cut, in_specs=in_specs, out_specs=out_specs, check_vma=False)
```

```python
import functools

import jax
import jax.numpy as jnp
from jax import lax
from jax.experimental import pallas as pl
from jax.experimental.pallas import tpu as pltpu
from jax.sharding import Mesh, PartitionSpec as P

QUERY_HEADS = 16
KEY_VALUE_HEADS = 8
HEAD_SIZE = 64
F = 512
E = 16
GROUPS = 4
EXPERTS_HERE = E // GROUPS
LANES = 128
PAIR = 2 * HEAD_SIZE
HEAD_PACK = 4 * HEAD_SIZE
BLOCK = 256
QUERY_BLOCK = 512

NORM_EPS = 1e-06
RESIDUAL_SCALE = 0.22
SCALE_OF_SCORES = 0.015625
ROPE_BASE = 10000.0
NEGATIVE_HUGE = -1e30
HIGHEST_DOT = lax.Precision.HIGHEST
VMEM_LIMIT = 60 * 1024 * 1024

PLANE = ("b", "y", "c")
SEQ = ("a", "b")
ALL = ("a", "b", "y", "c")
SWAP = [(0, 1), (1, 0)]

f32 = jnp.float32
bf16 = jnp.bfloat16


def rotation_tables(positions):
    half = HEAD_SIZE // 2
    freq = jnp.power(ROPE_BASE, -2.0 * jnp.arange(half, dtype=f32) / HEAD_SIZE)
    angle = positions.astype(f32)[:, None] * freq[None, :]
    return jnp.cos(angle), jnp.sin(angle)


def rms_back(values, gain, grad_norm):
    mean_square = jnp.mean(values * values, axis=-1, keepdims=True)
    inverse = lax.rsqrt(mean_square + NORM_EPS)
    scaled_grad = grad_norm * gain
    grad_values = inverse * scaled_grad - values * inverse**3 * jnp.mean(
        values * scaled_grad, axis=-1, keepdims=True
    )
    grad_gain = jnp.sum(grad_norm * values * inverse, axis=0)
    return (grad_values, grad_gain)


def rms_scale(values, gain):
    mean_square = jnp.mean(values * values, axis=-1, keepdims=True)
    return values * lax.rsqrt(mean_square + NORM_EPS) * gain


def contract_rows(left_side, right_side):
    return lax.dot_general(
        left_side, right_side, (((0,), (0,)), ((), ())), preferred_element_type=f32
    )


def contract_cols(left_side, right_side):
    return lax.dot_general(
        left_side, right_side, (((1,), (1,)), ((), ())), preferred_element_type=f32
    )


def gather(x, axes):
    return lax.all_gather(x, axes, axis=0, tiled=True)


def scatter_sum(x, axes):
    return lax.psum_scatter(x, axes, scatter_dimension=0, tiled=True)


def pad_lanes(x, lanes):
    return jnp.pad(x, ((0, 0), (0, lanes - x.shape[1])))


def line_pairs(n, step):
    return [(i, i + step) for i in range(n) if 0 <= i + step < n]


def grid_gather(x):
    n = lax.axis_size("a")

    def cross(block, ends):
        return lax.ppermute(
            block, SEQ, [(2 * i + j, 2 * i + 1 - j) for i in range(n) if ends(i) for j in (0, 1)]
        )

    pieces = [(0, 0, x), (0, 1, cross(x, lambda i: True))]
    up = down = x
    for k in range(1, n):
        up = lax.ppermute(up, "a", line_pairs(n, 1))
        down = lax.ppermute(down, "a", line_pairs(n, -1))
        pieces += [(-k, 0, up), (-k, 1, cross(up, lambda i: i >= k))]
        pieces += [(k, 0, down), (k, 1, cross(down, lambda i: i + k < n))]
    return pieces


def plane_gather(x):
    swap = SWAP
    half = x.shape[0] // 2
    from_y = lax.ppermute(x, "y", SWAP)
    from_b = lax.ppermute(x, "b", SWAP)
    upper = lax.ppermute(from_b[:half], "y", SWAP)
    lower = lax.ppermute(from_y[half:], "b", SWAP)
    return [
        (block, lax.ppermute(block, "c", SWAP)) for block in (x, from_y, from_b, upper, lower)
    ]


def quarter(v, b, y):
    return lax.dynamic_index_in_dim(lax.dynamic_index_in_dim(v, b, 0, False), y, 0, False)


def halve_add(terms):
    own, other = terms
    return (own.astype(f32) + other.astype(f32)).astype(own.dtype)


def rotate_lanes(x, cos, sin):
    width = x.shape[-1]
    lane = lax.broadcasted_iota(jnp.int32, x.shape, x.ndim - 1)
    swapped = jnp.where(
        lane % HEAD_SIZE < HEAD_SIZE // 2,
        pltpu.roll(x, width - HEAD_SIZE // 2, x.ndim - 1),
        pltpu.roll(x, HEAD_SIZE // 2, x.ndim - 1),
    )
    return x * cos + swapped * sin


def spread_tables(cos, sin):
    return jnp.concatenate([cos] * 4, axis=1), jnp.concatenate([-sin, sin, -sin, sin], axis=1)


def key_tables(cos, sin):
    low = lower_lanes(cos.shape)
    return jnp.where(low, cos, 1.0), jnp.where(low, sin, 0.0)


def project_kernel(places, place_ref, *refs):
    count = 1 if places is None else len(places)
    blocks, refs = refs[:count], refs[count:]
    small_ref, w_ref, cos_ref, sin_ref, qkv_ref, normed_ref, x_ref = refs[:7]
    wide_cos_ref, wide_sin_ref, gain, held, sems = refs[7:]
    i = pl.program_id(0)
    slots = held.shape[0]

    @pl.when(i == 0)
    def _():
        if places is None:
            for slot in range(slots):
                pltpu.make_async_copy(blocks[0].at[slot], held.at[slot], sems.at[slot]).start()
        else:
            for (distance, crossed), block in zip(places, blocks):
                at = place_ref[1] + distance
                member = 1 - place_ref[2] if crossed else place_ref[2]

                @pl.when((at >= 0) & (at < slots // 2))
                def _(block=block, slot=2 * at + member):
                    pltpu.make_async_copy(block, held.at[slot], sems.at[slot]).start()

        gain[...] = jnp.transpose(small_ref[...].astype(f32))[E : E + 8, :]

    arrived = blocks[0].at[0] if places is None else blocks[0]
    pltpu.make_async_copy(arrived, held.at[i], sems.at[i]).wait()
    x = held[i]
    x_ref[...] = x
    normed = rms_scale(x.astype(f32), gain[0:1, :]).astype(bf16)
    normed_ref[...] = normed
    pre = jnp.dot(normed, w_ref[...], preferred_element_type=f32)
    cos, sin = spread_tables(cos_ref[...], sin_ref[...])
    wide_cos_ref[...] = cos
    wide_sin_ref[...] = sin
    qkv_ref[:, :PAIR] = rotate_lanes(pre[:, :PAIR], cos, sin).astype(bf16)
    qkv_ref[:, PAIR:] = rotate_lanes(pre[:, PAIR:], *key_tables(cos, sin)).astype(bf16)


def project(place, places, blocks, rows, packed, cos, sin):
    width = packed.shape[0]
    small_at = packed.shape[1] // LANES - 1
    span = cos.shape[0]
    table = pl.BlockSpec((rows, HEAD_SIZE // 2), lambda i, h: (i, 0))
    token_rows = pl.BlockSpec((rows, width), lambda i, h: (i, 0))
    return pl.pallas_call(
        functools.partial(project_kernel, places),
        grid_spec=pltpu.PrefetchScalarGridSpec(
            num_scalar_prefetch=1,
            grid=(span // rows,),
            in_specs=[pl.BlockSpec(memory_space=pl.ANY)] * len(blocks)
            + [
                pl.BlockSpec((width, LANES), lambda i, h: (0, small_at)),
                pl.BlockSpec((width, HEAD_PACK), lambda i, h: (0, h[0])),
                table,
                table,
            ],
            out_specs=[
                pl.BlockSpec((rows, HEAD_PACK), lambda i, h: (i, 0)),
                token_rows,
                token_rows,
                pl.BlockSpec((rows, PAIR), lambda i, h: (i, 0)),
                pl.BlockSpec((rows, PAIR), lambda i, h: (i, 0)),
            ],
            scratch_shapes=[
                pltpu.VMEM((8, width), f32),
                pltpu.VMEM((span // rows, rows, width), bf16),
                pltpu.SemaphoreType.DMA((span // rows,)),
            ],
        ),
        out_shape=[
            jax.ShapeDtypeStruct((span, HEAD_PACK), bf16),
            jax.ShapeDtypeStruct((span, width), bf16),
            jax.ShapeDtypeStruct((span, width), bf16),
            jax.ShapeDtypeStruct((span, PAIR), f32),
            jax.ShapeDtypeStruct((span, PAIR), f32),
        ],
        compiler_params=pltpu.CompilerParams(vmem_limit_bytes=VMEM_LIMIT),
        cost_estimate=pl.CostEstimate(
            flops=2 * span * width * HEAD_PACK, bytes_accessed=18 * 2**20, transcendentals=0
        ),
        name="project",
    )(place, *blocks, packed, packed, cos, sin)


def head_grads_kernel(head_ref, x_ref, normed_ref, w_ref, grad_ref, out_ref, acc, gain):
    i = pl.program_id(0)

    @pl.when(i == 0)
    def _():
        acc[...] = jnp.zeros_like(acc)
        gain[...] = jnp.zeros_like(gain)

    grad = grad_ref[...]
    acc[...] += contract_rows(grad, normed_ref[...])
    x = x_ref[...].astype(f32)
    inverse = lax.rsqrt(jnp.mean(x * x, axis=-1, keepdims=True) + NORM_EPS)
    back = contract_cols(grad, w_ref[...]) * (x * inverse)
    gain[...] += jnp.sum(back.reshape(back.shape[0] // 8, 8, back.shape[1]), axis=0)

    @pl.when(i == pl.num_programs(0) - 1)
    def _():
        out_ref[:, :HEAD_PACK] = jnp.transpose(acc[...]).astype(bf16)
        total = jnp.sum(gain[...], axis=0, keepdims=True)
        rows = lax.broadcasted_iota(jnp.int32, (LANES, total.shape[1]), 0)
        out_ref[:, HEAD_PACK:] = jnp.transpose(
            jnp.where(rows == 0, jnp.broadcast_to(total, rows.shape), 0.0)
        ).astype(bf16)


def head_grads(head, x, normed, packed, grads):
    span, width = x.shape
    rows = 2 * BLOCK
    token_rows = pl.BlockSpec((rows, width), lambda i, h: (i, 0))
    return pl.pallas_call(
        head_grads_kernel,
        grid_spec=pltpu.PrefetchScalarGridSpec(
            num_scalar_prefetch=1,
            grid=(span // rows,),
            in_specs=[
                token_rows,
                token_rows,
                pl.BlockSpec((width, HEAD_PACK), lambda i, h: (0, h[0])),
                pl.BlockSpec((rows, HEAD_PACK), lambda i, h: (i, 0)),
            ],
            out_specs=pl.BlockSpec((width, HEAD_PACK + LANES), lambda i, h: (0, 0)),
            scratch_shapes=[pltpu.VMEM((HEAD_PACK, width), f32), pltpu.VMEM((8, width), f32)],
        ),
        out_shape=jax.ShapeDtypeStruct((width, HEAD_PACK + LANES), bf16),
        compiler_params=pltpu.CompilerParams(vmem_limit_bytes=VMEM_LIMIT),
        cost_estimate=pl.CostEstimate(
            flops=4 * span * width * HEAD_PACK, bytes_accessed=12 * 2**20, transcendentals=0
        ),
        name="head_grads",
    )(head, x, normed, packed, grads)


def lower_lanes(shape):
    return lax.broadcasted_iota(jnp.int32, shape, len(shape) - 1) < HEAD_SIZE


def both_heads_low(pair):
    low = lower_lanes(pair.shape)
    return jnp.concatenate(
        [jnp.where(low, pair, 0.0), jnp.where(low, pltpu.roll(pair, HEAD_SIZE, 1), 0.0)], axis=0
    )


def both_heads_high(pair):
    low = lower_lanes(pair.shape)
    return jnp.concatenate(
        [jnp.where(low, 0.0, pltpu.roll(pair, HEAD_SIZE, 1)), jnp.where(low, 0.0, pair)], axis=0
    )


def block_bounds(bounds_ref):
    i, steps = pl.program_id(0), pl.num_programs(0)
    query_start = (i + bounds_ref[2 * steps]) * QUERY_BLOCK
    diagonal = query_start // BLOCK
    full = jnp.minimum(bounds_ref[steps + i], diagonal)
    return query_start, bounds_ref[i], full, diagonal, diagonal + QUERY_BLOCK // BLOCK


def pair_mask(doc, query_start):
    doc = jnp.concatenate([doc, doc], axis=1)
    queries = lax.broadcasted_iota(jnp.int32, doc.shape, 1) % QUERY_BLOCK + query_start

    def masked(scores, start):
        keys = lax.broadcasted_iota(jnp.int32, scores.shape, 0) + start
        return jnp.where((keys >= doc) & (keys <= queries), scores, NEGATIVE_HUGE)

    return masked


def attend_kernel(bounds_ref, q_ref, kv_ref, doc_ref, o_ref, low_ref, lse_ref, acc):
    query_start, first, full, diagonal, end = block_bounds(bounds_ref)
    q = both_heads_low(q_ref[...].astype(f32) * SCALE_OF_SCORES).astype(bf16)
    masked = pair_mask(doc_ref[0], query_start)
    acc[...] = jnp.zeros_like(acc)

    def step(mask, j, carried):
        top, total = carried
        start = pl.multiple_of(j * BLOCK, BLOCK)
        kv = kv_ref[pl.ds(start, BLOCK), :]
        scores = contract_cols(kv, q)
        if mask:
            scores = masked(scores, start)
        new = jnp.maximum(top, jnp.max(scores, axis=0, keepdims=True))
        probs = jnp.exp(scores - new)
        keep = jnp.exp(top - new)
        acc[...] = acc[...] * keep + contract_rows(kv, probs.astype(bf16))
        return new, total * keep + jnp.sum(probs, axis=0, keepdims=True)

    row = (1, 2 * QUERY_BLOCK)
    carried = (jnp.full(row, NEGATIVE_HUGE, f32), jnp.zeros(row, f32))
    carried = lax.fori_loop(first, full, functools.partial(step, True), carried)
    carried = lax.fori_loop(full, diagonal, functools.partial(step, False), carried)
    top, total = lax.fori_loop(diagonal, end, functools.partial(step, True), carried)
    mixed = jnp.transpose(acc[...] / total)
    one, two = mixed[:QUERY_BLOCK], mixed[QUERY_BLOCK:]
    out = jnp.where(lower_lanes(one.shape), pltpu.roll(one, HEAD_SIZE, 1), two)
    o_ref[...] = out
    low_ref[...] = out.astype(bf16)
    lse_ref[0] = top + jnp.log(total)


def attention_specs(kv_at, keys):
    pair = pl.BlockSpec((QUERY_BLOCK, PAIR), lambda i, s: (i, 0))
    return (
        pair,
        pl.BlockSpec((keys, PAIR), lambda i, s: (0, kv_at)),
        pl.BlockSpec((1, 1, QUERY_BLOCK), lambda i, s: (i, 0, 0)),
        pl.BlockSpec((1, 1, 2 * QUERY_BLOCK), lambda i, s: (i, 0, 0)),
    )


def attend(bounds, qkv, kv, kv_at, doc):
    queries, keys = qkv.shape[0], kv.shape[0]
    steps = queries // QUERY_BLOCK
    pair, whole, doc_row, lse_row = attention_specs(kv_at, keys)
    return pl.pallas_call(
        attend_kernel,
        grid_spec=pltpu.PrefetchScalarGridSpec(
            num_scalar_prefetch=1,
            grid=(steps,),
            in_specs=[pair, whole, doc_row],
            out_specs=[pair, pair, lse_row],
            scratch_shapes=[pltpu.VMEM((PAIR, 2 * QUERY_BLOCK), f32)],
        ),
        out_shape=[
            jax.ShapeDtypeStruct((queries, PAIR), f32),
            jax.ShapeDtypeStruct((queries, PAIR), bf16),
            jax.ShapeDtypeStruct((steps, 1, 2 * QUERY_BLOCK), f32),
        ],
        compiler_params=pltpu.CompilerParams(vmem_limit_bytes=VMEM_LIMIT),
        cost_estimate=pl.CostEstimate(
            flops=4 * queries * keys * PAIR, bytes_accessed=6 * 2**20, transcendentals=queries * keys
        ),
        name="attend",
    )(bounds, qkv, kv, doc)


def attend_back_kernel(
    fold, bounds_ref, q_ref, kv_ref, doc_ref, do_ref, o_ref, lse_ref, cos_ref, sin_ref, *refs
):
    if fold:
        out_ref, acc, dkv_ref = refs
    else:
        dq_ref, dkv_ref, acc = refs
    i = pl.program_id(0)
    query_start, first, full, diagonal, end = block_bounds(bounds_ref)

    @pl.when(i == 0)
    def _():
        dkv_ref[...] = jnp.zeros_like(dkv_ref)

    q = both_heads_low(q_ref[...].astype(f32) * SCALE_OF_SCORES).astype(bf16)
    grad = do_ref[...].astype(f32)
    product = jnp.transpose(grad * o_ref[...])
    delta = jnp.concatenate(
        [
            jnp.sum(product[:HEAD_SIZE], axis=0, keepdims=True),
            jnp.sum(product[HEAD_SIZE:], axis=0, keepdims=True),
        ],
        axis=1,
    )
    grad = both_heads_high(grad).astype(bf16)
    sources = jnp.concatenate([q, grad], axis=0)
    masked = pair_mask(doc_ref[0], query_start)
    lse = lse_ref[0]
    acc[...] = jnp.zeros_like(acc)

    def step(mask, j, carried):
        start = pl.multiple_of(j * BLOCK, BLOCK)
        kv = kv_ref[pl.ds(start, BLOCK), :]
        scores = contract_cols(kv, q) - lse
        if mask:
            scores = masked(scores, start)
        probs = jnp.exp(scores)
        grad_scores = (probs * (contract_cols(kv, grad) - delta)).astype(bf16)
        acc[...] += contract_rows(kv, grad_scores)
        both = jnp.concatenate([grad_scores, probs.astype(bf16)], axis=1)
        dkv_ref[pl.ds(start, BLOCK), :] += jnp.dot(both, sources, preferred_element_type=f32)
        return carried

    lax.fori_loop(first, full, functools.partial(step, True), 0)
    lax.fori_loop(full, diagonal, functools.partial(step, False), 0)
    lax.fori_loop(diagonal, end, functools.partial(step, True), 0)
    dq = jnp.transpose(acc[...])
    one, two = dq[:QUERY_BLOCK], dq[QUERY_BLOCK:]
    dq = jnp.where(lower_lanes(one.shape), one, pltpu.roll(two, HEAD_SIZE, 1))
    if not fold:
        dq_ref[...] = dq
        return
    mine = pl.ds(pl.multiple_of(i * QUERY_BLOCK, QUERY_BLOCK), QUERY_BLOCK)
    out_ref[mine, :PAIR] = rotate_lanes(
        dq * SCALE_OF_SCORES, cos_ref[mine, :], -sin_ref[mine, :]
    ).astype(bf16)

    @pl.when(i == pl.num_programs(0) - 1)
    def _():
        def finish(j, carried):
            part = pl.ds(pl.multiple_of(j * BLOCK, BLOCK), BLOCK)
            cos, sin = key_tables(cos_ref[part, :], sin_ref[part, :])
            out_ref[part, PAIR:] = rotate_lanes(dkv_ref[part, :], cos, -sin).astype(bf16)
            return carried

        lax.fori_loop(0, dkv_ref.shape[0] // BLOCK, finish, 0)


def attend_back(bounds, qkv, kv, kv_at, doc, grad, out, lse, cos, sin, fold):
    queries, keys = qkv.shape[0], kv.shape[0]
    steps = queries // QUERY_BLOCK
    pair, whole, doc_row, lse_row = attention_specs(kv_at, keys)
    table = pl.BlockSpec(cos.shape, lambda i, s: (0, 0))
    acc = pltpu.VMEM((PAIR, 2 * QUERY_BLOCK), f32)
    if fold:
        out_specs = pl.BlockSpec((queries, HEAD_PACK), lambda i, s: (0, 0))
        out_shape = jax.ShapeDtypeStruct((queries, HEAD_PACK), bf16)
        scratch = [acc, pltpu.VMEM((keys, PAIR), f32)]
    else:
        out_specs = [pair, pl.BlockSpec((keys, PAIR), lambda i, s: (0, 0))]
        out_shape = [
            jax.ShapeDtypeStruct((queries, PAIR), f32),
            jax.ShapeDtypeStruct((keys, PAIR), f32),
        ]
        scratch = [acc]
    return pl.pallas_call(
        functools.partial(attend_back_kernel, fold),
        grid_spec=pltpu.PrefetchScalarGridSpec(
            num_scalar_prefetch=1,
            grid=(steps,),
            in_specs=[pair, whole, doc_row, pair, pair, lse_row, table, table],
            out_specs=out_specs,
            scratch_shapes=scratch,
        ),
        out_shape=out_shape,
        compiler_params=pltpu.CompilerParams(vmem_limit_bytes=VMEM_LIMIT),
        cost_estimate=pl.CostEstimate(
            flops=10 * queries * keys * PAIR,
            bytes_accessed=8 * 2**20,
            transcendentals=queries * keys,
        ),
        name="attend_back",
    )(bounds, qkv, kv, doc, grad, out, lse, cos, sin)


def unrotate_kernel(dq_ref, dkv_ref, cos_ref, sin_ref, out_ref):
    cos, sin = cos_ref[...], sin_ref[...]
    dq = rotate_lanes(dq_ref[...] * SCALE_OF_SCORES, cos, -sin)
    cos, sin = key_tables(cos, sin)
    dkv = rotate_lanes(dkv_ref[...], cos, -sin)
    out_ref[...] = jnp.concatenate([dq, dkv], axis=1).astype(bf16)


def unrotate(dq, dkv, cos, sin):
    rows = dq.shape[0]
    pair = pl.BlockSpec((BLOCK, PAIR), lambda i: (i, 0))
    return pl.pallas_call(
        unrotate_kernel,
        grid=(rows // BLOCK,),
        in_specs=[pair, pair, pair, pair],
        out_specs=pl.BlockSpec((BLOCK, HEAD_PACK), lambda i: (i, 0)),
        out_shape=jax.ShapeDtypeStruct((rows, HEAD_PACK), bf16),
        cost_estimate=pl.CostEstimate(
            flops=rows * HEAD_PACK * 8, bytes_accessed=rows * HEAD_PACK * 14, transcendentals=0
        ),
        name="unrotate",
    )(dq, dkv, cos, sin)


def place_experts_kernel(place_ref, *refs):
    blocks, (ct_ref, w_ref, z_ref, sems) = refs[:10], refs[10:]
    core = place_ref[1]
    rows = w_ref.shape[1] // 2
    half = rows // 2
    sources = [[(0, 0, rows)], [(1, 0, rows)], [(2, 0, rows)], [(3, 0, half), (4, half, half)]]
    for step, parts in enumerate(sources):

        @pl.when(pl.program_id(0) == step)
        def _(parts=parts):
            copies = []
            for source, start, length in parts:
                for other in (0, 1):
                    first = jnp.where(core == other, 0, rows) + start
                    at = pl.ds(pl.multiple_of(first, half), length)
                    copies.append(
                        pltpu.make_async_copy(
                            blocks[2 * source + other], w_ref.at[0, at, :], sems.at[len(copies)]
                        )
                    )
            for copy in copies:
                copy.start()
            for copy in copies:
                copy.wait()

    z_ref[0] = jnp.dot(ct_ref[...], w_ref[0, :, 2 * F :], preferred_element_type=f32)


def place_experts(place, parts, early, width):
    rows = early.shape[0]
    blocks = [block for pair in parts for block in pair]
    return pl.pallas_call(
        place_experts_kernel,
        grid_spec=pltpu.PrefetchScalarGridSpec(
            num_scalar_prefetch=1,
            grid=(EXPERTS_HERE,),
            in_specs=[pl.BlockSpec(memory_space=pl.ANY)] * len(blocks)
            + [pl.BlockSpec((rows, width), lambda r, s: (0, 0))],
            out_specs=[
                pl.BlockSpec((1, width, 3 * F), lambda r, s: (s[0] ^ r, 0, 0)),
                pl.BlockSpec((1, rows, F), lambda r, s: (s[0] ^ r, 0, 0)),
            ],
            scratch_shapes=[pltpu.SemaphoreType.DMA((4,))],
        ),
        out_shape=[
            jax.ShapeDtypeStruct((EXPERTS_HERE, width, 3 * F), bf16),
            jax.ShapeDtypeStruct((EXPERTS_HERE, rows, F), f32),
        ],
        compiler_params=pltpu.CompilerParams(vmem_limit_bytes=VMEM_LIMIT),
        cost_estimate=pl.CostEstimate(
            flops=2 * EXPERTS_HERE * rows * width * F, bytes_accessed=36 * 2**20, transcendentals=0
        ),
        name="place_experts",
    )(place, *blocks, early)


def lane_column(x, at):
    lane = lax.broadcasted_iota(jnp.int32, x.shape, 1)
    return jnp.sum(jnp.where(lane == at, x, 0.0), axis=1, keepdims=True)


def experts_kernel(
    group_ref, n_ref, routed_ref, router_ref, w_ref, z_ref,
    back_ref, gates_ref, hidden_ref, pre_ref, acc, dots,
):
    e = pl.program_id(0)
    own = group_ref[0] * EXPERTS_HERE + e
    rows = n_ref.shape[0]

    @pl.when(e == 0)
    def _():
        logits = jnp.dot(n_ref[...], router_ref[...], preferred_element_type=f32)
        routed = routed_ref[...].astype(f32) > 0.5
        highest = jnp.max(jnp.where(routed, logits, NEGATIVE_HUGE), axis=1, keepdims=True)
        weights = jnp.where(routed, jnp.exp(jnp.where(routed, logits - highest, 0.0)), 0.0)
        gates_ref[...] = weights / jnp.sum(weights, axis=1, keepdims=True)
        acc[...] = jnp.zeros_like(acc)
        dots[...] = jnp.zeros_like(dots)

    w_in = w_ref[0, :, : 2 * F]
    for t in range(rows // BLOCK):
        part = pl.ds(t * BLOCK, BLOCK)
        pre = jnp.dot(n_ref[part, :], w_in, preferred_element_type=f32)
        gate, up = pre[:, :F], pre[:, F:]
        z = z_ref[0, part, :]
        weight = lane_column(gates_ref[part, :], own)
        sig = 1.0 / (1.0 + jnp.exp(-gate))
        act = gate * sig
        hidden = act * up
        hidden_ref[0, part, :] = (weight * hidden).astype(bf16)
        dot = RESIDUAL_SCALE * jnp.sum(hidden.astype(bf16).astype(f32) * z, axis=1, keepdims=True)
        lane = lax.broadcasted_iota(jnp.int32, (BLOCK, LANES), 1)
        dots[part, :] += jnp.where(lane == own, dot, 0.0)
        scaled = (RESIDUAL_SCALE * weight) * z
        pre_ref[0, part, :F] = (scaled * up * (sig + act * (1.0 - sig))).astype(bf16)
        pre_ref[0, part, F:] = (scaled * act).astype(bf16)
        acc[part, :] += contract_cols(pre_ref[0, part, :], w_in)

    @pl.when(e == EXPERTS_HERE - 1)
    def _():
        width = n_ref.shape[1]
        back_ref[:, :width] = acc[...].astype(bf16)
        high = dots[...].astype(bf16)
        low = dots[...] - high.astype(f32)
        back_ref[:, width:] = (high.astype(f32) + pltpu.roll(low, E, 1)).astype(bf16)


def experts(group, normed, early, packed, w_all, z):
    rows, width = normed.shape
    count = w_all.shape[0]
    whole = pl.BlockSpec((rows, width), lambda e, g: (0, 0))
    column = width // LANES
    router_at = packed.shape[1] // LANES - 1
    return pl.pallas_call(
        experts_kernel,
        grid_spec=pltpu.PrefetchScalarGridSpec(
            num_scalar_prefetch=1,
            grid=(count,),
            in_specs=[
                whole,
                pl.BlockSpec((rows, LANES), lambda e, g: (0, column)),
                pl.BlockSpec((width, LANES), lambda e, g: (0, router_at)),
                pl.BlockSpec((1, width, 3 * F), lambda e, g: (e, 0, 0)),
                pl.BlockSpec((1, rows, F), lambda e, g: (e, 0, 0)),
            ],
            out_specs=[
                pl.BlockSpec((rows, width + LANES), lambda e, g: (0, 0)),
                pl.BlockSpec((rows, LANES), lambda e, g: (0, 0)),
                pl.BlockSpec((1, rows, F), lambda e, g: (e, 0, 0)),
                pl.BlockSpec((1, rows, 2 * F), lambda e, g: (e, 0, 0)),
            ],
            scratch_shapes=[pltpu.VMEM((rows, width), f32), pltpu.VMEM((rows, LANES), f32)],
        ),
        out_shape=[
            jax.ShapeDtypeStruct((rows, width + LANES), bf16),
            jax.ShapeDtypeStruct((rows, LANES), f32),
            jax.ShapeDtypeStruct((count, rows, F), bf16),
            jax.ShapeDtypeStruct((count, rows, 2 * F), bf16),
        ],
        compiler_params=pltpu.CompilerParams(vmem_limit_bytes=VMEM_LIMIT),
        cost_estimate=pl.CostEstimate(
            flops=2 * count * rows * width * 4 * F, bytes_accessed=40 * 2**20, transcendentals=0
        ),
        name="experts",
    )(group, normed, early, packed, w_all, z)


def expert_grads_kernel(with_y, half_ref, n_ref, ct_ref, w_ref, hidden_ref, pre_ref, *refs):
    if with_y:
        left_ref, right_ref, y_ref, n_t, ct_t, acc = refs
    else:
        left_ref, right_ref, n_t, ct_t = refs
    e = pl.program_id(0)
    cut = left_ref.shape[2]

    @pl.when(e == 0)
    def _():
        n_t[...] = jnp.transpose(n_ref[...])
        ct_t[...] = jnp.transpose(ct_ref[...])
        if with_y:
            acc[...] = jnp.zeros_like(acc)

    grads = jnp.dot(n_t[...], pre_ref[0], preferred_element_type=f32).astype(bf16)
    left_ref[0] = grads[:, :cut]
    right_ref[0, :, : 2 * F - cut] = grads[:, cut:]
    right_ref[0, :, 2 * F - cut :] = (
        RESIDUAL_SCALE * jnp.dot(ct_t[...], hidden_ref[0], preferred_element_type=f32)
    ).astype(bf16)
    if not with_y:
        return
    acc[...] += contract_cols(hidden_ref[0], w_ref[0, :, 2 * F :])

    @pl.when(e == pl.num_programs(0) - 1)
    def _():
        y_ref[...] = acc[...].astype(bf16)


def expert_grads(half, halves, normed, early, w_all, hidden, pre, with_y):
    rows, width = normed.shape
    count = w_all.shape[0]
    own, cut = width // halves, 3 * F // 2
    feature = pl.BlockSpec((rows, own), lambda e, h: (0, h[0]))
    out_specs = [pl.BlockSpec((1, own, cut), lambda e, h: (e, 0, 0))] * 2
    out_shape = [jax.ShapeDtypeStruct((count, own, cut), bf16)] * 2
    scratch = [pltpu.VMEM((own, rows), bf16), pltpu.VMEM((own, rows), bf16)]
    if with_y:
        out_specs.append(pl.BlockSpec((rows, width), lambda e, h: (0, 0)))
        out_shape.append(jax.ShapeDtypeStruct((rows, width), bf16))
        scratch.append(pltpu.VMEM((rows, width), f32))
    return pl.pallas_call(
        functools.partial(expert_grads_kernel, with_y),
        grid_spec=pltpu.PrefetchScalarGridSpec(
            num_scalar_prefetch=1,
            grid=(count,),
            in_specs=[
                feature,
                feature,
                pl.BlockSpec((1, width, 3 * F), lambda e, h: (e, 0, 0)),
                pl.BlockSpec((1, rows, F), lambda e, h: (e, 0, 0)),
                pl.BlockSpec((1, rows, 2 * F), lambda e, h: (e, 0, 0)),
            ],
            out_specs=out_specs,
            scratch_shapes=scratch,
        ),
        out_shape=out_shape,
        compiler_params=pltpu.CompilerParams(vmem_limit_bytes=VMEM_LIMIT),
        cost_estimate=pl.CostEstimate(
            flops=2 * count * rows * width * 3 * F // halves + 2 * with_y * count * rows * width * F,
            bytes_accessed=30 * 2**20,
            transcendentals=0,
        ),
        name="expert_grads",
    )(half, normed, early, w_all, hidden, pre)


def join_kernel(place_ref, o_ref, w_ref, small_ref, x_ref, normed_ref, resid_ref, own_ref, gain):
    t = pl.program_id(0)
    b = place_ref[2]

    @pl.when(t == 0)
    def _():
        gain[...] = jnp.transpose(small_ref[...].astype(f32))[E : E + 8, :]

    pairs = []
    for a in range(o_ref.shape[0]):
        same, other = o_ref[a, 0, 0], o_ref[a, 1, 0]
        pairs.append(jnp.where(b == 0, same, other))
        pairs.append(jnp.where(b == 0, other, same))
    attended = jnp.concatenate(pairs, axis=1)
    resid = x_ref[...].astype(f32) + RESIDUAL_SCALE * jnp.dot(
        attended, w_ref[...], preferred_element_type=f32
    )
    normed_ref[...] = rms_scale(resid, gain[1:2, :]).astype(bf16)

    @pl.when(t == place_ref[1])
    def _():
        resid_ref[...] = resid
        own_ref[...] = attended


def join(place, outs, packed, weights_at, x):
    width = packed.shape[0]
    lines, _, _, rows, pair = outs.shape
    small_at = packed.shape[1] // LANES - 1
    own = pl.BlockSpec((rows, width), lambda t, s: (0, 0))
    return pl.pallas_call(
        join_kernel,
        grid_spec=pltpu.PrefetchScalarGridSpec(
            num_scalar_prefetch=1,
            grid=(lines,),
            in_specs=[
                pl.BlockSpec((lines, 2, 1, rows, pair), lambda t, s: (0, 0, t, 0, 0)),
                pl.BlockSpec((width, width), lambda t, s: (0, weights_at)),
                pl.BlockSpec((width, LANES), lambda t, s: (0, small_at)),
                pl.BlockSpec((rows, width), lambda t, s: (2 * t + s[2], 0)),
            ],
            out_specs=[pl.BlockSpec((rows, width), lambda t, s: (t, 0)), own, own],
            scratch_shapes=[pltpu.VMEM((8, width), f32)],
        ),
        out_shape=[
            jax.ShapeDtypeStruct((lines * rows, width), bf16),
            jax.ShapeDtypeStruct((rows, width), f32),
            jax.ShapeDtypeStruct((rows, width), bf16),
        ],
        compiler_params=pltpu.CompilerParams(vmem_limit_bytes=VMEM_LIMIT),
        cost_estimate=pl.CostEstimate(
            flops=2 * lines * rows * width * width, bytes_accessed=12 * 2**20, transcendentals=0
        ),
        name="join",
    )(place, outs, packed, packed, x)


def weight_sums_kernel(sums_ref, q_ref, k_ref, v_ref, gain_ref):
    groups, heads, members = sums_ref.shape[:3]
    gain = jnp.zeros(gain_ref.shape, f32)
    values = []
    for h in range(heads):
        total = jnp.zeros(sums_ref.shape[3:], f32)
        for g in range(groups):
            for member in range(members):
                total += sums_ref[g, h, member].astype(f32)
        values.append(total)
        gain += total[:, HEAD_PACK:]
        q_ref[:, h * PAIR : (h + 1) * PAIR] = total[:, :PAIR]
    gain_ref[...] = gain
    for h in range(0, heads, 2):
        one, two = values[h][:, PAIR:HEAD_PACK], values[h + 1][:, PAIR:HEAD_PACK]
        low = lower_lanes(one.shape)
        at = slice(h // 2 * PAIR, (h // 2 + 1) * PAIR)
        k_ref[:, at] = jnp.where(low, one, pltpu.roll(two, HEAD_SIZE, 1))
        v_ref[:, at] = jnp.where(low, pltpu.roll(one, HEAD_SIZE, 1), two)


def weight_sums(sums):
    rows, heads = sums.shape[3], sums.shape[1]
    return pl.pallas_call(
        weight_sums_kernel,
        out_shape=[
            jax.ShapeDtypeStruct((rows, heads * PAIR), f32),
            jax.ShapeDtypeStruct((rows, heads * HEAD_SIZE), f32),
            jax.ShapeDtypeStruct((rows, heads * HEAD_SIZE), f32),
            jax.ShapeDtypeStruct((rows, LANES), f32),
        ],
        compiler_params=pltpu.CompilerParams(vmem_limit_bytes=VMEM_LIMIT),
        cost_estimate=pl.CostEstimate(flops=2**20, bytes_accessed=2 * 2**20, transcendentals=0),
        name="weight_sums",
    )(sums)


def exchange(x, axes):
    return lax.all_to_all(x, axes, 0, 0, tiled=True)


def body(
    tokens,
    cotangent,
    segment_ids,
    routes,
    norm_attn,
    w_query,
    key_weight_matrix,
    value_weight_matrix,
    w_output,
    norm_moe,
    w_router,
    expert_in,
    expert_out,
):
    x_local = tokens[0].astype(f32)
    token_count, width = x_local.shape
    seg_row = segment_ids[0]
    group = lax.axis_index("a")
    head_axes = SEQ if lax.axis_size(SEQ) == KEY_VALUE_HEADS else ("b",)
    whole_rows = head_axes == SEQ
    span = token_count * KEY_VALUE_HEADS
    span_start = 0 if whole_rows else group * span

    def start_of_doc(ids):
        return jnp.sum((seg_row[None, :] < ids[:, None]).astype(jnp.int32), axis=1)

    seg_span = lax.dynamic_slice_in_dim(seg_row, span_start, span)
    doc_span = start_of_doc(seg_span)
    cos_span, sin_span = rotation_tables(
        span_start + jnp.arange(span, dtype=jnp.int32) - doc_span
    )
    by_block = doc_span.reshape(-1, QUERY_BLOCK)
    bounds = jnp.concatenate(
        [
            by_block[:, 0] // BLOCK,
            (by_block[:, -1] + BLOCK - 1) // BLOCK,
            jnp.full((1,), span_start // QUERY_BLOCK, jnp.int32),
        ]
    )
    doc_rows = by_block[:, None, :]

    own_rows = w_query.shape[0]
    by_head = jnp.concatenate(
        [
            w_query.astype(bf16).reshape(own_rows, KEY_VALUE_HEADS, PAIR),
            key_weight_matrix.astype(bf16).reshape(own_rows, KEY_VALUE_HEADS, HEAD_SIZE),
            value_weight_matrix.astype(bf16).reshape(own_rows, KEY_VALUE_HEADS, HEAD_SIZE),
        ],
        axis=2,
    ).reshape(own_rows, KEY_VALUE_HEADS * HEAD_PACK)
    qkv_width = KEY_VALUE_HEADS * HEAD_PACK
    first_all = gather(
        jnp.concatenate(
            [
                by_head,
                w_output.astype(bf16),
                pad_lanes(
                    jnp.concatenate(
                        [
                            w_router.astype(bf16),
                            norm_attn.astype(bf16)[:, None],
                            norm_moe.astype(bf16)[:, None],
                        ],
                        axis=1,
                    ),
                    LANES,
                ),
            ],
            axis=1,
        ),
        ALL,
    )
    experts_low = jnp.concatenate([expert_in.astype(bf16), expert_out.astype(bf16)], axis=1)
    if whole_rows:
        pieces = grid_gather(tokens[0])
        places = [piece[:2] for piece in pieces]
        blocks = tuple(piece[2] for piece in pieces)
    else:
        places = None
        blocks = (gather(tokens[0], "b").reshape((-1,) + tokens.shape[1:]),)
    first_all, experts_low, blocks, cos_span, sin_span, bounds, doc_rows = (
        lax.optimization_barrier(
            (first_all, experts_low, blocks, cos_span, sin_span, bounds, doc_rows)
        )
    )
    output_w = first_all[:, qkv_width : qkv_width + width]
    small_at = qkv_width + width
    router_w = first_all[:, small_at : small_at + E]
    gain_one_f = first_all[:, small_at + E].astype(f32)
    gain_two_f = first_all[:, small_at + E + 1].astype(f32)

    expert_ids = jnp.arange(E, dtype=jnp.int32)
    routed_own = jnp.any(routes[0][:, :, None] == expert_ids[None, None, :], axis=1)
    early = jnp.concatenate([cotangent[0], pad_lanes(routed_own.astype(bf16), LANES)], axis=1)
    early, first_all = lax.optimization_barrier((early, first_all))
    early_all = gather(early, "a")
    small_plane = lax.axis_size("b") == 2 and lax.axis_size("y") == 2
    if small_plane:
        parts = plane_gather(experts_low)
    else:
        parts = gather(experts_low, PLANE)

    place = jnp.stack([lax.axis_index(head_axes), group, lax.axis_index("b")])
    qkv, normed_span, x_span, wide_cos, wide_sin = project(
        place, places, blocks, token_count, first_all, cos_span, sin_span
    )
    if whole_rows:
        kv, kv_at = qkv, 1
    else:
        kv, kv_at = gather(qkv[:, PAIR:], "a"), 0
    attention_result, attended, log_total = attend(bounds, qkv, kv, kv_at, doc_rows)
    if small_plane:
        member = lax.axis_index("b")
        by_column = attended.reshape(GROUPS, 2, token_count, PAIR)
        other = lax.ppermute(
            lax.dynamic_index_in_dim(by_column, 1 - member, 1, False), "b", SWAP
        )
        own = lax.dynamic_index_in_dim(by_column, member, 1, False)
        pair, early_all = lax.optimization_barrier((jnp.stack([own, other]), early_all))
        outs = lax.all_gather(pair, "a", axis=0, tiled=False)
        normed_all, resid, attended_low = join(place, outs, first_all, qkv_width // width, x_span)
        normed_two = lax.dynamic_slice_in_dim(normed_all, group * token_count, token_count)
        home = jnp.stack([member * 2 + lax.axis_index("y"), lax.axis_index("c")])
        experts_all, grad_hidden = place_experts(home, parts, early_all, width)
    else:
        attended_low = (
            exchange(attended.reshape(KEY_VALUE_HEADS, token_count, PAIR), head_axes)
            .transpose(1, 0, 2)
            .reshape(token_count, QUERY_HEADS * HEAD_SIZE)
        )
        attn_out = jnp.dot(attended_low, output_w, preferred_element_type=f32)
        resid = x_local + RESIDUAL_SCALE * attn_out
        normed_two = rms_scale(resid, gain_two_f).astype(bf16)
        normed_all = gather(normed_two, "a")
        experts_all = parts.reshape(EXPERTS_HERE, width, 3 * F)
        grad_hidden = jnp.einsum(
            "td,edf->etf",
            early_all[:, :width],
            experts_all[:, :, 2 * F :],
            preferred_element_type=f32,
        )
    back_part, gates_all, gated_hidden, grad_pre = experts(
        group.reshape(1), normed_all, early_all, first_all, experts_all, grad_hidden
    )
    back_own = scatter_sum(back_part, "a").astype(f32)
    inputs = (normed_all, early_all, experts_all, gated_hidden, grad_pre)
    if small_plane:
        core = lax.axis_index("c")
        send = expert_grads((1 - core).reshape(1), 2, *inputs, False)
        arrived = [lax.ppermute(x, "c", SWAP) for x in send]
        *keep, moe_part = expert_grads(core.reshape(1), 2, *inputs, True)
        left, right = (
            halve_add(terms).reshape((2, 2) + terms[0].shape[1:]) for terms in zip(keep, arrived)
        )
        back_own, moe_part, left, right = lax.optimization_barrier(
            (back_own, moe_part, left, right)
        )
        b, y = lax.axis_index("b"), lax.axis_index("y")
        left_on = quarter(left, 1 - b, y), lax.ppermute(quarter(left, 1 - b, 1 - y), "y", SWAP)
        right_on = quarter(right, b, 1 - y), lax.ppermute(quarter(right, 1 - b, 1 - y), "b", SWAP)
    else:
        *grads, moe_part = expert_grads(jnp.zeros((1,), jnp.int32), 1, *inputs, True)
        grad_experts = jnp.concatenate(grads, axis=2)
        back_own, moe_part, grad_experts = lax.optimization_barrier(
            (back_own, moe_part, grad_experts)
        )
        grad_experts = scatter_sum(grad_experts.reshape(EXPERTS_HERE * width, 3 * F), PLANE)
    moe_sum = scatter_sum(moe_part, "a")

    grad_out = cotangent[0].astype(f32)
    gates = lax.dynamic_slice_in_dim(gates_all, group * token_count, token_count)[:, :E]
    gate_grads_own = back_own[:, width : width + E] + back_own[:, width + E : width + 2 * E]
    grad_logits = gates * (gate_grads_own - jnp.sum(gates * gate_grads_own, axis=-1, keepdims=True))
    grad_normed_two = back_own[:, :width] + jnp.dot(
        grad_logits, router_w.astype(f32).T, precision=HIGHEST_DOT
    )
    grad_router = jnp.dot(normed_two.astype(f32).T, grad_logits, precision=HIGHEST_DOT)
    grad_resid_norm, grad_gain_two = rms_back(resid, gain_two_f, grad_normed_two)
    grad_resid = grad_out + grad_resid_norm
    grad_attn_low = (RESIDUAL_SCALE * grad_resid).astype(bf16)
    grad_heads = contract_cols(grad_attn_low, output_w).astype(bf16)
    grad_mixed = exchange(
        grad_heads.reshape(token_count, KEY_VALUE_HEADS, PAIR).transpose(1, 0, 2), head_axes
    ).reshape(span, PAIR)
    if small_plane:
        left_on, right_on = halve_add(left_on), halve_add(right_on)
        left_on, right_on, attended_low, grad_router = lax.optimization_barrier(
            (left_on, right_on, attended_low, grad_router)
        )
    small = jnp.concatenate([grad_router, grad_gain_two[:, None]], axis=1)
    second_part = jnp.concatenate(
        [contract_rows(attended_low, grad_attn_low), pad_lanes(small, LANES)], axis=1
    ).astype(bf16)
    cols = second_part.shape[1]
    second_part = second_part.reshape(GROUPS, -1, own_rows, cols).transpose(1, 0, 2, 3)
    if small_plane:
        second_part, left_on, right_on, grad_mixed = lax.optimization_barrier(
            (second_part, left_on, right_on, grad_mixed)
        )
        left_on, right_on = lax.ppermute(left_on, "b", SWAP), lax.ppermute(right_on, "y", SWAP)
    rest = scatter_sum(second_part.reshape(-1, cols), PLANE)
    grads = attend_back(
        bounds, qkv, kv, kv_at, doc_rows, grad_mixed, attention_result, log_total,
        wide_cos, wide_sin, whole_rows,
    )
    if whole_rows:
        grad_pack = grads
    else:
        grad_kv = scatter_sum(grads[1].astype(bf16), "a").astype(f32)
        grad_pack = unrotate(grads[0], grad_kv, wide_cos, wide_sin)
    if small_plane:
        left_on, right_on, left, right, moe_sum, grad_pack = lax.optimization_barrier(
            (left_on, right_on, left, right, moe_sum, grad_pack)
        )
        left_last = lax.ppermute(quarter(left, b, 1 - y), "y", SWAP)
        right_last = lax.ppermute(quarter(right, 1 - b, y), "b", SWAP)
    first_part = head_grads(place, x_span, normed_span, first_all, grad_pack)
    rest, first_part = lax.optimization_barrier((rest, first_part))
    rest = scatter_sum(rest, "a")
    by_tokens = exchange(grad_pack.reshape(KEY_VALUE_HEADS, token_count, HEAD_PACK), head_axes)
    by_tokens, first_part = lax.optimization_barrier((by_tokens, first_part))
    sums = exchange(first_part.reshape(-1, own_rows, first_part.shape[1]), ALL)
    sums, moe_sum, resid = lax.optimization_barrier((sums, moe_sum, resid))
    grad_q_w, grad_k_w, grad_v_w, grad_gain_one = weight_sums(
        sums.reshape(-1, KEY_VALUE_HEADS, lax.axis_size(("y", "c")), own_rows, first_part.shape[1])
    )
    rest = rest.astype(f32)
    grad_qkv = by_tokens.transpose(1, 0, 2).reshape(token_count, qkv_width)
    grad_normed_one = contract_cols(grad_qkv, first_all[:, :qkv_width])
    grad_x_norm, _ = rms_back(x_local, gain_one_f, grad_normed_one)
    grad_input = grad_resid + grad_x_norm
    layer_sum = resid + RESIDUAL_SCALE * moe_sum.astype(f32)
    if small_plane:
        grad_experts = jnp.concatenate(
            [
                quarter(left, b, y).astype(f32) + left_last.astype(f32) + left_on.astype(f32),
                quarter(right, b, y).astype(f32) + right_last.astype(f32) + right_on.astype(f32),
            ],
            axis=1,
        )
    else:
        grad_experts = grad_experts.astype(f32)
    return (
        layer_sum.astype(bf16)[None],
        grad_input[None],
        grad_gain_one[:, 0],
        grad_q_w,
        grad_k_w,
        grad_v_w,
        rest[:, :width],
        rest[:, width + E],
        rest[:, width : width + E],
        grad_experts[:, : 2 * F],
        grad_experts[:, 2 * F :],
    )


def solution(mesh):
    seq, row = mesh.shape["seq"], mesh.shape["row"]
    cut = Mesh(mesh.devices.reshape(GROUPS, seq // GROUPS, row // 2, 2), ALL)
    token_spec = P(("y", "c"), SEQ, None)
    row_spec = P(ALL, None)
    flat_spec = P(ALL)
    in_specs = (
        token_spec,
        token_spec,
        P(("y", "c"), None),
        token_spec,
        flat_spec,
        row_spec,
        row_spec,
        row_spec,
        row_spec,
        flat_spec,
        row_spec,
        row_spec,
        row_spec,
    )
    out_specs = (
        token_spec,
        token_spec,
        flat_spec,
        row_spec,
        row_spec,
        row_spec,
        row_spec,
        flat_spec,
        row_spec,
        row_spec,
        row_spec,
    )
    return jax.shard_map(body, mesh=cut, in_specs=in_specs, out_specs=out_specs, check_vma=False)
```

```python
import functools

import jax
import jax.numpy as jnp
from jax import lax
from jax.experimental import pallas as pl
from jax.experimental.pallas import tpu as pltpu
from jax.sharding import Mesh, PartitionSpec as P

QUERY_HEADS = 16
KEY_VALUE_HEADS = 8
HEAD_SIZE = 64
F = 512
E = 16
GROUPS = 4
EXPERTS_HERE = E // GROUPS
LANES = 128
PAIR = 2 * HEAD_SIZE
HEAD_PACK = 4 * HEAD_SIZE
BLOCK = 256
QUERY_BLOCK = 512

NORM_EPS = 1e-06
RESIDUAL_SCALE = 0.22
SCALE_OF_SCORES = 0.015625
ROPE_BASE = 10000.0
NEGATIVE_HUGE = -1e30
HIGHEST_DOT = lax.Precision.HIGHEST
VMEM_LIMIT = 60 * 1024 * 1024

PLANE = ("b", "y", "c")
SEQ = ("a", "b")
ALL = ("a", "b", "y", "c")
SWAP = [(0, 1), (1, 0)]

f32 = jnp.float32
bf16 = jnp.bfloat16


def rotation_tables(positions):
    half = HEAD_SIZE // 2
    freq = jnp.power(ROPE_BASE, -2.0 * jnp.arange(half, dtype=f32) / HEAD_SIZE)
    angle = positions.astype(f32)[:, None] * freq[None, :]
    return jnp.cos(angle), jnp.sin(angle)


def rms_back(values, gain, grad_norm):
    mean_square = jnp.mean(values * values, axis=-1, keepdims=True)
    inverse = lax.rsqrt(mean_square + NORM_EPS)
    scaled_grad = grad_norm * gain
    grad_values = inverse * scaled_grad - values * inverse**3 * jnp.mean(
        values * scaled_grad, axis=-1, keepdims=True
    )
    grad_gain = jnp.sum(grad_norm * values * inverse, axis=0)
    return (grad_values, grad_gain)


def rms_scale(values, gain):
    mean_square = jnp.mean(values * values, axis=-1, keepdims=True)
    return values * lax.rsqrt(mean_square + NORM_EPS) * gain


def contract_rows(left_side, right_side):
    return lax.dot_general(
        left_side, right_side, (((0,), (0,)), ((), ())), preferred_element_type=f32
    )


def contract_cols(left_side, right_side):
    return lax.dot_general(
        left_side, right_side, (((1,), (1,)), ((), ())), preferred_element_type=f32
    )


def gather(x, axes):
    return lax.all_gather(x, axes, axis=0, tiled=True)


def scatter_sum(x, axes):
    return lax.psum_scatter(x, axes, scatter_dimension=0, tiled=True)


def pad_lanes(x, lanes):
    return jnp.pad(x, ((0, 0), (0, lanes - x.shape[1])))


def line_pairs(n, step):
    return [(i, i + step) for i in range(n) if 0 <= i + step < n]


def grid_gather(x):
    n = lax.axis_size("a")

    def cross(block, ends):
        return lax.ppermute(
            block, SEQ, [(2 * i + j, 2 * i + 1 - j) for i in range(n) if ends(i) for j in (0, 1)]
        )

    pieces = [(0, 0, x), (0, 1, cross(x, lambda i: True))]
    up = down = x
    for k in range(1, n):
        up = lax.ppermute(up, "a", line_pairs(n, 1))
        down = lax.ppermute(down, "a", line_pairs(n, -1))
        pieces += [(-k, 0, up), (-k, 1, cross(up, lambda i: i >= k))]
        pieces += [(k, 0, down), (k, 1, cross(down, lambda i: i + k < n))]
    return pieces


def plane_gather(x):
    swap = SWAP
    half = x.shape[0] // 2
    from_y = lax.ppermute(x, "y", SWAP)
    from_b = lax.ppermute(x, "b", SWAP)
    upper = lax.ppermute(from_b[:half], "y", SWAP)
    lower = lax.ppermute(from_y[half:], "b", SWAP)
    return [
        (block, lax.ppermute(block, "c", SWAP)) for block in (x, from_y, from_b, upper, lower)
    ]


def quarter(v, b, y):
    return lax.dynamic_index_in_dim(lax.dynamic_index_in_dim(v, b, 0, False), y, 0, False)


def halve_add(terms):
    own, other = terms
    return (own.astype(f32) + other.astype(f32)).astype(own.dtype)


def rotate_lanes(x, cos, sin):
    width = x.shape[-1]
    lane = lax.broadcasted_iota(jnp.int32, x.shape, x.ndim - 1)
    swapped = jnp.where(
        lane % HEAD_SIZE < HEAD_SIZE // 2,
        pltpu.roll(x, width - HEAD_SIZE // 2, x.ndim - 1),
        pltpu.roll(x, HEAD_SIZE // 2, x.ndim - 1),
    )
    return x * cos + swapped * sin


def spread_tables(cos, sin):
    return jnp.concatenate([cos] * 4, axis=1), jnp.concatenate([-sin, sin, -sin, sin], axis=1)


def key_tables(cos, sin):
    low = lower_lanes(cos.shape)
    return jnp.where(low, cos, 1.0), jnp.where(low, sin, 0.0)


def project_kernel(places, place_ref, *refs):
    count = 1 if places is None else len(places)
    blocks, refs = refs[:count], refs[count:]
    small_ref, w_ref, cos_ref, sin_ref, qkv_ref, normed_ref, x_ref = refs[:7]
    wide_cos_ref, wide_sin_ref, gain, held, sems = refs[7:]
    i = pl.program_id(0)
    slots = held.shape[0]

    @pl.when(i == 0)
    def _():
        if places is None:
            for slot in range(slots):
                pltpu.make_async_copy(blocks[0].at[slot], held.at[slot], sems.at[slot]).start()
        else:
            for (distance, crossed), block in zip(places, blocks):
                at = place_ref[1] + distance
                member = 1 - place_ref[2] if crossed else place_ref[2]

                @pl.when((at >= 0) & (at < slots // 2))
                def _(block=block, slot=2 * at + member):
                    pltpu.make_async_copy(block, held.at[slot], sems.at[slot]).start()

        gain[...] = jnp.transpose(small_ref[...].astype(f32))[E : E + 8, :]

    arrived = blocks[0].at[0] if places is None else blocks[0]
    pltpu.make_async_copy(arrived, held.at[i], sems.at[i]).wait()
    x = held[i]
    x_ref[...] = x
    normed = rms_scale(x.astype(f32), gain[0:1, :]).astype(bf16)
    normed_ref[...] = normed
    pre = jnp.dot(normed, w_ref[...], preferred_element_type=f32)
    cos, sin = spread_tables(cos_ref[...], sin_ref[...])
    wide_cos_ref[...] = cos
    wide_sin_ref[...] = sin
    qkv_ref[:, :PAIR] = rotate_lanes(pre[:, :PAIR], cos, sin).astype(bf16)
    qkv_ref[:, PAIR:] = rotate_lanes(pre[:, PAIR:], *key_tables(cos, sin)).astype(bf16)


def project(place, places, blocks, rows, packed, cos, sin):
    width = packed.shape[0]
    small_at = packed.shape[1] // LANES - 1
    span = cos.shape[0]
    table = pl.BlockSpec((rows, HEAD_SIZE // 2), lambda i, h: (i, 0))
    token_rows = pl.BlockSpec((rows, width), lambda i, h: (i, 0))
    return pl.pallas_call(
        functools.partial(project_kernel, places),
        grid_spec=pltpu.PrefetchScalarGridSpec(
            num_scalar_prefetch=1,
            grid=(span // rows,),
            in_specs=[pl.BlockSpec(memory_space=pl.ANY)] * len(blocks)
            + [
                pl.BlockSpec((width, LANES), lambda i, h: (0, small_at)),
                pl.BlockSpec((width, HEAD_PACK), lambda i, h: (0, h[0])),
                table,
                table,
            ],
            out_specs=[
                pl.BlockSpec((rows, HEAD_PACK), lambda i, h: (i, 0)),
                token_rows,
                token_rows,
                pl.BlockSpec((rows, PAIR), lambda i, h: (i, 0)),
                pl.BlockSpec((rows, PAIR), lambda i, h: (i, 0)),
            ],
            scratch_shapes=[
                pltpu.VMEM((8, width), f32),
                pltpu.VMEM((span // rows, rows, width), bf16),
                pltpu.SemaphoreType.DMA((span // rows,)),
            ],
        ),
        out_shape=[
            jax.ShapeDtypeStruct((span, HEAD_PACK), bf16),
            jax.ShapeDtypeStruct((span, width), bf16),
            jax.ShapeDtypeStruct((span, width), bf16),
            jax.ShapeDtypeStruct((span, PAIR), f32),
            jax.ShapeDtypeStruct((span, PAIR), f32),
        ],
        compiler_params=pltpu.CompilerParams(vmem_limit_bytes=VMEM_LIMIT),
        cost_estimate=pl.CostEstimate(
            flops=2 * span * width * HEAD_PACK, bytes_accessed=18 * 2**20, transcendentals=0
        ),
        name="project",
    )(place, *blocks, packed, packed, cos, sin)


def head_grads_kernel(head_ref, x_ref, normed_ref, w_ref, grad_ref, out_ref, acc, gain):
    i = pl.program_id(0)

    @pl.when(i == 0)
    def _():
        acc[...] = jnp.zeros_like(acc)
        gain[...] = jnp.zeros_like(gain)

    grad = grad_ref[...]
    acc[...] += contract_rows(grad, normed_ref[...])
    x = x_ref[...].astype(f32)
    inverse = lax.rsqrt(jnp.mean(x * x, axis=-1, keepdims=True) + NORM_EPS)
    back = contract_cols(grad, w_ref[...]) * (x * inverse)
    gain[...] += jnp.sum(back.reshape(back.shape[0] // 8, 8, back.shape[1]), axis=0)

    @pl.when(i == pl.num_programs(0) - 1)
    def _():
        out_ref[:, :HEAD_PACK] = jnp.transpose(acc[...]).astype(bf16)
        total = jnp.sum(gain[...], axis=0, keepdims=True)
        rows = lax.broadcasted_iota(jnp.int32, (LANES, total.shape[1]), 0)
        out_ref[:, HEAD_PACK:] = jnp.transpose(
            jnp.where(rows == 0, jnp.broadcast_to(total, rows.shape), 0.0)
        ).astype(bf16)


def head_grads(head, x, normed, packed, grads):
    span, width = x.shape
    rows = 2 * BLOCK
    token_rows = pl.BlockSpec((rows, width), lambda i, h: (i, 0))
    return pl.pallas_call(
        head_grads_kernel,
        grid_spec=pltpu.PrefetchScalarGridSpec(
            num_scalar_prefetch=1,
            grid=(span // rows,),
            in_specs=[
                token_rows,
                token_rows,
                pl.BlockSpec((width, HEAD_PACK), lambda i, h: (0, h[0])),
                pl.BlockSpec((rows, HEAD_PACK), lambda i, h: (i, 0)),
            ],
            out_specs=pl.BlockSpec((width, HEAD_PACK + LANES), lambda i, h: (0, 0)),
            scratch_shapes=[pltpu.VMEM((HEAD_PACK, width), f32), pltpu.VMEM((8, width), f32)],
        ),
        out_shape=jax.ShapeDtypeStruct((width, HEAD_PACK + LANES), bf16),
        compiler_params=pltpu.CompilerParams(vmem_limit_bytes=VMEM_LIMIT),
        cost_estimate=pl.CostEstimate(
            flops=4 * span * width * HEAD_PACK, bytes_accessed=12 * 2**20, transcendentals=0
        ),
        name="head_grads",
    )(head, x, normed, packed, grads)


def lower_lanes(shape):
    return lax.broadcasted_iota(jnp.int32, shape, len(shape) - 1) < HEAD_SIZE


def both_heads_low(pair):
    low = lower_lanes(pair.shape)
    return jnp.concatenate(
        [jnp.where(low, pair, 0.0), jnp.where(low, pltpu.roll(pair, HEAD_SIZE, 1), 0.0)], axis=0
    )


def both_heads_high(pair):
    low = lower_lanes(pair.shape)
    return jnp.concatenate(
        [jnp.where(low, 0.0, pltpu.roll(pair, HEAD_SIZE, 1)), jnp.where(low, 0.0, pair)], axis=0
    )


def block_bounds(bounds_ref):
    i, steps = pl.program_id(0), pl.num_programs(0)
    query_start = (i + bounds_ref[2 * steps]) * QUERY_BLOCK
    diagonal = query_start // BLOCK
    full = jnp.minimum(bounds_ref[steps + i], diagonal)
    return query_start, bounds_ref[i], full, diagonal, diagonal + QUERY_BLOCK // BLOCK


def pair_mask(doc, query_start):
    doc = jnp.concatenate([doc, doc], axis=1)
    queries = lax.broadcasted_iota(jnp.int32, doc.shape, 1) % QUERY_BLOCK + query_start

    def masked(scores, start):
        keys = lax.broadcasted_iota(jnp.int32, scores.shape, 0) + start
        return jnp.where((keys >= doc) & (keys <= queries), scores, NEGATIVE_HUGE)

    return masked


def attend_kernel(bounds_ref, q_ref, kv_ref, doc_ref, o_ref, low_ref, lse_ref, acc):
    query_start, first, full, diagonal, end = block_bounds(bounds_ref)
    q = both_heads_low(q_ref[...].astype(f32) * SCALE_OF_SCORES).astype(bf16)
    masked = pair_mask(doc_ref[0], query_start)
    acc[...] = jnp.zeros_like(acc)

    def step(mask, j, carried):
        top, total = carried
        start = pl.multiple_of(j * BLOCK, BLOCK)
        kv = kv_ref[pl.ds(start, BLOCK), :]
        scores = contract_cols(kv, q)
        if mask:
            scores = masked(scores, start)
        new = jnp.maximum(top, jnp.max(scores, axis=0, keepdims=True))
        probs = jnp.exp(scores - new)
        keep = jnp.exp(top - new)
        acc[...] = acc[...] * keep + contract_rows(kv, probs.astype(bf16))
        return new, total * keep + jnp.sum(probs, axis=0, keepdims=True)

    row = (1, 2 * QUERY_BLOCK)
    carried = (jnp.full(row, NEGATIVE_HUGE, f32), jnp.zeros(row, f32))
    carried = lax.fori_loop(first, full, functools.partial(step, True), carried)
    carried = lax.fori_loop(full, diagonal, functools.partial(step, False), carried)
    top, total = lax.fori_loop(diagonal, end, functools.partial(step, True), carried)
    mixed = jnp.transpose(acc[...] / total)
    one, two = mixed[:QUERY_BLOCK], mixed[QUERY_BLOCK:]
    out = jnp.where(lower_lanes(one.shape), pltpu.roll(one, HEAD_SIZE, 1), two)
    o_ref[...] = out
    low_ref[...] = out.astype(bf16)
    lse_ref[0] = top + jnp.log(total)


def attention_specs(kv_at, keys):
    pair = pl.BlockSpec((QUERY_BLOCK, PAIR), lambda i, s: (i, 0))
    return (
        pair,
        pl.BlockSpec((keys, PAIR), lambda i, s: (0, kv_at)),
        pl.BlockSpec((1, 1, QUERY_BLOCK), lambda i, s: (i, 0, 0)),
        pl.BlockSpec((1, 1, 2 * QUERY_BLOCK), lambda i, s: (i, 0, 0)),
    )


def attend(bounds, qkv, kv, kv_at, doc):
    queries, keys = qkv.shape[0], kv.shape[0]
    steps = queries // QUERY_BLOCK
    pair, whole, doc_row, lse_row = attention_specs(kv_at, keys)
    return pl.pallas_call(
        attend_kernel,
        grid_spec=pltpu.PrefetchScalarGridSpec(
            num_scalar_prefetch=1,
            grid=(steps,),
            in_specs=[pair, whole, doc_row],
            out_specs=[pair, pair, lse_row],
            scratch_shapes=[pltpu.VMEM((PAIR, 2 * QUERY_BLOCK), f32)],
        ),
        out_shape=[
            jax.ShapeDtypeStruct((queries, PAIR), f32),
            jax.ShapeDtypeStruct((queries, PAIR), bf16),
            jax.ShapeDtypeStruct((steps, 1, 2 * QUERY_BLOCK), f32),
        ],
        compiler_params=pltpu.CompilerParams(vmem_limit_bytes=VMEM_LIMIT),
        cost_estimate=pl.CostEstimate(
            flops=4 * queries * keys * PAIR, bytes_accessed=6 * 2**20, transcendentals=queries * keys
        ),
        name="attend",
    )(bounds, qkv, kv, doc)


def attend_back_kernel(
    fold, bounds_ref, q_ref, kv_ref, doc_ref, do_ref, o_ref, lse_ref, cos_ref, sin_ref, *refs
):
    if fold:
        out_ref, acc, dkv_ref = refs
    else:
        dq_ref, dkv_ref, acc = refs
    i = pl.program_id(0)
    query_start, first, full, diagonal, end = block_bounds(bounds_ref)

    @pl.when(i == 0)
    def _():
        dkv_ref[...] = jnp.zeros_like(dkv_ref)

    q = both_heads_low(q_ref[...].astype(f32) * SCALE_OF_SCORES).astype(bf16)
    grad = do_ref[...].astype(f32)
    product = jnp.transpose(grad * o_ref[...])
    delta = jnp.concatenate(
        [
            jnp.sum(product[:HEAD_SIZE], axis=0, keepdims=True),
            jnp.sum(product[HEAD_SIZE:], axis=0, keepdims=True),
        ],
        axis=1,
    )
    grad = both_heads_high(grad).astype(bf16)
    sources = jnp.concatenate([q, grad], axis=0)
    masked = pair_mask(doc_ref[0], query_start)
    lse = lse_ref[0]
    acc[...] = jnp.zeros_like(acc)

    def step(mask, j, carried):
        start = pl.multiple_of(j * BLOCK, BLOCK)
        kv = kv_ref[pl.ds(start, BLOCK), :]
        scores = contract_cols(kv, q) - lse
        if mask:
            scores = masked(scores, start)
        probs = jnp.exp(scores)
        grad_scores = (probs * (contract_cols(kv, grad) - delta)).astype(bf16)
        acc[...] += contract_rows(kv, grad_scores)
        both = jnp.concatenate([grad_scores, probs.astype(bf16)], axis=1)
        dkv_ref[pl.ds(start, BLOCK), :] += jnp.dot(both, sources, preferred_element_type=f32)
        return carried

    lax.fori_loop(first, full, functools.partial(step, True), 0)
    lax.fori_loop(full, diagonal, functools.partial(step, False), 0)
    lax.fori_loop(diagonal, end, functools.partial(step, True), 0)
    dq = jnp.transpose(acc[...])
    one, two = dq[:QUERY_BLOCK], dq[QUERY_BLOCK:]
    dq = jnp.where(lower_lanes(one.shape), one, pltpu.roll(two, HEAD_SIZE, 1))
    if not fold:
        dq_ref[...] = dq
        return
    mine = pl.ds(pl.multiple_of(i * QUERY_BLOCK, QUERY_BLOCK), QUERY_BLOCK)
    out_ref[mine, :PAIR] = rotate_lanes(
        dq * SCALE_OF_SCORES, cos_ref[mine, :], -sin_ref[mine, :]
    ).astype(bf16)

    @pl.when(i == pl.num_programs(0) - 1)
    def _():
        def finish(j, carried):
            part = pl.ds(pl.multiple_of(j * BLOCK, BLOCK), BLOCK)
            cos, sin = key_tables(cos_ref[part, :], sin_ref[part, :])
            out_ref[part, PAIR:] = rotate_lanes(dkv_ref[part, :], cos, -sin).astype(bf16)
            return carried

        lax.fori_loop(0, dkv_ref.shape[0] // BLOCK, finish, 0)


def attend_back(bounds, qkv, kv, kv_at, doc, grad, out, lse, cos, sin, fold):
    queries, keys = qkv.shape[0], kv.shape[0]
    steps = queries // QUERY_BLOCK
    pair, whole, doc_row, lse_row = attention_specs(kv_at, keys)
    table = pl.BlockSpec(cos.shape, lambda i, s: (0, 0))
    acc = pltpu.VMEM((PAIR, 2 * QUERY_BLOCK), f32)
    if fold:
        out_specs = pl.BlockSpec((queries, HEAD_PACK), lambda i, s: (0, 0))
        out_shape = jax.ShapeDtypeStruct((queries, HEAD_PACK), bf16)
        scratch = [acc, pltpu.VMEM((keys, PAIR), f32)]
    else:
        out_specs = [pair, pl.BlockSpec((keys, PAIR), lambda i, s: (0, 0))]
        out_shape = [
            jax.ShapeDtypeStruct((queries, PAIR), f32),
            jax.ShapeDtypeStruct((keys, PAIR), f32),
        ]
        scratch = [acc]
    return pl.pallas_call(
        functools.partial(attend_back_kernel, fold),
        grid_spec=pltpu.PrefetchScalarGridSpec(
            num_scalar_prefetch=1,
            grid=(steps,),
            in_specs=[pair, whole, doc_row, pair, pair, lse_row, table, table],
            out_specs=out_specs,
            scratch_shapes=scratch,
        ),
        out_shape=out_shape,
        compiler_params=pltpu.CompilerParams(vmem_limit_bytes=VMEM_LIMIT),
        cost_estimate=pl.CostEstimate(
            flops=10 * queries * keys * PAIR,
            bytes_accessed=8 * 2**20,
            transcendentals=queries * keys,
        ),
        name="attend_back",
    )(bounds, qkv, kv, doc, grad, out, lse, cos, sin)


def unrotate_kernel(dq_ref, dkv_ref, cos_ref, sin_ref, out_ref):
    cos, sin = cos_ref[...], sin_ref[...]
    dq = rotate_lanes(dq_ref[...] * SCALE_OF_SCORES, cos, -sin)
    cos, sin = key_tables(cos, sin)
    dkv = rotate_lanes(dkv_ref[...], cos, -sin)
    out_ref[...] = jnp.concatenate([dq, dkv], axis=1).astype(bf16)


def unrotate(dq, dkv, cos, sin):
    rows = dq.shape[0]
    pair = pl.BlockSpec((BLOCK, PAIR), lambda i: (i, 0))
    return pl.pallas_call(
        unrotate_kernel,
        grid=(rows // BLOCK,),
        in_specs=[pair, pair, pair, pair],
        out_specs=pl.BlockSpec((BLOCK, HEAD_PACK), lambda i: (i, 0)),
        out_shape=jax.ShapeDtypeStruct((rows, HEAD_PACK), bf16),
        cost_estimate=pl.CostEstimate(
            flops=rows * HEAD_PACK * 8, bytes_accessed=rows * HEAD_PACK * 14, transcendentals=0
        ),
        name="unrotate",
    )(dq, dkv, cos, sin)


def place_experts_kernel(place_ref, *refs):
    blocks, (ct_ref, w_ref, z_ref, sems) = refs[:10], refs[10:]
    core = place_ref[1]
    rows = w_ref.shape[1] // 2
    half = rows // 2
    sources = [[(0, 0, rows)], [(1, 0, rows)], [(2, 0, rows)], [(3, 0, half), (4, half, half)]]
    for step, parts in enumerate(sources):

        @pl.when(pl.program_id(0) == step)
        def _(parts=parts):
            copies = []
            for source, start, length in parts:
                for other in (0, 1):
                    first = jnp.where(core == other, 0, rows) + start
                    at = pl.ds(pl.multiple_of(first, half), length)
                    copies.append(
                        pltpu.make_async_copy(
                            blocks[2 * source + other], w_ref.at[0, at, :], sems.at[len(copies)]
                        )
                    )
            for copy in copies:
                copy.start()
            for copy in copies:
                copy.wait()

    z_ref[0] = jnp.dot(ct_ref[...], w_ref[0, :, 2 * F :], preferred_element_type=f32)


def place_experts(place, parts, early, width):
    rows = early.shape[0]
    blocks = [block for pair in parts for block in pair]
    return pl.pallas_call(
        place_experts_kernel,
        grid_spec=pltpu.PrefetchScalarGridSpec(
            num_scalar_prefetch=1,
            grid=(EXPERTS_HERE,),
            in_specs=[pl.BlockSpec(memory_space=pl.ANY)] * len(blocks)
            + [pl.BlockSpec((rows, width), lambda r, s: (0, 0))],
            out_specs=[
                pl.BlockSpec((1, width, 3 * F), lambda r, s: (s[0] ^ r, 0, 0)),
                pl.BlockSpec((1, rows, F), lambda r, s: (s[0] ^ r, 0, 0)),
            ],
            scratch_shapes=[pltpu.SemaphoreType.DMA((4,))],
        ),
        out_shape=[
            jax.ShapeDtypeStruct((EXPERTS_HERE, width, 3 * F), bf16),
            jax.ShapeDtypeStruct((EXPERTS_HERE, rows, F), f32),
        ],
        compiler_params=pltpu.CompilerParams(vmem_limit_bytes=VMEM_LIMIT),
        cost_estimate=pl.CostEstimate(
            flops=2 * EXPERTS_HERE * rows * width * F, bytes_accessed=36 * 2**20, transcendentals=0
        ),
        name="place_experts",
    )(place, *blocks, early)


def lane_column(x, at):
    lane = lax.broadcasted_iota(jnp.int32, x.shape, 1)
    return jnp.sum(jnp.where(lane == at, x, 0.0), axis=1, keepdims=True)


def experts_kernel(
    group_ref, n_ref, routed_ref, router_ref, w_ref, z_ref,
    back_ref, gates_ref, hidden_ref, pre_ref, acc, dots,
):
    e = pl.program_id(0)
    own = group_ref[0] * EXPERTS_HERE + e
    rows = n_ref.shape[0]

    @pl.when(e == 0)
    def _():
        logits = jnp.dot(n_ref[...], router_ref[...], preferred_element_type=f32)
        routed = routed_ref[...].astype(f32) > 0.5
        highest = jnp.max(jnp.where(routed, logits, NEGATIVE_HUGE), axis=1, keepdims=True)
        weights = jnp.where(routed, jnp.exp(jnp.where(routed, logits - highest, 0.0)), 0.0)
        gates_ref[...] = weights / jnp.sum(weights, axis=1, keepdims=True)
        acc[...] = jnp.zeros_like(acc)
        dots[...] = jnp.zeros_like(dots)

    w_in = w_ref[0, :, : 2 * F]
    for t in range(rows // BLOCK):
        part = pl.ds(t * BLOCK, BLOCK)
        pre = jnp.dot(n_ref[part, :], w_in, preferred_element_type=f32)
        gate, up = pre[:, :F], pre[:, F:]
        z = z_ref[0, part, :]
        weight = lane_column(gates_ref[part, :], own)
        sig = 1.0 / (1.0 + jnp.exp(-gate))
        act = gate * sig
        hidden = act * up
        hidden_ref[0, part, :] = (weight * hidden).astype(bf16)
        dot = RESIDUAL_SCALE * jnp.sum(hidden.astype(bf16).astype(f32) * z, axis=1, keepdims=True)
        lane = lax.broadcasted_iota(jnp.int32, (BLOCK, LANES), 1)
        dots[part, :] += jnp.where(lane == own, dot, 0.0)
        scaled = (RESIDUAL_SCALE * weight) * z
        pre_ref[0, part, :F] = (scaled * up * (sig + act * (1.0 - sig))).astype(bf16)
        pre_ref[0, part, F:] = (scaled * act).astype(bf16)
        acc[part, :] += contract_cols(pre_ref[0, part, :], w_in)

    @pl.when(e == EXPERTS_HERE - 1)
    def _():
        width = n_ref.shape[1]
        back_ref[:, :width] = acc[...].astype(bf16)
        high = dots[...].astype(bf16)
        low = dots[...] - high.astype(f32)
        back_ref[:, width:] = (high.astype(f32) + pltpu.roll(low, E, 1)).astype(bf16)


def experts(group, normed, early, packed, w_all, z):
    rows, width = normed.shape
    count = w_all.shape[0]
    whole = pl.BlockSpec((rows, width), lambda e, g: (0, 0))
    column = width // LANES
    router_at = packed.shape[1] // LANES - 1
    return pl.pallas_call(
        experts_kernel,
        grid_spec=pltpu.PrefetchScalarGridSpec(
            num_scalar_prefetch=1,
            grid=(count,),
            in_specs=[
                whole,
                pl.BlockSpec((rows, LANES), lambda e, g: (0, column)),
                pl.BlockSpec((width, LANES), lambda e, g: (0, router_at)),
                pl.BlockSpec((1, width, 3 * F), lambda e, g: (e, 0, 0)),
                pl.BlockSpec((1, rows, F), lambda e, g: (e, 0, 0)),
            ],
            out_specs=[
                pl.BlockSpec((rows, width + LANES), lambda e, g: (0, 0)),
                pl.BlockSpec((rows, LANES), lambda e, g: (0, 0)),
                pl.BlockSpec((1, rows, F), lambda e, g: (e, 0, 0)),
                pl.BlockSpec((1, rows, 2 * F), lambda e, g: (e, 0, 0)),
            ],
            scratch_shapes=[pltpu.VMEM((rows, width), f32), pltpu.VMEM((rows, LANES), f32)],
        ),
        out_shape=[
            jax.ShapeDtypeStruct((rows, width + LANES), bf16),
            jax.ShapeDtypeStruct((rows, LANES), f32),
            jax.ShapeDtypeStruct((count, rows, F), bf16),
            jax.ShapeDtypeStruct((count, rows, 2 * F), bf16),
        ],
        compiler_params=pltpu.CompilerParams(vmem_limit_bytes=VMEM_LIMIT),
        cost_estimate=pl.CostEstimate(
            flops=2 * count * rows * width * 4 * F, bytes_accessed=40 * 2**20, transcendentals=0
        ),
        name="experts",
    )(group, normed, early, packed, w_all, z)


def expert_grads_kernel(with_y, half_ref, n_ref, ct_ref, w_ref, hidden_ref, pre_ref, *refs):
    if with_y:
        left_ref, right_ref, y_ref, n_t, ct_t, acc = refs
    else:
        left_ref, right_ref, n_t, ct_t = refs
    e = pl.program_id(0)
    cut = left_ref.shape[2]

    @pl.when(e == 0)
    def _():
        n_t[...] = jnp.transpose(n_ref[...])
        ct_t[...] = jnp.transpose(ct_ref[...])
        if with_y:
            acc[...] = jnp.zeros_like(acc)

    grads = jnp.dot(n_t[...], pre_ref[0], preferred_element_type=f32).astype(bf16)
    left_ref[0] = grads[:, :cut]
    right_ref[0, :, : 2 * F - cut] = grads[:, cut:]
    right_ref[0, :, 2 * F - cut :] = (
        RESIDUAL_SCALE * jnp.dot(ct_t[...], hidden_ref[0], preferred_element_type=f32)
    ).astype(bf16)
    if not with_y:
        return
    acc[...] += contract_cols(hidden_ref[0], w_ref[0, :, 2 * F :])

    @pl.when(e == pl.num_programs(0) - 1)
    def _():
        y_ref[...] = acc[...].astype(bf16)


def expert_grads(half, halves, normed, early, w_all, hidden, pre, with_y):
    rows, width = normed.shape
    count = w_all.shape[0]
    own, cut = width // halves, 3 * F // 2
    feature = pl.BlockSpec((rows, own), lambda e, h: (0, h[0]))
    out_specs = [pl.BlockSpec((1, own, cut), lambda e, h: (e, 0, 0))] * 2
    out_shape = [jax.ShapeDtypeStruct((count, own, cut), bf16)] * 2
    scratch = [pltpu.VMEM((own, rows), bf16), pltpu.VMEM((own, rows), bf16)]
    if with_y:
        out_specs.append(pl.BlockSpec((rows, width), lambda e, h: (0, 0)))
        out_shape.append(jax.ShapeDtypeStruct((rows, width), bf16))
        scratch.append(pltpu.VMEM((rows, width), f32))
    return pl.pallas_call(
        functools.partial(expert_grads_kernel, with_y),
        grid_spec=pltpu.PrefetchScalarGridSpec(
            num_scalar_prefetch=1,
            grid=(count,),
            in_specs=[
                feature,
                feature,
                pl.BlockSpec((1, width, 3 * F), lambda e, h: (e, 0, 0)),
                pl.BlockSpec((1, rows, F), lambda e, h: (e, 0, 0)),
                pl.BlockSpec((1, rows, 2 * F), lambda e, h: (e, 0, 0)),
            ],
            out_specs=out_specs,
            scratch_shapes=scratch,
        ),
        out_shape=out_shape,
        compiler_params=pltpu.CompilerParams(vmem_limit_bytes=VMEM_LIMIT),
        cost_estimate=pl.CostEstimate(
            flops=2 * count * rows * width * 3 * F // halves + 2 * with_y * count * rows * width * F,
            bytes_accessed=30 * 2**20,
            transcendentals=0,
        ),
        name="expert_grads",
    )(half, normed, early, w_all, hidden, pre)


def join_kernel(place_ref, o_ref, w_ref, small_ref, x_ref, normed_ref, resid_ref, own_ref, gain):
    t = pl.program_id(0)
    b = place_ref[2]

    @pl.when(t == 0)
    def _():
        gain[...] = jnp.transpose(small_ref[...].astype(f32))[E : E + 8, :]

    pairs = []
    for a in range(o_ref.shape[0]):
        same, other = o_ref[a, 0, 0], o_ref[a, 1, 0]
        pairs.append(jnp.where(b == 0, same, other))
        pairs.append(jnp.where(b == 0, other, same))
    attended = jnp.concatenate(pairs, axis=1)
    resid = x_ref[...].astype(f32) + RESIDUAL_SCALE * jnp.dot(
        attended, w_ref[...], preferred_element_type=f32
    )
    normed_ref[...] = rms_scale(resid, gain[1:2, :]).astype(bf16)

    @pl.when(t == place_ref[1])
    def _():
        resid_ref[...] = resid
        own_ref[...] = attended


def join(place, outs, packed, weights_at, x):
    width = packed.shape[0]
    lines, _, _, rows, pair = outs.shape
    small_at = packed.shape[1] // LANES - 1
    own = pl.BlockSpec((rows, width), lambda t, s: (0, 0))
    return pl.pallas_call(
        join_kernel,
        grid_spec=pltpu.PrefetchScalarGridSpec(
            num_scalar_prefetch=1,
            grid=(lines,),
            in_specs=[
                pl.BlockSpec((lines, 2, 1, rows, pair), lambda t, s: (0, 0, t, 0, 0)),
                pl.BlockSpec((width, width), lambda t, s: (0, weights_at)),
                pl.BlockSpec((width, LANES), lambda t, s: (0, small_at)),
                pl.BlockSpec((rows, width), lambda t, s: (2 * t + s[2], 0)),
            ],
            out_specs=[pl.BlockSpec((rows, width), lambda t, s: (t, 0)), own, own],
            scratch_shapes=[pltpu.VMEM((8, width), f32)],
        ),
        out_shape=[
            jax.ShapeDtypeStruct((lines * rows, width), bf16),
            jax.ShapeDtypeStruct((rows, width), f32),
            jax.ShapeDtypeStruct((rows, width), bf16),
        ],
        compiler_params=pltpu.CompilerParams(vmem_limit_bytes=VMEM_LIMIT),
        cost_estimate=pl.CostEstimate(
            flops=2 * lines * rows * width * width, bytes_accessed=12 * 2**20, transcendentals=0
        ),
        name="join",
    )(place, outs, packed, packed, x)


def weight_sums_kernel(sums_ref, q_ref, k_ref, v_ref, gain_ref):
    groups, heads, members = sums_ref.shape[:3]
    gain = jnp.zeros(gain_ref.shape, f32)
    values = []
    for h in range(heads):
        total = jnp.zeros(sums_ref.shape[3:], f32)
        for g in range(groups):
            for member in range(members):
                total += sums_ref[g, h, member].astype(f32)
        values.append(total)
        gain += total[:, HEAD_PACK:]
        q_ref[:, h * PAIR : (h + 1) * PAIR] = total[:, :PAIR]
    gain_ref[...] = gain
    for h in range(0, heads, 2):
        one, two = values[h][:, PAIR:HEAD_PACK], values[h + 1][:, PAIR:HEAD_PACK]
        low = lower_lanes(one.shape)
        at = slice(h // 2 * PAIR, (h // 2 + 1) * PAIR)
        k_ref[:, at] = jnp.where(low, one, pltpu.roll(two, HEAD_SIZE, 1))
        v_ref[:, at] = jnp.where(low, pltpu.roll(one, HEAD_SIZE, 1), two)


def weight_sums(sums):
    rows, heads = sums.shape[3], sums.shape[1]
    return pl.pallas_call(
        weight_sums_kernel,
        out_shape=[
            jax.ShapeDtypeStruct((rows, heads * PAIR), f32),
            jax.ShapeDtypeStruct((rows, heads * HEAD_SIZE), f32),
            jax.ShapeDtypeStruct((rows, heads * HEAD_SIZE), f32),
            jax.ShapeDtypeStruct((rows, LANES), f32),
        ],
        compiler_params=pltpu.CompilerParams(vmem_limit_bytes=VMEM_LIMIT),
        cost_estimate=pl.CostEstimate(flops=2**20, bytes_accessed=2 * 2**20, transcendentals=0),
        name="weight_sums",
    )(sums)


def exchange(x, axes):
    return lax.all_to_all(x, axes, 0, 0, tiled=True)


def body(
    tokens,
    cotangent,
    segment_ids,
    routes,
    norm_attn,
    w_query,
    key_weight_matrix,
    value_weight_matrix,
    w_output,
    norm_moe,
    w_router,
    expert_in,
    expert_out,
):
    x_local = tokens[0].astype(f32)
    token_count, width = x_local.shape
    seg_row = segment_ids[0]
    group = lax.axis_index("a")
    head_axes = SEQ if lax.axis_size(SEQ) == KEY_VALUE_HEADS else ("b",)
    whole_rows = head_axes == SEQ
    span = token_count * KEY_VALUE_HEADS
    span_start = 0 if whole_rows else group * span

    def start_of_doc(ids):
        return jnp.sum((seg_row[None, :] < ids[:, None]).astype(jnp.int32), axis=1)

    seg_span = lax.dynamic_slice_in_dim(seg_row, span_start, span)
    doc_span = start_of_doc(seg_span)
    cos_span, sin_span = rotation_tables(
        span_start + jnp.arange(span, dtype=jnp.int32) - doc_span
    )
    by_block = doc_span.reshape(-1, QUERY_BLOCK)
    bounds = jnp.concatenate(
        [
            by_block[:, 0] // BLOCK,
            (by_block[:, -1] + BLOCK - 1) // BLOCK,
            jnp.full((1,), span_start // QUERY_BLOCK, jnp.int32),
        ]
    )
    doc_rows = by_block[:, None, :]

    own_rows = w_query.shape[0]
    by_head = jnp.concatenate(
        [
            w_query.astype(bf16).reshape(own_rows, KEY_VALUE_HEADS, PAIR),
            key_weight_matrix.astype(bf16).reshape(own_rows, KEY_VALUE_HEADS, HEAD_SIZE),
            value_weight_matrix.astype(bf16).reshape(own_rows, KEY_VALUE_HEADS, HEAD_SIZE),
        ],
        axis=2,
    ).reshape(own_rows, KEY_VALUE_HEADS * HEAD_PACK)
    qkv_width = KEY_VALUE_HEADS * HEAD_PACK
    first_all = gather(
        jnp.concatenate(
            [
                by_head,
                w_output.astype(bf16),
                pad_lanes(
                    jnp.concatenate(
                        [
                            w_router.astype(bf16),
                            norm_attn.astype(bf16)[:, None],
                            norm_moe.astype(bf16)[:, None],
                        ],
                        axis=1,
                    ),
                    LANES,
                ),
            ],
            axis=1,
        ),
        ALL,
    )
    experts_low = jnp.concatenate([expert_in.astype(bf16), expert_out.astype(bf16)], axis=1)
    if whole_rows:
        pieces = grid_gather(tokens[0])
        places = [piece[:2] for piece in pieces]
        blocks = tuple(piece[2] for piece in pieces)
    else:
        places = None
        blocks = (gather(tokens[0], "b").reshape((-1,) + tokens.shape[1:]),)
    first_all, experts_low, blocks, cos_span, sin_span, bounds, doc_rows = (
        lax.optimization_barrier(
            (first_all, experts_low, blocks, cos_span, sin_span, bounds, doc_rows)
        )
    )
    output_w = first_all[:, qkv_width : qkv_width + width]
    small_at = qkv_width + width
    router_w = first_all[:, small_at : small_at + E]
    gain_one_f = first_all[:, small_at + E].astype(f32)
    gain_two_f = first_all[:, small_at + E + 1].astype(f32)

    expert_ids = jnp.arange(E, dtype=jnp.int32)
    routed_own = jnp.any(routes[0][:, :, None] == expert_ids[None, None, :], axis=1)
    early = jnp.concatenate([cotangent[0], pad_lanes(routed_own.astype(bf16), LANES)], axis=1)
    early, first_all = lax.optimization_barrier((early, first_all))
    early_all = gather(early, "a")
    small_plane = lax.axis_size("b") == 2 and lax.axis_size("y") == 2
    if small_plane:
        parts = plane_gather(experts_low)
    else:
        parts = gather(experts_low, PLANE)

    place = jnp.stack([lax.axis_index(head_axes), group, lax.axis_index("b")])
    qkv, normed_span, x_span, wide_cos, wide_sin = project(
        place, places, blocks, token_count, first_all, cos_span, sin_span
    )
    if whole_rows:
        kv, kv_at = qkv, 1
    else:
        kv, kv_at = gather(qkv[:, PAIR:], "a"), 0
    attention_result, attended, log_total = attend(bounds, qkv, kv, kv_at, doc_rows)
    if small_plane:
        member = lax.axis_index("b")
        by_column = attended.reshape(GROUPS, 2, token_count, PAIR)
        other = lax.ppermute(
            lax.dynamic_index_in_dim(by_column, 1 - member, 1, False), "b", SWAP
        )
        own = lax.dynamic_index_in_dim(by_column, member, 1, False)
        pair, early_all = lax.optimization_barrier((jnp.stack([own, other]), early_all))
        outs = lax.all_gather(pair, "a", axis=0, tiled=False)
        normed_all, resid, attended_low = join(place, outs, first_all, qkv_width // width, x_span)
        normed_two = lax.dynamic_slice_in_dim(normed_all, group * token_count, token_count)
        home = jnp.stack([member * 2 + lax.axis_index("y"), lax.axis_index("c")])
        experts_all, grad_hidden = place_experts(home, parts, early_all, width)
    else:
        attended_low = (
            exchange(attended.reshape(KEY_VALUE_HEADS, token_count, PAIR), head_axes)
            .transpose(1, 0, 2)
            .reshape(token_count, QUERY_HEADS * HEAD_SIZE)
        )
        attn_out = jnp.dot(attended_low, output_w, preferred_element_type=f32)
        resid = x_local + RESIDUAL_SCALE * attn_out
        normed_two = rms_scale(resid, gain_two_f).astype(bf16)
        normed_all = gather(normed_two, "a")
        experts_all = parts.reshape(EXPERTS_HERE, width, 3 * F)
        grad_hidden = jnp.einsum(
            "td,edf->etf",
            early_all[:, :width],
            experts_all[:, :, 2 * F :],
            preferred_element_type=f32,
        )
    back_part, gates_all, gated_hidden, grad_pre = experts(
        group.reshape(1), normed_all, early_all, first_all, experts_all, grad_hidden
    )
    back_own = scatter_sum(back_part, "a").astype(f32)
    inputs = (normed_all, early_all, experts_all, gated_hidden, grad_pre)
    if small_plane:
        core = lax.axis_index("c")
        send = expert_grads((1 - core).reshape(1), 2, *inputs, False)
        arrived = [lax.ppermute(x, "c", SWAP) for x in send]
        *keep, moe_part = expert_grads(core.reshape(1), 2, *inputs, True)
        left, right = (
            halve_add(terms).reshape((2, 2) + terms[0].shape[1:]) for terms in zip(keep, arrived)
        )
        back_own, moe_part, left, right = lax.optimization_barrier(
            (back_own, moe_part, left, right)
        )
        b, y = lax.axis_index("b"), lax.axis_index("y")
        left_on = quarter(left, 1 - b, y), lax.ppermute(quarter(left, 1 - b, 1 - y), "y", SWAP)
        right_on = quarter(right, b, 1 - y), lax.ppermute(quarter(right, 1 - b, 1 - y), "b", SWAP)
    else:
        *grads, moe_part = expert_grads(jnp.zeros((1,), jnp.int32), 1, *inputs, True)
        grad_experts = jnp.concatenate(grads, axis=2)
        back_own, moe_part, grad_experts = lax.optimization_barrier(
            (back_own, moe_part, grad_experts)
        )
        grad_experts = scatter_sum(grad_experts.reshape(EXPERTS_HERE * width, 3 * F), PLANE)
    moe_sum = scatter_sum(moe_part, "a")

    grad_out = cotangent[0].astype(f32)
    gates = lax.dynamic_slice_in_dim(gates_all, group * token_count, token_count)[:, :E]
    gate_grads_own = back_own[:, width : width + E] + back_own[:, width + E : width + 2 * E]
    grad_logits = gates * (gate_grads_own - jnp.sum(gates * gate_grads_own, axis=-1, keepdims=True))
    grad_normed_two = back_own[:, :width] + jnp.dot(
        grad_logits, router_w.astype(f32).T, precision=HIGHEST_DOT
    )
    grad_router = jnp.dot(normed_two.astype(f32).T, grad_logits, precision=HIGHEST_DOT)
    grad_resid_norm, grad_gain_two = rms_back(resid, gain_two_f, grad_normed_two)
    grad_resid = grad_out + grad_resid_norm
    grad_attn_low = (RESIDUAL_SCALE * grad_resid).astype(bf16)
    grad_heads = contract_cols(grad_attn_low, output_w).astype(bf16)
    grad_mixed = exchange(
        grad_heads.reshape(token_count, KEY_VALUE_HEADS, PAIR).transpose(1, 0, 2), head_axes
    ).reshape(span, PAIR)
    if small_plane:
        left_on, right_on = halve_add(left_on), halve_add(right_on)
        left_on, right_on, attended_low, grad_router = lax.optimization_barrier(
            (left_on, right_on, attended_low, grad_router)
        )
    small = jnp.concatenate([grad_router, grad_gain_two[:, None]], axis=1)
    second_part = jnp.concatenate(
        [contract_rows(attended_low, grad_attn_low), pad_lanes(small, LANES)], axis=1
    ).astype(bf16)
    cols = second_part.shape[1]
    second_part = second_part.reshape(GROUPS, -1, own_rows, cols).transpose(1, 0, 2, 3)
    if small_plane:
        second_part, left_on, right_on, grad_mixed = lax.optimization_barrier(
            (second_part, left_on, right_on, grad_mixed)
        )
        left_on, right_on = lax.ppermute(left_on, "b", SWAP), lax.ppermute(right_on, "y", SWAP)
    rest = scatter_sum(second_part.reshape(-1, cols), PLANE)
    grads = attend_back(
        bounds, qkv, kv, kv_at, doc_rows, grad_mixed, attention_result, log_total,
        wide_cos, wide_sin, whole_rows,
    )
    if whole_rows:
        grad_pack = grads
    else:
        grad_kv = scatter_sum(grads[1].astype(bf16), "a").astype(f32)
        grad_pack = unrotate(grads[0], grad_kv, wide_cos, wide_sin)
    if small_plane:
        left_on, right_on, left, right, moe_sum, grad_pack = lax.optimization_barrier(
            (left_on, right_on, left, right, moe_sum, grad_pack)
        )
    first_part = head_grads(place, x_span, normed_span, first_all, grad_pack)
    rest, first_part = lax.optimization_barrier((rest, first_part))
    rest = scatter_sum(rest, "a")
    by_tokens = exchange(grad_pack.reshape(KEY_VALUE_HEADS, token_count, HEAD_PACK), head_axes)
    by_tokens, first_part = lax.optimization_barrier((by_tokens, first_part))
    if small_plane:
        left, right, by_tokens = lax.optimization_barrier((left, right, by_tokens))
        left_last = lax.ppermute(quarter(left, b, 1 - y), "y", SWAP)
        right_last = lax.ppermute(quarter(right, 1 - b, y), "b", SWAP)
    sums = exchange(first_part.reshape(-1, own_rows, first_part.shape[1]), ALL)
    sums, moe_sum, resid, rest = lax.optimization_barrier((sums, moe_sum, resid, rest))
    grad_q_w, grad_k_w, grad_v_w, grad_gain_one = weight_sums(
        sums.reshape(-1, KEY_VALUE_HEADS, lax.axis_size(("y", "c")), own_rows, first_part.shape[1])
    )
    rest = rest.astype(f32)
    grad_qkv = by_tokens.transpose(1, 0, 2).reshape(token_count, qkv_width)
    grad_normed_one = contract_cols(grad_qkv, first_all[:, :qkv_width])
    grad_x_norm, _ = rms_back(x_local, gain_one_f, grad_normed_one)
    grad_input = grad_resid + grad_x_norm
    layer_sum = resid + RESIDUAL_SCALE * moe_sum.astype(f32)
    if small_plane:
        grad_experts = jnp.concatenate(
            [
                quarter(left, b, y).astype(f32) + left_last.astype(f32) + left_on.astype(f32),
                quarter(right, b, y).astype(f32) + right_last.astype(f32) + right_on.astype(f32),
            ],
            axis=1,
        )
    else:
        grad_experts = grad_experts.astype(f32)
    return (
        layer_sum.astype(bf16)[None],
        grad_input[None],
        grad_gain_one[:, 0],
        grad_q_w,
        grad_k_w,
        grad_v_w,
        rest[:, :width],
        rest[:, width + E],
        rest[:, width : width + E],
        grad_experts[:, : 2 * F],
        grad_experts[:, 2 * F :],
    )


def solution(mesh):
    seq, row = mesh.shape["seq"], mesh.shape["row"]
    cut = Mesh(mesh.devices.reshape(GROUPS, seq // GROUPS, row // 2, 2), ALL)
    token_spec = P(("y", "c"), SEQ, None)
    row_spec = P(ALL, None)
    flat_spec = P(ALL)
    in_specs = (
        token_spec,
        token_spec,
        P(("y", "c"), None),
        token_spec,
        flat_spec,
        row_spec,
        row_spec,
        row_spec,
        row_spec,
        flat_spec,
        row_spec,
        row_spec,
        row_spec,
    )
    out_specs = (
        token_spec,
        token_spec,
        flat_spec,
        row_spec,
        row_spec,
        row_spec,
        row_spec,
        flat_spec,
        row_spec,
        row_spec,
        row_spec,
    )
    return jax.shard_map(body, mesh=cut, in_specs=in_specs, out_specs=out_specs, check_vma=False)
```

```python
import functools

import jax
import jax.numpy as jnp
from jax import lax
from jax.experimental import pallas as pl
from jax.experimental.pallas import tpu as pltpu
from jax.sharding import Mesh, PartitionSpec as P

QUERY_HEADS = 16
KEY_VALUE_HEADS = 8
HEAD_SIZE = 64
F = 512
E = 16
GROUPS = 4
EXPERTS_HERE = E // GROUPS
LANES = 128
PAIR = 2 * HEAD_SIZE
HEAD_PACK = 4 * HEAD_SIZE
BLOCK = 256
QUERY_BLOCK = 512

NORM_EPS = 1e-06
RESIDUAL_SCALE = 0.22
SCALE_OF_SCORES = 0.015625
ROPE_BASE = 10000.0
NEGATIVE_HUGE = -1e30
HIGHEST_DOT = lax.Precision.HIGHEST
VMEM_LIMIT = 60 * 1024 * 1024

PLANE = ("b", "y", "c")
SEQ = ("a", "b")
ALL = ("a", "b", "y", "c")
SWAP = [(0, 1), (1, 0)]

f32 = jnp.float32
bf16 = jnp.bfloat16


def rotation_tables(positions):
    half = HEAD_SIZE // 2
    freq = jnp.power(ROPE_BASE, -2.0 * jnp.arange(half, dtype=f32) / HEAD_SIZE)
    angle = positions.astype(f32)[:, None] * freq[None, :]
    return jnp.cos(angle), jnp.sin(angle)


def rms_back(values, gain, grad_norm):
    mean_square = jnp.mean(values * values, axis=-1, keepdims=True)
    inverse = lax.rsqrt(mean_square + NORM_EPS)
    scaled_grad = grad_norm * gain
    grad_values = inverse * scaled_grad - values * inverse**3 * jnp.mean(
        values * scaled_grad, axis=-1, keepdims=True
    )
    grad_gain = jnp.sum(grad_norm * values * inverse, axis=0)
    return (grad_values, grad_gain)


def rms_scale(values, gain):
    mean_square = jnp.mean(values * values, axis=-1, keepdims=True)
    return values * lax.rsqrt(mean_square + NORM_EPS) * gain


def contract_rows(left_side, right_side):
    return lax.dot_general(
        left_side, right_side, (((0,), (0,)), ((), ())), preferred_element_type=f32
    )


def contract_cols(left_side, right_side):
    return lax.dot_general(
        left_side, right_side, (((1,), (1,)), ((), ())), preferred_element_type=f32
    )


def gather(x, axes):
    return lax.all_gather(x, axes, axis=0, tiled=True)


def scatter_sum(x, axes):
    return lax.psum_scatter(x, axes, scatter_dimension=0, tiled=True)


def pad_lanes(x, lanes):
    return jnp.pad(x, ((0, 0), (0, lanes - x.shape[1])))


def line_pairs(n, step):
    return [(i, i + step) for i in range(n) if 0 <= i + step < n]


def grid_gather(x):
    n = lax.axis_size("a")

    def cross(block, ends):
        return lax.ppermute(
            block, SEQ, [(2 * i + j, 2 * i + 1 - j) for i in range(n) if ends(i) for j in (0, 1)]
        )

    pieces = [(0, 0, x), (0, 1, cross(x, lambda i: True))]
    up = down = x
    for k in range(1, n):
        up = lax.ppermute(up, "a", line_pairs(n, 1))
        down = lax.ppermute(down, "a", line_pairs(n, -1))
        pieces += [(-k, 0, up), (-k, 1, cross(up, lambda i: i >= k))]
        pieces += [(k, 0, down), (k, 1, cross(down, lambda i: i + k < n))]
    return pieces


def plane_gather(x):
    swap = SWAP
    half = x.shape[0] // 2
    from_y = lax.ppermute(x, "y", SWAP)
    from_b = lax.ppermute(x, "b", SWAP)
    upper = lax.ppermute(from_b[:half], "y", SWAP)
    lower = lax.ppermute(from_y[half:], "b", SWAP)
    return [
        (block, lax.ppermute(block, "c", SWAP)) for block in (x, from_y, from_b, upper, lower)
    ]


def quarter(v, b, y):
    return lax.dynamic_index_in_dim(lax.dynamic_index_in_dim(v, b, 0, False), y, 0, False)


def halve_add(terms):
    own, other = terms
    return (own.astype(f32) + other.astype(f32)).astype(own.dtype)


def rotate_lanes(x, cos, sin):
    width = x.shape[-1]
    lane = lax.broadcasted_iota(jnp.int32, x.shape, x.ndim - 1)
    swapped = jnp.where(
        lane % HEAD_SIZE < HEAD_SIZE // 2,
        pltpu.roll(x, width - HEAD_SIZE // 2, x.ndim - 1),
        pltpu.roll(x, HEAD_SIZE // 2, x.ndim - 1),
    )
    return x * cos + swapped * sin


def spread_tables(cos, sin):
    return jnp.concatenate([cos] * 4, axis=1), jnp.concatenate([-sin, sin, -sin, sin], axis=1)


def key_tables(cos, sin):
    low = lower_lanes(cos.shape)
    return jnp.where(low, cos, 1.0), jnp.where(low, sin, 0.0)


def project_kernel(places, place_ref, *refs):
    count = 1 if places is None else len(places)
    blocks, refs = refs[:count], refs[count:]
    small_ref, w_ref, cos_ref, sin_ref, qkv_ref, normed_ref, x_ref = refs[:7]
    wide_cos_ref, wide_sin_ref, gain, held, sems = refs[7:]
    i = pl.program_id(0)
    slots = held.shape[0]

    @pl.when(i == 0)
    def _():
        if places is None:
            for slot in range(slots):
                pltpu.make_async_copy(blocks[0].at[slot], held.at[slot], sems.at[slot]).start()
        else:
            for (distance, crossed), block in zip(places, blocks):
                at = place_ref[1] + distance
                member = 1 - place_ref[2] if crossed else place_ref[2]

                @pl.when((at >= 0) & (at < slots // 2))
                def _(block=block, slot=2 * at + member):
                    pltpu.make_async_copy(block, held.at[slot], sems.at[slot]).start()

        gain[...] = jnp.transpose(small_ref[...].astype(f32))[E : E + 8, :]

    arrived = blocks[0].at[0] if places is None else blocks[0]
    pltpu.make_async_copy(arrived, held.at[i], sems.at[i]).wait()
    x = held[i]
    x_ref[...] = x
    normed = rms_scale(x.astype(f32), gain[0:1, :]).astype(bf16)
    normed_ref[...] = normed
    pre = jnp.dot(normed, w_ref[...], preferred_element_type=f32)
    cos, sin = spread_tables(cos_ref[...], sin_ref[...])
    wide_cos_ref[...] = cos
    wide_sin_ref[...] = sin
    qkv_ref[:, :PAIR] = rotate_lanes(pre[:, :PAIR], cos, sin).astype(bf16)
    qkv_ref[:, PAIR:] = rotate_lanes(pre[:, PAIR:], *key_tables(cos, sin)).astype(bf16)


def project(place, places, blocks, rows, packed, cos, sin):
    width = packed.shape[0]
    small_at = packed.shape[1] // LANES - 1
    span = cos.shape[0]
    table = pl.BlockSpec((rows, HEAD_SIZE // 2), lambda i, h: (i, 0))
    token_rows = pl.BlockSpec((rows, width), lambda i, h: (i, 0))
    return pl.pallas_call(
        functools.partial(project_kernel, places),
        grid_spec=pltpu.PrefetchScalarGridSpec(
            num_scalar_prefetch=1,
            grid=(span // rows,),
            in_specs=[pl.BlockSpec(memory_space=pl.ANY)] * len(blocks)
            + [
                pl.BlockSpec((width, LANES), lambda i, h: (0, small_at)),
                pl.BlockSpec((width, HEAD_PACK), lambda i, h: (0, h[0])),
                table,
                table,
            ],
            out_specs=[
                pl.BlockSpec((rows, HEAD_PACK), lambda i, h: (i, 0)),
                token_rows,
                token_rows,
                pl.BlockSpec((rows, PAIR), lambda i, h: (i, 0)),
                pl.BlockSpec((rows, PAIR), lambda i, h: (i, 0)),
            ],
            scratch_shapes=[
                pltpu.VMEM((8, width), f32),
                pltpu.VMEM((span // rows, rows, width), bf16),
                pltpu.SemaphoreType.DMA((span // rows,)),
            ],
        ),
        out_shape=[
            jax.ShapeDtypeStruct((span, HEAD_PACK), bf16),
            jax.ShapeDtypeStruct((span, width), bf16),
            jax.ShapeDtypeStruct((span, width), bf16),
            jax.ShapeDtypeStruct((span, PAIR), f32),
            jax.ShapeDtypeStruct((span, PAIR), f32),
        ],
        compiler_params=pltpu.CompilerParams(vmem_limit_bytes=VMEM_LIMIT),
        cost_estimate=pl.CostEstimate(
            flops=2 * span * width * HEAD_PACK, bytes_accessed=18 * 2**20, transcendentals=0
        ),
        name="project",
    )(place, *blocks, packed, packed, cos, sin)


def head_grads_kernel(head_ref, x_ref, normed_ref, w_ref, grad_ref, out_ref, acc, gain):
    i = pl.program_id(0)

    @pl.when(i == 0)
    def _():
        acc[...] = jnp.zeros_like(acc)
        gain[...] = jnp.zeros_like(gain)

    grad = grad_ref[...]
    acc[...] += contract_rows(grad, normed_ref[...])
    x = x_ref[...].astype(f32)
    inverse = lax.rsqrt(jnp.mean(x * x, axis=-1, keepdims=True) + NORM_EPS)
    back = contract_cols(grad, w_ref[...]) * (x * inverse)
    gain[...] += jnp.sum(back.reshape(back.shape[0] // 8, 8, back.shape[1]), axis=0)

    @pl.when(i == pl.num_programs(0) - 1)
    def _():
        out_ref[:, :HEAD_PACK] = jnp.transpose(acc[...]).astype(bf16)
        total = jnp.sum(gain[...], axis=0, keepdims=True)
        rows = lax.broadcasted_iota(jnp.int32, (LANES, total.shape[1]), 0)
        out_ref[:, HEAD_PACK:] = jnp.transpose(
            jnp.where(rows == 0, jnp.broadcast_to(total, rows.shape), 0.0)
        ).astype(bf16)


def head_grads(head, x, normed, packed, grads):
    span, width = x.shape
    rows = 2 * BLOCK
    token_rows = pl.BlockSpec((rows, width), lambda i, h: (i, 0))
    return pl.pallas_call(
        head_grads_kernel,
        grid_spec=pltpu.PrefetchScalarGridSpec(
            num_scalar_prefetch=1,
            grid=(span // rows,),
            in_specs=[
                token_rows,
                token_rows,
                pl.BlockSpec((width, HEAD_PACK), lambda i, h: (0, h[0])),
                pl.BlockSpec((rows, HEAD_PACK), lambda i, h: (i, 0)),
            ],
            out_specs=pl.BlockSpec((width, HEAD_PACK + LANES), lambda i, h: (0, 0)),
            scratch_shapes=[pltpu.VMEM((HEAD_PACK, width), f32), pltpu.VMEM((8, width), f32)],
        ),
        out_shape=jax.ShapeDtypeStruct((width, HEAD_PACK + LANES), bf16),
        compiler_params=pltpu.CompilerParams(vmem_limit_bytes=VMEM_LIMIT),
        cost_estimate=pl.CostEstimate(
            flops=4 * span * width * HEAD_PACK, bytes_accessed=12 * 2**20, transcendentals=0
        ),
        name="head_grads",
    )(head, x, normed, packed, grads)


def lower_lanes(shape):
    return lax.broadcasted_iota(jnp.int32, shape, len(shape) - 1) < HEAD_SIZE


def both_heads_low(pair):
    low = lower_lanes(pair.shape)
    return jnp.concatenate(
        [jnp.where(low, pair, 0.0), jnp.where(low, pltpu.roll(pair, HEAD_SIZE, 1), 0.0)], axis=0
    )


def both_heads_high(pair):
    low = lower_lanes(pair.shape)
    return jnp.concatenate(
        [jnp.where(low, 0.0, pltpu.roll(pair, HEAD_SIZE, 1)), jnp.where(low, 0.0, pair)], axis=0
    )


def block_bounds(bounds_ref):
    i, steps = pl.program_id(0), pl.num_programs(0)
    query_start = (i + bounds_ref[2 * steps]) * QUERY_BLOCK
    diagonal = query_start // BLOCK
    full = jnp.minimum(bounds_ref[steps + i], diagonal)
    return query_start, bounds_ref[i], full, diagonal, diagonal + QUERY_BLOCK // BLOCK


def pair_mask(doc, query_start):
    doc = jnp.concatenate([doc, doc], axis=1)
    queries = lax.broadcasted_iota(jnp.int32, doc.shape, 1) % QUERY_BLOCK + query_start

    def masked(scores, start):
        keys = lax.broadcasted_iota(jnp.int32, scores.shape, 0) + start
        return jnp.where((keys >= doc) & (keys <= queries), scores, NEGATIVE_HUGE)

    return masked


def attend_kernel(bounds_ref, q_ref, kv_ref, doc_ref, o_ref, low_ref, lse_ref, acc):
    query_start, first, full, diagonal, end = block_bounds(bounds_ref)
    q = both_heads_low(q_ref[...].astype(f32) * SCALE_OF_SCORES).astype(bf16)
    masked = pair_mask(doc_ref[0], query_start)
    acc[...] = jnp.zeros_like(acc)

    def step(mask, j, carried):
        top, total = carried
        start = pl.multiple_of(j * BLOCK, BLOCK)
        kv = kv_ref[pl.ds(start, BLOCK), :]
        scores = contract_cols(kv, q)
        if mask:
            scores = masked(scores, start)
        new = jnp.maximum(top, jnp.max(scores, axis=0, keepdims=True))
        probs = jnp.exp(scores - new)
        keep = jnp.exp(top - new)
        acc[...] = acc[...] * keep + contract_rows(kv, probs.astype(bf16))
        return new, total * keep + jnp.sum(probs, axis=0, keepdims=True)

    row = (1, 2 * QUERY_BLOCK)
    carried = (jnp.full(row, NEGATIVE_HUGE, f32), jnp.zeros(row, f32))
    carried = lax.fori_loop(first, full, functools.partial(step, True), carried)
    carried = lax.fori_loop(full, diagonal, functools.partial(step, False), carried)
    top, total = lax.fori_loop(diagonal, end, functools.partial(step, True), carried)
    mixed = jnp.transpose(acc[...] / total)
    one, two = mixed[:QUERY_BLOCK], mixed[QUERY_BLOCK:]
    out = jnp.where(lower_lanes(one.shape), pltpu.roll(one, HEAD_SIZE, 1), two)
    o_ref[...] = out
    low_ref[...] = out.astype(bf16)
    lse_ref[0] = top + jnp.log(total)


def attention_specs(kv_at, keys):
    pair = pl.BlockSpec((QUERY_BLOCK, PAIR), lambda i, s: (i, 0))
    return (
        pair,
        pl.BlockSpec((keys, PAIR), lambda i, s: (0, kv_at)),
        pl.BlockSpec((1, 1, QUERY_BLOCK), lambda i, s: (i, 0, 0)),
        pl.BlockSpec((1, 1, 2 * QUERY_BLOCK), lambda i, s: (i, 0, 0)),
    )


def attend(bounds, qkv, kv, kv_at, doc):
    queries, keys = qkv.shape[0], kv.shape[0]
    steps = queries // QUERY_BLOCK
    pair, whole, doc_row, lse_row = attention_specs(kv_at, keys)
    return pl.pallas_call(
        attend_kernel,
        grid_spec=pltpu.PrefetchScalarGridSpec(
            num_scalar_prefetch=1,
            grid=(steps,),
            in_specs=[pair, whole, doc_row],
            out_specs=[pair, pair, lse_row],
            scratch_shapes=[pltpu.VMEM((PAIR, 2 * QUERY_BLOCK), f32)],
        ),
        out_shape=[
            jax.ShapeDtypeStruct((queries, PAIR), f32),
            jax.ShapeDtypeStruct((queries, PAIR), bf16),
            jax.ShapeDtypeStruct((steps, 1, 2 * QUERY_BLOCK), f32),
        ],
        compiler_params=pltpu.CompilerParams(vmem_limit_bytes=VMEM_LIMIT),
        cost_estimate=pl.CostEstimate(
            flops=4 * queries * keys * PAIR, bytes_accessed=6 * 2**20, transcendentals=queries * keys
        ),
        name="attend",
    )(bounds, qkv, kv, doc)


def attend_back_kernel(
    fold, bounds_ref, q_ref, kv_ref, doc_ref, do_ref, o_ref, lse_ref, cos_ref, sin_ref, *refs
):
    if fold:
        out_ref, acc, dkv_ref = refs
    else:
        dq_ref, dkv_ref, acc = refs
    i = pl.program_id(0)
    query_start, first, full, diagonal, end = block_bounds(bounds_ref)

    @pl.when(i == 0)
    def _():
        dkv_ref[...] = jnp.zeros_like(dkv_ref)

    q = both_heads_low(q_ref[...].astype(f32) * SCALE_OF_SCORES).astype(bf16)
    grad = do_ref[...].astype(f32)
    product = jnp.transpose(grad * o_ref[...])
    delta = jnp.concatenate(
        [
            jnp.sum(product[:HEAD_SIZE], axis=0, keepdims=True),
            jnp.sum(product[HEAD_SIZE:], axis=0, keepdims=True),
        ],
        axis=1,
    )
    grad = both_heads_high(grad).astype(bf16)
    sources = jnp.concatenate([q, grad], axis=0)
    masked = pair_mask(doc_ref[0], query_start)
    lse = lse_ref[0]
    acc[...] = jnp.zeros_like(acc)

    def step(mask, j, carried):
        start = pl.multiple_of(j * BLOCK, BLOCK)
        kv = kv_ref[pl.ds(start, BLOCK), :]
        scores = contract_cols(kv, q) - lse
        if mask:
            scores = masked(scores, start)
        probs = jnp.exp(scores)
        grad_scores = (probs * (contract_cols(kv, grad) - delta)).astype(bf16)
        acc[...] += contract_rows(kv, grad_scores)
        both = jnp.concatenate([grad_scores, probs.astype(bf16)], axis=1)
        dkv_ref[pl.ds(start, BLOCK), :] += jnp.dot(both, sources, preferred_element_type=f32)
        return carried

    lax.fori_loop(first, full, functools.partial(step, True), 0)
    lax.fori_loop(full, diagonal, functools.partial(step, False), 0)
    lax.fori_loop(diagonal, end, functools.partial(step, True), 0)
    dq = jnp.transpose(acc[...])
    one, two = dq[:QUERY_BLOCK], dq[QUERY_BLOCK:]
    dq = jnp.where(lower_lanes(one.shape), one, pltpu.roll(two, HEAD_SIZE, 1))
    if not fold:
        dq_ref[...] = dq
        return
    mine = pl.ds(pl.multiple_of(i * QUERY_BLOCK, QUERY_BLOCK), QUERY_BLOCK)
    out_ref[mine, :PAIR] = rotate_lanes(
        dq * SCALE_OF_SCORES, cos_ref[mine, :], -sin_ref[mine, :]
    ).astype(bf16)

    @pl.when(i == pl.num_programs(0) - 1)
    def _():
        def finish(j, carried):
            part = pl.ds(pl.multiple_of(j * BLOCK, BLOCK), BLOCK)
            cos, sin = key_tables(cos_ref[part, :], sin_ref[part, :])
            out_ref[part, PAIR:] = rotate_lanes(dkv_ref[part, :], cos, -sin).astype(bf16)
            return carried

        lax.fori_loop(0, dkv_ref.shape[0] // BLOCK, finish, 0)


def attend_back(bounds, qkv, kv, kv_at, doc, grad, out, lse, cos, sin, fold):
    queries, keys = qkv.shape[0], kv.shape[0]
    steps = queries // QUERY_BLOCK
    pair, whole, doc_row, lse_row = attention_specs(kv_at, keys)
    table = pl.BlockSpec(cos.shape, lambda i, s: (0, 0))
    acc = pltpu.VMEM((PAIR, 2 * QUERY_BLOCK), f32)
    if fold:
        out_specs = pl.BlockSpec((queries, HEAD_PACK), lambda i, s: (0, 0))
        out_shape = jax.ShapeDtypeStruct((queries, HEAD_PACK), bf16)
        scratch = [acc, pltpu.VMEM((keys, PAIR), f32)]
    else:
        out_specs = [pair, pl.BlockSpec((keys, PAIR), lambda i, s: (0, 0))]
        out_shape = [
            jax.ShapeDtypeStruct((queries, PAIR), f32),
            jax.ShapeDtypeStruct((keys, PAIR), f32),
        ]
        scratch = [acc]
    return pl.pallas_call(
        functools.partial(attend_back_kernel, fold),
        grid_spec=pltpu.PrefetchScalarGridSpec(
            num_scalar_prefetch=1,
            grid=(steps,),
            in_specs=[pair, whole, doc_row, pair, pair, lse_row, table, table],
            out_specs=out_specs,
            scratch_shapes=scratch,
        ),
        out_shape=out_shape,
        compiler_params=pltpu.CompilerParams(vmem_limit_bytes=VMEM_LIMIT),
        cost_estimate=pl.CostEstimate(
            flops=10 * queries * keys * PAIR,
            bytes_accessed=8 * 2**20,
            transcendentals=queries * keys,
        ),
        name="attend_back",
    )(bounds, qkv, kv, doc, grad, out, lse, cos, sin)


def unrotate_kernel(dq_ref, dkv_ref, cos_ref, sin_ref, out_ref):
    cos, sin = cos_ref[...], sin_ref[...]
    dq = rotate_lanes(dq_ref[...] * SCALE_OF_SCORES, cos, -sin)
    cos, sin = key_tables(cos, sin)
    dkv = rotate_lanes(dkv_ref[...], cos, -sin)
    out_ref[...] = jnp.concatenate([dq, dkv], axis=1).astype(bf16)


def unrotate(dq, dkv, cos, sin):
    rows = dq.shape[0]
    pair = pl.BlockSpec((BLOCK, PAIR), lambda i: (i, 0))
    return pl.pallas_call(
        unrotate_kernel,
        grid=(rows // BLOCK,),
        in_specs=[pair, pair, pair, pair],
        out_specs=pl.BlockSpec((BLOCK, HEAD_PACK), lambda i: (i, 0)),
        out_shape=jax.ShapeDtypeStruct((rows, HEAD_PACK), bf16),
        cost_estimate=pl.CostEstimate(
            flops=rows * HEAD_PACK * 8, bytes_accessed=rows * HEAD_PACK * 14, transcendentals=0
        ),
        name="unrotate",
    )(dq, dkv, cos, sin)


def place_experts_kernel(place_ref, *refs):
    blocks, (ct_ref, w_ref, z_ref, sems) = refs[:10], refs[10:]
    core = place_ref[1]
    rows = w_ref.shape[1] // 2
    half = rows // 2
    sources = [[(0, 0, rows)], [(1, 0, rows)], [(2, 0, rows)], [(3, 0, half), (4, half, half)]]
    for step, parts in enumerate(sources):

        @pl.when(pl.program_id(0) == step)
        def _(parts=parts):
            copies = []
            for source, start, length in parts:
                for other in (0, 1):
                    first = jnp.where(core == other, 0, rows) + start
                    at = pl.ds(pl.multiple_of(first, half), length)
                    copies.append(
                        pltpu.make_async_copy(
                            blocks[2 * source + other], w_ref.at[0, at, :], sems.at[len(copies)]
                        )
                    )
            for copy in copies:
                copy.start()
            for copy in copies:
                copy.wait()

    z_ref[0] = jnp.dot(ct_ref[...], w_ref[0, :, 2 * F :], preferred_element_type=f32)


def place_experts(place, parts, early, width):
    rows = early.shape[0]
    blocks = [block for pair in parts for block in pair]
    return pl.pallas_call(
        place_experts_kernel,
        grid_spec=pltpu.PrefetchScalarGridSpec(
            num_scalar_prefetch=1,
            grid=(EXPERTS_HERE,),
            in_specs=[pl.BlockSpec(memory_space=pl.ANY)] * len(blocks)
            + [pl.BlockSpec((rows, width), lambda r, s: (0, 0))],
            out_specs=[
                pl.BlockSpec((1, width, 3 * F), lambda r, s: (s[0] ^ r, 0, 0)),
                pl.BlockSpec((1, rows, F), lambda r, s: (s[0] ^ r, 0, 0)),
            ],
            scratch_shapes=[pltpu.SemaphoreType.DMA((4,))],
        ),
        out_shape=[
            jax.ShapeDtypeStruct((EXPERTS_HERE, width, 3 * F), bf16),
            jax.ShapeDtypeStruct((EXPERTS_HERE, rows, F), f32),
        ],
        compiler_params=pltpu.CompilerParams(vmem_limit_bytes=VMEM_LIMIT),
        cost_estimate=pl.CostEstimate(
            flops=2 * EXPERTS_HERE * rows * width * F, bytes_accessed=36 * 2**20, transcendentals=0
        ),
        name="place_experts",
    )(place, *blocks, early)


def lane_column(x, at):
    lane = lax.broadcasted_iota(jnp.int32, x.shape, 1)
    return jnp.sum(jnp.where(lane == at, x, 0.0), axis=1, keepdims=True)


def experts_kernel(
    group_ref, n_ref, routed_ref, router_ref, w_ref, z_ref,
    back_ref, gates_ref, hidden_ref, pre_ref, acc, dots,
):
    e = pl.program_id(0)
    own = group_ref[0] * EXPERTS_HERE + e
    rows = n_ref.shape[0]

    @pl.when(e == 0)
    def _():
        logits = jnp.dot(n_ref[...], router_ref[...], preferred_element_type=f32)
        routed = routed_ref[...].astype(f32) > 0.5
        highest = jnp.max(jnp.where(routed, logits, NEGATIVE_HUGE), axis=1, keepdims=True)
        weights = jnp.where(routed, jnp.exp(jnp.where(routed, logits - highest, 0.0)), 0.0)
        gates_ref[...] = weights / jnp.sum(weights, axis=1, keepdims=True)
        acc[...] = jnp.zeros_like(acc)
        dots[...] = jnp.zeros_like(dots)

    w_in = w_ref[0, :, : 2 * F]
    for t in range(rows // BLOCK):
        part = pl.ds(t * BLOCK, BLOCK)
        pre = jnp.dot(n_ref[part, :], w_in, preferred_element_type=f32)
        gate, up = pre[:, :F], pre[:, F:]
        z = z_ref[0, part, :]
        weight = lane_column(gates_ref[part, :], own)
        sig = 1.0 / (1.0 + jnp.exp(-gate))
        act = gate * sig
        hidden = act * up
        hidden_ref[0, part, :] = (weight * hidden).astype(bf16)
        dot = RESIDUAL_SCALE * jnp.sum(hidden.astype(bf16).astype(f32) * z, axis=1, keepdims=True)
        lane = lax.broadcasted_iota(jnp.int32, (BLOCK, LANES), 1)
        dots[part, :] += jnp.where(lane == own, dot, 0.0)
        scaled = (RESIDUAL_SCALE * weight) * z
        pre_ref[0, part, :F] = (scaled * up * (sig + act * (1.0 - sig))).astype(bf16)
        pre_ref[0, part, F:] = (scaled * act).astype(bf16)
        acc[part, :] += contract_cols(pre_ref[0, part, :], w_in)

    @pl.when(e == EXPERTS_HERE - 1)
    def _():
        width = n_ref.shape[1]
        back_ref[:, :width] = acc[...].astype(bf16)
        high = dots[...].astype(bf16)
        low = dots[...] - high.astype(f32)
        back_ref[:, width:] = (high.astype(f32) + pltpu.roll(low, E, 1)).astype(bf16)


def experts(group, normed, early, packed, w_all, z):
    rows, width = normed.shape
    count = w_all.shape[0]
    whole = pl.BlockSpec((rows, width), lambda e, g: (0, 0))
    column = width // LANES
    router_at = packed.shape[1] // LANES - 1
    return pl.pallas_call(
        experts_kernel,
        grid_spec=pltpu.PrefetchScalarGridSpec(
            num_scalar_prefetch=1,
            grid=(count,),
            in_specs=[
                whole,
                pl.BlockSpec((rows, LANES), lambda e, g: (0, column)),
                pl.BlockSpec((width, LANES), lambda e, g: (0, router_at)),
                pl.BlockSpec((1, width, 3 * F), lambda e, g: (e, 0, 0)),
                pl.BlockSpec((1, rows, F), lambda e, g: (e, 0, 0)),
            ],
            out_specs=[
                pl.BlockSpec((rows, width + LANES), lambda e, g: (0, 0)),
                pl.BlockSpec((rows, LANES), lambda e, g: (0, 0)),
                pl.BlockSpec((1, rows, F), lambda e, g: (e, 0, 0)),
                pl.BlockSpec((1, rows, 2 * F), lambda e, g: (e, 0, 0)),
            ],
            scratch_shapes=[pltpu.VMEM((rows, width), f32), pltpu.VMEM((rows, LANES), f32)],
        ),
        out_shape=[
            jax.ShapeDtypeStruct((rows, width + LANES), bf16),
            jax.ShapeDtypeStruct((rows, LANES), f32),
            jax.ShapeDtypeStruct((count, rows, F), bf16),
            jax.ShapeDtypeStruct((count, rows, 2 * F), bf16),
        ],
        compiler_params=pltpu.CompilerParams(vmem_limit_bytes=VMEM_LIMIT),
        cost_estimate=pl.CostEstimate(
            flops=2 * count * rows * width * 4 * F, bytes_accessed=40 * 2**20, transcendentals=0
        ),
        name="experts",
    )(group, normed, early, packed, w_all, z)


def expert_grads_kernel(with_y, half_ref, n_ref, ct_ref, w_ref, hidden_ref, pre_ref, *refs):
    if with_y:
        left_ref, right_ref, y_ref, n_t, ct_t, acc = refs
    else:
        left_ref, right_ref, n_t, ct_t = refs
    e = pl.program_id(0)
    cut = left_ref.shape[2]

    @pl.when(e == 0)
    def _():
        n_t[...] = jnp.transpose(n_ref[...])
        ct_t[...] = jnp.transpose(ct_ref[...])
        if with_y:
            acc[...] = jnp.zeros_like(acc)

    grads = jnp.dot(n_t[...], pre_ref[0], preferred_element_type=f32).astype(bf16)
    left_ref[0] = grads[:, :cut]
    right_ref[0, :, : 2 * F - cut] = grads[:, cut:]
    right_ref[0, :, 2 * F - cut :] = (
        RESIDUAL_SCALE * jnp.dot(ct_t[...], hidden_ref[0], preferred_element_type=f32)
    ).astype(bf16)
    if not with_y:
        return
    acc[...] += contract_cols(hidden_ref[0], w_ref[0, :, 2 * F :])

    @pl.when(e == pl.num_programs(0) - 1)
    def _():
        y_ref[...] = acc[...].astype(bf16)


def expert_grads(half, halves, normed, early, w_all, hidden, pre, with_y):
    rows, width = normed.shape
    count = w_all.shape[0]
    own, cut = width // halves, 3 * F // 2
    feature = pl.BlockSpec((rows, own), lambda e, h: (0, h[0]))
    out_specs = [pl.BlockSpec((1, own, cut), lambda e, h: (e, 0, 0))] * 2
    out_shape = [jax.ShapeDtypeStruct((count, own, cut), bf16)] * 2
    scratch = [pltpu.VMEM((own, rows), bf16), pltpu.VMEM((own, rows), bf16)]
    if with_y:
        out_specs.append(pl.BlockSpec((rows, width), lambda e, h: (0, 0)))
        out_shape.append(jax.ShapeDtypeStruct((rows, width), bf16))
        scratch.append(pltpu.VMEM((rows, width), f32))
    return pl.pallas_call(
        functools.partial(expert_grads_kernel, with_y),
        grid_spec=pltpu.PrefetchScalarGridSpec(
            num_scalar_prefetch=1,
            grid=(count,),
            in_specs=[
                feature,
                feature,
                pl.BlockSpec((1, width, 3 * F), lambda e, h: (e, 0, 0)),
                pl.BlockSpec((1, rows, F), lambda e, h: (e, 0, 0)),
                pl.BlockSpec((1, rows, 2 * F), lambda e, h: (e, 0, 0)),
            ],
            out_specs=out_specs,
            scratch_shapes=scratch,
        ),
        out_shape=out_shape,
        compiler_params=pltpu.CompilerParams(vmem_limit_bytes=VMEM_LIMIT),
        cost_estimate=pl.CostEstimate(
            flops=2 * count * rows * width * 3 * F // halves + 2 * with_y * count * rows * width * F,
            bytes_accessed=30 * 2**20,
            transcendentals=0,
        ),
        name="expert_grads",
    )(half, normed, early, w_all, hidden, pre)


def join_kernel(place_ref, o_ref, w_ref, small_ref, x_ref, normed_ref, resid_ref, own_ref, gain):
    t = pl.program_id(0)
    b = place_ref[2]

    @pl.when(t == 0)
    def _():
        gain[...] = jnp.transpose(small_ref[...].astype(f32))[E : E + 8, :]

    pairs = []
    for a in range(o_ref.shape[0]):
        same, other = o_ref[a, 0, 0], o_ref[a, 1, 0]
        pairs.append(jnp.where(b == 0, same, other))
        pairs.append(jnp.where(b == 0, other, same))
    attended = jnp.concatenate(pairs, axis=1)
    resid = x_ref[...].astype(f32) + RESIDUAL_SCALE * jnp.dot(
        attended, w_ref[...], preferred_element_type=f32
    )
    normed_ref[...] = rms_scale(resid, gain[1:2, :]).astype(bf16)

    @pl.when(t == place_ref[1])
    def _():
        resid_ref[...] = resid
        own_ref[...] = attended


def join(place, outs, packed, weights_at, x):
    width = packed.shape[0]
    lines, _, _, rows, pair = outs.shape
    small_at = packed.shape[1] // LANES - 1
    own = pl.BlockSpec((rows, width), lambda t, s: (0, 0))
    return pl.pallas_call(
        join_kernel,
        grid_spec=pltpu.PrefetchScalarGridSpec(
            num_scalar_prefetch=1,
            grid=(lines,),
            in_specs=[
                pl.BlockSpec((lines, 2, 1, rows, pair), lambda t, s: (0, 0, t, 0, 0)),
                pl.BlockSpec((width, width), lambda t, s: (0, weights_at)),
                pl.BlockSpec((width, LANES), lambda t, s: (0, small_at)),
                pl.BlockSpec((rows, width), lambda t, s: (2 * t + s[2], 0)),
            ],
            out_specs=[pl.BlockSpec((rows, width), lambda t, s: (t, 0)), own, own],
            scratch_shapes=[pltpu.VMEM((8, width), f32)],
        ),
        out_shape=[
            jax.ShapeDtypeStruct((lines * rows, width), bf16),
            jax.ShapeDtypeStruct((rows, width), f32),
            jax.ShapeDtypeStruct((rows, width), bf16),
        ],
        compiler_params=pltpu.CompilerParams(vmem_limit_bytes=VMEM_LIMIT),
        cost_estimate=pl.CostEstimate(
            flops=2 * lines * rows * width * width, bytes_accessed=12 * 2**20, transcendentals=0
        ),
        name="join",
    )(place, outs, packed, packed, x)


def weight_sums_kernel(sums_ref, q_ref, k_ref, v_ref, gain_ref):
    groups, heads, members = sums_ref.shape[:3]
    gain = jnp.zeros(gain_ref.shape, f32)
    values = []
    for h in range(heads):
        total = jnp.zeros(sums_ref.shape[3:], f32)
        for g in range(groups):
            for member in range(members):
                total += sums_ref[g, h, member].astype(f32)
        values.append(total)
        gain += total[:, HEAD_PACK:]
        q_ref[:, h * PAIR : (h + 1) * PAIR] = total[:, :PAIR]
    gain_ref[...] = gain
    for h in range(0, heads, 2):
        one, two = values[h][:, PAIR:HEAD_PACK], values[h + 1][:, PAIR:HEAD_PACK]
        low = lower_lanes(one.shape)
        at = slice(h // 2 * PAIR, (h // 2 + 1) * PAIR)
        k_ref[:, at] = jnp.where(low, one, pltpu.roll(two, HEAD_SIZE, 1))
        v_ref[:, at] = jnp.where(low, pltpu.roll(one, HEAD_SIZE, 1), two)


def weight_sums(sums):
    rows, heads = sums.shape[3], sums.shape[1]
    return pl.pallas_call(
        weight_sums_kernel,
        out_shape=[
            jax.ShapeDtypeStruct((rows, heads * PAIR), f32),
            jax.ShapeDtypeStruct((rows, heads * HEAD_SIZE), f32),
            jax.ShapeDtypeStruct((rows, heads * HEAD_SIZE), f32),
            jax.ShapeDtypeStruct((rows, LANES), f32),
        ],
        compiler_params=pltpu.CompilerParams(vmem_limit_bytes=VMEM_LIMIT),
        cost_estimate=pl.CostEstimate(flops=2**20, bytes_accessed=2 * 2**20, transcendentals=0),
        name="weight_sums",
    )(sums)


def exchange(x, axes):
    return lax.all_to_all(x, axes, 0, 0, tiled=True)


def body(
    tokens,
    cotangent,
    segment_ids,
    routes,
    norm_attn,
    w_query,
    key_weight_matrix,
    value_weight_matrix,
    w_output,
    norm_moe,
    w_router,
    expert_in,
    expert_out,
):
    x_local = tokens[0].astype(f32)
    token_count, width = x_local.shape
    seg_row = segment_ids[0]
    group = lax.axis_index("a")
    head_axes = SEQ if lax.axis_size(SEQ) == KEY_VALUE_HEADS else ("b",)
    whole_rows = head_axes == SEQ
    span = token_count * KEY_VALUE_HEADS
    span_start = 0 if whole_rows else group * span

    def start_of_doc(ids):
        return jnp.sum((seg_row[None, :] < ids[:, None]).astype(jnp.int32), axis=1)

    seg_span = lax.dynamic_slice_in_dim(seg_row, span_start, span)
    doc_span = start_of_doc(seg_span)
    cos_span, sin_span = rotation_tables(
        span_start + jnp.arange(span, dtype=jnp.int32) - doc_span
    )
    by_block = doc_span.reshape(-1, QUERY_BLOCK)
    bounds = jnp.concatenate(
        [
            by_block[:, 0] // BLOCK,
            (by_block[:, -1] + BLOCK - 1) // BLOCK,
            jnp.full((1,), span_start // QUERY_BLOCK, jnp.int32),
        ]
    )
    doc_rows = by_block[:, None, :]

    own_rows = w_query.shape[0]
    by_head = jnp.concatenate(
        [
            w_query.astype(bf16).reshape(own_rows, KEY_VALUE_HEADS, PAIR),
            key_weight_matrix.astype(bf16).reshape(own_rows, KEY_VALUE_HEADS, HEAD_SIZE),
            value_weight_matrix.astype(bf16).reshape(own_rows, KEY_VALUE_HEADS, HEAD_SIZE),
        ],
        axis=2,
    ).reshape(own_rows, KEY_VALUE_HEADS * HEAD_PACK)
    qkv_width = KEY_VALUE_HEADS * HEAD_PACK
    first_all = gather(
        jnp.concatenate(
            [
                by_head,
                w_output.astype(bf16),
                pad_lanes(
                    jnp.concatenate(
                        [
                            w_router.astype(bf16),
                            norm_attn.astype(bf16)[:, None],
                            norm_moe.astype(bf16)[:, None],
                        ],
                        axis=1,
                    ),
                    LANES,
                ),
            ],
            axis=1,
        ),
        ALL,
    )
    experts_low = jnp.concatenate([expert_in.astype(bf16), expert_out.astype(bf16)], axis=1)
    if whole_rows:
        pieces = grid_gather(tokens[0])
        places = [piece[:2] for piece in pieces]
        blocks = tuple(piece[2] for piece in pieces)
    else:
        places = None
        blocks = (gather(tokens[0], "b").reshape((-1,) + tokens.shape[1:]),)
    first_all, experts_low, blocks, cos_span, sin_span, bounds, doc_rows = (
        lax.optimization_barrier(
            (first_all, experts_low, blocks, cos_span, sin_span, bounds, doc_rows)
        )
    )
    output_w = first_all[:, qkv_width : qkv_width + width]
    small_at = qkv_width + width
    router_w = first_all[:, small_at : small_at + E]
    gain_one_f = first_all[:, small_at + E].astype(f32)
    gain_two_f = first_all[:, small_at + E + 1].astype(f32)

    expert_ids = jnp.arange(E, dtype=jnp.int32)
    routed_own = jnp.any(routes[0][:, :, None] == expert_ids[None, None, :], axis=1)
    early = jnp.concatenate([cotangent[0], pad_lanes(routed_own.astype(bf16), LANES)], axis=1)
    early, first_all = lax.optimization_barrier((early, first_all))
    early_all = gather(early, "a")
    small_plane = lax.axis_size("b") == 2 and lax.axis_size("y") == 2
    if small_plane:
        parts = plane_gather(experts_low)
    else:
        parts = gather(experts_low, PLANE)

    place = jnp.stack([lax.axis_index(head_axes), group, lax.axis_index("b")])
    qkv, normed_span, x_span, wide_cos, wide_sin = project(
        place, places, blocks, token_count, first_all, cos_span, sin_span
    )
    if whole_rows:
        kv, kv_at = qkv, 1
    else:
        kv, kv_at = gather(qkv[:, PAIR:], "a"), 0
    attention_result, attended, log_total = attend(bounds, qkv, kv, kv_at, doc_rows)
    if small_plane:
        member = lax.axis_index("b")
        by_column = attended.reshape(GROUPS, 2, token_count, PAIR)
        other = lax.ppermute(
            lax.dynamic_index_in_dim(by_column, 1 - member, 1, False), "b", SWAP
        )
        own = lax.dynamic_index_in_dim(by_column, member, 1, False)
        pair, early_all = lax.optimization_barrier((jnp.stack([own, other]), early_all))
        outs = lax.all_gather(pair, "a", axis=0, tiled=False)
        normed_all, resid, attended_low = join(place, outs, first_all, qkv_width // width, x_span)
        normed_two = lax.dynamic_slice_in_dim(normed_all, group * token_count, token_count)
        home = jnp.stack([member * 2 + lax.axis_index("y"), lax.axis_index("c")])
        experts_all, grad_hidden = place_experts(home, parts, early_all, width)
    else:
        attended_low = (
            exchange(attended.reshape(KEY_VALUE_HEADS, token_count, PAIR), head_axes)
            .transpose(1, 0, 2)
            .reshape(token_count, QUERY_HEADS * HEAD_SIZE)
        )
        attn_out = jnp.dot(attended_low, output_w, preferred_element_type=f32)
        resid = x_local + RESIDUAL_SCALE * attn_out
        normed_two = rms_scale(resid, gain_two_f).astype(bf16)
        normed_all = gather(normed_two, "a")
        experts_all = parts.reshape(EXPERTS_HERE, width, 3 * F)
        grad_hidden = jnp.einsum(
            "td,edf->etf",
            early_all[:, :width],
            experts_all[:, :, 2 * F :],
            preferred_element_type=f32,
        )
    back_part, gates_all, gated_hidden, grad_pre = experts(
        group.reshape(1), normed_all, early_all, first_all, experts_all, grad_hidden
    )
    back_own = scatter_sum(back_part, "a").astype(f32)
    inputs = (normed_all, early_all, experts_all, gated_hidden, grad_pre)
    if small_plane:
        core = lax.axis_index("c")
        send = expert_grads((1 - core).reshape(1), 2, *inputs, False)
        arrived = [lax.ppermute(x, "c", SWAP) for x in send]
        *keep, moe_part = expert_grads(core.reshape(1), 2, *inputs, True)
        left, right = (
            halve_add(terms).reshape((2, 2) + terms[0].shape[1:]) for terms in zip(keep, arrived)
        )
        back_own, moe_part, left, right = lax.optimization_barrier(
            (back_own, moe_part, left, right)
        )
        b, y = lax.axis_index("b"), lax.axis_index("y")
        left_on = quarter(left, 1 - b, y), lax.ppermute(quarter(left, 1 - b, 1 - y), "y", SWAP)
        right_on = quarter(right, b, 1 - y), lax.ppermute(quarter(right, 1 - b, 1 - y), "b", SWAP)
    else:
        *grads, moe_part = expert_grads(jnp.zeros((1,), jnp.int32), 1, *inputs, True)
        grad_experts = jnp.concatenate(grads, axis=2)
        back_own, moe_part, grad_experts = lax.optimization_barrier(
            (back_own, moe_part, grad_experts)
        )
        grad_experts = scatter_sum(grad_experts.reshape(EXPERTS_HERE * width, 3 * F), PLANE)
    moe_sum = scatter_sum(moe_part, "a")

    grad_out = cotangent[0].astype(f32)
    gates = lax.dynamic_slice_in_dim(gates_all, group * token_count, token_count)[:, :E]
    gate_grads_own = back_own[:, width : width + E] + back_own[:, width + E : width + 2 * E]
    grad_logits = gates * (gate_grads_own - jnp.sum(gates * gate_grads_own, axis=-1, keepdims=True))
    grad_normed_two = back_own[:, :width] + jnp.dot(
        grad_logits, router_w.astype(f32).T, precision=HIGHEST_DOT
    )
    grad_router = jnp.dot(normed_two.astype(f32).T, grad_logits, precision=HIGHEST_DOT)
    grad_resid_norm, grad_gain_two = rms_back(resid, gain_two_f, grad_normed_two)
    grad_resid = grad_out + grad_resid_norm
    grad_attn_low = (RESIDUAL_SCALE * grad_resid).astype(bf16)
    grad_heads = contract_cols(grad_attn_low, output_w).astype(bf16)
    grad_mixed = exchange(
        grad_heads.reshape(token_count, KEY_VALUE_HEADS, PAIR).transpose(1, 0, 2), head_axes
    ).reshape(span, PAIR)
    if small_plane:
        left_on, right_on = halve_add(left_on), halve_add(right_on)
        left_on, right_on, attended_low, grad_router = lax.optimization_barrier(
            (left_on, right_on, attended_low, grad_router)
        )
    small = jnp.concatenate([grad_router, grad_gain_two[:, None]], axis=1)
    second_part = jnp.concatenate(
        [contract_rows(attended_low, grad_attn_low), pad_lanes(small, LANES)], axis=1
    ).astype(bf16)
    cols = second_part.shape[1]
    second_part = second_part.reshape(GROUPS, -1, own_rows, cols).transpose(1, 0, 2, 3)
    if small_plane:
        left_last = lax.ppermute(quarter(left, b, 1 - y), "y", SWAP)
        right_last = lax.ppermute(quarter(right, 1 - b, y), "b", SWAP)
        second_part, left_on, right_on, left_last, right_last, grad_mixed = (
            lax.optimization_barrier(
                (second_part, left_on, right_on, left_last, right_last, grad_mixed)
            )
        )
        left_on, right_on = lax.ppermute(left_on, "b", SWAP), lax.ppermute(right_on, "y", SWAP)
    rest = scatter_sum(second_part.reshape(-1, cols), PLANE)
    grads = attend_back(
        bounds, qkv, kv, kv_at, doc_rows, grad_mixed, attention_result, log_total,
        wide_cos, wide_sin, whole_rows,
    )
    if whole_rows:
        grad_pack = grads
    else:
        grad_kv = scatter_sum(grads[1].astype(bf16), "a").astype(f32)
        grad_pack = unrotate(grads[0], grad_kv, wide_cos, wide_sin)
    if small_plane:
        left_on, right_on, left, right, moe_sum, grad_pack = lax.optimization_barrier(
            (left_on, right_on, left, right, moe_sum, grad_pack)
        )
    first_part = head_grads(place, x_span, normed_span, first_all, grad_pack)
    by_tokens = exchange(grad_pack.reshape(KEY_VALUE_HEADS, token_count, HEAD_PACK), head_axes)
    by_tokens, first_part = lax.optimization_barrier((by_tokens, first_part))
    rest, by_tokens = lax.optimization_barrier((rest, by_tokens))
    rest = scatter_sum(rest, "a")
    sums = exchange(first_part.reshape(-1, own_rows, first_part.shape[1]), ALL)
    sums, moe_sum, resid, rest = lax.optimization_barrier((sums, moe_sum, resid, rest))
    grad_q_w, grad_k_w, grad_v_w, grad_gain_one = weight_sums(
        sums.reshape(-1, KEY_VALUE_HEADS, lax.axis_size(("y", "c")), own_rows, first_part.shape[1])
    )
    rest = rest.astype(f32)
    grad_qkv = by_tokens.transpose(1, 0, 2).reshape(token_count, qkv_width)
    grad_normed_one = contract_cols(grad_qkv, first_all[:, :qkv_width])
    grad_x_norm, _ = rms_back(x_local, gain_one_f, grad_normed_one)
    grad_input = grad_resid + grad_x_norm
    layer_sum = resid + RESIDUAL_SCALE * moe_sum.astype(f32)
    if small_plane:
        grad_experts = jnp.concatenate(
            [
                quarter(left, b, y).astype(f32) + left_last.astype(f32) + left_on.astype(f32),
                quarter(right, b, y).astype(f32) + right_last.astype(f32) + right_on.astype(f32),
            ],
            axis=1,
        )
    else:
        grad_experts = grad_experts.astype(f32)
    return (
        layer_sum.astype(bf16)[None],
        grad_input[None],
        grad_gain_one[:, 0],
        grad_q_w,
        grad_k_w,
        grad_v_w,
        rest[:, :width],
        rest[:, width + E],
        rest[:, width : width + E],
        grad_experts[:, : 2 * F],
        grad_experts[:, 2 * F :],
    )


def solution(mesh):
    seq, row = mesh.shape["seq"], mesh.shape["row"]
    cut = Mesh(mesh.devices.reshape(GROUPS, seq // GROUPS, row // 2, 2), ALL)
    token_spec = P(("y", "c"), SEQ, None)
    row_spec = P(ALL, None)
    flat_spec = P(ALL)
    in_specs = (
        token_spec,
        token_spec,
        P(("y", "c"), None),
        token_spec,
        flat_spec,
        row_spec,
        row_spec,
        row_spec,
        row_spec,
        flat_spec,
        row_spec,
        row_spec,
        row_spec,
    )
    out_specs = (
        token_spec,
        token_spec,
        flat_spec,
        row_spec,
        row_spec,
        row_spec,
        row_spec,
        flat_spec,
        row_spec,
        row_spec,
        row_spec,
    )
    return jax.shard_map(body, mesh=cut, in_specs=in_specs, out_specs=out_specs, check_vma=False)
```

```python
import functools

import jax
import jax.numpy as jnp
from jax import lax
from jax.experimental import pallas as pl
from jax.experimental.pallas import tpu as pltpu
from jax.sharding import Mesh, PartitionSpec as P

QUERY_HEADS = 16
KEY_VALUE_HEADS = 8
HEAD_SIZE = 64
F = 512
E = 16
GROUPS = 4
EXPERTS_HERE = E // GROUPS
LANES = 128
PAIR = 2 * HEAD_SIZE
HEAD_PACK = 4 * HEAD_SIZE
BLOCK = 256
QUERY_BLOCK = 512

NORM_EPS = 1e-06
RESIDUAL_SCALE = 0.22
SCALE_OF_SCORES = 0.015625
ROPE_BASE = 10000.0
NEGATIVE_HUGE = -1e30
HIGHEST_DOT = lax.Precision.HIGHEST
VMEM_LIMIT = 60 * 1024 * 1024

PLANE = ("b", "y", "c")
SEQ = ("a", "b")
ALL = ("a", "b", "y", "c")
SWAP = [(0, 1), (1, 0)]

f32 = jnp.float32
bf16 = jnp.bfloat16


def rotation_tables(positions):
    half = HEAD_SIZE // 2
    freq = jnp.power(ROPE_BASE, -2.0 * jnp.arange(half, dtype=f32) / HEAD_SIZE)
    angle = positions.astype(f32)[:, None] * freq[None, :]
    return jnp.cos(angle), jnp.sin(angle)


def rms_back(values, gain, grad_norm):
    mean_square = jnp.mean(values * values, axis=-1, keepdims=True)
    inverse = lax.rsqrt(mean_square + NORM_EPS)
    scaled_grad = grad_norm * gain
    grad_values = inverse * scaled_grad - values * inverse**3 * jnp.mean(
        values * scaled_grad, axis=-1, keepdims=True
    )
    grad_gain = jnp.sum(grad_norm * values * inverse, axis=0)
    return (grad_values, grad_gain)


def rms_scale(values, gain):
    mean_square = jnp.mean(values * values, axis=-1, keepdims=True)
    return values * lax.rsqrt(mean_square + NORM_EPS) * gain


def contract_rows(left_side, right_side):
    return lax.dot_general(
        left_side, right_side, (((0,), (0,)), ((), ())), preferred_element_type=f32
    )


def contract_cols(left_side, right_side):
    return lax.dot_general(
        left_side, right_side, (((1,), (1,)), ((), ())), preferred_element_type=f32
    )


def gather(x, axes):
    return lax.all_gather(x, axes, axis=0, tiled=True)


def scatter_sum(x, axes):
    return lax.psum_scatter(x, axes, scatter_dimension=0, tiled=True)


def pad_lanes(x, lanes):
    return jnp.pad(x, ((0, 0), (0, lanes - x.shape[1])))


def line_pairs(n, step):
    return [(i, i + step) for i in range(n) if 0 <= i + step < n]


def grid_gather(x):
    n = lax.axis_size("a")

    def cross(block, ends):
        return lax.ppermute(
            block, SEQ, [(2 * i + j, 2 * i + 1 - j) for i in range(n) if ends(i) for j in (0, 1)]
        )

    pieces = [(0, 0, x), (0, 1, cross(x, lambda i: True))]
    up = down = x
    for k in range(1, n):
        up = lax.ppermute(up, "a", line_pairs(n, 1))
        down = lax.ppermute(down, "a", line_pairs(n, -1))
        pieces += [(-k, 0, up), (-k, 1, cross(up, lambda i: i >= k))]
        pieces += [(k, 0, down), (k, 1, cross(down, lambda i: i + k < n))]
    return pieces


def plane_gather(x):
    swap = SWAP
    half = x.shape[0] // 2
    from_y = lax.ppermute(x, "y", SWAP)
    from_b = lax.ppermute(x, "b", SWAP)
    upper = lax.ppermute(from_b[:half], "y", SWAP)
    lower = lax.ppermute(from_y[half:], "b", SWAP)
    return [
        (block, lax.ppermute(block, "c", SWAP)) for block in (x, from_y, from_b, upper, lower)
    ]


def quarter(v, b, y):
    return lax.dynamic_index_in_dim(lax.dynamic_index_in_dim(v, b, 0, False), y, 0, False)


def halve_add(terms):
    own, other = terms
    return (own.astype(f32) + other.astype(f32)).astype(own.dtype)


def rotate_lanes(x, cos, sin):
    width = x.shape[-1]
    lane = lax.broadcasted_iota(jnp.int32, x.shape, x.ndim - 1)
    swapped = jnp.where(
        lane % HEAD_SIZE < HEAD_SIZE // 2,
        pltpu.roll(x, width - HEAD_SIZE // 2, x.ndim - 1),
        pltpu.roll(x, HEAD_SIZE // 2, x.ndim - 1),
    )
    return x * cos + swapped * sin


def spread_tables(cos, sin):
    return jnp.concatenate([cos] * 4, axis=1), jnp.concatenate([-sin, sin, -sin, sin], axis=1)


def key_tables(cos, sin):
    low = lower_lanes(cos.shape)
    return jnp.where(low, cos, 1.0), jnp.where(low, sin, 0.0)


def project_kernel(places, place_ref, *refs):
    count = 1 if places is None else len(places)
    blocks, refs = refs[:count], refs[count:]
    small_ref, w_ref, cos_ref, sin_ref, qkv_ref, normed_ref, x_ref = refs[:7]
    wide_cos_ref, wide_sin_ref, gain, held, sems = refs[7:]
    i = pl.program_id(0)
    slots = held.shape[0]

    @pl.when(i == 0)
    def _():
        if places is None:
            for slot in range(slots):
                pltpu.make_async_copy(blocks[0].at[slot], held.at[slot], sems.at[slot]).start()
        else:
            for (distance, crossed), block in zip(places, blocks):
                at = place_ref[1] + distance
                member = 1 - place_ref[2] if crossed else place_ref[2]

                @pl.when((at >= 0) & (at < slots // 2))
                def _(block=block, slot=2 * at + member):
                    pltpu.make_async_copy(block, held.at[slot], sems.at[slot]).start()

        gain[...] = jnp.transpose(small_ref[...].astype(f32))[E : E + 8, :]

    arrived = blocks[0].at[0] if places is None else blocks[0]
    pltpu.make_async_copy(arrived, held.at[i], sems.at[i]).wait()
    x = held[i]
    x_ref[...] = x
    normed = rms_scale(x.astype(f32), gain[0:1, :]).astype(bf16)
    normed_ref[...] = normed
    pre = jnp.dot(normed, w_ref[...], preferred_element_type=f32)
    cos, sin = spread_tables(cos_ref[...], sin_ref[...])
    wide_cos_ref[...] = cos
    wide_sin_ref[...] = sin
    qkv_ref[:, :PAIR] = rotate_lanes(pre[:, :PAIR], cos, sin).astype(bf16)
    qkv_ref[:, PAIR:] = rotate_lanes(pre[:, PAIR:], *key_tables(cos, sin)).astype(bf16)


def project(place, places, blocks, rows, packed, cos, sin):
    width = packed.shape[0]
    small_at = packed.shape[1] // LANES - 1
    span = cos.shape[0]
    table = pl.BlockSpec((rows, HEAD_SIZE // 2), lambda i, h: (i, 0))
    token_rows = pl.BlockSpec((rows, width), lambda i, h: (i, 0))
    return pl.pallas_call(
        functools.partial(project_kernel, places),
        grid_spec=pltpu.PrefetchScalarGridSpec(
            num_scalar_prefetch=1,
            grid=(span // rows,),
            in_specs=[pl.BlockSpec(memory_space=pl.ANY)] * len(blocks)
            + [
                pl.BlockSpec((width, LANES), lambda i, h: (0, small_at)),
                pl.BlockSpec((width, HEAD_PACK), lambda i, h: (0, h[0])),
                table,
                table,
            ],
            out_specs=[
                pl.BlockSpec((rows, HEAD_PACK), lambda i, h: (i, 0)),
                token_rows,
                token_rows,
                pl.BlockSpec((rows, PAIR), lambda i, h: (i, 0)),
                pl.BlockSpec((rows, PAIR), lambda i, h: (i, 0)),
            ],
            scratch_shapes=[
                pltpu.VMEM((8, width), f32),
                pltpu.VMEM((span // rows, rows, width), bf16),
                pltpu.SemaphoreType.DMA((span // rows,)),
            ],
        ),
        out_shape=[
            jax.ShapeDtypeStruct((span, HEAD_PACK), bf16),
            jax.ShapeDtypeStruct((span, width), bf16),
            jax.ShapeDtypeStruct((span, width), bf16),
            jax.ShapeDtypeStruct((span, PAIR), f32),
            jax.ShapeDtypeStruct((span, PAIR), f32),
        ],
        compiler_params=pltpu.CompilerParams(vmem_limit_bytes=VMEM_LIMIT),
        cost_estimate=pl.CostEstimate(
            flops=2 * span * width * HEAD_PACK, bytes_accessed=18 * 2**20, transcendentals=0
        ),
        name="project",
    )(place, *blocks, packed, packed, cos, sin)


def head_grads_kernel(head_ref, x_ref, normed_ref, w_ref, grad_ref, out_ref, acc, gain):
    i = pl.program_id(0)

    @pl.when(i == 0)
    def _():
        acc[...] = jnp.zeros_like(acc)
        gain[...] = jnp.zeros_like(gain)

    grad = grad_ref[...]
    acc[...] += contract_rows(grad, normed_ref[...])
    x = x_ref[...].astype(f32)
    inverse = lax.rsqrt(jnp.mean(x * x, axis=-1, keepdims=True) + NORM_EPS)
    back = contract_cols(grad, w_ref[...]) * (x * inverse)
    gain[...] += jnp.sum(back.reshape(back.shape[0] // 8, 8, back.shape[1]), axis=0)

    @pl.when(i == pl.num_programs(0) - 1)
    def _():
        out_ref[:, :HEAD_PACK] = jnp.transpose(acc[...]).astype(bf16)
        total = jnp.sum(gain[...], axis=0, keepdims=True)
        rows = lax.broadcasted_iota(jnp.int32, (LANES, total.shape[1]), 0)
        out_ref[:, HEAD_PACK:] = jnp.transpose(
            jnp.where(rows == 0, jnp.broadcast_to(total, rows.shape), 0.0)
        ).astype(bf16)


def head_grads(head, x, normed, packed, grads):
    span, width = x.shape
    rows = 2 * BLOCK
    token_rows = pl.BlockSpec((rows, width), lambda i, h: (i, 0))
    return pl.pallas_call(
        head_grads_kernel,
        grid_spec=pltpu.PrefetchScalarGridSpec(
            num_scalar_prefetch=1,
            grid=(span // rows,),
            in_specs=[
                token_rows,
                token_rows,
                pl.BlockSpec((width, HEAD_PACK), lambda i, h: (0, h[0])),
                pl.BlockSpec((rows, HEAD_PACK), lambda i, h: (i, 0)),
            ],
            out_specs=pl.BlockSpec((width, HEAD_PACK + LANES), lambda i, h: (0, 0)),
            scratch_shapes=[pltpu.VMEM((HEAD_PACK, width), f32), pltpu.VMEM((8, width), f32)],
        ),
        out_shape=jax.ShapeDtypeStruct((width, HEAD_PACK + LANES), bf16),
        compiler_params=pltpu.CompilerParams(vmem_limit_bytes=VMEM_LIMIT),
        cost_estimate=pl.CostEstimate(
            flops=4 * span * width * HEAD_PACK, bytes_accessed=12 * 2**20, transcendentals=0
        ),
        name="head_grads",
    )(head, x, normed, packed, grads)


def lower_lanes(shape):
    return lax.broadcasted_iota(jnp.int32, shape, len(shape) - 1) < HEAD_SIZE


def both_heads_low(pair):
    low = lower_lanes(pair.shape)
    return jnp.concatenate(
        [jnp.where(low, pair, 0.0), jnp.where(low, pltpu.roll(pair, HEAD_SIZE, 1), 0.0)], axis=0
    )


def both_heads_high(pair):
    low = lower_lanes(pair.shape)
    return jnp.concatenate(
        [jnp.where(low, 0.0, pltpu.roll(pair, HEAD_SIZE, 1)), jnp.where(low, 0.0, pair)], axis=0
    )


def block_bounds(bounds_ref):
    i, steps = pl.program_id(0), pl.num_programs(0)
    query_start = (i + bounds_ref[2 * steps]) * QUERY_BLOCK
    diagonal = query_start // BLOCK
    full = jnp.minimum(bounds_ref[steps + i], diagonal)
    return query_start, bounds_ref[i], full, diagonal, diagonal + QUERY_BLOCK // BLOCK


def pair_mask(doc, query_start):
    doc = jnp.concatenate([doc, doc], axis=1)
    queries = lax.broadcasted_iota(jnp.int32, doc.shape, 1) % QUERY_BLOCK + query_start

    def masked(scores, start):
        keys = lax.broadcasted_iota(jnp.int32, scores.shape, 0) + start
        return jnp.where((keys >= doc) & (keys <= queries), scores, NEGATIVE_HUGE)

    return masked


def attend_kernel(bounds_ref, q_ref, kv_ref, doc_ref, o_ref, low_ref, lse_ref, acc):
    query_start, first, full, diagonal, end = block_bounds(bounds_ref)
    q = both_heads_low(q_ref[...].astype(f32) * SCALE_OF_SCORES).astype(bf16)
    masked = pair_mask(doc_ref[0], query_start)
    acc[...] = jnp.zeros_like(acc)

    def step(mask, j, carried):
        top, total = carried
        start = pl.multiple_of(j * BLOCK, BLOCK)
        kv = kv_ref[pl.ds(start, BLOCK), :]
        scores = contract_cols(kv, q)
        if mask:
            scores = masked(scores, start)
        new = jnp.maximum(top, jnp.max(scores, axis=0, keepdims=True))
        probs = jnp.exp(scores - new)
        keep = jnp.exp(top - new)
        acc[...] = acc[...] * keep + contract_rows(kv, probs.astype(bf16))
        return new, total * keep + jnp.sum(probs, axis=0, keepdims=True)

    row = (1, 2 * QUERY_BLOCK)
    carried = (jnp.full(row, NEGATIVE_HUGE, f32), jnp.zeros(row, f32))
    carried = lax.fori_loop(first, full, functools.partial(step, True), carried)
    carried = lax.fori_loop(full, diagonal, functools.partial(step, False), carried)
    top, total = lax.fori_loop(diagonal, end, functools.partial(step, True), carried)
    mixed = jnp.transpose(acc[...] / total)
    one, two = mixed[:QUERY_BLOCK], mixed[QUERY_BLOCK:]
    out = jnp.where(lower_lanes(one.shape), pltpu.roll(one, HEAD_SIZE, 1), two)
    o_ref[...] = out
    low_ref[...] = out.astype(bf16)
    lse_ref[0] = top + jnp.log(total)


def attention_specs(kv_at, keys):
    pair = pl.BlockSpec((QUERY_BLOCK, PAIR), lambda i, s: (i, 0))
    return (
        pair,
        pl.BlockSpec((keys, PAIR), lambda i, s: (0, kv_at)),
        pl.BlockSpec((1, 1, QUERY_BLOCK), lambda i, s: (i, 0, 0)),
        pl.BlockSpec((1, 1, 2 * QUERY_BLOCK), lambda i, s: (i, 0, 0)),
    )


def attend(bounds, qkv, kv, kv_at, doc):
    queries, keys = qkv.shape[0], kv.shape[0]
    steps = queries // QUERY_BLOCK
    pair, whole, doc_row, lse_row = attention_specs(kv_at, keys)
    return pl.pallas_call(
        attend_kernel,
        grid_spec=pltpu.PrefetchScalarGridSpec(
            num_scalar_prefetch=1,
            grid=(steps,),
            in_specs=[pair, whole, doc_row],
            out_specs=[pair, pair, lse_row],
            scratch_shapes=[pltpu.VMEM((PAIR, 2 * QUERY_BLOCK), f32)],
        ),
        out_shape=[
            jax.ShapeDtypeStruct((queries, PAIR), f32),
            jax.ShapeDtypeStruct((queries, PAIR), bf16),
            jax.ShapeDtypeStruct((steps, 1, 2 * QUERY_BLOCK), f32),
        ],
        compiler_params=pltpu.CompilerParams(vmem_limit_bytes=VMEM_LIMIT),
        cost_estimate=pl.CostEstimate(
            flops=4 * queries * keys * PAIR, bytes_accessed=6 * 2**20, transcendentals=queries * keys
        ),
        name="attend",
    )(bounds, qkv, kv, doc)


def attend_back_kernel(
    fold, bounds_ref, q_ref, kv_ref, doc_ref, do_ref, o_ref, lse_ref, cos_ref, sin_ref, *refs
):
    if fold:
        out_ref, acc, dkv_ref = refs
    else:
        dq_ref, dkv_ref, acc = refs
    i = pl.program_id(0)
    query_start, first, full, diagonal, end = block_bounds(bounds_ref)

    @pl.when(i == 0)
    def _():
        dkv_ref[...] = jnp.zeros_like(dkv_ref)

    q = both_heads_low(q_ref[...].astype(f32) * SCALE_OF_SCORES).astype(bf16)
    grad = do_ref[...].astype(f32)
    product = jnp.transpose(grad * o_ref[...])
    delta = jnp.concatenate(
        [
            jnp.sum(product[:HEAD_SIZE], axis=0, keepdims=True),
            jnp.sum(product[HEAD_SIZE:], axis=0, keepdims=True),
        ],
        axis=1,
    )
    grad = both_heads_high(grad).astype(bf16)
    sources = jnp.concatenate([q, grad], axis=0)
    masked = pair_mask(doc_ref[0], query_start)
    lse = lse_ref[0]
    acc[...] = jnp.zeros_like(acc)

    def step(mask, j, carried):
        start = pl.multiple_of(j * BLOCK, BLOCK)
        kv = kv_ref[pl.ds(start, BLOCK), :]
        scores = contract_cols(kv, q) - lse
        if mask:
            scores = masked(scores, start)
        probs = jnp.exp(scores)
        grad_scores = (probs * (contract_cols(kv, grad) - delta)).astype(bf16)
        acc[...] += contract_rows(kv, grad_scores)
        both = jnp.concatenate([grad_scores, probs.astype(bf16)], axis=1)
        dkv_ref[pl.ds(start, BLOCK), :] += jnp.dot(both, sources, preferred_element_type=f32)
        return carried

    lax.fori_loop(first, full, functools.partial(step, True), 0)
    lax.fori_loop(full, diagonal, functools.partial(step, False), 0)
    lax.fori_loop(diagonal, end, functools.partial(step, True), 0)
    dq = jnp.transpose(acc[...])
    one, two = dq[:QUERY_BLOCK], dq[QUERY_BLOCK:]
    dq = jnp.where(lower_lanes(one.shape), one, pltpu.roll(two, HEAD_SIZE, 1))
    if not fold:
        dq_ref[...] = dq
        return
    mine = pl.ds(pl.multiple_of(i * QUERY_BLOCK, QUERY_BLOCK), QUERY_BLOCK)
    out_ref[mine, :PAIR] = rotate_lanes(
        dq * SCALE_OF_SCORES, cos_ref[mine, :], -sin_ref[mine, :]
    ).astype(bf16)

    @pl.when(i == pl.num_programs(0) - 1)
    def _():
        def finish(j, carried):
            part = pl.ds(pl.multiple_of(j * BLOCK, BLOCK), BLOCK)
            cos, sin = key_tables(cos_ref[part, :], sin_ref[part, :])
            out_ref[part, PAIR:] = rotate_lanes(dkv_ref[part, :], cos, -sin).astype(bf16)
            return carried

        lax.fori_loop(0, dkv_ref.shape[0] // BLOCK, finish, 0)


def attend_back(bounds, qkv, kv, kv_at, doc, grad, out, lse, cos, sin, fold):
    queries, keys = qkv.shape[0], kv.shape[0]
    steps = queries // QUERY_BLOCK
    pair, whole, doc_row, lse_row = attention_specs(kv_at, keys)
    table = pl.BlockSpec(cos.shape, lambda i, s: (0, 0))
    acc = pltpu.VMEM((PAIR, 2 * QUERY_BLOCK), f32)
    if fold:
        out_specs = pl.BlockSpec((queries, HEAD_PACK), lambda i, s: (0, 0))
        out_shape = jax.ShapeDtypeStruct((queries, HEAD_PACK), bf16)
        scratch = [acc, pltpu.VMEM((keys, PAIR), f32)]
    else:
        out_specs = [pair, pl.BlockSpec((keys, PAIR), lambda i, s: (0, 0))]
        out_shape = [
            jax.ShapeDtypeStruct((queries, PAIR), f32),
            jax.ShapeDtypeStruct((keys, PAIR), f32),
        ]
        scratch = [acc]
    return pl.pallas_call(
        functools.partial(attend_back_kernel, fold),
        grid_spec=pltpu.PrefetchScalarGridSpec(
            num_scalar_prefetch=1,
            grid=(steps,),
            in_specs=[pair, whole, doc_row, pair, pair, lse_row, table, table],
            out_specs=out_specs,
            scratch_shapes=scratch,
        ),
        out_shape=out_shape,
        compiler_params=pltpu.CompilerParams(vmem_limit_bytes=VMEM_LIMIT),
        cost_estimate=pl.CostEstimate(
            flops=10 * queries * keys * PAIR,
            bytes_accessed=8 * 2**20,
            transcendentals=queries * keys,
        ),
        name="attend_back",
    )(bounds, qkv, kv, doc, grad, out, lse, cos, sin)


def unrotate_kernel(dq_ref, dkv_ref, cos_ref, sin_ref, out_ref):
    cos, sin = cos_ref[...], sin_ref[...]
    dq = rotate_lanes(dq_ref[...] * SCALE_OF_SCORES, cos, -sin)
    cos, sin = key_tables(cos, sin)
    dkv = rotate_lanes(dkv_ref[...], cos, -sin)
    out_ref[...] = jnp.concatenate([dq, dkv], axis=1).astype(bf16)


def unrotate(dq, dkv, cos, sin):
    rows = dq.shape[0]
    pair = pl.BlockSpec((BLOCK, PAIR), lambda i: (i, 0))
    return pl.pallas_call(
        unrotate_kernel,
        grid=(rows // BLOCK,),
        in_specs=[pair, pair, pair, pair],
        out_specs=pl.BlockSpec((BLOCK, HEAD_PACK), lambda i: (i, 0)),
        out_shape=jax.ShapeDtypeStruct((rows, HEAD_PACK), bf16),
        cost_estimate=pl.CostEstimate(
            flops=rows * HEAD_PACK * 8, bytes_accessed=rows * HEAD_PACK * 14, transcendentals=0
        ),
        name="unrotate",
    )(dq, dkv, cos, sin)


def place_experts_kernel(place_ref, *refs):
    blocks, (ct_ref, w_ref, z_ref, sems) = refs[:10], refs[10:]
    core = place_ref[1]
    rows = w_ref.shape[1] // 2
    half = rows // 2
    sources = [[(0, 0, rows)], [(1, 0, rows)], [(2, 0, rows)], [(3, 0, half), (4, half, half)]]
    for step, parts in enumerate(sources):

        @pl.when(pl.program_id(0) == step)
        def _(parts=parts):
            copies = []
            for source, start, length in parts:
                for other in (0, 1):
                    first = jnp.where(core == other, 0, rows) + start
                    at = pl.ds(pl.multiple_of(first, half), length)
                    copies.append(
                        pltpu.make_async_copy(
                            blocks[2 * source + other], w_ref.at[0, at, :], sems.at[len(copies)]
                        )
                    )
            for copy in copies:
                copy.start()
            for copy in copies:
                copy.wait()

    z_ref[0] = jnp.dot(ct_ref[...], w_ref[0, :, 2 * F :], preferred_element_type=f32)


def place_experts(place, parts, early, width):
    rows = early.shape[0]
    blocks = [block for pair in parts for block in pair]
    return pl.pallas_call(
        place_experts_kernel,
        grid_spec=pltpu.PrefetchScalarGridSpec(
            num_scalar_prefetch=1,
            grid=(EXPERTS_HERE,),
            in_specs=[pl.BlockSpec(memory_space=pl.ANY)] * len(blocks)
            + [pl.BlockSpec((rows, width), lambda r, s: (0, 0))],
            out_specs=[
                pl.BlockSpec((1, width, 3 * F), lambda r, s: (s[0] ^ r, 0, 0)),
                pl.BlockSpec((1, rows, F), lambda r, s: (s[0] ^ r, 0, 0)),
            ],
            scratch_shapes=[pltpu.SemaphoreType.DMA((4,))],
        ),
        out_shape=[
            jax.ShapeDtypeStruct((EXPERTS_HERE, width, 3 * F), bf16),
            jax.ShapeDtypeStruct((EXPERTS_HERE, rows, F), f32),
        ],
        compiler_params=pltpu.CompilerParams(vmem_limit_bytes=VMEM_LIMIT),
        cost_estimate=pl.CostEstimate(
            flops=2 * EXPERTS_HERE * rows * width * F, bytes_accessed=36 * 2**20, transcendentals=0
        ),
        name="place_experts",
    )(place, *blocks, early)


def lane_column(x, at):
    lane = lax.broadcasted_iota(jnp.int32, x.shape, 1)
    return jnp.sum(jnp.where(lane == at, x, 0.0), axis=1, keepdims=True)


def experts_kernel(
    group_ref, n_ref, routed_ref, router_ref, w_ref, z_ref,
    back_ref, gates_ref, hidden_ref, pre_ref, acc, dots,
):
    e = pl.program_id(0)
    own = group_ref[0] * EXPERTS_HERE + e
    rows = n_ref.shape[0]

    @pl.when(e == 0)
    def _():
        logits = jnp.dot(n_ref[...], router_ref[...], preferred_element_type=f32)
        routed = routed_ref[...].astype(f32) > 0.5
        highest = jnp.max(jnp.where(routed, logits, NEGATIVE_HUGE), axis=1, keepdims=True)
        weights = jnp.where(routed, jnp.exp(jnp.where(routed, logits - highest, 0.0)), 0.0)
        gates_ref[...] = weights / jnp.sum(weights, axis=1, keepdims=True)
        acc[...] = jnp.zeros_like(acc)
        dots[...] = jnp.zeros_like(dots)

    w_in = w_ref[0, :, : 2 * F]
    for t in range(rows // BLOCK):
        part = pl.ds(t * BLOCK, BLOCK)
        pre = jnp.dot(n_ref[part, :], w_in, preferred_element_type=f32)
        gate, up = pre[:, :F], pre[:, F:]
        z = z_ref[0, part, :]
        weight = lane_column(gates_ref[part, :], own)
        sig = 1.0 / (1.0 + jnp.exp(-gate))
        act = gate * sig
        hidden = act * up
        hidden_ref[0, part, :] = (weight * hidden).astype(bf16)
        dot = RESIDUAL_SCALE * jnp.sum(hidden.astype(bf16).astype(f32) * z, axis=1, keepdims=True)
        lane = lax.broadcasted_iota(jnp.int32, (BLOCK, LANES), 1)
        dots[part, :] += jnp.where(lane == own, dot, 0.0)
        scaled = (RESIDUAL_SCALE * weight) * z
        pre_ref[0, part, :F] = (scaled * up * (sig + act * (1.0 - sig))).astype(bf16)
        pre_ref[0, part, F:] = (scaled * act).astype(bf16)
        acc[part, :] += contract_cols(pre_ref[0, part, :], w_in)

    @pl.when(e == EXPERTS_HERE - 1)
    def _():
        width = n_ref.shape[1]
        back_ref[:, :width] = acc[...].astype(bf16)
        high = dots[...].astype(bf16)
        low = dots[...] - high.astype(f32)
        back_ref[:, width:] = (high.astype(f32) + pltpu.roll(low, E, 1)).astype(bf16)


def experts(group, normed, early, packed, w_all, z):
    rows, width = normed.shape
    count = w_all.shape[0]
    whole = pl.BlockSpec((rows, width), lambda e, g: (0, 0))
    column = width // LANES
    router_at = packed.shape[1] // LANES - 1
    return pl.pallas_call(
        experts_kernel,
        grid_spec=pltpu.PrefetchScalarGridSpec(
            num_scalar_prefetch=1,
            grid=(count,),
            in_specs=[
                whole,
                pl.BlockSpec((rows, LANES), lambda e, g: (0, column)),
                pl.BlockSpec((width, LANES), lambda e, g: (0, router_at)),
                pl.BlockSpec((1, width, 3 * F), lambda e, g: (e, 0, 0)),
                pl.BlockSpec((1, rows, F), lambda e, g: (e, 0, 0)),
            ],
            out_specs=[
                pl.BlockSpec((rows, width + LANES), lambda e, g: (0, 0)),
                pl.BlockSpec((rows, LANES), lambda e, g: (0, 0)),
                pl.BlockSpec((1, rows, F), lambda e, g: (e, 0, 0)),
                pl.BlockSpec((1, rows, 2 * F), lambda e, g: (e, 0, 0)),
            ],
            scratch_shapes=[pltpu.VMEM((rows, width), f32), pltpu.VMEM((rows, LANES), f32)],
        ),
        out_shape=[
            jax.ShapeDtypeStruct((rows, width + LANES), bf16),
            jax.ShapeDtypeStruct((rows, LANES), f32),
            jax.ShapeDtypeStruct((count, rows, F), bf16),
            jax.ShapeDtypeStruct((count, rows, 2 * F), bf16),
        ],
        compiler_params=pltpu.CompilerParams(vmem_limit_bytes=VMEM_LIMIT),
        cost_estimate=pl.CostEstimate(
            flops=2 * count * rows * width * 4 * F, bytes_accessed=40 * 2**20, transcendentals=0
        ),
        name="experts",
    )(group, normed, early, packed, w_all, z)


def expert_grads_kernel(with_y, half_ref, n_ref, ct_ref, w_ref, hidden_ref, pre_ref, *refs):
    if with_y:
        left_ref, right_ref, y_ref, n_t, ct_t, acc = refs
    else:
        left_ref, right_ref, n_t, ct_t = refs
    e = pl.program_id(0)
    cut = left_ref.shape[2]

    @pl.when(e == 0)
    def _():
        n_t[...] = jnp.transpose(n_ref[...])
        ct_t[...] = jnp.transpose(ct_ref[...])
        if with_y:
            acc[...] = jnp.zeros_like(acc)

    grads = jnp.dot(n_t[...], pre_ref[0], preferred_element_type=f32).astype(bf16)
    left_ref[0] = grads[:, :cut]
    right_ref[0, :, : 2 * F - cut] = grads[:, cut:]
    right_ref[0, :, 2 * F - cut :] = (
        RESIDUAL_SCALE * jnp.dot(ct_t[...], hidden_ref[0], preferred_element_type=f32)
    ).astype(bf16)
    if not with_y:
        return
    acc[...] += contract_cols(hidden_ref[0], w_ref[0, :, 2 * F :])

    @pl.when(e == pl.num_programs(0) - 1)
    def _():
        y_ref[...] = acc[...].astype(bf16)


def expert_grads(half, halves, normed, early, w_all, hidden, pre, with_y):
    rows, width = normed.shape
    count = w_all.shape[0]
    own, cut = width // halves, 3 * F // 2
    feature = pl.BlockSpec((rows, own), lambda e, h: (0, h[0]))
    out_specs = [pl.BlockSpec((1, own, cut), lambda e, h: (e, 0, 0))] * 2
    out_shape = [jax.ShapeDtypeStruct((count, own, cut), bf16)] * 2
    scratch = [pltpu.VMEM((own, rows), bf16), pltpu.VMEM((own, rows), bf16)]
    if with_y:
        out_specs.append(pl.BlockSpec((rows, width), lambda e, h: (0, 0)))
        out_shape.append(jax.ShapeDtypeStruct((rows, width), bf16))
        scratch.append(pltpu.VMEM((rows, width), f32))
    return pl.pallas_call(
        functools.partial(expert_grads_kernel, with_y),
        grid_spec=pltpu.PrefetchScalarGridSpec(
            num_scalar_prefetch=1,
            grid=(count,),
            in_specs=[
                feature,
                feature,
                pl.BlockSpec((1, width, 3 * F), lambda e, h: (e, 0, 0)),
                pl.BlockSpec((1, rows, F), lambda e, h: (e, 0, 0)),
                pl.BlockSpec((1, rows, 2 * F), lambda e, h: (e, 0, 0)),
            ],
            out_specs=out_specs,
            scratch_shapes=scratch,
        ),
        out_shape=out_shape,
        compiler_params=pltpu.CompilerParams(vmem_limit_bytes=VMEM_LIMIT),
        cost_estimate=pl.CostEstimate(
            flops=2 * count * rows * width * 3 * F // halves + 2 * with_y * count * rows * width * F,
            bytes_accessed=30 * 2**20,
            transcendentals=0,
        ),
        name="expert_grads",
    )(half, normed, early, w_all, hidden, pre)


def join_kernel(place_ref, o_ref, w_ref, small_ref, x_ref, normed_ref, resid_ref, own_ref, gain):
    t = pl.program_id(0)
    b = place_ref[2]

    @pl.when(t == 0)
    def _():
        gain[...] = jnp.transpose(small_ref[...].astype(f32))[E : E + 8, :]

    pairs = []
    for a in range(o_ref.shape[0]):
        same, other = o_ref[a, 0, 0], o_ref[a, 1, 0]
        pairs.append(jnp.where(b == 0, same, other))
        pairs.append(jnp.where(b == 0, other, same))
    attended = jnp.concatenate(pairs, axis=1)
    resid = x_ref[...].astype(f32) + RESIDUAL_SCALE * jnp.dot(
        attended, w_ref[...], preferred_element_type=f32
    )
    normed_ref[...] = rms_scale(resid, gain[1:2, :]).astype(bf16)

    @pl.when(t == place_ref[1])
    def _():
        resid_ref[...] = resid
        own_ref[...] = attended


def join(place, outs, packed, weights_at, x):
    width = packed.shape[0]
    lines, _, _, rows, pair = outs.shape
    small_at = packed.shape[1] // LANES - 1
    own = pl.BlockSpec((rows, width), lambda t, s: (0, 0))
    return pl.pallas_call(
        join_kernel,
        grid_spec=pltpu.PrefetchScalarGridSpec(
            num_scalar_prefetch=1,
            grid=(lines,),
            in_specs=[
                pl.BlockSpec((lines, 2, 1, rows, pair), lambda t, s: (0, 0, t, 0, 0)),
                pl.BlockSpec((width, width), lambda t, s: (0, weights_at)),
                pl.BlockSpec((width, LANES), lambda t, s: (0, small_at)),
                pl.BlockSpec((rows, width), lambda t, s: (2 * t + s[2], 0)),
            ],
            out_specs=[pl.BlockSpec((rows, width), lambda t, s: (t, 0)), own, own],
            scratch_shapes=[pltpu.VMEM((8, width), f32)],
        ),
        out_shape=[
            jax.ShapeDtypeStruct((lines * rows, width), bf16),
            jax.ShapeDtypeStruct((rows, width), f32),
            jax.ShapeDtypeStruct((rows, width), bf16),
        ],
        compiler_params=pltpu.CompilerParams(vmem_limit_bytes=VMEM_LIMIT),
        cost_estimate=pl.CostEstimate(
            flops=2 * lines * rows * width * width, bytes_accessed=12 * 2**20, transcendentals=0
        ),
        name="join",
    )(place, outs, packed, packed, x)


def weight_sums_kernel(sums_ref, q_ref, k_ref, v_ref, gain_ref):
    groups, heads, members = sums_ref.shape[:3]
    gain = jnp.zeros(gain_ref.shape, f32)
    values = []
    for h in range(heads):
        total = jnp.zeros(sums_ref.shape[3:], f32)
        for g in range(groups):
            for member in range(members):
                total += sums_ref[g, h, member].astype(f32)
        values.append(total)
        gain += total[:, HEAD_PACK:]
        q_ref[:, h * PAIR : (h + 1) * PAIR] = total[:, :PAIR]
    gain_ref[...] = gain
    for h in range(0, heads, 2):
        one, two = values[h][:, PAIR:HEAD_PACK], values[h + 1][:, PAIR:HEAD_PACK]
        low = lower_lanes(one.shape)
        at = slice(h // 2 * PAIR, (h // 2 + 1) * PAIR)
        k_ref[:, at] = jnp.where(low, one, pltpu.roll(two, HEAD_SIZE, 1))
        v_ref[:, at] = jnp.where(low, pltpu.roll(one, HEAD_SIZE, 1), two)


def weight_sums(sums):
    rows, heads = sums.shape[3], sums.shape[1]
    return pl.pallas_call(
        weight_sums_kernel,
        out_shape=[
            jax.ShapeDtypeStruct((rows, heads * PAIR), f32),
            jax.ShapeDtypeStruct((rows, heads * HEAD_SIZE), f32),
            jax.ShapeDtypeStruct((rows, heads * HEAD_SIZE), f32),
            jax.ShapeDtypeStruct((rows, LANES), f32),
        ],
        compiler_params=pltpu.CompilerParams(vmem_limit_bytes=VMEM_LIMIT),
        cost_estimate=pl.CostEstimate(flops=2**20, bytes_accessed=2 * 2**20, transcendentals=0),
        name="weight_sums",
    )(sums)


def exchange(x, axes):
    return lax.all_to_all(x, axes, 0, 0, tiled=True)


def body(
    tokens,
    cotangent,
    segment_ids,
    routes,
    norm_attn,
    w_query,
    key_weight_matrix,
    value_weight_matrix,
    w_output,
    norm_moe,
    w_router,
    expert_in,
    expert_out,
):
    x_local = tokens[0].astype(f32)
    token_count, width = x_local.shape
    seg_row = segment_ids[0]
    group = lax.axis_index("a")
    head_axes = SEQ if lax.axis_size(SEQ) == KEY_VALUE_HEADS else ("b",)
    whole_rows = head_axes == SEQ
    span = token_count * KEY_VALUE_HEADS
    span_start = 0 if whole_rows else group * span

    def start_of_doc(ids):
        return jnp.sum((seg_row[None, :] < ids[:, None]).astype(jnp.int32), axis=1)

    seg_span = lax.dynamic_slice_in_dim(seg_row, span_start, span)
    doc_span = start_of_doc(seg_span)
    cos_span, sin_span = rotation_tables(
        span_start + jnp.arange(span, dtype=jnp.int32) - doc_span
    )
    by_block = doc_span.reshape(-1, QUERY_BLOCK)
    bounds = jnp.concatenate(
        [
            by_block[:, 0] // BLOCK,
            (by_block[:, -1] + BLOCK - 1) // BLOCK,
            jnp.full((1,), span_start // QUERY_BLOCK, jnp.int32),
        ]
    )
    doc_rows = by_block[:, None, :]

    own_rows = w_query.shape[0]
    by_head = jnp.concatenate(
        [
            w_query.astype(bf16).reshape(own_rows, KEY_VALUE_HEADS, PAIR),
            key_weight_matrix.astype(bf16).reshape(own_rows, KEY_VALUE_HEADS, HEAD_SIZE),
            value_weight_matrix.astype(bf16).reshape(own_rows, KEY_VALUE_HEADS, HEAD_SIZE),
        ],
        axis=2,
    ).reshape(own_rows, KEY_VALUE_HEADS * HEAD_PACK)
    qkv_width = KEY_VALUE_HEADS * HEAD_PACK
    first_all = gather(
        jnp.concatenate(
            [
                by_head,
                w_output.astype(bf16),
                pad_lanes(
                    jnp.concatenate(
                        [
                            w_router.astype(bf16),
                            norm_attn.astype(bf16)[:, None],
                            norm_moe.astype(bf16)[:, None],
                        ],
                        axis=1,
                    ),
                    LANES,
                ),
            ],
            axis=1,
        ),
        ALL,
    )
    experts_low = jnp.concatenate([expert_in.astype(bf16), expert_out.astype(bf16)], axis=1)
    if whole_rows:
        pieces = grid_gather(tokens[0])
        places = [piece[:2] for piece in pieces]
        blocks = tuple(piece[2] for piece in pieces)
    else:
        places = None
        blocks = (gather(tokens[0], "b").reshape((-1,) + tokens.shape[1:]),)
    first_all, experts_low, blocks, cos_span, sin_span, bounds, doc_rows = (
        lax.optimization_barrier(
            (first_all, experts_low, blocks, cos_span, sin_span, bounds, doc_rows)
        )
    )
    output_w = first_all[:, qkv_width : qkv_width + width]
    small_at = qkv_width + width
    router_w = first_all[:, small_at : small_at + E]
    gain_one_f = first_all[:, small_at + E].astype(f32)
    gain_two_f = first_all[:, small_at + E + 1].astype(f32)

    expert_ids = jnp.arange(E, dtype=jnp.int32)
    routed_own = jnp.any(routes[0][:, :, None] == expert_ids[None, None, :], axis=1)
    early = jnp.concatenate([cotangent[0], pad_lanes(routed_own.astype(bf16), LANES)], axis=1)
    early, first_all = lax.optimization_barrier((early, first_all))
    early_all = gather(early, "a")
    small_plane = lax.axis_size("b") == 2 and lax.axis_size("y") == 2
    if small_plane:
        parts = plane_gather(experts_low)
    else:
        parts = gather(experts_low, PLANE)

    place = jnp.stack([lax.axis_index(head_axes), group, lax.axis_index("b")])
    qkv, normed_span, x_span, wide_cos, wide_sin = project(
        place, places, blocks, token_count, first_all, cos_span, sin_span
    )
    if whole_rows:
        kv, kv_at = qkv, 1
    else:
        kv, kv_at = gather(qkv[:, PAIR:], "a"), 0
    attention_result, attended, log_total = attend(bounds, qkv, kv, kv_at, doc_rows)
    if small_plane:
        member = lax.axis_index("b")
        by_column = attended.reshape(GROUPS, 2, token_count, PAIR)
        other = lax.ppermute(
            lax.dynamic_index_in_dim(by_column, 1 - member, 1, False), "b", SWAP
        )
        own = lax.dynamic_index_in_dim(by_column, member, 1, False)
        pair, early_all = lax.optimization_barrier((jnp.stack([own, other]), early_all))
        outs = lax.all_gather(pair, "a", axis=0, tiled=False)
        normed_all, resid, attended_low = join(place, outs, first_all, qkv_width // width, x_span)
        normed_two = lax.dynamic_slice_in_dim(normed_all, group * token_count, token_count)
        home = jnp.stack([member * 2 + lax.axis_index("y"), lax.axis_index("c")])
        experts_all, grad_hidden = place_experts(home, parts, early_all, width)
    else:
        attended_low = (
            exchange(attended.reshape(KEY_VALUE_HEADS, token_count, PAIR), head_axes)
            .transpose(1, 0, 2)
            .reshape(token_count, QUERY_HEADS * HEAD_SIZE)
        )
        attn_out = jnp.dot(attended_low, output_w, preferred_element_type=f32)
        resid = x_local + RESIDUAL_SCALE * attn_out
        normed_two = rms_scale(resid, gain_two_f).astype(bf16)
        normed_all = gather(normed_two, "a")
        experts_all = parts.reshape(EXPERTS_HERE, width, 3 * F)
        grad_hidden = jnp.einsum(
            "td,edf->etf",
            early_all[:, :width],
            experts_all[:, :, 2 * F :],
            preferred_element_type=f32,
        )
    back_part, gates_all, gated_hidden, grad_pre = experts(
        group.reshape(1), normed_all, early_all, first_all, experts_all, grad_hidden
    )
    back_own = scatter_sum(back_part, "a").astype(f32)
    inputs = (normed_all, early_all, experts_all, gated_hidden, grad_pre)
    if small_plane:
        core = lax.axis_index("c")
        send = expert_grads((1 - core).reshape(1), 2, *inputs, False)
        arrived = [lax.ppermute(x, "c", SWAP) for x in send]
        *keep, moe_part = expert_grads(core.reshape(1), 2, *inputs, True)
        left, right = (
            halve_add(terms).reshape((2, 2) + terms[0].shape[1:]) for terms in zip(keep, arrived)
        )
        back_own, moe_part, left, right = lax.optimization_barrier(
            (back_own, moe_part, left, right)
        )
        b, y = lax.axis_index("b"), lax.axis_index("y")
        left_on = quarter(left, 1 - b, y), lax.ppermute(quarter(left, 1 - b, 1 - y), "y", SWAP)
        right_on = quarter(right, b, 1 - y), lax.ppermute(quarter(right, 1 - b, 1 - y), "b", SWAP)
    else:
        *grads, moe_part = expert_grads(jnp.zeros((1,), jnp.int32), 1, *inputs, True)
        grad_experts = jnp.concatenate(grads, axis=2)
        back_own, moe_part, grad_experts = lax.optimization_barrier(
            (back_own, moe_part, grad_experts)
        )
        grad_experts = scatter_sum(grad_experts.reshape(EXPERTS_HERE * width, 3 * F), PLANE)
    moe_sum = scatter_sum(moe_part, "a")

    grad_out = cotangent[0].astype(f32)
    gates = lax.dynamic_slice_in_dim(gates_all, group * token_count, token_count)[:, :E]
    gate_grads_own = back_own[:, width : width + E] + back_own[:, width + E : width + 2 * E]
    grad_logits = gates * (gate_grads_own - jnp.sum(gates * gate_grads_own, axis=-1, keepdims=True))
    grad_normed_two = back_own[:, :width] + jnp.dot(
        grad_logits, router_w.astype(f32).T, precision=HIGHEST_DOT
    )
    grad_router = jnp.dot(normed_two.astype(f32).T, grad_logits, precision=HIGHEST_DOT)
    grad_resid_norm, grad_gain_two = rms_back(resid, gain_two_f, grad_normed_two)
    grad_resid = grad_out + grad_resid_norm
    grad_attn_low = (RESIDUAL_SCALE * grad_resid).astype(bf16)
    grad_heads = contract_cols(grad_attn_low, output_w).astype(bf16)
    grad_mixed = exchange(
        grad_heads.reshape(token_count, KEY_VALUE_HEADS, PAIR).transpose(1, 0, 2), head_axes
    ).reshape(span, PAIR)
    if small_plane:
        left_on, right_on = halve_add(left_on), halve_add(right_on)
        left_on, right_on, attended_low, grad_router = lax.optimization_barrier(
            (left_on, right_on, attended_low, grad_router)
        )
    small = jnp.concatenate([grad_router, grad_gain_two[:, None]], axis=1)
    second_part = jnp.concatenate(
        [contract_rows(attended_low, grad_attn_low), pad_lanes(small, LANES)], axis=1
    ).astype(bf16)
    cols = second_part.shape[1]
    second_part = second_part.reshape(GROUPS, -1, own_rows, cols).transpose(1, 0, 2, 3)
    if small_plane:
        left_last = lax.ppermute(quarter(left, b, 1 - y), "y", SWAP)
        right_last = lax.ppermute(quarter(right, 1 - b, y), "b", SWAP)
        second_part, left_on, right_on, left_last, right_last, grad_mixed = (
            lax.optimization_barrier(
                (second_part, left_on, right_on, left_last, right_last, grad_mixed)
            )
        )
        left_on, right_on = lax.ppermute(left_on, "b", SWAP), lax.ppermute(right_on, "y", SWAP)
    rest = scatter_sum(second_part.reshape(-1, cols), PLANE)
    grads = attend_back(
        bounds, qkv, kv, kv_at, doc_rows, grad_mixed, attention_result, log_total,
        wide_cos, wide_sin, whole_rows,
    )
    if whole_rows:
        grad_pack = grads
    else:
        grad_kv = scatter_sum(grads[1].astype(bf16), "a").astype(f32)
        grad_pack = unrotate(grads[0], grad_kv, wide_cos, wide_sin)
    if small_plane:
        left_on, right_on, left, right, moe_sum, grad_pack = lax.optimization_barrier(
            (left_on, right_on, left, right, moe_sum, grad_pack)
        )
    first_part = head_grads(place, x_span, normed_span, first_all, grad_pack)
    rest, first_part = lax.optimization_barrier((rest, first_part))
    rest = scatter_sum(rest, "a")
    by_tokens = exchange(grad_pack.reshape(KEY_VALUE_HEADS, token_count, HEAD_PACK), head_axes)
    by_tokens, first_part = lax.optimization_barrier((by_tokens, first_part))
    sums = exchange(first_part.reshape(-1, own_rows, first_part.shape[1]), ALL)
    sums, moe_sum, resid, rest = lax.optimization_barrier((sums, moe_sum, resid, rest))
    grad_q_w, grad_k_w, grad_v_w, grad_gain_one = weight_sums(
        sums.reshape(-1, KEY_VALUE_HEADS, lax.axis_size(("y", "c")), own_rows, first_part.shape[1])
    )
    rest = rest.astype(f32)
    grad_qkv = by_tokens.transpose(1, 0, 2).reshape(token_count, qkv_width)
    grad_normed_one = contract_cols(grad_qkv, first_all[:, :qkv_width])
    grad_x_norm, _ = rms_back(x_local, gain_one_f, grad_normed_one)
    grad_input = grad_resid + grad_x_norm
    layer_sum = resid + RESIDUAL_SCALE * moe_sum.astype(f32)
    if small_plane:
        grad_experts = jnp.concatenate(
            [
                quarter(left, b, y).astype(f32) + left_last.astype(f32) + left_on.astype(f32),
                quarter(right, b, y).astype(f32) + right_last.astype(f32) + right_on.astype(f32),
            ],
            axis=1,
        )
    else:
        grad_experts = grad_experts.astype(f32)
    return (
        layer_sum.astype(bf16)[None],
        grad_input[None],
        grad_gain_one[:, 0],
        grad_q_w,
        grad_k_w,
        grad_v_w,
        rest[:, :width],
        rest[:, width + E],
        rest[:, width : width + E],
        grad_experts[:, : 2 * F],
        grad_experts[:, 2 * F :],
    )


def solution(mesh):
    seq, row = mesh.shape["seq"], mesh.shape["row"]
    cut = Mesh(mesh.devices.reshape(GROUPS, seq // GROUPS, row // 2, 2), ALL)
    token_spec = P(("y", "c"), SEQ, None)
    row_spec = P(ALL, None)
    flat_spec = P(ALL)
    in_specs = (
        token_spec,
        token_spec,
        P(("y", "c"), None),
        token_spec,
        flat_spec,
        row_spec,
        row_spec,
        row_spec,
        row_spec,
        flat_spec,
        row_spec,
        row_spec,
        row_spec,
    )
    out_specs = (
        token_spec,
        token_spec,
        flat_spec,
        row_spec,
        row_spec,
        row_spec,
        row_spec,
        flat_spec,
        row_spec,
        row_spec,
        row_spec,
    )
    return jax.shard_map(body, mesh=cut, in_specs=in_specs, out_specs=out_specs, check_vma=False)
```
